32 devices in a mesh: rep: 2 (over x), fsdp: 16 (over z, y, core).
Axes of the slice: x: 2, y: 2, z: 4, core: 2. Of those that a mesh axis runs over, the one named last changes fastest.
Arguments:
- prompt_rows: bfloat16 [8192, 1024], P(('rep', 'fsdp')), may hold values from -12 to 12
- suffix_rows: bfloat16 [8192, 1024], P(('rep', 'fsdp')), may hold values from -12 to 12
- assignment: int32 [2, 32], P('rep', 'fsdp'), may hold values from 0 to 31, each once within a row
- lengths: int32 [2, 32], P('rep', 'fsdp'), may hold values from 1 to 128, 3072 in all within a row
- attention_gain: bfloat16 [1024], P('fsdp'), may hold values from 0.5 to 1.5
- query_weight: bfloat16 [1024, 2048], P('fsdp'), may hold values from -0.1875 to 0.1875
- key_matrix: bfloat16 [1024, 1024], P('fsdp'), may hold values from -0.1875 to 0.1875
- value_matrix: bfloat16 [1024, 1024], P('fsdp'), may hold values from -0.1875 to 0.1875
- query_gain: bfloat16 [128], P('fsdp'), may hold values from 0.5 to 1.5
- key_norm_gain: bfloat16 [128], P('fsdp'), may hold values from 0.5 to 1.5
- out_weight: bfloat16 [2048, 1024], P('fsdp'), may hold values from -2 to 2
- mlp_gain: bfloat16 [1024], P('fsdp'), may hold values from 0.5 to 1.5
- gate_weight: bfloat16 [1024, 3072], P('fsdp'), may hold values from -0.1875 to 0.1875
- up_weight: bfloat16 [1024, 3072], P('fsdp'), may hold values from -0.1875 to 0.1875
- down_weight: bfloat16 [3072, 1024], P('fsdp'), may hold values from -0.109375 to 0.109375
- prompt_cotangent: bfloat16 [8192, 1024], P(('rep', 'fsdp')), may hold values from -18 to 18
- suffix_cotangent: bfloat16 [8192, 1024], P(('rep', 'fsdp')), may hold values from -18 to 18
Outputs:
- prompt_mixed: bfloat16 [8192, 1024], P(('rep', 'fsdp'))
- suffix_mixed: bfloat16 [8192, 1024], P(('rep', 'fsdp'))
- prompt_grad: float32 [8192, 1024], P(('rep', 'fsdp'))
- suffix_grad: float32 [8192, 1024], P(('rep', 'fsdp'))
- grad_attention_gain: float32 [1024], P('fsdp')
- grad_query_weight: float32 [1024, 2048], P('fsdp')
- grad_key_weight: float32 [1024, 1024], P('fsdp')
- grad_value_weight: float32 [1024, 1024], P('fsdp')
- grad_query_gain: float32 [128], P('fsdp')
- grad_key_gain: float32 [128], P('fsdp')
- grad_out_weight: float32 [2048, 1024], P('fsdp')
- grad_mlp_gain: float32 [1024], P('fsdp')
- grad_gate_weight: float32 [1024, 3072], P('fsdp')
- grad_up_weight: float32 [1024, 3072], P('fsdp')
- grad_down_weight: float32 [3072, 1024], P('fsdp')
- token_norms: float32 [3], replicated
The draws below stay inside these ranges and needn't reach their ends.
Inputs may be any that keep to these rules, and one draw needn't show every extreme that they name: Each row of assignment is a permutation; so every prompt has exactly 8 continuation slots. Each row of lengths sums to 3072 and holds 128 at least once.
All inputs are finite; a program needn't handle non-finite values. No bound on the sum of `lengths` on one device may be relied on, other than what follows from the above.
Results may differ from the reference program's by a relative error of at most 0.024.
Values may be sent and summed in bfloat16 or wider, within the bound.
A program may use at most 256 MiB of HBM per device.

```python
import math
import jax
import jax.numpy as jnp
import numpy as np
from jax import lax

MODEL_WIDTH = 1024
QUERY_HEADS = 16
KEY_VALUE_HEADS = 8
HEAD_SIZE = 128
FF = 3072
PROMPT_LENGTH = 1024
CONT = 8
CONTINUATION_LEN = 128
GRP = 4
REPLICAS = 2
SLOTS = 32
PROMPT_ROWS = 8192
SUFFIX_ROWS = 8192


def ramped_rows(key, count_rows, shown_top, shown_clip):
    base = jnp.clip(jax.random.normal(key, (count_rows, MODEL_WIDTH), jnp.float32), -shown_clip, shown_clip)
    top_factor = shown_top
    ramp = 1.0 + (top_factor - 1.0) * jnp.arange(count_rows, dtype=jnp.float32) / max(count_rows - 1, 1)
    return (base * ramp[:, None]).astype(jnp.bfloat16)


def draw_prompt_rows(key, part):
    return ramped_rows(jax.random.fold_in(key, 5), PROMPT_ROWS, 3.0, 4.0)


def draw_suffix_rows(key, part):
    return ramped_rows(jax.random.fold_in(key, 7), SUFFIX_ROWS, 3.0, 4.0)


def draw_prompt_cotangent(key, part):
    return ramped_rows(jax.random.fold_in(key, 11), PROMPT_ROWS, 6.0, 3.0)


def draw_suffix_cotangent(key, part):
    return ramped_rows(jax.random.fold_in(key, 23), SUFFIX_ROWS, 6.0, 3.0)


def steps_of(key, extent, pieces, smallest, top_value):
    factor_of, own = 1.0, jax.random.fold_in(key, 6)
    for position, parts in pieces:
        draws = jnp.exp(jax.random.uniform(jax.random.fold_in(own, position), (parts,), jnp.float32, smallest / len(pieces), top_value / len(pieces)))
        factor_of = factor_of * jnp.repeat(draws, extent[position] // parts).reshape([-1 if axis == position else 1 for axis in range(len(extent))])
    return factor_of


def length_profile(number_of, total, most, skew):
    weights = [(1 << 20) // math.isqrt(grade ** skew) + 1 for grade in range(2, number_of + 1)]
    rest, given = total - most - (number_of - 1), [1] * (number_of - 1)
    while rest > 0:
        candidates = [i for i in range(number_of - 1) if given[i] < most]
        whole, remaining = sum([weights[i] for i in candidates]), rest
        for i in candidates:
            extra = min(most - given[i], max(1, remaining * weights[i] // whole), rest)
            given[i] = given[i] + extra
            rest = rest - extra
    return np.array([most] + given)


def ragged(own_key, count, total, limit, lean):
    if count == 2:
        one = jax.random.randint(own_key, (), max(1, total - limit), min(limit, total - 1) + 1)
        return jnp.stack([one, total - one])
    sizes = jnp.asarray(length_profile(count, total, limit, lean), jnp.int32)
    pairs = (count - 1) // 2
    giver, sink = sizes[1:1 + 2 * pairs:2], sizes[2:2 + 2 * pairs:2]
    room = jnp.minimum(giver - 1, limit - sink)
    shifted = jax.random.randint(jax.random.fold_in(own_key, 1), (pairs,), 0, 1 << 20) % (room + 1)
    sizes = sizes.at[1:1 + 2 * pairs:2].set(giver - shifted).at[2:2 + 2 * pairs:2].set(sink + shifted)
    return sizes[jax.random.permutation(jax.random.fold_in(own_key, 2), count)]


def scatter_about(stream_key, shape, width, bound, split=(), held_as=jnp.bfloat16):
    values = jax.random.normal(stream_key, shape, jnp.float32) * width
    if len(split) > 0:
        values = steps_of(stream_key, shape, split, -0.22, 0.18) * values
    return jnp.clip(values, min=-bound, max=bound).astype(held_as)


def setup_inputs(seed: int = 0) -> dict:
    seeds = jax.random.split(jax.random.key(seed), 18)
    return {
        "prompt_rows": draw_prompt_rows(jax.random.fold_in(seeds[17], 71), 0),
        "suffix_rows": draw_suffix_rows(jax.random.fold_in(seeds[17], 71), 0),
        "assignment": jax.vmap(lambda own: jax.random.permutation(own, SLOTS))(jax.random.split(seeds[2], REPLICAS)).reshape((REPLICAS, SLOTS)).astype(jnp.int32),
        "lengths": jax.vmap(lambda own: ragged(own, SLOTS, SLOTS * CONTINUATION_LEN * 3 // 4, CONTINUATION_LEN, 1))(jax.random.split(seeds[3], REPLICAS)).reshape((REPLICAS, SLOTS)).astype(jnp.int32),
        "attention_gain": jnp.clip(1.0 + 0.1 * jax.random.normal(seeds[4], (MODEL_WIDTH,), jnp.float32), 0.5, 1.5).astype(jnp.bfloat16),
        "query_weight": scatter_about(seeds[5], (MODEL_WIDTH, QUERY_HEADS * HEAD_SIZE), MODEL_WIDTH ** -0.5, 0.1875, ((0, 16),)),
        "key_matrix": scatter_about(seeds[6], (MODEL_WIDTH, KEY_VALUE_HEADS * HEAD_SIZE), MODEL_WIDTH ** -0.5, 0.1875, ((0, 16),)),
        "value_matrix": scatter_about(seeds[7], (MODEL_WIDTH, KEY_VALUE_HEADS * HEAD_SIZE), MODEL_WIDTH ** -0.5, 0.1875, ((0, 16),)),
        "query_gain": jnp.clip(1.0 + 0.1 * jax.random.normal(seeds[8], (HEAD_SIZE,), jnp.float32), 0.5, 1.5).astype(jnp.bfloat16),
        "key_norm_gain": jnp.clip(1.0 + 0.1 * jax.random.normal(seeds[9], (HEAD_SIZE,), jnp.float32), 0.5, 1.5).astype(jnp.bfloat16),
        "out_weight": scatter_about(seeds[10], (QUERY_HEADS * HEAD_SIZE, MODEL_WIDTH), (max(4, QUERY_HEADS * HEAD_SIZE // 256)) ** -0.5, 2.0, ((0, 16),)),
        "mlp_gain": jnp.clip(1.0 + 0.1 * jax.random.normal(seeds[11], (MODEL_WIDTH,), jnp.float32), 0.5, 1.5).astype(jnp.bfloat16),
        "gate_weight": scatter_about(seeds[12], (MODEL_WIDTH, FF), MODEL_WIDTH ** -0.5, 0.1875, ((0, 16),)),
        "up_weight": scatter_about(seeds[13], (MODEL_WIDTH, FF), MODEL_WIDTH ** -0.5, 0.1875, ((0, 16),)),
        "down_weight": scatter_about(seeds[14], (FF, MODEL_WIDTH), FF ** -0.5, 0.109375, ((0, 16),)),
        "prompt_cotangent": draw_prompt_cotangent(jax.random.fold_in(seeds[17], 71), 0),
        "suffix_cotangent": draw_suffix_cotangent(jax.random.fold_in(seeds[17], 71), 0),
    }


norm_epsilon = 1e-06
rope_theta = 1000000.0
masked_score = -1e+30

@jax.custom_vjp
def reduced_input(v):
    return lax.optimization_barrier(v.astype(jnp.bfloat16)).astype(jnp.float32)

@jax.custom_vjp
def reduced_pullback(v):
    return v

def low_keep(v):
    return (reduced_input(v), None)

def low_pass(kept, grad):
    return (grad,)

def back_keep(v):
    return (v, None)

def back_low(kept, grad):
    return (reduced_input(grad),)
reduced_input.defvjp(low_keep, low_pass)
reduced_pullback.defvjp(back_keep, back_low)

def root_mean_scale(values, gain_vector):
    return values * lax.rsqrt(lax.optimization_barrier(jnp.mean(values * values, axis=-1, keepdims=True)) + norm_epsilon) * gain_vector

def rotary_embed(values, token_positions):
    half_size = values.shape[-1] // 2
    inverse = rope_theta ** (jnp.arange(half_size, dtype=jnp.float32) * (-2.0 / values.shape[-1]))
    angles = token_positions.astype(jnp.float32)[:, None] * inverse[None, :]
    cosine = jnp.cos(angles)[:, None, :]
    sine_part = jnp.sin(angles)[:, None, :]
    first_half = values[..., :half_size]
    second_half = values[..., half_size:]
    return jnp.concatenate([first_half * cosine - second_half * sine_part, second_half * cosine + first_half * sine_part], axis=-1)

def matrix_product(left, right):
    return jnp.dot(left, right, precision=lax.Precision.HIGHEST)

def attend(query_rotated, key_rotated, value_matrix_rows, allowed):
    count_of_rows = query_rotated.shape[0]
    grouped_heads = query_rotated.reshape(count_of_rows, KEY_VALUE_HEADS, QUERY_HEADS // KEY_VALUE_HEADS, HEAD_SIZE)
    scores = jnp.einsum('rhgd,khd->hgrk', grouped_heads, key_rotated, precision=lax.Precision.HIGHEST)
    scores = reduced_pullback(scores * HEAD_SIZE ** (-0.5))
    scores = jnp.where(allowed, scores, masked_score)
    weights = reduced_input(jax.nn.softmax(scores, axis=-1))
    result = jnp.einsum('hgrk,khd->rhgd', weights, value_matrix_rows, precision=lax.Precision.HIGHEST)
    return result.reshape(count_of_rows, QUERY_HEADS * HEAD_SIZE)

def layer(prompt_in, suffix_in, params, owning_group, slot_validity):
    attention_gain, query_weight, key_matrix, value_matrix, query_gain, key_norm_gain, out_weight, mlp_gain, gate_weight, up_weight, down_weight = params
    prompt_count = prompt_in.shape[0]
    suffix_total = suffix_in.shape[0]
    total_groups = prompt_count // PROMPT_LENGTH
    slot_count = suffix_total // CONTINUATION_LEN
    rows_all = jnp.concatenate([prompt_in, suffix_in], 0)
    hidden_state = reduced_input(root_mean_scale(rows_all, attention_gain))
    query_pre = reduced_pullback(matrix_product(hidden_state, query_weight))
    key_before_norm = reduced_pullback(matrix_product(hidden_state, key_matrix))
    value_matrix_rows = reduced_input(reduced_pullback(matrix_product(hidden_state, value_matrix))).reshape(-1, KEY_VALUE_HEADS, HEAD_SIZE)
    token_positions = jnp.concatenate([jnp.arange(prompt_count, dtype=jnp.int32) % PROMPT_LENGTH, PROMPT_LENGTH + jnp.arange(suffix_total, dtype=jnp.int32) % CONTINUATION_LEN])
    query_rotated = reduced_input(rotary_embed(root_mean_scale(query_pre.reshape(-1, QUERY_HEADS, HEAD_SIZE), query_gain), token_positions))
    key_rotated = reduced_input(rotary_embed(root_mean_scale(key_before_norm.reshape(-1, KEY_VALUE_HEADS, HEAD_SIZE), key_norm_gain), token_positions))
    prompt_query = query_rotated[:prompt_count].reshape(total_groups, PROMPT_LENGTH, QUERY_HEADS, HEAD_SIZE)
    prompt_key_rows = key_rotated[:prompt_count].reshape(total_groups, PROMPT_LENGTH, KEY_VALUE_HEADS, HEAD_SIZE)
    prompt_value_rows = value_matrix_rows[:prompt_count].reshape(total_groups, PROMPT_LENGTH, KEY_VALUE_HEADS, HEAD_SIZE)
    causal = jnp.arange(PROMPT_LENGTH, dtype=jnp.int32)[None, :] <= jnp.arange(PROMPT_LENGTH, dtype=jnp.int32)[:, None]

    def prompt_attend(block_items):
        return attend(block_items[0], block_items[1], block_items[2], causal)
    prompt_attended = lax.map(jax.checkpoint(prompt_attend), (prompt_query, prompt_key_rows, prompt_value_rows))
    slot_causal = jnp.arange(CONTINUATION_LEN, dtype=jnp.int32)[None, :] <= jnp.arange(CONTINUATION_LEN, dtype=jnp.int32)[:, None]

    def slot_attention(block_items):
        query_slot, key_slot, value_slot, group_index, valid_slot = block_items
        key_prompt = lax.dynamic_index_in_dim(prompt_key_rows, group_index, 0, keepdims=False)
        value_prompt = lax.dynamic_index_in_dim(prompt_value_rows, group_index, 0, keepdims=False)
        keys_all = jnp.concatenate([key_prompt, key_slot], 0)
        values_all = jnp.concatenate([value_prompt, value_slot], 0)
        allowed = jnp.concatenate([jnp.ones((CONTINUATION_LEN, PROMPT_LENGTH), dtype=bool), slot_causal & valid_slot[None, :]], axis=1)
        return attend(query_slot, keys_all, values_all, allowed)
    continuation_attended = lax.map(jax.checkpoint(slot_attention), (query_rotated[prompt_count:].reshape(slot_count, CONTINUATION_LEN, QUERY_HEADS, HEAD_SIZE), key_rotated[prompt_count:].reshape(slot_count, CONTINUATION_LEN, KEY_VALUE_HEADS, HEAD_SIZE), value_matrix_rows[prompt_count:].reshape(slot_count, CONTINUATION_LEN, KEY_VALUE_HEADS, HEAD_SIZE), owning_group, slot_validity))
    attended = jnp.concatenate([prompt_attended.reshape(-1, QUERY_HEADS * HEAD_SIZE), continuation_attended.reshape(-1, QUERY_HEADS * HEAD_SIZE)], 0)
    attended = reduced_input(reduced_pullback(attended))
    attn_out = reduced_pullback(matrix_product(attended, out_weight))
    residual = rows_all + attn_out
    hidden_two = reduced_input(root_mean_scale(residual, mlp_gain))
    gate_pre = reduced_pullback(matrix_product(hidden_two, gate_weight))
    up_pre = reduced_pullback(matrix_product(hidden_two, up_weight))
    act_rows = reduced_input(jax.nn.silu(gate_pre) * up_pre)
    mlp_out = reduced_pullback(matrix_product(act_rows, down_weight))
    return (residual + mlp_out, residual)

def reference(prompt_rows, suffix_rows, assignment, lengths, attention_gain, query_weight, key_matrix, value_matrix, query_gain, key_norm_gain, out_weight, mlp_gain, gate_weight, up_weight, down_weight, prompt_cotangent, suffix_cotangent):
    params = tuple((weight.astype(jnp.float32) for weight in (attention_gain, query_weight, key_matrix, value_matrix, query_gain, key_norm_gain, out_weight, mlp_gain, gate_weight, up_weight, down_weight)))
    slot_validity = jnp.arange(CONTINUATION_LEN, dtype=jnp.int32)[None, :] < lengths.reshape(-1)[:, None]
    owning_group = (jnp.arange(REPLICAS, dtype=jnp.int32)[:, None] * GRP + assignment // CONT).reshape(-1).astype(jnp.int32)

    def forward(prompt_in, suffix_in, weights):
        return layer(prompt_in, suffix_in, weights, owning_group, slot_validity)
    mixed_rows, pullback, residual = jax.vjp(forward, prompt_rows.astype(jnp.float32), suffix_rows.astype(jnp.float32), params, has_aux=True)
    valid_rows = jnp.concatenate([jnp.ones((PROMPT_ROWS,), jnp.float32), slot_validity.reshape(-1).astype(jnp.float32)])
    cotangent = jnp.concatenate([prompt_cotangent, suffix_cotangent], 0).astype(jnp.float32) * valid_rows[:, None]
    d_prompt, d_suffix, d_params = pullback(cotangent)
    d_rows = jnp.concatenate([d_prompt, d_suffix], 0)
    valid_total = jnp.sum(valid_rows) * MODEL_WIDTH
    token_norms = jnp.sqrt(jnp.stack([jnp.sum(valid_rows[:, None] * mixed_rows * mixed_rows), jnp.sum(valid_rows[:, None] * residual * residual), jnp.sum(valid_rows[:, None] * d_rows * d_rows)]) / valid_total)
    return (mixed_rows[:PROMPT_ROWS].astype(jnp.bfloat16), mixed_rows[PROMPT_ROWS:].astype(jnp.bfloat16), d_prompt, d_suffix, d_params[0], d_params[1], d_params[2], d_params[3], d_params[4], d_params[5], d_params[6], d_params[7], d_params[8], d_params[9], d_params[10], token_norms)
```

```python
from functools import partial

import jax
import jax.numpy as jnp
from jax import lax
from jax.experimental import pallas as pl
from jax.experimental.pallas import tpu as pltpu
from jax.sharding import PartitionSpec as P

MODEL_WIDTH = 1024
QUERY_HEADS = 16
KEY_VALUE_HEADS = 8
HEAD_SIZE = 128
PROMPT_LENGTH = 1024
CONT = 8
CONTINUATION_LEN = 128


norm_epsilon = 1e-06
rope_theta = 1000000.0
masked_score = -1e30


MESH = pl.DeviceIdType.MESH

def position(n):
    rep = lax.axis_index("rep")
    rank = lax.axis_index("fsdp")
    return rep, rank // 4, (rank // 2) % 2, rank % 2

def gather_kernel(n, m, *refs):
    A = n // 4
    own, tile = refs[:m], refs[m]
    full, tiles = refs[m + 1:2 * m + 1], refs[2 * m + 1]
    zs, zr, s2s, s2r, s3s, s3r, cs, cr, ls, ts, tr = refs[2 * m + 2:]
    rep, a, b, c = position(n)
    h = rep % 2
    mate = rep + 1 - 2 * h
    def dev(r, a, b, c):
        return (r, (a * 2 + b) * 2 + c)
    barrier = pltpu.get_barrier_semaphore()
    me = (a * 2 + b) * 2 + c
    peers = [(rep, (me + d) % n) for d in range(1, n)] + [dev(mate, a, b, c)]
    for p in peers:
        pl.semaphore_signal(barrier, inc=1, device_id=p, device_id_type=MESH)
    pl.semaphore_wait(barrier, len(peers))

    def local(i):
        return pltpu.make_async_copy(own[i].at[:, h], full[i].at[a, b, c, :, h], ls.at[i])
    def zc(i, d):
        return pltpu.make_async_remote_copy(own[i].at[:, h], full[i].at[a, b, c, :, h], zs.at[i, d - 1], zr.at[i, d - 1],
            device_id=dev(rep, (a + d) % A, b, c), device_id_type=MESH)
    def pair(ref, ss, rs, to):
        return pltpu.make_async_remote_copy(ref, ref, ss, rs, device_id=to, device_id_type=MESH)
    ydev, xdev, cdev = dev(rep, a, 1 - b, c), dev(mate, a, b, c), dev(rep, a, b, 1 - c)
    def s2(i):
        return [pair(full[i].at[:, b, c, 0, h], s2s.at[i, 0], s2r.at[i, 0], ydev),
                pair(full[i].at[:, b, c, 1, h], s2s.at[i, 1], s2r.at[i, 1], xdev)]
    def s3(i):
        return [pair(full[i].at[:, :, c, 0, h], s3s.at[i, 0], s3r.at[i, 0], xdev),
                pair(full[i].at[:, b, c, 1], s3s.at[i, 1], s3r.at[i, 1], ydev)]
    def s4(i):
        return [pair(full[i].at[:, :, c], cs.at[i], cr.at[i], cdev)]
    def share(d):
        return pltpu.make_async_remote_copy(tile, tiles.at[me], ts.at[d - 1], tr.at[d - 1], device_id=(rep, (me + d) % n), device_id_type=MESH)
    for d in range(1, n):
        share(d).start()
    tiles[me] = tile[...]
    for i in range(m):
        local(i).start()
        for d in range(1, A):
            zc(i, d).start()
    for t in range(m + 3):
        if t < m:
            local(t).wait()
            for d in range(1, A):
                zc(t, d).wait_recv()
            for q in s2(t): q.start()
        if 0 <= t - 1 < m:
            for q in s2(t - 1): q.wait_recv()
            for q in s3(t - 1): q.start()
        if 0 <= t - 2 < m:
            for q in s3(t - 2): q.wait_recv()
            for q in s4(t - 2): q.start()
        if 0 <= t - 3 < m:
            for q in s4(t - 3): q.wait_recv()
    for d in range(1, n):
        share(d).wait()
    for t in range(m):
        for d in range(1, A):
            zc(t, d).wait_send()
        for q in s2(t) + s3(t) + s4(t):
            q.wait_send()

def gather(shards, tile, n, cid):
    m = len(shards)
    A = n // 4
    views = [s.reshape(2, 2, s.shape[0] // 4, s.shape[1]) for s in shards]
    outs = [jax.ShapeDtypeStruct((A, 2, 2) + v.shape, v.dtype) for v in views] + [jax.ShapeDtypeStruct((n,) + tile.shape, tile.dtype)]
    full = pl.pallas_call(
        partial(gather_kernel, n, m),
        out_shape=outs,
        in_specs=[pl.BlockSpec(memory_space=pltpu.VMEM)] * (m + 1),
        out_specs=[pl.BlockSpec(memory_space=pl.ANY)] * m + [pl.BlockSpec(memory_space=pltpu.VMEM)],
        scratch_shapes=[pltpu.SemaphoreType.DMA((m, A - 1))] * 2 + [pltpu.SemaphoreType.DMA((m, 2))] * 4 + [pltpu.SemaphoreType.DMA((m,))] * 3 + [pltpu.SemaphoreType.DMA((n - 1,))] * 2,
        compiler_params=pltpu.CompilerParams(collective_id=cid, has_side_effects=True),
        name="gather",
    )(*views, tile)
    return [f.reshape(-1, s.shape[1]) for f, s in zip(full, shards)], full[m]


def add_rows(count, out, first, second, step=None):
    def one(j, _):
        o = out(j)
        total = first(j)[...].astype(jnp.float32)
        for s in second:
            total = total + s(j)[...].astype(jnp.float32)
        o[...] = total.astype(o.dtype)
        return 0
    lax.fori_loop(0, count, one, 0)

def scatter_kernel(n, R, m, has_vec, *refs):
    A = n // 4
    bits = R.bit_length() - 1
    it = iter(refs)
    take = lambda k: [next(it) for _ in range(k)]
    grads = take(m)
    vec = next(it) if has_vec else None
    outs = take(m)
    vout = next(it) if has_vec else None
    own, b1, b2y, b2x, b3, b4, b5 = [take(m) for _ in range(7)]
    s4 = take(m)
    vb = next(it) if has_vec else None
    vz = next(it) if has_vec else None
    ls, s1s, s1r, s2s, s2r, s3s, s3r, s4s, s4r, s5s, s5r, ws = take(12)
    if has_vec:
        vs, vr = take(2)
    rep, a, b, c = position(n)
    h = rep % 2
    mate = rep + 1 - 2 * h
    def dev(r, a, b, c):
        return (r, (a * 2 + b) * 2 + c)
    ydev, xdev, cdev = dev(rep, a, 1 - b, c), dev(mate, a, b, c), dev(rep, a, b, 1 - c)
    zdev = lambda d: dev(rep, (a + d) % A, b, c)
    def flip(bit):
        w = 1 << bit
        return dev(rep + w - 2 * w * ((rep // w) % 2), a, b, c)
    barrier = pltpu.get_barrier_semaphore()
    peers = [zdev(d) for d in range(1, A)] + [ydev, xdev, cdev] + [flip(k) for k in range(1, bits)]
    for p in peers:
        pl.semaphore_signal(barrier, inc=1, device_id=p, device_id_type=MESH)
    pl.semaphore_wait(barrier, len(peers))
    def rc(src, dst, ss, rs, to):
        return pltpu.make_async_remote_copy(src, dst, ss, rs, device_id=to, device_id_type=MESH)
    def load(i): return pltpu.make_async_copy(grads[i].at[:, :, c], own[i], ls.at[i])
    def S1(i): return [rc(grads[i].at[:, :, 1 - c], b1[i], s1s.at[i], s1r.at[i], cdev)]
    def S2(i): return [rc(b1[i].at[:, 1 - b, 0], b2y[i], s2s.at[i, 0], s2r.at[i, 0], ydev),
                       rc(b1[i].at[:, :, 1, 1 - h], b2x[i], s2s.at[i, 1], s2r.at[i, 1], xdev)]
    def S3(i): return [rc(b2y[i].at[:, 1 - h], b3[i].at[0], s3s.at[i, 0], s3r.at[i, 0], xdev),
                       rc(b2x[i].at[:, 1 - b], b3[i].at[1], s3s.at[i, 1], s3r.at[i, 1], ydev)]
    def S4(i): return [rc(b3[i].at[:, (a + d) % A], b4[i].at[d - 1], s4s.at[i, d - 1], s4r.at[i, d - 1], zdev(d)) for d in range(1, A)]
    def S5(i, k): return rc(s4[i].at[0] if k == bits - 1 else s4[i].at[k], b5[i].at[k], s5s.at[i, k], s5r.at[i, k], xdev if k == bits - 1 else flip(k + 1))
    def put(i, k): return pltpu.make_async_copy((s4[i].at[0] if bits == 1 else s4[i].at[bits - 1]) if k == 0 else b5[i].at[bits - 1], outs[i].at[:, h if k == 0 else 1 - h], ws.at[i, k])
    for i in range(m):
        load(i).start()
        for q in S1(i): q.start()
    if has_vec:
        rounds = [cdev, ydev, xdev] + [flip(k) for k in range(1, bits)]
        vb[0] = vec[...]
        for k, to in enumerate(rounds):
            q = rc(vb.at[2 * k], vb.at[2 * k + 1], vs.at[k], vr.at[k], to)
            q.start(); q.wait()
            vb[2 * k + 2] = vb[2 * k] + vb[2 * k + 1]
        last = 2 * len(rounds)
        nr = len(rounds)
        qs = [rc(vb.at[last], vz.at[a], vs.at[nr + d - 1], vr.at[nr + d - 1], zdev(d)) for d in range(1, A)]
        for q in qs: q.start()
        vz[a] = vb[last]
        for q in qs: q.wait()
        total = vz[0]
        for k in range(1, A):
            total = total + vz[k]
        vout[...] = total
    for t in range(m + 4):
        i = t
        if t < m:
            load(i).wait()
            for q in S1(i): q.wait_recv()
            add_rows(A * 2 * 4, lambda j, i=i: b1[i].at[j // 8, (j // 4) % 2, (j // 2) % 2, j % 2],
                     lambda j, i=i: b1[i].at[j // 8, (j // 4) % 2, (j // 2) % 2, j % 2],
                     [lambda j, i=i: own[i].at[j // 8, (j // 4) % 2, (j // 2) % 2, j % 2]])
            for q in S2(i): q.start()
        i = t - 1
        if 0 <= i < m:
            for q in S2(i): q.wait_recv()
            add_rows(A * 2, lambda j, i=i: b2y[i].at[j // 2, j % 2], lambda j, i=i: b2y[i].at[j // 2, j % 2],
                     [lambda j, i=i: b1[i].at[j // 2, b, 0, j % 2]])
            add_rows(A * 2, lambda j, i=i: b2x[i].at[j // 2, j % 2], lambda j, i=i: b2x[i].at[j // 2, j % 2],
                     [lambda j, i=i: b1[i].at[j // 2, j % 2, 1, h]])
            for q in S3(i): q.start()
        i = t - 2
        if 0 <= i < m:
            for q in S3(i): q.wait_recv()
            add_rows(A, lambda j, i=i: b3[i].at[0, j], lambda j, i=i: b3[i].at[0, j], [lambda j, i=i: b2y[i].at[j, h]])
            add_rows(A, lambda j, i=i: b3[i].at[1, j], lambda j, i=i: b3[i].at[1, j], [lambda j, i=i: b2x[i].at[j, b]])
            for q in S4(i): q.start()
        i = t - 3
        if 0 <= i < m:
            for q in S4(i): q.wait_recv()
            add_rows(2, lambda j, i=i: s4[i].at[0, j], lambda j, i=i: b3[i].at[j, a], [lambda j, i=i, d=d: b4[i].at[d, j] for d in range(A - 1)])
            for k in range(bits - 1):
                q = S5(i, k); q.start(); q.wait()
                add_rows(2, lambda j, i=i, k=k: s4[i].at[k + 1, j], lambda j, i=i, k=k: s4[i].at[k, j], [lambda j, i=i, k=k: b5[i].at[k, j]])
            rc(s4[i].at[bits - 1], b5[i].at[bits - 1], s5s.at[i, bits - 1], s5r.at[i, bits - 1], xdev).start()
            put(i, 0).start()
        i = t - 4
        if 0 <= i < m:
            rc(s4[i].at[bits - 1], b5[i].at[bits - 1], s5s.at[i, bits - 1], s5r.at[i, bits - 1], xdev).wait_recv()
            put(i, 1).start()
    for i in range(m):
        for q in S1(i) + S2(i) + S3(i) + S4(i): q.wait_send()
        rc(s4[i].at[bits - 1], b5[i].at[bits - 1], s5s.at[i, bits - 1], s5r.at[i, bits - 1], xdev).wait_send()
        put(i, 0).wait(); put(i, 1).wait()

def scatter(grads, n, R, cid, vec=None):
    m, A, bits = len(grads), n // 4, R.bit_length() - 1
    views = [g.reshape(A, 2, 2, 2, 2, g.shape[0] // (4 * n), g.shape[1]) for g in grads]
    sub = [v.shape[-2:] for v in views]
    bf = jnp.bfloat16
    V, D = pltpu.VMEM, pltpu.SemaphoreType.DMA
    scratch = ([V((A, 2, 2, 2) + s, bf) for s in sub] * 2 + [V((A, 2) + s, bf) for s in sub] * 2 + [V((2, A) + s, bf) for s in sub]
        + [V((A - 1, 2) + s, bf) for s in sub] + [V((bits, 2) + s, bf) for s in sub] + [V((bits, 2) + s, bf) for s in sub])
    ins, ispec = list(views), [pl.BlockSpec(memory_space=pl.ANY)] * m
    outs, ospec = [jax.ShapeDtypeStruct((2, 2) + s, bf) for s in sub], [pl.BlockSpec(memory_space=pl.ANY)] * m
    sems = [D((m,)), D((m,)), D((m,)), D((m, 2)), D((m, 2)), D((m, 2)), D((m, 2)), D((m, A - 1)), D((m, A - 1)), D((m, bits)), D((m, bits)), D((m, 2))]
    if vec is not None:
        ins.append(vec); ispec.append(pl.BlockSpec(memory_space=pltpu.VMEM))
        outs.append(jax.ShapeDtypeStruct(vec.shape, vec.dtype)); ospec.append(pl.BlockSpec(memory_space=pltpu.VMEM))
        scratch += [V((2 * (2 + bits) + 1,) + vec.shape, vec.dtype), V((A,) + vec.shape, vec.dtype)]
        sems += [D((2 + bits + A - 1,))] * 2
    res = pl.pallas_call(partial(scatter_kernel, n, R, m, vec is not None), out_shape=outs, in_specs=ispec, out_specs=ospec,
        scratch_shapes=scratch + sems,
        compiler_params=pltpu.CompilerParams(collective_id=cid, has_side_effects=True, vmem_limit_bytes=60 << 20),
        name="scatter")(*ins)
    shards = [r.reshape(-1, r.shape[-1]) for r in res[:m]]
    return (shards, res[m]) if vec is not None else shards


def as_sent(shard):
    return jax.tree.map(lambda a: a.astype(jnp.bfloat16) if a.dtype == jnp.float32 else a, shard)


def root_mean_scale(values, gain_vector):
    return (
        values
        * lax.rsqrt(jnp.mean(values * values, axis=-1, keepdims=True) + norm_epsilon)
        * gain_vector
    )


def rotary_embed(values, token_positions):
    half_size = values.shape[-1] // 2
    inverse = rope_theta ** (jnp.arange(half_size, dtype=jnp.float32) * (-2.0 / values.shape[-1]))
    angles = token_positions.astype(jnp.float32)[:, None] * inverse[None, :]
    cosine = jnp.cos(angles)[:, None, :]
    sine_part = jnp.sin(angles)[:, None, :]
    first_half = values[..., :half_size]
    second_half = values[..., half_size:]
    return jnp.concatenate(
        [
            first_half * cosine - second_half * sine_part,
            second_half * cosine + first_half * sine_part,
        ],
        axis=-1,
    )


def query_key(token_positions, query_pre, key_before_norm, query_scale, key_norm_scale):
    count_of_rows = query_pre.shape[0]
    query_rotated = rotary_embed(
        root_mean_scale(query_pre.reshape(count_of_rows, QUERY_HEADS, HEAD_SIZE), query_scale),
        token_positions,
    )
    key_rotated = rotary_embed(
        root_mean_scale(
            key_before_norm.reshape(count_of_rows, KEY_VALUE_HEADS, HEAD_SIZE), key_norm_scale
        ),
        token_positions,
    )
    return (query_rotated, key_rotated)


def swiglu(gate_pre, up_pre):
    return jax.nn.silu(gate_pre) * up_pre


def unit_scores(grouped_query, key_block):
    return jnp.einsum(
        "rhgd,khd->hgrk", grouped_query, key_block, preferred_element_type=jnp.float32
    ) * HEAD_SIZE ** (-0.5)


def unit_forward(grouped_query, key_block, value_block, allowed):
    scores = unit_scores(grouped_query, key_block)
    masked = jnp.where(allowed, scores, masked_score)
    top_score = jnp.max(masked, axis=-1)
    total = jnp.sum(jnp.where(allowed, jnp.exp(masked - top_score[..., None]), 0.0), axis=-1)
    log_total = top_score + jnp.log(total)
    probs_low = jnp.where(allowed, jnp.exp(scores - log_total[..., None]), 0.0).astype(jnp.bfloat16)
    result = jnp.einsum(
        "hgrk,khd->rhgd", probs_low, value_block, preferred_element_type=jnp.float32
    )
    return (result, log_total)


def unit_backward(
    grouped_query,
    key_block,
    value_block,
    allowed,
    log_total,
    grad_attended_per_group,
    row_difference,
):
    scores = unit_scores(grouped_query, key_block)
    probs_wide = jnp.where(allowed, jnp.exp(scores - log_total[..., None]), 0.0)
    probs_low = probs_wide.astype(jnp.bfloat16)
    d_value_block = jnp.einsum(
        "hgrk,rhgd->khd", probs_low, grad_attended_per_group, preferred_element_type=jnp.float32
    )
    d_probs = jnp.einsum(
        "rhgd,khd->hgrk", grad_attended_per_group, value_block, preferred_element_type=jnp.float32
    )
    d_scores = (probs_wide * (d_probs - row_difference[..., None])).astype(jnp.bfloat16)
    d_query = jnp.einsum(
        "hgrk,khd->rhgd", d_scores, key_block, preferred_element_type=jnp.float32
    ) * HEAD_SIZE ** (-0.5)
    d_key_block = jnp.einsum(
        "hgrk,rhgd->khd", d_scores, grouped_query, preferred_element_type=jnp.float32
    ) * HEAD_SIZE ** (-0.5)
    return (d_query, d_key_block, d_value_block)


def per_device(
    prompt_rows,
    suffix_rows,
    assignment,
    lengths,
    attention_gain,
    query_weight,
    key_matrix,
    value_matrix,
    query_gain,
    key_norm_gain,
    out_weight,
    mlp_gain,
    gate_weight,
    up_weight,
    down_weight,
    prompt_cotangent,
    suffix_cotangent,
):
    fsdp_rank = lax.axis_index("fsdp")
    prompt_on_device = prompt_rows.shape[0]
    continuation_on_device = suffix_rows.shape[0]
    device_slots = continuation_on_device // CONTINUATION_LEN
    number_of_rows = prompt_on_device + continuation_on_device
    heads_per_group = QUERY_HEADS // KEY_VALUE_HEADS
    first_row = fsdp_rank * prompt_on_device
    owned_group = first_row // PROMPT_LENGTH
    prompt_place = first_row % PROMPT_LENGTH + jnp.arange(prompt_on_device, dtype=jnp.int32)
    suffix_place = jnp.arange(continuation_on_device, dtype=jnp.int32) % CONTINUATION_LEN
    owner_slots = assignment[0] // CONT
    length_rows = jnp.repeat(lengths[0], CONTINUATION_LEN)
    suffix_valid = suffix_place < length_rows
    slot_validity = suffix_valid.reshape(device_slots, CONTINUATION_LEN)
    token_positions = jnp.concatenate([prompt_place, PROMPT_LENGTH + suffix_place])
    valid_rows = jnp.concatenate(
        [jnp.ones((prompt_on_device,), jnp.float32), suffix_valid.astype(jnp.float32)]
    )
    prompt_allowed = jnp.arange(PROMPT_LENGTH, dtype=jnp.int32)[None, :] <= prompt_place[:, None]
    slot_causal = (
        jnp.arange(CONTINUATION_LEN, dtype=jnp.int32)[None, :]
        <= jnp.arange(CONTINUATION_LEN, dtype=jnp.int32)[:, None]
    )

    def slot_allowed(valid_slot):
        return jnp.concatenate(
            [
                jnp.ones((CONTINUATION_LEN, PROMPT_LENGTH), dtype=bool),
                slot_causal & valid_slot[None, :],
            ],
            axis=1,
        )

    n = lax.axis_size("fsdp")
    R = lax.axis_size("rep")
    tile = jnp.stack(
        [
            jnp.pad(v.astype(jnp.float32), (0, 128 - v.shape[0]))
            for v in (attention_gain, mlp_gain, query_gain, key_norm_gain)
        ]
    )
    tile = jnp.pad(tile, ((0, 4), (0, 0)))
    (key_full, value_full, query_full, out_full, gate_full, up_full, down_full), tiles = gather(
        [key_matrix, value_matrix, query_weight, out_weight, gate_weight, up_weight, down_weight],
        tile,
        n,
        0,
    )
    gain_first = tiles[:, 0, : attention_gain.shape[0]].reshape(-1)
    gain_second = tiles[:, 1, : mlp_gain.shape[0]].reshape(-1)
    query_scale = tiles[:, 2, : query_gain.shape[0]].reshape(-1)
    key_norm_scale = tiles[:, 3, : key_norm_gain.shape[0]].reshape(-1)
    query_back, key_back, value_back, out_back = query_full, key_full, value_full, out_full
    gate_back, up_back, down_back = gate_full, up_full, down_full
    rows_wide = jnp.concatenate([prompt_rows, suffix_rows], 0).astype(jnp.float32)
    hidden_wide, first_pull = jax.vjp(root_mean_scale, rows_wide, gain_first.astype(jnp.float32))
    hidden_state = hidden_wide.astype(jnp.bfloat16)
    query_pre = jnp.dot(hidden_state, query_full, preferred_element_type=jnp.float32)
    key_before_norm = jnp.dot(hidden_state, key_full, preferred_element_type=jnp.float32)
    value_matrix_rows = (
        jnp.dot(hidden_state, value_full, preferred_element_type=jnp.float32)
        .astype(jnp.bfloat16)
        .reshape(number_of_rows, KEY_VALUE_HEADS, HEAD_SIZE)
    )
    (query_rotated, key_rotated), rotary_pull = jax.vjp(
        partial(query_key, token_positions),
        query_pre,
        key_before_norm,
        query_scale.astype(jnp.float32),
        key_norm_scale.astype(jnp.float32),
    )
    grouped_query = query_rotated.astype(jnp.bfloat16).reshape(
        number_of_rows, KEY_VALUE_HEADS, heads_per_group, HEAD_SIZE
    )
    key_reduced = key_rotated.astype(jnp.bfloat16)
    gathered_keys, gathered_values = (
        lax.all_gather(key_reduced[:prompt_on_device], "fsdp", axis=0, tiled=True),
        lax.all_gather(value_matrix_rows[:prompt_on_device], "fsdp", axis=0, tiled=True),
    )
    prompt_count = gathered_keys.shape[0]
    prompt_query = grouped_query[:prompt_on_device]
    own_prompt_keys = lax.dynamic_slice_in_dim(
        gathered_keys, owned_group * PROMPT_LENGTH, PROMPT_LENGTH, 0
    )
    own_prompt_values = lax.dynamic_slice_in_dim(
        gathered_values, owned_group * PROMPT_LENGTH, PROMPT_LENGTH, 0
    )
    slot_query_rows = grouped_query[prompt_on_device:].reshape(
        device_slots, CONTINUATION_LEN, KEY_VALUE_HEADS, heads_per_group, HEAD_SIZE
    )
    slot_key_rows = key_reduced[prompt_on_device:].reshape(
        device_slots, CONTINUATION_LEN, KEY_VALUE_HEADS, HEAD_SIZE
    )
    slot_value_rows = value_matrix_rows[prompt_on_device:].reshape(
        device_slots, CONTINUATION_LEN, KEY_VALUE_HEADS, HEAD_SIZE
    )

    def slot_keys_of(owner, own_keys, own_values):
        keys_all = jnp.concatenate(
            [
                lax.dynamic_slice_in_dim(gathered_keys, owner * PROMPT_LENGTH, PROMPT_LENGTH, 0),
                own_keys,
            ],
            0,
        )
        values_all = jnp.concatenate(
            [
                lax.dynamic_slice_in_dim(gathered_values, owner * PROMPT_LENGTH, PROMPT_LENGTH, 0),
                own_values,
            ],
            0,
        )
        return (keys_all, values_all)

    prompt_output, prompt_lse = unit_forward(
        prompt_query, own_prompt_keys, own_prompt_values, prompt_allowed
    )

    def slot_forward(slot_items):
        query_slot, own_keys, own_values, owner, valid_slot = slot_items
        keys_all, values_all = slot_keys_of(owner, own_keys, own_values)
        return unit_forward(query_slot, keys_all, values_all, slot_allowed(valid_slot))

    slot_output, slot_lse = lax.map(
        slot_forward, (slot_query_rows, slot_key_rows, slot_value_rows, owner_slots, slot_validity)
    )
    attended_group = jnp.concatenate(
        [
            prompt_output,
            slot_output.reshape(
                continuation_on_device, KEY_VALUE_HEADS, heads_per_group, HEAD_SIZE
            ),
        ],
        0,
    )
    attended = attended_group.reshape(number_of_rows, QUERY_HEADS * HEAD_SIZE)
    attended_low = attended.astype(jnp.bfloat16)
    residual = rows_wide + jnp.dot(attended_low, out_full, preferred_element_type=jnp.float32)
    hidden_two_wide, second_pull = jax.vjp(
        root_mean_scale, residual, gain_second.astype(jnp.float32)
    )
    hidden_two = hidden_two_wide.astype(jnp.bfloat16)
    gate_pre = jnp.dot(hidden_two, gate_full, preferred_element_type=jnp.float32)
    up_pre = jnp.dot(hidden_two, up_full, preferred_element_type=jnp.float32)
    act_wide, act_pull = jax.vjp(swiglu, gate_pre, up_pre)
    act_low = act_wide.astype(jnp.bfloat16)
    mixed_full = residual + jnp.dot(act_low, down_full, preferred_element_type=jnp.float32)
    d_mixed = (
        jnp.concatenate([prompt_cotangent, suffix_cotangent], 0).astype(jnp.float32)
        * valid_rows[:, None]
    )
    d_mixed_low = d_mixed.astype(jnp.bfloat16)
    grad_down = jnp.einsum("rf,rd->fd", act_low, d_mixed_low, preferred_element_type=jnp.float32)
    d_act = jnp.einsum("rd,fd->rf", d_mixed_low, down_back, preferred_element_type=jnp.float32)
    d_gate_wide, d_up_wide = act_pull(d_act)
    d_gate = d_gate_wide.astype(jnp.bfloat16)
    d_up = d_up_wide.astype(jnp.bfloat16)
    grad_gate = jnp.einsum("rd,rf->df", hidden_two, d_gate, preferred_element_type=jnp.float32)
    grad_up = jnp.einsum("rd,rf->df", hidden_two, d_up, preferred_element_type=jnp.float32)
    d_hidden_two = jnp.einsum(
        "rf,df->rd", d_gate, gate_back, preferred_element_type=jnp.float32
    ) + jnp.einsum("rf,df->rd", d_up, up_back, preferred_element_type=jnp.float32)
    d_resid_mlp, grad_second_gain = second_pull(d_hidden_two)
    d_resid = d_mixed + d_resid_mlp
    d_resid_low = d_resid.astype(jnp.bfloat16)
    grad_out = jnp.einsum(
        "ra,rd->ad", attended_low, d_resid_low, preferred_element_type=jnp.float32
    )
    grad_attended_rows = jnp.einsum(
        "rd,ad->ra", d_resid_low, out_back, preferred_element_type=jnp.float32
    ).astype(jnp.bfloat16)
    grad_attended_per_group = grad_attended_rows.reshape(
        number_of_rows, KEY_VALUE_HEADS, heads_per_group, HEAD_SIZE
    )
    row_difference = jnp.einsum(
        "rhgd,rhgd->hgr", grad_attended_per_group.astype(jnp.float32), attended_group
    )
    grad_prompt_query, grad_prompt_keys, grad_prompt_values = unit_backward(
        prompt_query,
        own_prompt_keys,
        own_prompt_values,
        prompt_allowed,
        prompt_lse,
        grad_attended_per_group[:prompt_on_device],
        row_difference[..., :prompt_on_device],
    )
    key_buffer = lax.dynamic_update_slice_in_dim(
        jnp.zeros((prompt_count, KEY_VALUE_HEADS, HEAD_SIZE), jnp.float32),
        grad_prompt_keys,
        owned_group * PROMPT_LENGTH,
        0,
    )
    value_buffer = lax.dynamic_update_slice_in_dim(
        jnp.zeros((prompt_count, KEY_VALUE_HEADS, HEAD_SIZE), jnp.float32),
        grad_prompt_values,
        owned_group * PROMPT_LENGTH,
        0,
    )
    slot_d_attended = grad_attended_per_group[prompt_on_device:].reshape(
        device_slots, CONTINUATION_LEN, KEY_VALUE_HEADS, heads_per_group, HEAD_SIZE
    )
    slot_delta = jnp.moveaxis(
        row_difference[..., prompt_on_device:].reshape(
            KEY_VALUE_HEADS, heads_per_group, device_slots, CONTINUATION_LEN
        ),
        2,
        0,
    )

    def slot_backward(buffers, slot_items):
        query_slot, own_keys, own_values, owner, valid_slot, lse_slot, d_att_slot, delta_slot = (
            slot_items
        )
        keys_all, values_all = slot_keys_of(owner, own_keys, own_values)
        d_query_slot, d_keys_all, d_values_all = unit_backward(
            query_slot,
            keys_all,
            values_all,
            slot_allowed(valid_slot),
            lse_slot,
            d_att_slot,
            delta_slot,
        )
        key_acc, value_acc = buffers
        start = owner * PROMPT_LENGTH
        key_acc = lax.dynamic_update_slice_in_dim(
            key_acc,
            lax.dynamic_slice_in_dim(key_acc, start, PROMPT_LENGTH, 0) + d_keys_all[:PROMPT_LENGTH],
            start,
            0,
        )
        value_acc = lax.dynamic_update_slice_in_dim(
            value_acc,
            lax.dynamic_slice_in_dim(value_acc, start, PROMPT_LENGTH, 0)
            + d_values_all[:PROMPT_LENGTH],
            start,
            0,
        )
        return (
            (key_acc, value_acc),
            (d_query_slot, d_keys_all[PROMPT_LENGTH:], d_values_all[PROMPT_LENGTH:]),
        )

    (key_buffer, value_buffer), (grad_slot_queries, owned_key_grads, owned_value_grads) = lax.scan(
        slot_backward,
        (key_buffer, value_buffer),
        (
            slot_query_rows,
            slot_key_rows,
            slot_value_rows,
            owner_slots,
            slot_validity,
            slot_lse,
            slot_d_attended,
            slot_delta,
        ),
    )
    owned_keys, owned_values = (
        lax.psum_scatter(
            key_buffer.astype(jnp.bfloat16), "fsdp", scatter_dimension=0, tiled=True
        ).astype(jnp.float32),
        lax.psum_scatter(
            value_buffer.astype(jnp.bfloat16), "fsdp", scatter_dimension=0, tiled=True
        ).astype(jnp.float32),
    )
    d_query = jnp.concatenate(
        [
            grad_prompt_query,
            grad_slot_queries.reshape(
                continuation_on_device, KEY_VALUE_HEADS, heads_per_group, HEAD_SIZE
            ),
        ],
        0,
    )
    grad_key_rotated = jnp.concatenate(
        [owned_keys, owned_key_grads.reshape(continuation_on_device, KEY_VALUE_HEADS, HEAD_SIZE)], 0
    )
    d_values_low = (
        jnp.concatenate(
            [
                owned_values,
                owned_value_grads.reshape(continuation_on_device, KEY_VALUE_HEADS, HEAD_SIZE),
            ],
            0,
        )
        .astype(jnp.bfloat16)
        .reshape(number_of_rows, KEY_VALUE_HEADS * HEAD_SIZE)
    )
    d_query_pre, d_key_pre, grad_query_scale, grad_key_scale = rotary_pull(
        (d_query.reshape(number_of_rows, QUERY_HEADS, HEAD_SIZE), grad_key_rotated)
    )
    d_query_low = d_query_pre.astype(jnp.bfloat16)
    d_key_low = d_key_pre.astype(jnp.bfloat16)
    grad_query = jnp.einsum(
        "rd,rq->dq", hidden_state, d_query_low, preferred_element_type=jnp.float32
    )
    grad_key = jnp.einsum("rd,rq->dq", hidden_state, d_key_low, preferred_element_type=jnp.float32)
    grad_value = jnp.einsum(
        "rd,rq->dq", hidden_state, d_values_low, preferred_element_type=jnp.float32
    )
    d_hidden = (
        jnp.einsum("rq,dq->rd", d_query_low, query_back, preferred_element_type=jnp.float32)
        + jnp.einsum("rq,dq->rd", d_key_low, key_back, preferred_element_type=jnp.float32)
        + jnp.einsum("rq,dq->rd", d_values_low, value_back, preferred_element_type=jnp.float32)
    )
    d_rows_attn, grad_first_gain = first_pull(d_hidden)
    d_rows = d_resid + d_rows_attn
    stats = jnp.stack(
        [
            jnp.sum(valid_rows * jnp.sum(mixed_full * mixed_full, axis=-1)),
            jnp.sum(valid_rows * jnp.sum(residual * residual, axis=-1)),
            jnp.sum(valid_rows * jnp.sum(d_rows * d_rows, axis=-1)),
            jnp.sum(valid_rows),
        ]
    )
    vec = jnp.concatenate(
        [grad_first_gain, grad_second_gain, grad_query_scale, grad_key_scale, jnp.pad(stats, (0, 124))]
    )
    vec = jnp.pad(vec.reshape(-1, 128), ((0, (-vec.shape[0] // 128) % 8), (0, 0)))
    bf = jnp.bfloat16
    shards, vec_sum = scatter(
        [
            grad_down.astype(bf),
            grad_gate.astype(bf),
            grad_up.astype(bf),
            grad_out.astype(bf),
            grad_query.astype(bf),
            grad_key.astype(bf),
            grad_value.astype(bf),
        ],
        n,
        R,
        1,
        vec,
    )
    g_down, g_gate, g_up, g_out, g_query, g_key, g_value = [g.astype(jnp.float32) for g in shards]
    flat = vec_sum.reshape(-1)
    def mine(first, whole, part):
        return lax.dynamic_slice_in_dim(flat[first : first + whole], fsdp_rank * part, part)
    w = MODEL_WIDTH
    g_first = mine(0, w, attention_gain.shape[0])
    g_second = mine(w, w, mlp_gain.shape[0])
    g_qs = mine(2 * w, HEAD_SIZE, query_gain.shape[0])
    g_ks = mine(2 * w + HEAD_SIZE, HEAD_SIZE, key_norm_gain.shape[0])
    stat_sums = flat[2 * w + 2 * HEAD_SIZE : 2 * w + 2 * HEAD_SIZE + 4]
    token_norms = jnp.sqrt(stat_sums[:3] / (stat_sums[3] * MODEL_WIDTH))
    mixed_low = mixed_full.astype(jnp.bfloat16)
    return (
        mixed_low[:prompt_on_device],
        mixed_low[prompt_on_device:],
        d_rows[:prompt_on_device],
        d_rows[prompt_on_device:],
        g_first,
        g_query,
        g_key,
        g_value,
        g_qs,
        g_ks,
        g_out,
        g_second,
        g_gate,
        g_up,
        g_down,
        token_norms,
    )


def solution(mesh):
    placed = (
        P(("rep", "fsdp"), None),
        P(("rep", "fsdp"), None),
        P("rep", "fsdp"),
        P("rep", "fsdp"),
        P("fsdp"),
        P("fsdp", None),
        P("fsdp", None),
        P("fsdp", None),
        P("fsdp"),
        P("fsdp"),
        P("fsdp", None),
        P("fsdp"),
        P("fsdp", None),
        P("fsdp", None),
        P("fsdp", None),
        P(("rep", "fsdp"), None),
        P(("rep", "fsdp"), None),
    )
    return jax.shard_map(
        per_device,
        mesh=mesh,
        in_specs=placed,
        out_specs=(
            P(("rep", "fsdp"), None),
            P(("rep", "fsdp"), None),
            P(("rep", "fsdp"), None),
            P(("rep", "fsdp"), None),
            P("fsdp"),
            P("fsdp", None),
            P("fsdp", None),
            P("fsdp", None),
            P("fsdp"),
            P("fsdp"),
            P("fsdp", None),
            P("fsdp"),
            P("fsdp", None),
            P("fsdp", None),
            P("fsdp", None),
            P(),
        ),
        check_vma=False,
    )
```

```python
from functools import partial

import jax
import jax.numpy as jnp
from jax import lax
from jax.experimental import pallas as pl
from jax.experimental.pallas import tpu as pltpu
from jax.sharding import PartitionSpec as P

MODEL_WIDTH = 1024
QUERY_HEADS = 16
KEY_VALUE_HEADS = 8
HEAD_SIZE = 128
PROMPT_LENGTH = 1024
CONT = 8
CONTINUATION_LEN = 128

norm_epsilon = 1e-06
rope_theta = 1000000.0
masked_score = -1e30
MESH = pl.DeviceIdType.MESH
bf16 = jnp.bfloat16
f32 = jnp.float32

def position(n):
    rep = lax.axis_index("rep")
    rank = lax.axis_index("fsdp")
    return rep, rank // 4, (rank // 2) % 2, rank % 2


def meet(peers):
    barrier = pltpu.get_barrier_semaphore()
    for p in peers:
        pl.semaphore_signal(barrier, inc=1, device_id=p, device_id_type=MESH)
    pl.semaphore_wait(barrier, len(peers))


def remote(src, dst, send, recv, to):
    return pltpu.make_async_remote_copy(src, dst, send, recv, device_id=to, device_id_type=MESH)


def gather_kernel(n, m, k, *refs):
    A = n // 4
    it = iter(refs)
    take = lambda count: [next(it) for _ in range(count)]
    own, (tile,), pieces = take(m), take(1), take(k)
    full, (tiles,), staged = take(m), take(1), take(k)
    zs, zr, s2s, s2r, s3s, s3r, cs, cr, ls, ts, tr, ps, pr, pls = take(14)
    rep, a, b, c = position(n)
    me = (a * 2 + b) * 2 + c
    h = rep % 2
    mate = rep + 1 - 2 * h

    def dev(r, a, b, c):
        return (r, (a * 2 + b) * 2 + c)

    meet([(rep, (me + d) % n) for d in range(1, n)] + [dev(mate, a, b, c)])
    ydev, xdev, cdev = dev(rep, a, 1 - b, c), dev(mate, a, b, c), dev(rep, a, b, 1 - c)

    def local(i):
        return pltpu.make_async_copy(own[i].at[:, h], full[i].at[a, b, c, :, h], ls.at[i])

    def along(i, d):
        return remote(own[i].at[:, h], full[i].at[a, b, c, :, h], zs.at[i, d - 1], zr.at[i, d - 1], dev(rep, (a + d) % A, b, c))

    def s2(i):
        y, x = full[i].at[:, b, c, 0, h], full[i].at[:, b, c, 1, h]
        return [remote(y, y, s2s.at[i, 0], s2r.at[i, 0], ydev), remote(x, x, s2s.at[i, 1], s2r.at[i, 1], xdev)]

    def s3(i):
        x, y = full[i].at[:, :, c, 0, h], full[i].at[:, b, c, 1]
        return [remote(x, x, s3s.at[i, 0], s3r.at[i, 0], xdev), remote(y, y, s3s.at[i, 1], s3r.at[i, 1], ydev)]

    def s4(i):
        both = full[i].at[:, :, c]
        return [remote(both, both, cs.at[i], cr.at[i], cdev)]

    def share(d):
        return remote(tile, tiles.at[me], ts.at[d - 1], tr.at[d - 1], (rep, (me + d) % n))

    def piece(i, d):
        to = (me + d) % n
        return remote(pieces[i].at[:, to], staged[i].at[me], ps.at[i, d - 1], pr.at[i, d - 1], (rep, to))

    def own_piece(i):
        return pltpu.make_async_copy(pieces[i].at[:, me], staged[i].at[me], pls.at[i])

    for d in range(1, n):
        share(d).start()
    tiles[me] = tile[...]
    for i in range(k):
        own_piece(i).start()
        for d in range(1, n):
            piece(i, d).start()
    for i in range(m):
        local(i).start()
        for d in range(1, A):
            along(i, d).start()
    for t in range(m + 3):
        if t < m:
            local(t).wait()
            for d in range(1, A):
                along(t, d).wait_recv()
            for q in s2(t):
                q.start()
        if 0 <= t - 1 < m:
            for q in s2(t - 1):
                q.wait_recv()
            for q in s3(t - 1):
                q.start()
        if 0 <= t - 2 < m:
            for q in s3(t - 2):
                q.wait_recv()
            for q in s4(t - 2):
                q.start()
        if 0 <= t - 3 < m:
            for q in s4(t - 3):
                q.wait_recv()
    for d in range(1, n):
        share(d).wait()
    for i in range(k):
        own_piece(i).wait()
        for d in range(1, n):
            piece(i, d).wait()
    for t in range(m):
        for d in range(1, A):
            along(t, d).wait_send()
        for q in s2(t) + s3(t) + s4(t):
            q.wait_send()


def gather(shards, tile, slots, n, cid):
    m, k, A = len(shards), len(slots), n // 4
    views = [s.reshape(2, 2, s.shape[0] // 4, s.shape[1]) for s in shards]
    outs = [jax.ShapeDtypeStruct((A, 2, 2) + v.shape, v.dtype) for v in views]
    outs += [jax.ShapeDtypeStruct((n,) + tile.shape, tile.dtype)]
    outs += [jax.ShapeDtypeStruct((n, s.shape[0]) + s.shape[2:], s.dtype) for s in slots]
    D = pltpu.SemaphoreType.DMA
    vm, hbm = pl.BlockSpec(memory_space=pltpu.VMEM), pl.BlockSpec(memory_space=pl.ANY)
    res = pl.pallas_call(
        partial(gather_kernel, n, m, k),
        out_shape=outs,
        in_specs=[vm] * (m + 1 + k),
        out_specs=[hbm] * m + [vm] + [hbm] * k,
        scratch_shapes=[D((m, A - 1))] * 2 + [D((m, 2))] * 4 + [D((m,))] * 3 + [D((n - 1,))] * 2 + [D((max(k, 1), n - 1))] * 2 + [D((max(k, 1),))],
        compiler_params=pltpu.CompilerParams(collective_id=cid, has_side_effects=True),
        name="gather",
    )(*views, tile, *slots)
    return [f.reshape(-1, s.shape[1]) for f, s in zip(res, shards)], res[m], res[m + 1:]


def spread_kernel(n, k, *refs):
    it = iter(refs)
    take = lambda count: [next(it) for _ in range(count)]
    pieces, staged, (ps, pr, pls) = take(k), take(k), take(3)
    rep, a, b, c = position(n)
    me = (a * 2 + b) * 2 + c
    meet([(rep, (me + d) % n) for d in range(1, n)])

    def piece(i, d):
        to = (me + d) % n
        return remote(pieces[i].at[:, to], staged[i].at[me], ps.at[i, d - 1], pr.at[i, d - 1], (rep, to))

    def own_piece(i):
        return pltpu.make_async_copy(pieces[i].at[:, me], staged[i].at[me], pls.at[i])

    for i in range(k):
        own_piece(i).start()
        for d in range(1, n):
            piece(i, d).start()
    for i in range(k):
        own_piece(i).wait()
        for d in range(1, n):
            piece(i, d).wait()


def spread(slots, n, cid):
    k = len(slots)
    D = pltpu.SemaphoreType.DMA
    vm, hbm = pl.BlockSpec(memory_space=pltpu.VMEM), pl.BlockSpec(memory_space=pl.ANY)
    return pl.pallas_call(
        partial(spread_kernel, n, k),
        out_shape=[jax.ShapeDtypeStruct((n, s.shape[0]) + s.shape[2:], s.dtype) for s in slots],
        in_specs=[vm] * k,
        out_specs=[hbm] * k,
        scratch_shapes=[D((k, n - 1))] * 2 + [D((k,))],
        compiler_params=pltpu.CompilerParams(collective_id=cid, has_side_effects=True),
        name="spread",
    )(*slots)


def collect_kernel(n, k, *refs):
    it = iter(refs)
    take = lambda count: [next(it) for _ in range(count)]
    (index,), staged, final, ordered, (ps, pr, pls) = take(1), take(k), take(k), take(k), take(3)
    rep, a, b, c = position(n)
    me = (a * 2 + b) * 2 + c
    meet([(rep, (me + d) % n) for d in range(1, n)])
    S = ordered[0].shape[1]
    for i in range(k):
        def place(j, _):
            ordered[i][j // S, j % S] = staged[i][index[j]]
            return 0
        lax.fori_loop(0, n * S, place, 0)

    def piece(i, d):
        to = (me + d) % n
        return remote(ordered[i].at[to], final[i].at[:, me], ps.at[i, d - 1], pr.at[i, d - 1], (rep, to))

    def own_piece(i):
        return pltpu.make_async_copy(ordered[i].at[me], final[i].at[:, me], pls.at[i])

    for i in range(k):
        own_piece(i).start()
        for d in range(1, n):
            piece(i, d).start()
    for i in range(k):
        own_piece(i).wait()
        for d in range(1, n):
            piece(i, d).wait()


def collect(index, staged, n, cid):
    k = len(staged)
    flat = [s.reshape((-1,) + s.shape[2:]) for s in staged]
    D = pltpu.SemaphoreType.DMA
    vm, hbm, sm = pl.BlockSpec(memory_space=pltpu.VMEM), pl.BlockSpec(memory_space=pl.ANY), pl.BlockSpec(memory_space=pltpu.SMEM)
    return pl.pallas_call(
        partial(collect_kernel, n, k),
        out_shape=[jax.ShapeDtypeStruct((s.shape[1], n) + s.shape[2:], s.dtype) for s in staged],
        in_specs=[sm] + [vm] * k,
        out_specs=[hbm] * k,
        scratch_shapes=[pltpu.VMEM(s.shape, s.dtype) for s in staged] + [D((k, n - 1))] * 2 + [D((k,))],
        compiler_params=pltpu.CompilerParams(collective_id=cid, has_side_effects=True),
        name="collect",
    )(index, *flat)


def add_rows(count, out, first, second, step=None):
    def one(j, _):
        o = out(j)
        total = first(j)[...].astype(jnp.float32)
        for s in second:
            total = total + s(j)[...].astype(jnp.float32)
        o[...] = total.astype(o.dtype)
        return 0
    lax.fori_loop(0, count, one, 0)

def scatter_kernel(n, R, m, has_vec, *refs):
    A = n // 4
    bits = R.bit_length() - 1
    it = iter(refs)
    take = lambda k: [next(it) for _ in range(k)]
    grads = take(m)
    vec = next(it) if has_vec else None
    outs = take(m)
    vout = next(it) if has_vec else None
    own, b1, b2y, b2x, b3, b4, b5 = [take(m) for _ in range(7)]
    s4 = take(m)
    vb = next(it) if has_vec else None
    vz = next(it) if has_vec else None
    ls, s1s, s1r, s2s, s2r, s3s, s3r, s4s, s4r, s5s, s5r, ws = take(12)
    if has_vec:
        vs, vr = take(2)
    rep, a, b, c = position(n)
    h = rep % 2
    mate = rep + 1 - 2 * h
    def dev(r, a, b, c):
        return (r, (a * 2 + b) * 2 + c)
    ydev, xdev, cdev = dev(rep, a, 1 - b, c), dev(mate, a, b, c), dev(rep, a, b, 1 - c)
    zdev = lambda d: dev(rep, (a + d) % A, b, c)
    def flip(bit):
        w = 1 << bit
        return dev(rep + w - 2 * w * ((rep // w) % 2), a, b, c)
    barrier = pltpu.get_barrier_semaphore()
    peers = [zdev(d) for d in range(1, A)] + [ydev, xdev, cdev] + [flip(k) for k in range(1, bits)]
    for p in peers:
        pl.semaphore_signal(barrier, inc=1, device_id=p, device_id_type=MESH)
    pl.semaphore_wait(barrier, len(peers))
    def rc(src, dst, ss, rs, to):
        return pltpu.make_async_remote_copy(src, dst, ss, rs, device_id=to, device_id_type=MESH)
    def load(i): return pltpu.make_async_copy(grads[i].at[:, :, c], own[i], ls.at[i])
    def S1(i): return [rc(grads[i].at[:, :, 1 - c], b1[i], s1s.at[i], s1r.at[i], cdev)]
    def S2(i): return [rc(b1[i].at[:, 1 - b, 0], b2y[i], s2s.at[i, 0], s2r.at[i, 0], ydev),
                       rc(b1[i].at[:, :, 1, 1 - h], b2x[i], s2s.at[i, 1], s2r.at[i, 1], xdev)]
    def S3(i): return [rc(b2y[i].at[:, 1 - h], b3[i].at[0], s3s.at[i, 0], s3r.at[i, 0], xdev),
                       rc(b2x[i].at[:, 1 - b], b3[i].at[1], s3s.at[i, 1], s3r.at[i, 1], ydev)]
    def S4(i): return [rc(b3[i].at[:, (a + d) % A], b4[i].at[d - 1], s4s.at[i, d - 1], s4r.at[i, d - 1], zdev(d)) for d in range(1, A)]
    def S5(i, k): return rc(s4[i].at[0] if k == bits - 1 else s4[i].at[k], b5[i].at[k], s5s.at[i, k], s5r.at[i, k], xdev if k == bits - 1 else flip(k + 1))
    def put(i, k): return pltpu.make_async_copy((s4[i].at[0] if bits == 1 else s4[i].at[bits - 1]) if k == 0 else b5[i].at[bits - 1], outs[i].at[:, h if k == 0 else 1 - h], ws.at[i, k])
    for i in range(m):
        load(i).start()
        for q in S1(i): q.start()
    if has_vec:
        rounds = [cdev, ydev, xdev] + [flip(k) for k in range(1, bits)]
        vb[0] = vec[...]
        for k, to in enumerate(rounds):
            q = rc(vb.at[2 * k], vb.at[2 * k + 1], vs.at[k], vr.at[k], to)
            q.start(); q.wait()
            vb[2 * k + 2] = vb[2 * k] + vb[2 * k + 1]
        last = 2 * len(rounds)
        nr = len(rounds)
        qs = [rc(vb.at[last], vz.at[a], vs.at[nr + d - 1], vr.at[nr + d - 1], zdev(d)) for d in range(1, A)]
        for q in qs: q.start()
        vz[a] = vb[last]
        for q in qs: q.wait()
        total = vz[0]
        for k in range(1, A):
            total = total + vz[k]
        vout[...] = total
    for t in range(m + 4):
        i = t
        if t < m:
            load(i).wait()
            for q in S1(i): q.wait_recv()
            add_rows(A * 2 * 4, lambda j, i=i: b1[i].at[j // 8, (j // 4) % 2, (j // 2) % 2, j % 2],
                     lambda j, i=i: b1[i].at[j // 8, (j // 4) % 2, (j // 2) % 2, j % 2],
                     [lambda j, i=i: own[i].at[j // 8, (j // 4) % 2, (j // 2) % 2, j % 2]])
            for q in S2(i): q.start()
        i = t - 1
        if 0 <= i < m:
            for q in S2(i): q.wait_recv()
            add_rows(A * 2, lambda j, i=i: b2y[i].at[j // 2, j % 2], lambda j, i=i: b2y[i].at[j // 2, j % 2],
                     [lambda j, i=i: b1[i].at[j // 2, b, 0, j % 2]])
            add_rows(A * 2, lambda j, i=i: b2x[i].at[j // 2, j % 2], lambda j, i=i: b2x[i].at[j // 2, j % 2],
                     [lambda j, i=i: b1[i].at[j // 2, j % 2, 1, h]])
            for q in S3(i): q.start()
        i = t - 2
        if 0 <= i < m:
            for q in S3(i): q.wait_recv()
            add_rows(A, lambda j, i=i: b3[i].at[0, j], lambda j, i=i: b3[i].at[0, j], [lambda j, i=i: b2y[i].at[j, h]])
            add_rows(A, lambda j, i=i: b3[i].at[1, j], lambda j, i=i: b3[i].at[1, j], [lambda j, i=i: b2x[i].at[j, b]])
            for q in S4(i): q.start()
        i = t - 3
        if 0 <= i < m:
            for q in S4(i): q.wait_recv()
            add_rows(2, lambda j, i=i: s4[i].at[0, j], lambda j, i=i: b3[i].at[j, a], [lambda j, i=i, d=d: b4[i].at[d, j] for d in range(A - 1)])
            for k in range(bits - 1):
                q = S5(i, k); q.start(); q.wait()
                add_rows(2, lambda j, i=i, k=k: s4[i].at[k + 1, j], lambda j, i=i, k=k: s4[i].at[k, j], [lambda j, i=i, k=k: b5[i].at[k, j]])
            rc(s4[i].at[bits - 1], b5[i].at[bits - 1], s5s.at[i, bits - 1], s5r.at[i, bits - 1], xdev).start()
            put(i, 0).start()
        i = t - 4
        if 0 <= i < m:
            rc(s4[i].at[bits - 1], b5[i].at[bits - 1], s5s.at[i, bits - 1], s5r.at[i, bits - 1], xdev).wait_recv()
            put(i, 1).start()
    for i in range(m):
        for q in S1(i) + S2(i) + S3(i) + S4(i): q.wait_send()
        rc(s4[i].at[bits - 1], b5[i].at[bits - 1], s5s.at[i, bits - 1], s5r.at[i, bits - 1], xdev).wait_send()
        put(i, 0).wait(); put(i, 1).wait()

def scatter(grads, n, R, cid, vec=None):
    m, A, bits = len(grads), n // 4, R.bit_length() - 1
    views = [g.reshape(A, 2, 2, 2, 2, g.shape[0] // (4 * n), g.shape[1]) for g in grads]
    sub = [v.shape[-2:] for v in views]
    bf = jnp.bfloat16
    V, D = pltpu.VMEM, pltpu.SemaphoreType.DMA
    scratch = ([V((A, 2, 2, 2) + s, bf) for s in sub] * 2 + [V((A, 2) + s, bf) for s in sub] * 2 + [V((2, A) + s, bf) for s in sub]
        + [V((A - 1, 2) + s, bf) for s in sub] + [V((bits, 2) + s, bf) for s in sub] + [V((bits, 2) + s, bf) for s in sub])
    ins, ispec = list(views), [pl.BlockSpec(memory_space=pl.ANY)] * m
    outs, ospec = [jax.ShapeDtypeStruct((2, 2) + s, bf) for s in sub], [pl.BlockSpec(memory_space=pl.ANY)] * m
    sems = [D((m,)), D((m,)), D((m,)), D((m, 2)), D((m, 2)), D((m, 2)), D((m, 2)), D((m, A - 1)), D((m, A - 1)), D((m, bits)), D((m, bits)), D((m, 2))]
    if vec is not None:
        ins.append(vec); ispec.append(pl.BlockSpec(memory_space=pltpu.VMEM))
        outs.append(jax.ShapeDtypeStruct(vec.shape, vec.dtype)); ospec.append(pl.BlockSpec(memory_space=pltpu.VMEM))
        scratch += [V((2 * (2 + bits) + 1,) + vec.shape, vec.dtype), V((A,) + vec.shape, vec.dtype)]
        sems += [D((2 + bits + A - 1,))] * 2
    res = pl.pallas_call(partial(scatter_kernel, n, R, m, vec is not None), out_shape=outs, in_specs=ispec, out_specs=ospec,
        scratch_shapes=scratch + sems,
        compiler_params=pltpu.CompilerParams(collective_id=cid, has_side_effects=True, vmem_limit_bytes=60 << 20),
        name="scatter")(*ins)
    shards = [r.reshape(-1, r.shape[-1]) for r in res[:m]]
    return (shards, res[m]) if vec is not None else shards


LOG2E = 1.4426950408889634


def mm(x, y, cx, cy):
    return lax.dot_general(x, y, (((cx,), (cy,)), ((), ())), preferred_element_type=f32)


def keys_kernel(n, group, k_pre, v, gain, cos, sin, k_out, ks, vs, fs, fr, gs, gr, ls):
    rows = ks.shape[2]
    half = group // 2
    rep, a, b, c = position(n)
    me = (a * 2 + b) * 2 + c
    first = (me // group) * half
    slot = (me // 2) % half

    def at(s, c):
        return (rep, (first + s) * 2 + c)

    others = [(slot + d) % half for d in range(1, half)]
    meet([at(s, c) for s in others] + [at(slot, 1 - c)])

    def head(j, _):
        lanes = pl.ds(pl.multiple_of(j * HEAD_SIZE, HEAD_SIZE), HEAD_SIZE)
        x = k_pre[:, lanes]
        x = x * lax.rsqrt(jnp.mean(x * x, axis=-1, keepdims=True) + norm_epsilon) * gain[...]
        k_out[:, lanes] = (x * cos[...] + pltpu.roll(x, HEAD_SIZE // 2, 1) * sin[...]).astype(bf16)
        return 0

    lax.fori_loop(0, KEY_VALUE_HEADS, head, 0)
    parts = [(k_out, ks), (v, vs)]

    def local(i):
        return pltpu.make_async_copy(parts[i][0].at[pl.ds(0, rows)], parts[i][1].at[slot, c], ls.at[i])

    def across(i, d):
        return remote(parts[i][0].at[pl.ds(0, rows)], parts[i][1].at[slot, c], fs.at[i, d - 1], fr.at[i, d - 1], at((slot + d) % half, c))

    def sibling(i, d):
        if d == 0:
            return remote(parts[i][0].at[pl.ds(0, rows)], parts[i][1].at[slot, c], gs.at[i, d], gr.at[i, d], at(slot, 1 - c))
        there = parts[i][1].at[(slot + half - d) % half, c]
        return remote(there, there, gs.at[i, d], gr.at[i, d], at(slot, 1 - c))

    for i in range(2):
        for d in range(1, half):
            across(i, d).start()
        sibling(i, 0).start()
        local(i).start()
    for i in range(2):
        for d in range(1, half):
            across(i, d).wait_recv()
            sibling(i, d).start()
    for i in range(2):
        local(i).wait()
        sibling(i, 0).wait()
        for d in range(1, half):
            across(i, d).wait_send()
            sibling(i, d).wait()


def gather_keys(k_pre, v, gain, cos, sin, rows, n, cid):
    group = PROMPT_LENGTH // rows
    half = group // 2
    width = k_pre.shape[1]
    D = pltpu.SemaphoreType.DMA
    vm, hbm = pl.BlockSpec(memory_space=pltpu.VMEM), pl.BlockSpec(memory_space=pl.ANY)
    wide = jax.ShapeDtypeStruct((half, 2, rows, width), bf16)
    k_rot, ks, vs = pl.pallas_call(
        partial(keys_kernel, n, group),
        out_shape=[jax.ShapeDtypeStruct(k_pre.shape, bf16), wide, wide],
        in_specs=[vm] * 5,
        out_specs=[vm, hbm, hbm],
        scratch_shapes=[D((2, max(half - 1, 1)))] * 2 + [D((2, half))] * 2 + [D((2,))],
        compiler_params=pltpu.CompilerParams(collective_id=cid, has_side_effects=True),
        name="prompt_keys",
    )(k_pre, v, gain, cos, sin)
    return k_rot, ks.reshape(PROMPT_LENGTH, width), vs.reshape(PROMPT_LENGTH, width)


def key_grads_kernel(n, group, dk, dv, dks, dvs, k_pre, gain, cos, sin, dk_out, dv_out, g_out, s1, r1, s2, r2, dk_rot, gs, gr, fs, fr):
    rows = dk.shape[2]
    half = group // 2
    rep, a, b, c = position(n)
    me = (a * 2 + b) * 2 + c
    first = (me // group) * half
    slot = (me // 2) % half

    def at(s, c):
        return (rep, (first + s) * 2 + c)

    meet([at((slot + d) % half, c) for d in range(1, half)] + [at(slot, 1 - c)])
    parts = [dk, dv]

    def to_sibling(i, d):
        s = (slot + d) % half
        return remote(parts[i].at[s, 1 - c], r1.at[i, d], gs.at[i, d], gr.at[i, d], at(slot, 1 - c))

    def across(i, d):
        return remote(s1.at[i, d], r2.at[i, d - 1], fs.at[i, d - 1], fr.at[i, d - 1], at((slot + d) % half, c))

    order = list(range(1, half)) + [0]
    for d in order:
        for i in range(2):
            to_sibling(i, d).start()
    for d in order:
        for i in range(2):
            to_sibling(i, d).wait_recv()
            s1[i, d] = (parts[i][(slot + d) % half, c].astype(f32) + r1[i, d].astype(f32)).astype(bf16)
            if d:
                across(i, d).start()
    for i in range(2):
        for d in range(1, half):
            across(i, d).wait_recv()

    def total(i):
        t = s1[i, 0].astype(f32)
        for d in range(1, half):
            t = t + r2[i, d - 1].astype(f32)
        return t

    dv_out[pl.ds(0, rows), :] = total(1).astype(bf16)
    dv_out[pl.ds(rows, dvs.shape[0]), :] = dvs[...].astype(bf16)
    dk_rot[pl.ds(0, rows), :] = total(0)
    dk_rot[pl.ds(rows, dks.shape[0]), :] = dks[...].astype(f32)
    g_out[...] = jnp.zeros_like(g_out)

    def head(j, _):
        lanes = pl.ds(pl.multiple_of(j * HEAD_SIZE, HEAD_SIZE), HEAD_SIZE)
        x = k_pre[:, lanes]
        rs = lax.rsqrt(jnp.mean(x * x, axis=-1, keepdims=True) + norm_epsilon)
        unit = x * rs
        dy = dk_rot[:, lanes]
        dy = dy * cos[...] - pltpu.roll(dy, HEAD_SIZE // 2, 1) * sin[...]
        g_out[0:1, :] += jnp.sum(dy * unit, axis=0, keepdims=True)
        dy = dy * gain[...]
        dk_out[:, lanes] = (rs * (dy - unit * jnp.mean(dy * unit, axis=-1, keepdims=True))).astype(bf16)
        return 0

    lax.fori_loop(0, KEY_VALUE_HEADS, head, 0)
    for i in range(2):
        for d in range(half):
            to_sibling(i, d).wait_send()
            if d:
                across(i, d).wait_send()


def key_grads(dk, dv, dks, dvs, k_pre, gain, cos, sin, rows, n, cid):
    group = PROMPT_LENGTH // rows
    half = group // 2
    width = k_pre.shape[1]
    D = pltpu.SemaphoreType.DMA
    vm = pl.BlockSpec(memory_space=pltpu.VMEM)
    V = pltpu.VMEM
    block = (rows, width)
    return pl.pallas_call(
        partial(key_grads_kernel, n, group),
        out_shape=[jax.ShapeDtypeStruct(k_pre.shape, bf16), jax.ShapeDtypeStruct(k_pre.shape, bf16), jax.ShapeDtypeStruct((8, HEAD_SIZE), f32)],
        in_specs=[vm] * 8,
        out_specs=[vm] * 3,
        scratch_shapes=[V((2, half) + block, bf16), V((2, half) + block, bf16), V((1, 8, 128), bf16), V((2, max(half - 1, 1)) + block, bf16), V(k_pre.shape, f32)]
        + [D((2, half))] * 2 + [D((2, max(half - 1, 1)))] * 2,
        compiler_params=pltpu.CompilerParams(collective_id=cid, has_side_effects=True, vmem_limit_bytes=60 << 20),
        name="prompt_key_grads",
    )(dk.reshape(half, 2, rows, width), dv.reshape(half, 2, rows, width), dks, dvs, k_pre, gain, cos, sin)


def attend_kernel(rows, q_pre, ks, vs, k_own, v_own, gain, cos, sin, past, inside, out, q_out, lse_out, rs_out):
    scale = HEAD_SIZE ** -0.5 * LOG2E
    for g in range(QUERY_HEADS // KEY_VALUE_HEADS):
        lanes = slice(g * HEAD_SIZE, (g + 1) * HEAD_SIZE)
        q = q_pre[:, lanes].T
        rs = lax.rsqrt(jnp.mean(q * q, axis=0, keepdims=True) + norm_epsilon)
        rs_out[0, g:g + 1, :] = rs
        q = q * rs * gain[:, 0:1]
        lo, hi = q[:HEAD_SIZE // 2], q[HEAD_SIZE // 2:]
        q = jnp.concatenate([lo * cos[...] - hi * sin[...], hi * cos[...] + lo * sin[...]], axis=0).astype(bf16)
        q_out[lanes, :] = q
        p = jnp.exp2(mm(ks[...], q[:, :rows], 1, 0) * scale + past[...])
        total = jnp.sum(p, axis=0, keepdims=True)
        o = mm(vs[...], p.astype(bf16), 0, 0) / total
        out[:rows, lanes] = o.T.astype(bf16)
        lse_out[0, g:g + 1, :rows] = jnp.log2(total)
        p = jnp.exp2(mm(ks[...], q[:, rows:], 1, 0) * scale)
        r = jnp.exp2(mm(k_own[rows:, :], q[:, rows:], 1, 0) * scale + inside[...])
        total = jnp.sum(p, axis=0, keepdims=True) + jnp.sum(r, axis=0, keepdims=True)
        o = (mm(vs[...], p.astype(bf16), 0, 0) + mm(v_own[rows:, :], r.astype(bf16), 0, 0)) / total
        out[rows:, lanes] = o.T.astype(bf16)
        lse_out[0, g:g + 1, rows:] = jnp.log2(total)


def attend(q_pre, ks, vs, k_own, v_own, gain, cos, sin, past, inside, rows):
    total = q_pre.shape[0]
    pair = 2 * HEAD_SIZE
    whole = lambda x: pl.BlockSpec(x.shape, lambda j: (0,) * x.ndim)
    col = lambda r, w: pl.BlockSpec((r, w), lambda j: (0, j))
    small = pl.BlockSpec((1, 2, total), lambda j: (j, 0, 0))
    return pl.pallas_call(
        partial(attend_kernel, rows),
        grid=(KEY_VALUE_HEADS,),
        in_specs=[col(total, pair), col(PROMPT_LENGTH, HEAD_SIZE), col(PROMPT_LENGTH, HEAD_SIZE), col(total, HEAD_SIZE), col(total, HEAD_SIZE),
                  whole(gain), whole(cos), whole(sin), whole(past), whole(inside)],
        out_specs=[col(total, pair), pl.BlockSpec((pair, total), lambda j: (j, 0)), small, small],
        out_shape=[jax.ShapeDtypeStruct((total, QUERY_HEADS * HEAD_SIZE), bf16), jax.ShapeDtypeStruct((QUERY_HEADS * HEAD_SIZE, total), bf16),
                   jax.ShapeDtypeStruct((KEY_VALUE_HEADS, 2, total), f32), jax.ShapeDtypeStruct((KEY_VALUE_HEADS, 2, total), f32)],
        compiler_params=pltpu.CompilerParams(vmem_limit_bytes=60 << 20),
        name="attend",
    )(q_pre, ks, vs, k_own, v_own, gain, cos, sin, past, inside)


def attend_back_kernel(rows, q_rot, ks, vs, k_own, v_own, d_out, out, lse, rs_in, gain, cos, sin, past, inside, dq_out, dk_out, dv_out, dks_out, dvs_out, g_out):
    scale = HEAD_SIZE ** -0.5
    dk = dv = dks = dvs = None
    plus = lambda x, y: y if x is None else x + y
    gain_grad = None
    for g in range(QUERY_HEADS // KEY_VALUE_HEADS):
        lanes = slice(g * HEAD_SIZE, (g + 1) * HEAD_SIZE)
        q = q_rot[lanes, :]
        do = d_out[:, lanes]
        delta = jnp.sum((do.astype(f32) * out[:, lanes].astype(f32)).T, axis=0, keepdims=True)
        log_total = lse[0, g:g + 1, :]
        dq = []
        for suffix in range(2):
            part = slice(rows, None) if suffix else slice(0, rows)
            qp, dop, lp, dp = q[:, part], do[part], log_total[:, part], delta[:, part]
            blocks = [(ks[...], vs[...], None if suffix else past[...])]
            if suffix:
                blocks.append((k_own[rows:, :], v_own[rows:, :], inside[...]))
            dqp = None
            for i, (kb, vb, bias) in enumerate(blocks):
                s = mm(kb, qp, 1, 0) * (scale * LOG2E) - lp
                p = jnp.exp2(s if bias is None else s + bias)
                ds = (p * (mm(vb, dop, 1, 1) - dp)).astype(bf16)
                dvp = mm(p.astype(bf16), dop, 1, 0)
                dkp = mm(ds, qp, 1, 1)
                dqp = plus(dqp, mm(kb, ds, 0, 0))
                if i:
                    dks, dvs = plus(dks, dkp), plus(dvs, dvp)
                else:
                    dk, dv = plus(dk, dkp), plus(dv, dvp)
            dq.append(dqp)
        dq = jnp.concatenate(dq, axis=1) * scale
        half = HEAD_SIZE // 2
        c, s = cos[...], sin[...]
        dy = jnp.concatenate([dq[:half] * c + dq[half:] * s, dq[half:] * c - dq[:half] * s], axis=0)
        qf = q.astype(f32)
        unit = jnp.concatenate([qf[:half] * c + qf[half:] * s, qf[half:] * c - qf[:half] * s], axis=0) / gain[:, 0:1]
        gg = dy * unit
        for t in range(gg.shape[1] // 128):
            gain_grad = plus(gain_grad, gg[:, t * 128:(t + 1) * 128])
        dy = dy * gain[:, 0:1]
        dx = rs_in[0, g:g + 1, :] * (dy - unit * jnp.mean(dy * unit, axis=0, keepdims=True))
        dq_out[:, lanes] = dx.T.astype(bf16)
    dk_out[...] = (dk * scale).astype(bf16)
    dv_out[...] = dv.astype(bf16)
    dks_out[...] = (dks * scale).astype(bf16)
    dvs_out[...] = dvs.astype(bf16)

    @pl.when(pl.program_id(0) == 0)
    def _():
        g_out[...] = gain_grad

    @pl.when(pl.program_id(0) > 0)
    def _():
        g_out[...] += gain_grad


def attend_back(q_rot, ks, vs, k_own, v_own, d_out, out, lse, rs, gain, cos, sin, past, inside, rows):
    total = k_own.shape[0]
    pair = 2 * HEAD_SIZE
    whole = lambda x: pl.BlockSpec(x.shape, lambda j: (0,) * x.ndim)
    col = lambda r, w: pl.BlockSpec((r, w), lambda j: (0, j))
    small = pl.BlockSpec((1, 2, total), lambda j: (j, 0, 0))
    width = KEY_VALUE_HEADS * HEAD_SIZE
    kv, own = jax.ShapeDtypeStruct((PROMPT_LENGTH, width), bf16), jax.ShapeDtypeStruct((total - rows, width), bf16)
    return pl.pallas_call(
        partial(attend_back_kernel, rows),
        grid=(KEY_VALUE_HEADS,),
        in_specs=[pl.BlockSpec((pair, total), lambda j: (j, 0)), col(PROMPT_LENGTH, HEAD_SIZE), col(PROMPT_LENGTH, HEAD_SIZE), col(total, HEAD_SIZE),
                  col(total, HEAD_SIZE), col(total, pair), col(total, pair), small, small, whole(gain), whole(cos), whole(sin), whole(past), whole(inside)],
        out_specs=[col(total, pair), col(PROMPT_LENGTH, HEAD_SIZE), col(PROMPT_LENGTH, HEAD_SIZE), col(total - rows, HEAD_SIZE), col(total - rows, HEAD_SIZE),
                   pl.BlockSpec((HEAD_SIZE, 128), lambda j: (0, 0))],
        out_shape=[jax.ShapeDtypeStruct((total, QUERY_HEADS * HEAD_SIZE), bf16), kv, kv, own, own, jax.ShapeDtypeStruct((HEAD_SIZE, 128), f32)],
        compiler_params=pltpu.CompilerParams(vmem_limit_bytes=60 << 20),
        name="attend_back",
    )(q_rot, ks, vs, k_own, v_own, d_out, out, lse, rs, gain, cos, sin, past, inside)


def root_mean_scale(values, gain_vector):
    return (
        values
        * lax.rsqrt(jnp.mean(values * values, axis=-1, keepdims=True) + norm_epsilon)
        * gain_vector
    )


def swiglu(gate_pre, up_pre):
    return jax.nn.silu(gate_pre) * up_pre


def dot(x, y):
    return jnp.dot(x, y, preferred_element_type=f32)


def dot_tn(x, y):
    return jnp.einsum("ra,rb->ab", x, y, preferred_element_type=f32)


def dot_nt(x, y):
    return jnp.einsum("ra,ba->rb", x, y, preferred_element_type=f32)


def per_device(
    prompt_rows,
    suffix_rows,
    assignment,
    lengths,
    attention_gain,
    query_weight,
    key_matrix,
    value_matrix,
    query_gain,
    key_norm_gain,
    out_weight,
    mlp_gain,
    gate_weight,
    up_weight,
    down_weight,
    prompt_cotangent,
    suffix_cotangent,
):
    n, R = lax.axis_size("fsdp"), lax.axis_size("rep")
    rank = lax.axis_index("fsdp")
    rows = prompt_rows.shape[0]
    suffix = suffix_rows.shape[0]
    S = suffix // CONTINUATION_LEN
    total = rows + suffix
    width = MODEL_WIDTH

    pad = lambda v: jnp.pad(v.astype(f32).reshape(-1), (0, 128 - v.size))
    tile = jnp.stack([pad(v) for v in (attention_gain, mlp_gain, query_gain, key_norm_gain, assignment, lengths)])
    tile = jnp.pad(tile, ((0, 2), (0, 0)))
    cut = lambda v: v.reshape(S, n, CONTINUATION_LEN // n, width)
    weights, tiles, staged = gather(
        [key_matrix, value_matrix, query_weight, out_weight, gate_weight, up_weight, down_weight],
        tile,
        [cut(suffix_rows), cut(suffix_cotangent)],
        n,
        0,
    )
    w_key, w_value, w_query, w_out, w_gate, w_up, w_down = weights
    gain_first = tiles[:, 0, : attention_gain.size].reshape(-1)
    gain_second = tiles[:, 1, : mlp_gain.size].reshape(-1)
    query_scale = tiles[:, 2, : query_gain.size].reshape(-1)
    key_scale = tiles[:, 3, : key_norm_gain.size].reshape(-1)

    owner = tiles[:, 4, :S].reshape(-1).astype(jnp.int32) // CONT
    slot_count = n * S
    ids = jnp.arange(slot_count, dtype=jnp.int32)
    ahead = (owner[None, :] < owner[:, None]) | ((owner[None, :] == owner[:, None]) & (ids[None, :] < ids[:, None]))
    place = jnp.sum(ahead.astype(jnp.int32), axis=1)
    hits = place[None, :] == ids[:, None]
    order = jnp.sum(jnp.where(hits, ids[None, :], 0), axis=1)
    slot_lengths = jnp.sum(jnp.where(hits, tiles[:, 5, :S].reshape(-1).astype(jnp.int32)[None, :], 0), axis=1)
    own_lengths = lax.dynamic_slice_in_dim(slot_lengths, rank * S, S)

    moved_rows, moved_cotangent = [v.reshape(suffix, width) for v in collect(order, staged, n, 1)]

    prompt_place = (rank * rows) % PROMPT_LENGTH + jnp.arange(rows, dtype=jnp.int32)
    suffix_place = jnp.arange(suffix, dtype=jnp.int32) % CONTINUATION_LEN
    suffix_slot = jnp.arange(suffix, dtype=jnp.int32) // CONTINUATION_LEN
    length_rows = jnp.repeat(own_lengths, CONTINUATION_LEN)
    suffix_valid = suffix_place < length_rows
    valid_rows = jnp.concatenate([jnp.ones((rows,), f32), suffix_valid.astype(f32)])
    token_positions = jnp.concatenate([prompt_place, PROMPT_LENGTH + suffix_place]).astype(f32)
    half = HEAD_SIZE // 2
    inverse = rope_theta ** (jnp.arange(half, dtype=f32) * (-2.0 / HEAD_SIZE))
    angles_t = inverse[:, None] * token_positions[None, :]
    cos_t, sin_t = jnp.cos(angles_t), jnp.sin(angles_t)
    cos_r, sin_r = cos_t.T, sin_t.T
    cos_rows = jnp.concatenate([cos_r, cos_r], axis=1)
    sin_rows = jnp.concatenate([-sin_r, sin_r], axis=1)
    past = jnp.where(jnp.arange(PROMPT_LENGTH, dtype=jnp.int32)[:, None] <= prompt_place[None, :], 0.0, masked_score).astype(f32)
    inside = jnp.where(
        (suffix_slot[:, None] == suffix_slot[None, :]) & (suffix_place[:, None] <= suffix_place[None, :]) & suffix_valid[:, None], 0.0, masked_score
    ).astype(f32)

    rows_wide = jnp.concatenate([prompt_rows, moved_rows], 0).astype(f32)
    hidden_wide, first_pull = jax.vjp(root_mean_scale, rows_wide, gain_first)
    hidden = hidden_wide.astype(bf16)
    key_pre = dot(hidden, w_key)
    values = dot(hidden, w_value).astype(bf16)
    query_pre = dot(hidden, w_query)
    key_gain_row = key_scale.reshape(1, HEAD_SIZE)
    query_gain_col = jnp.broadcast_to(query_scale[:, None], (HEAD_SIZE, 128))
    key_rot, prompt_keys, prompt_values = gather_keys(key_pre, values, key_gain_row, cos_rows, sin_rows, rows, n, 2)
    attended, query_rot, lse, query_rs = attend(
        query_pre, prompt_keys, prompt_values, key_rot, values, query_gain_col, cos_t, sin_t, past, inside, rows
    )
    residual = rows_wide + dot(attended, w_out)
    hidden_two_wide, second_pull = jax.vjp(root_mean_scale, residual, gain_second)
    hidden_two = hidden_two_wide.astype(bf16)
    gate_pre = dot(hidden_two, w_gate)
    up_pre = dot(hidden_two, w_up)
    act_wide, act_pull = jax.vjp(swiglu, gate_pre, up_pre)
    act = act_wide.astype(bf16)
    mixed_full = residual + dot(act, w_down)
    d_mixed = jnp.concatenate([prompt_cotangent, moved_cotangent], 0).astype(f32) * valid_rows[:, None]
    d_mixed_low = d_mixed.astype(bf16)
    grad_down = dot_tn(act, d_mixed_low).astype(bf16)
    d_act = dot_nt(d_mixed_low, w_down)
    d_gate_wide, d_up_wide = act_pull(d_act)
    d_gate, d_up = d_gate_wide.astype(bf16), d_up_wide.astype(bf16)
    grad_gate = dot_tn(hidden_two, d_gate).astype(bf16)
    grad_up = dot_tn(hidden_two, d_up).astype(bf16)
    d_hidden_two = dot_nt(d_gate, w_gate) + dot_nt(d_up, w_up)
    d_resid_mlp, grad_second_gain = second_pull(d_hidden_two)
    d_resid = d_mixed + d_resid_mlp
    d_resid_low = d_resid.astype(bf16)
    grad_out = dot_tn(attended, d_resid_low).astype(bf16)
    d_attended = dot_nt(d_resid_low, w_out).astype(bf16)
    d_query, dk, dv, dk_own, dv_own, gain_part = attend_back(
        query_rot, prompt_keys, prompt_values, key_rot, values, d_attended, attended, lse, query_rs, query_gain_col, cos_t, sin_t, past, inside, rows
    )
    grad_query_gain = jnp.sum(gain_part, axis=1)
    d_key, d_value, key_gain_part = key_grads(dk, dv, dk_own, dv_own, key_pre, key_gain_row, cos_rows, sin_rows, rows, n, 3)
    grad_key_gain = key_gain_part[0]
    grad_query = dot_tn(hidden, d_query).astype(bf16)
    grad_key = dot_tn(hidden, d_key).astype(bf16)
    grad_value = dot_tn(hidden, d_value).astype(bf16)
    d_hidden = dot_nt(d_query, w_query) + dot_nt(d_key, w_key) + dot_nt(d_value, w_value)
    d_rows_attn, grad_first_gain = first_pull(d_hidden)
    d_rows = d_resid + d_rows_attn
    stats = jnp.stack(
        [
            jnp.sum(valid_rows * jnp.sum(mixed_full * mixed_full, axis=-1)),
            jnp.sum(valid_rows * jnp.sum(residual * residual, axis=-1)),
            jnp.sum(valid_rows * jnp.sum(d_rows * d_rows, axis=-1)),
            jnp.sum(valid_rows),
        ]
    )
    vec = jnp.concatenate([grad_first_gain, grad_second_gain, grad_query_gain, grad_key_gain, jnp.pad(stats, (0, 124))])
    vec = jnp.pad(vec.reshape(-1, 128), ((0, (-vec.shape[0] // 128) % 8), (0, 0)))
    mixed_low = mixed_full.astype(bf16)
    back = spread([cut(mixed_low[rows:]), cut(d_rows[rows:].astype(bf16))], n, 4)
    shards, vec_sum = scatter([grad_down, grad_gate, grad_up, grad_out, grad_query, grad_key, grad_value], n, R, 5, vec)
    suffix_mixed, suffix_grad = [v.reshape(suffix, width) for v in collect(place, back, n, 6)]
    g_down, g_gate, g_up, g_out, g_query, g_key, g_value = [g.astype(f32) for g in shards]
    flat = vec_sum.reshape(-1)

    def mine(first, size, part):
        return lax.dynamic_slice_in_dim(flat[first : first + size], rank * part, part)

    g_first = mine(0, width, attention_gain.size)
    g_second = mine(width, width, mlp_gain.size)
    g_query_gain = mine(2 * width, HEAD_SIZE, query_gain.size)
    g_key_gain = mine(2 * width + HEAD_SIZE, HEAD_SIZE, key_norm_gain.size)
    stat_sums = flat[2 * width + 2 * HEAD_SIZE : 2 * width + 2 * HEAD_SIZE + 4]
    token_norms = jnp.sqrt(stat_sums[:3] / (stat_sums[3] * width))
    return (
        mixed_low[:rows],
        suffix_mixed,
        d_rows[:rows],
        suffix_grad.astype(f32),
        g_first,
        g_query,
        g_key,
        g_value,
        g_query_gain,
        g_key_gain,
        g_out,
        g_second,
        g_gate,
        g_up,
        g_down,
        token_norms,
    )


def solution(mesh):
    placed = (
        P(("rep", "fsdp"), None),
        P(("rep", "fsdp"), None),
        P("rep", "fsdp"),
        P("rep", "fsdp"),
        P("fsdp"),
        P("fsdp", None),
        P("fsdp", None),
        P("fsdp", None),
        P("fsdp"),
        P("fsdp"),
        P("fsdp", None),
        P("fsdp"),
        P("fsdp", None),
        P("fsdp", None),
        P("fsdp", None),
        P(("rep", "fsdp"), None),
        P(("rep", "fsdp"), None),
    )
    return jax.shard_map(
        per_device,
        mesh=mesh,
        in_specs=placed,
        out_specs=(
            P(("rep", "fsdp"), None),
            P(("rep", "fsdp"), None),
            P(("rep", "fsdp"), None),
            P(("rep", "fsdp"), None),
            P("fsdp"),
            P("fsdp", None),
            P("fsdp", None),
            P("fsdp", None),
            P("fsdp"),
            P("fsdp"),
            P("fsdp", None),
            P("fsdp"),
            P("fsdp", None),
            P("fsdp", None),
            P("fsdp", None),
            P(),
        ),
        check_vma=False,
    )
```

```python
from functools import partial

import jax
import jax.numpy as jnp
from jax import lax
from jax.experimental import pallas as pl
from jax.experimental.pallas import tpu as pltpu
from jax.sharding import PartitionSpec as P

MODEL_WIDTH = 1024
QUERY_HEADS = 16
KEY_VALUE_HEADS = 8
HEAD_SIZE = 128
PROMPT_LENGTH = 1024
CONT = 8
CONTINUATION_LEN = 128

norm_epsilon = 1e-06
rope_theta = 1000000.0
masked_score = -1e30
MESH = pl.DeviceIdType.MESH
bf16 = jnp.bfloat16
f32 = jnp.float32

def position(n):
    rep = lax.axis_index("rep")
    rank = lax.axis_index("fsdp")
    return rep, rank // 4, (rank // 2) % 2, rank % 2


def meet(peers):
    barrier = pltpu.get_barrier_semaphore()
    for p in peers:
        pl.semaphore_signal(barrier, inc=1, device_id=p, device_id_type=MESH)
    pl.semaphore_wait(barrier, len(peers))


def remote(src, dst, send, recv, to):
    return pltpu.make_async_remote_copy(src, dst, send, recv, device_id=to, device_id_type=MESH)


def gather_kernel(n, m, k, *refs):
    A = n // 4
    it = iter(refs)
    take = lambda count: [next(it) for _ in range(count)]
    own, (tile,), pieces = take(m), take(1), take(k)
    full, (tiles,), staged = take(m), take(1), take(k)
    zs, zr, s2s, s2r, s3s, s3r, cs, cr, ls, ts, tr, ps, pr, pls = take(14)
    rep, a, b, c = position(n)
    me = (a * 2 + b) * 2 + c
    h = rep % 2
    mate = rep + 1 - 2 * h

    def dev(r, a, b, c):
        return (r, (a * 2 + b) * 2 + c)

    meet([(rep, (me + d) % n) for d in range(1, n)] + [dev(mate, a, b, c)])
    ydev, xdev, cdev = dev(rep, a, 1 - b, c), dev(mate, a, b, c), dev(rep, a, b, 1 - c)

    def local(i):
        return pltpu.make_async_copy(own[i].at[:, h], full[i].at[a, b, c, :, h], ls.at[i])

    def along(i, d):
        return remote(own[i].at[:, h], full[i].at[a, b, c, :, h], zs.at[i, d - 1], zr.at[i, d - 1], dev(rep, (a + d) % A, b, c))

    def s2(i):
        y, x = full[i].at[:, b, c, 0, h], full[i].at[:, b, c, 1, h]
        return [remote(y, y, s2s.at[i, 0], s2r.at[i, 0], ydev), remote(x, x, s2s.at[i, 1], s2r.at[i, 1], xdev)]

    def s3(i):
        x, y = full[i].at[:, :, c, 0, h], full[i].at[:, b, c, 1]
        return [remote(x, x, s3s.at[i, 0], s3r.at[i, 0], xdev), remote(y, y, s3s.at[i, 1], s3r.at[i, 1], ydev)]

    def s4(i):
        both = full[i].at[:, :, c]
        return [remote(both, both, cs.at[i], cr.at[i], cdev)]

    def share(d):
        return remote(tile, tiles.at[me], ts.at[d - 1], tr.at[d - 1], (rep, (me + d) % n))

    def piece(i, d):
        to = (me + d) % n
        return remote(pieces[i].at[:, to], staged[i].at[me], ps.at[i, d - 1], pr.at[i, d - 1], (rep, to))

    def own_piece(i):
        return pltpu.make_async_copy(pieces[i].at[:, me], staged[i].at[me], pls.at[i])

    for d in range(1, n):
        share(d).start()
    tiles[me] = tile[...]
    for i in range(k):
        own_piece(i).start()
        for d in range(1, n):
            piece(i, d).start()
    for i in range(m):
        local(i).start()
        for d in range(1, A):
            along(i, d).start()
    for t in range(m + 3):
        if t < m:
            local(t).wait()
            for d in range(1, A):
                along(t, d).wait_recv()
            for q in s2(t):
                q.start()
        if 0 <= t - 1 < m:
            for q in s2(t - 1):
                q.wait_recv()
            for q in s3(t - 1):
                q.start()
        if 0 <= t - 2 < m:
            for q in s3(t - 2):
                q.wait_recv()
            for q in s4(t - 2):
                q.start()
        if 0 <= t - 3 < m:
            for q in s4(t - 3):
                q.wait_recv()
    for d in range(1, n):
        share(d).wait()
    for i in range(k):
        own_piece(i).wait()
        for d in range(1, n):
            piece(i, d).wait()
    for t in range(m):
        for d in range(1, A):
            along(t, d).wait_send()
        for q in s2(t) + s3(t) + s4(t):
            q.wait_send()


def gather(shards, tile, slots, n, cid):
    m, k, A = len(shards), len(slots), n // 4
    views = [s.reshape(2, 2, s.shape[0] // 4, s.shape[1]) for s in shards]
    outs = [jax.ShapeDtypeStruct((A, 2, 2) + v.shape, v.dtype) for v in views]
    outs += [jax.ShapeDtypeStruct((n,) + tile.shape, tile.dtype)]
    outs += [jax.ShapeDtypeStruct((n, s.shape[0]) + s.shape[2:], s.dtype) for s in slots]
    D = pltpu.SemaphoreType.DMA
    vm, hbm = pl.BlockSpec(memory_space=pltpu.VMEM), pl.BlockSpec(memory_space=pl.ANY)
    res = pl.pallas_call(
        partial(gather_kernel, n, m, k),
        out_shape=outs,
        in_specs=[vm] * (m + 1 + k),
        out_specs=[hbm] * m + [vm] + [hbm] * k,
        scratch_shapes=[D((m, A - 1))] * 2 + [D((m, 2))] * 4 + [D((m,))] * 3 + [D((n - 1,))] * 2 + [D((max(k, 1), n - 1))] * 2 + [D((max(k, 1),))],
        compiler_params=pltpu.CompilerParams(collective_id=cid, has_side_effects=True),
        name="gather",
    )(*views, tile, *slots)
    return [f.reshape(-1, s.shape[1]) for f, s in zip(res, shards)], res[m], res[m + 1:]


def spread_kernel(n, k, *refs):
    it = iter(refs)
    take = lambda count: [next(it) for _ in range(count)]
    pieces, staged, (ps, pr, pls) = take(k), take(k), take(3)
    rep, a, b, c = position(n)
    me = (a * 2 + b) * 2 + c
    meet([(rep, (me + d) % n) for d in range(1, n)])

    def piece(i, d):
        to = (me + d) % n
        return remote(pieces[i].at[:, to], staged[i].at[me], ps.at[i, d - 1], pr.at[i, d - 1], (rep, to))

    def own_piece(i):
        return pltpu.make_async_copy(pieces[i].at[:, me], staged[i].at[me], pls.at[i])

    for i in range(k):
        own_piece(i).start()
        for d in range(1, n):
            piece(i, d).start()
    for i in range(k):
        own_piece(i).wait()
        for d in range(1, n):
            piece(i, d).wait()


def spread(slots, n, cid):
    k = len(slots)
    D = pltpu.SemaphoreType.DMA
    vm, hbm = pl.BlockSpec(memory_space=pltpu.VMEM), pl.BlockSpec(memory_space=pl.ANY)
    return pl.pallas_call(
        partial(spread_kernel, n, k),
        out_shape=[jax.ShapeDtypeStruct((n, s.shape[0]) + s.shape[2:], s.dtype) for s in slots],
        in_specs=[vm] * k,
        out_specs=[hbm] * k,
        scratch_shapes=[D((k, n - 1))] * 2 + [D((k,))],
        compiler_params=pltpu.CompilerParams(collective_id=cid, has_side_effects=True),
        name="spread",
    )(*slots)


def collect_kernel(n, k, *refs):
    it = iter(refs)
    take = lambda count: [next(it) for _ in range(count)]
    (index,), staged, final, ordered, (ps, pr, pls) = take(1), take(k), take(k), take(k), take(3)
    rep, a, b, c = position(n)
    me = (a * 2 + b) * 2 + c
    meet([(rep, (me + d) % n) for d in range(1, n)])
    S = ordered[0].shape[1]
    for i in range(k):
        def place(j, _):
            ordered[i][j // S, j % S] = staged[i][index[j]]
            return 0
        lax.fori_loop(0, n * S, place, 0)

    def piece(i, d):
        to = (me + d) % n
        return remote(ordered[i].at[to], final[i].at[:, me], ps.at[i, d - 1], pr.at[i, d - 1], (rep, to))

    def own_piece(i):
        return pltpu.make_async_copy(ordered[i].at[me], final[i].at[:, me], pls.at[i])

    for i in range(k):
        own_piece(i).start()
        for d in range(1, n):
            piece(i, d).start()
    for i in range(k):
        own_piece(i).wait()
        for d in range(1, n):
            piece(i, d).wait()


def collect(index, staged, n, cid):
    k = len(staged)
    flat = [s.reshape((-1,) + s.shape[2:]) for s in staged]
    D = pltpu.SemaphoreType.DMA
    vm, hbm, sm = pl.BlockSpec(memory_space=pltpu.VMEM), pl.BlockSpec(memory_space=pl.ANY), pl.BlockSpec(memory_space=pltpu.SMEM)
    return pl.pallas_call(
        partial(collect_kernel, n, k),
        out_shape=[jax.ShapeDtypeStruct((s.shape[1], n) + s.shape[2:], s.dtype) for s in staged],
        in_specs=[sm] + [vm] * k,
        out_specs=[hbm] * k,
        scratch_shapes=[pltpu.VMEM(s.shape, s.dtype) for s in staged] + [D((k, n - 1))] * 2 + [D((k,))],
        compiler_params=pltpu.CompilerParams(collective_id=cid, has_side_effects=True),
        name="collect",
    )(index, *flat)


def add_rows(count, out, first, second, step=None):
    def one(j, _):
        o = out(j)
        total = first(j)[...].astype(jnp.float32)
        for s in second:
            total = total + s(j)[...].astype(jnp.float32)
        o[...] = total.astype(o.dtype)
        return 0
    lax.fori_loop(0, count, one, 0)

def scatter_kernel(n, R, m, has_vec, *refs):
    A = n // 4
    bits = R.bit_length() - 1
    it = iter(refs)
    take = lambda k: [next(it) for _ in range(k)]
    grads = take(m)
    vec = next(it) if has_vec else None
    outs = take(m)
    vout = next(it) if has_vec else None
    own, b1, b2y, b2x, b3, b4, b5 = [take(m) for _ in range(7)]
    s4 = take(m)
    vb = next(it) if has_vec else None
    vz = next(it) if has_vec else None
    ls, s1s, s1r, s2s, s2r, s3s, s3r, s4s, s4r, s5s, s5r, ws = take(12)
    if has_vec:
        vs, vr = take(2)
    rep, a, b, c = position(n)
    h = rep % 2
    mate = rep + 1 - 2 * h
    def dev(r, a, b, c):
        return (r, (a * 2 + b) * 2 + c)
    ydev, xdev, cdev = dev(rep, a, 1 - b, c), dev(mate, a, b, c), dev(rep, a, b, 1 - c)
    zdev = lambda d: dev(rep, (a + d) % A, b, c)
    def flip(bit):
        w = 1 << bit
        return dev(rep + w - 2 * w * ((rep // w) % 2), a, b, c)
    barrier = pltpu.get_barrier_semaphore()
    peers = [zdev(d) for d in range(1, A)] + [ydev, xdev, cdev] + [flip(k) for k in range(1, bits)]
    for p in peers:
        pl.semaphore_signal(barrier, inc=1, device_id=p, device_id_type=MESH)
    pl.semaphore_wait(barrier, len(peers))
    def rc(src, dst, ss, rs, to):
        return pltpu.make_async_remote_copy(src, dst, ss, rs, device_id=to, device_id_type=MESH)
    def load(i): return pltpu.make_async_copy(grads[i].at[:, :, c], own[i], ls.at[i])
    def S1(i): return [rc(grads[i].at[:, :, 1 - c], b1[i], s1s.at[i], s1r.at[i], cdev)]
    def S2(i): return [rc(b1[i].at[:, 1 - b, 0], b2y[i], s2s.at[i, 0], s2r.at[i, 0], ydev),
                       rc(b1[i].at[:, :, 1, 1 - h], b2x[i], s2s.at[i, 1], s2r.at[i, 1], xdev)]
    def S3(i): return [rc(b2y[i].at[:, 1 - h], b3[i].at[0], s3s.at[i, 0], s3r.at[i, 0], xdev),
                       rc(b2x[i].at[:, 1 - b], b3[i].at[1], s3s.at[i, 1], s3r.at[i, 1], ydev)]
    def S4(i): return [rc(b3[i].at[:, (a + d) % A], b4[i].at[d - 1], s4s.at[i, d - 1], s4r.at[i, d - 1], zdev(d)) for d in range(1, A)]
    def S5(i, k): return rc(s4[i].at[0] if k == bits - 1 else s4[i].at[k], b5[i].at[k], s5s.at[i, k], s5r.at[i, k], xdev if k == bits - 1 else flip(k + 1))
    def put(i, k): return pltpu.make_async_copy((s4[i].at[0] if bits == 1 else s4[i].at[bits - 1]) if k == 0 else b5[i].at[bits - 1], outs[i].at[:, h if k == 0 else 1 - h], ws.at[i, k])
    for i in range(m):
        load(i).start()
        for q in S1(i): q.start()
    if has_vec:
        rounds = [cdev, ydev, xdev] + [flip(k) for k in range(1, bits)]
        vb[0] = vec[...]
        for k, to in enumerate(rounds):
            q = rc(vb.at[2 * k], vb.at[2 * k + 1], vs.at[k], vr.at[k], to)
            q.start(); q.wait()
            vb[2 * k + 2] = vb[2 * k] + vb[2 * k + 1]
        last = 2 * len(rounds)
        nr = len(rounds)
        qs = [rc(vb.at[last], vz.at[a], vs.at[nr + d - 1], vr.at[nr + d - 1], zdev(d)) for d in range(1, A)]
        for q in qs: q.start()
        vz[a] = vb[last]
        for q in qs: q.wait()
        total = vz[0]
        for k in range(1, A):
            total = total + vz[k]
        vout[...] = total
    for t in range(m + 4):
        i = t
        if t < m:
            load(i).wait()
            for q in S1(i): q.wait_recv()
            add_rows(A * 2 * 4, lambda j, i=i: b1[i].at[j // 8, (j // 4) % 2, (j // 2) % 2, j % 2],
                     lambda j, i=i: b1[i].at[j // 8, (j // 4) % 2, (j // 2) % 2, j % 2],
                     [lambda j, i=i: own[i].at[j // 8, (j // 4) % 2, (j // 2) % 2, j % 2]])
            for q in S2(i): q.start()
        i = t - 1
        if 0 <= i < m:
            for q in S2(i): q.wait_recv()
            add_rows(A * 2, lambda j, i=i: b2y[i].at[j // 2, j % 2], lambda j, i=i: b2y[i].at[j // 2, j % 2],
                     [lambda j, i=i: b1[i].at[j // 2, b, 0, j % 2]])
            add_rows(A * 2, lambda j, i=i: b2x[i].at[j // 2, j % 2], lambda j, i=i: b2x[i].at[j // 2, j % 2],
                     [lambda j, i=i: b1[i].at[j // 2, j % 2, 1, h]])
            for q in S3(i): q.start()
        i = t - 2
        if 0 <= i < m:
            for q in S3(i): q.wait_recv()
            add_rows(A, lambda j, i=i: b3[i].at[0, j], lambda j, i=i: b3[i].at[0, j], [lambda j, i=i: b2y[i].at[j, h]])
            add_rows(A, lambda j, i=i: b3[i].at[1, j], lambda j, i=i: b3[i].at[1, j], [lambda j, i=i: b2x[i].at[j, b]])
            for q in S4(i): q.start()
        i = t - 3
        if 0 <= i < m:
            for q in S4(i): q.wait_recv()
            add_rows(2, lambda j, i=i: s4[i].at[0, j], lambda j, i=i: b3[i].at[j, a], [lambda j, i=i, d=d: b4[i].at[d, j] for d in range(A - 1)])
            for k in range(bits - 1):
                q = S5(i, k); q.start(); q.wait()
                add_rows(2, lambda j, i=i, k=k: s4[i].at[k + 1, j], lambda j, i=i, k=k: s4[i].at[k, j], [lambda j, i=i, k=k: b5[i].at[k, j]])
            rc(s4[i].at[bits - 1], b5[i].at[bits - 1], s5s.at[i, bits - 1], s5r.at[i, bits - 1], xdev).start()
            put(i, 0).start()
        i = t - 4
        if 0 <= i < m:
            rc(s4[i].at[bits - 1], b5[i].at[bits - 1], s5s.at[i, bits - 1], s5r.at[i, bits - 1], xdev).wait_recv()
            put(i, 1).start()
    for i in range(m):
        for q in S1(i) + S2(i) + S3(i) + S4(i): q.wait_send()
        rc(s4[i].at[bits - 1], b5[i].at[bits - 1], s5s.at[i, bits - 1], s5r.at[i, bits - 1], xdev).wait_send()
        put(i, 0).wait(); put(i, 1).wait()

def scatter(grads, n, R, cid, vec=None):
    m, A, bits = len(grads), n // 4, R.bit_length() - 1
    views = [g.reshape(A, 2, 2, 2, 2, g.shape[0] // (4 * n), g.shape[1]) for g in grads]
    sub = [v.shape[-2:] for v in views]
    bf = jnp.bfloat16
    V, D = pltpu.VMEM, pltpu.SemaphoreType.DMA
    scratch = ([V((A, 2, 2, 2) + s, bf) for s in sub] * 2 + [V((A, 2) + s, bf) for s in sub] * 2 + [V((2, A) + s, bf) for s in sub]
        + [V((A - 1, 2) + s, bf) for s in sub] + [V((bits, 2) + s, bf) for s in sub] + [V((bits, 2) + s, bf) for s in sub])
    ins, ispec = list(views), [pl.BlockSpec(memory_space=pl.ANY)] * m
    outs, ospec = [jax.ShapeDtypeStruct((2, 2) + s, bf) for s in sub], [pl.BlockSpec(memory_space=pl.ANY)] * m
    sems = [D((m,)), D((m,)), D((m,)), D((m, 2)), D((m, 2)), D((m, 2)), D((m, 2)), D((m, A - 1)), D((m, A - 1)), D((m, bits)), D((m, bits)), D((m, 2))]
    if vec is not None:
        ins.append(vec); ispec.append(pl.BlockSpec(memory_space=pltpu.VMEM))
        outs.append(jax.ShapeDtypeStruct(vec.shape, vec.dtype)); ospec.append(pl.BlockSpec(memory_space=pltpu.VMEM))
        scratch += [V((2 * (2 + bits) + 1,) + vec.shape, vec.dtype), V((A,) + vec.shape, vec.dtype)]
        sems += [D((2 + bits + A - 1,))] * 2
    res = pl.pallas_call(partial(scatter_kernel, n, R, m, vec is not None), out_shape=outs, in_specs=ispec, out_specs=ospec,
        scratch_shapes=scratch + sems,
        compiler_params=pltpu.CompilerParams(collective_id=cid, has_side_effects=True, vmem_limit_bytes=60 << 20),
        name="scatter")(*ins)
    shards = [r.reshape(-1, r.shape[-1]) for r in res[:m]]
    return (shards, res[m]) if vec is not None else shards


LOG2E = 1.4426950408889634


def mm(x, y, cx, cy):
    return lax.dot_general(x, y, (((cx,), (cy,)), ((), ())), preferred_element_type=f32)


def keys_kernel(n, group, k_pre, v, gain, cos, sin, k_out, ks, vs, fs, fr, gs, gr, ls):
    rows = ks.shape[2]
    half = group // 2
    rep, a, b, c = position(n)
    me = (a * 2 + b) * 2 + c
    first = (me // group) * half
    slot = (me // 2) % half

    def at(s, c):
        return (rep, (first + s) * 2 + c)

    others = [(slot + d) % half for d in range(1, half)]
    meet([at(s, c) for s in others] + [at(slot, 1 - c)])

    def head(j, _):
        lanes = pl.ds(pl.multiple_of(j * HEAD_SIZE, HEAD_SIZE), HEAD_SIZE)
        x = k_pre[:, lanes]
        x = x * lax.rsqrt(jnp.mean(x * x, axis=-1, keepdims=True) + norm_epsilon) * gain[...]
        k_out[:, lanes] = (x * cos[...] + pltpu.roll(x, HEAD_SIZE // 2, 1) * sin[...]).astype(bf16)
        return 0

    lax.fori_loop(0, KEY_VALUE_HEADS, head, 0)
    parts = [(k_out, ks), (v, vs)]

    def local(i):
        return pltpu.make_async_copy(parts[i][0].at[pl.ds(0, rows)], parts[i][1].at[slot, c], ls.at[i])

    def across(i, d):
        return remote(parts[i][0].at[pl.ds(0, rows)], parts[i][1].at[slot, c], fs.at[i, d - 1], fr.at[i, d - 1], at((slot + d) % half, c))

    def sibling(i, d):
        if d == 0:
            return remote(parts[i][0].at[pl.ds(0, rows)], parts[i][1].at[slot, c], gs.at[i, d], gr.at[i, d], at(slot, 1 - c))
        there = parts[i][1].at[(slot + half - d) % half, c]
        return remote(there, there, gs.at[i, d], gr.at[i, d], at(slot, 1 - c))

    for i in range(2):
        for d in range(1, half):
            across(i, d).start()
        sibling(i, 0).start()
        local(i).start()
    for i in range(2):
        for d in range(1, half):
            across(i, d).wait_recv()
            sibling(i, d).start()
    for i in range(2):
        local(i).wait()
        sibling(i, 0).wait()
        for d in range(1, half):
            across(i, d).wait_send()
            sibling(i, d).wait()


def gather_keys(k_pre, v, gain, cos, sin, rows, n, cid):
    group = PROMPT_LENGTH // rows
    half = group // 2
    width = k_pre.shape[1]
    D = pltpu.SemaphoreType.DMA
    vm, hbm = pl.BlockSpec(memory_space=pltpu.VMEM), pl.BlockSpec(memory_space=pl.ANY)
    wide = jax.ShapeDtypeStruct((half, 2, rows, width), bf16)
    k_rot, ks, vs = pl.pallas_call(
        partial(keys_kernel, n, group),
        out_shape=[jax.ShapeDtypeStruct(k_pre.shape, bf16), wide, wide],
        in_specs=[vm] * 5,
        out_specs=[vm, hbm, hbm],
        scratch_shapes=[D((2, max(half - 1, 1)))] * 2 + [D((2, half))] * 2 + [D((2,))],
        compiler_params=pltpu.CompilerParams(collective_id=cid, has_side_effects=True),
        name="prompt_keys",
    )(k_pre, v, gain, cos, sin)
    return k_rot, ks.reshape(PROMPT_LENGTH, width), vs.reshape(PROMPT_LENGTH, width)


def key_grads_kernel(n, group, dk, dv, dks, dvs, k_pre, gain, cos, sin, dk_out, dv_out, g_out, s1, r1, s2, r2, dk_rot, gs, gr, fs, fr):
    rows = dk.shape[2]
    half = group // 2
    rep, a, b, c = position(n)
    me = (a * 2 + b) * 2 + c
    first = (me // group) * half
    slot = (me // 2) % half

    def at(s, c):
        return (rep, (first + s) * 2 + c)

    meet([at((slot + d) % half, c) for d in range(1, half)] + [at(slot, 1 - c)])
    parts = [dk, dv]

    def to_sibling(i, d):
        s = (slot + d) % half
        return remote(parts[i].at[s, 1 - c], r1.at[i, d], gs.at[i, d], gr.at[i, d], at(slot, 1 - c))

    def across(i, d):
        return remote(s1.at[i, d], r2.at[i, d - 1], fs.at[i, d - 1], fr.at[i, d - 1], at((slot + d) % half, c))

    order = list(range(1, half)) + [0]
    for d in order:
        for i in range(2):
            to_sibling(i, d).start()
    for d in order:
        for i in range(2):
            to_sibling(i, d).wait_recv()
            s1[i, d] = (parts[i][(slot + d) % half, c].astype(f32) + r1[i, d].astype(f32)).astype(bf16)
            if d:
                across(i, d).start()
    for i in range(2):
        for d in range(1, half):
            across(i, d).wait_recv()

    def total(i):
        t = s1[i, 0].astype(f32)
        for d in range(1, half):
            t = t + r2[i, d - 1].astype(f32)
        return t

    dv_out[pl.ds(0, rows), :] = total(1).astype(bf16)
    dv_out[pl.ds(rows, dvs.shape[0]), :] = dvs[...].astype(bf16)
    dk_rot[pl.ds(0, rows), :] = total(0)
    dk_rot[pl.ds(rows, dks.shape[0]), :] = dks[...].astype(f32)
    g_out[...] = jnp.zeros_like(g_out)

    def head(j, _):
        lanes = pl.ds(pl.multiple_of(j * HEAD_SIZE, HEAD_SIZE), HEAD_SIZE)
        x = k_pre[:, lanes]
        rs = lax.rsqrt(jnp.mean(x * x, axis=-1, keepdims=True) + norm_epsilon)
        unit = x * rs
        dy = dk_rot[:, lanes]
        dy = dy * cos[...] - pltpu.roll(dy, HEAD_SIZE // 2, 1) * sin[...]
        g_out[0:1, :] += jnp.sum(dy * unit, axis=0, keepdims=True)
        dy = dy * gain[...]
        dk_out[:, lanes] = (rs * (dy - unit * jnp.mean(dy * unit, axis=-1, keepdims=True))).astype(bf16)
        return 0

    lax.fori_loop(0, KEY_VALUE_HEADS, head, 0)
    for i in range(2):
        for d in range(half):
            to_sibling(i, d).wait_send()
            if d:
                across(i, d).wait_send()


def key_grads(dk, dv, dks, dvs, k_pre, gain, cos, sin, rows, n, cid):
    group = PROMPT_LENGTH // rows
    half = group // 2
    width = k_pre.shape[1]
    D = pltpu.SemaphoreType.DMA
    vm = pl.BlockSpec(memory_space=pltpu.VMEM)
    V = pltpu.VMEM
    block = (rows, width)
    return pl.pallas_call(
        partial(key_grads_kernel, n, group),
        out_shape=[jax.ShapeDtypeStruct(k_pre.shape, bf16), jax.ShapeDtypeStruct(k_pre.shape, bf16), jax.ShapeDtypeStruct((8, HEAD_SIZE), f32)],
        in_specs=[vm] * 8,
        out_specs=[vm] * 3,
        scratch_shapes=[V((2, half) + block, bf16), V((2, half) + block, bf16), V((1, 8, 128), bf16), V((2, max(half - 1, 1)) + block, bf16), V(k_pre.shape, f32)]
        + [D((2, half))] * 2 + [D((2, max(half - 1, 1)))] * 2,
        compiler_params=pltpu.CompilerParams(collective_id=cid, has_side_effects=True, vmem_limit_bytes=60 << 20),
        name="prompt_key_grads",
    )(dk.reshape(half, 2, rows, width), dv.reshape(half, 2, rows, width), dks, dvs, k_pre, gain, cos, sin)


def attend_kernel(rows, q_pre, ks, vs, k_own, v_own, gain, cos, sin, past, inside, out, q_out, lse_out, rs_out):
    scale = HEAD_SIZE ** -0.5 * LOG2E
    for g in range(QUERY_HEADS // KEY_VALUE_HEADS):
        lanes = slice(g * HEAD_SIZE, (g + 1) * HEAD_SIZE)
        q = q_pre[:, lanes].T
        rs = lax.rsqrt(jnp.mean(q * q, axis=0, keepdims=True) + norm_epsilon)
        rs_out[0, g:g + 1, :] = rs
        q = q * rs * gain[:, 0:1]
        lo, hi = q[:HEAD_SIZE // 2], q[HEAD_SIZE // 2:]
        q = jnp.concatenate([lo * cos[...] - hi * sin[...], hi * cos[...] + lo * sin[...]], axis=0).astype(bf16)
        q_out[lanes, :] = q
        p = jnp.exp2(mm(ks[...], q[:, :rows], 1, 0) * scale + past[...])
        total = jnp.sum(p, axis=0, keepdims=True)
        o = mm(vs[...], p.astype(bf16), 0, 0) / total
        out[:rows, lanes] = o.T.astype(bf16)
        lse_out[0, g:g + 1, :rows] = jnp.log2(total)
        p = jnp.exp2(mm(ks[...], q[:, rows:], 1, 0) * scale)
        r = jnp.exp2(mm(k_own[rows:, :], q[:, rows:], 1, 0) * scale + inside[...])
        total = jnp.sum(p, axis=0, keepdims=True) + jnp.sum(r, axis=0, keepdims=True)
        o = (mm(vs[...], p.astype(bf16), 0, 0) + mm(v_own[rows:, :], r.astype(bf16), 0, 0)) / total
        out[rows:, lanes] = o.T.astype(bf16)
        lse_out[0, g:g + 1, rows:] = jnp.log2(total)


def attend(q_pre, ks, vs, k_own, v_own, gain, cos, sin, past, inside, rows):
    total = q_pre.shape[0]
    pair = 2 * HEAD_SIZE
    whole = lambda x: pl.BlockSpec(x.shape, lambda j: (0,) * x.ndim)
    col = lambda r, w: pl.BlockSpec((r, w), lambda j: (0, j))
    small = pl.BlockSpec((1, 2, total), lambda j: (j, 0, 0))
    return pl.pallas_call(
        partial(attend_kernel, rows),
        grid=(KEY_VALUE_HEADS,),
        in_specs=[col(total, pair), col(PROMPT_LENGTH, HEAD_SIZE), col(PROMPT_LENGTH, HEAD_SIZE), col(total, HEAD_SIZE), col(total, HEAD_SIZE),
                  whole(gain), whole(cos), whole(sin), whole(past), whole(inside)],
        out_specs=[col(total, pair), pl.BlockSpec((pair, total), lambda j: (j, 0)), small, small],
        out_shape=[jax.ShapeDtypeStruct((total, QUERY_HEADS * HEAD_SIZE), bf16), jax.ShapeDtypeStruct((QUERY_HEADS * HEAD_SIZE, total), bf16),
                   jax.ShapeDtypeStruct((KEY_VALUE_HEADS, 2, total), f32), jax.ShapeDtypeStruct((KEY_VALUE_HEADS, 2, total), f32)],
        compiler_params=pltpu.CompilerParams(vmem_limit_bytes=60 << 20),
        name="attend",
    )(q_pre, ks, vs, k_own, v_own, gain, cos, sin, past, inside)


def attend_back_kernel(rows, q_rot, ks, vs, k_own, v_own, d_out, out, lse, rs_in, gain, cos, sin, past, inside, dq_out, dk_out, dv_out, dks_out, dvs_out, g_out):
    scale = HEAD_SIZE ** -0.5
    dk = dv = dks = dvs = None
    plus = lambda x, y: y if x is None else x + y
    gain_grad = None
    for g in range(QUERY_HEADS // KEY_VALUE_HEADS):
        lanes = slice(g * HEAD_SIZE, (g + 1) * HEAD_SIZE)
        q = q_rot[lanes, :]
        do = d_out[:, lanes]
        delta = jnp.sum((do.astype(f32) * out[:, lanes].astype(f32)).T, axis=0, keepdims=True)
        log_total = lse[0, g:g + 1, :]
        dq = []
        for suffix in range(2):
            part = slice(rows, None) if suffix else slice(0, rows)
            qp, dop, lp, dp = q[:, part], do[part], log_total[:, part], delta[:, part]
            blocks = [(ks[...], vs[...], None if suffix else past[...])]
            if suffix:
                blocks.append((k_own[rows:, :], v_own[rows:, :], inside[...]))
            dqp = None
            for i, (kb, vb, bias) in enumerate(blocks):
                s = mm(kb, qp, 1, 0) * (scale * LOG2E) - lp
                p = jnp.exp2(s if bias is None else s + bias)
                ds = (p * (mm(vb, dop, 1, 1) - dp)).astype(bf16)
                dvp = mm(p.astype(bf16), dop, 1, 0)
                dkp = mm(ds, qp, 1, 1)
                dqp = plus(dqp, mm(kb, ds, 0, 0))
                if i:
                    dks, dvs = plus(dks, dkp), plus(dvs, dvp)
                else:
                    dk, dv = plus(dk, dkp), plus(dv, dvp)
            dq.append(dqp)
        dq = jnp.concatenate(dq, axis=1) * scale
        half = HEAD_SIZE // 2
        c, s = cos[...], sin[...]
        dy = jnp.concatenate([dq[:half] * c + dq[half:] * s, dq[half:] * c - dq[:half] * s], axis=0)
        qf = q.astype(f32)
        unit = jnp.concatenate([qf[:half] * c + qf[half:] * s, qf[half:] * c - qf[:half] * s], axis=0) / gain[:, 0:1]
        gg = dy * unit
        for t in range(gg.shape[1] // 128):
            gain_grad = plus(gain_grad, gg[:, t * 128:(t + 1) * 128])
        dy = dy * gain[:, 0:1]
        dx = rs_in[0, g:g + 1, :] * (dy - unit * jnp.mean(dy * unit, axis=0, keepdims=True))
        dq_out[:, lanes] = dx.T.astype(bf16)
    dk_out[...] = (dk * scale).astype(bf16)
    dv_out[...] = dv.astype(bf16)
    dks_out[...] = (dks * scale).astype(bf16)
    dvs_out[...] = dvs.astype(bf16)

    @pl.when(pl.program_id(0) == 0)
    def _():
        g_out[...] = gain_grad

    @pl.when(pl.program_id(0) > 0)
    def _():
        g_out[...] += gain_grad


def attend_back(q_rot, ks, vs, k_own, v_own, d_out, out, lse, rs, gain, cos, sin, past, inside, rows):
    total = k_own.shape[0]
    pair = 2 * HEAD_SIZE
    whole = lambda x: pl.BlockSpec(x.shape, lambda j: (0,) * x.ndim)
    col = lambda r, w: pl.BlockSpec((r, w), lambda j: (0, j))
    small = pl.BlockSpec((1, 2, total), lambda j: (j, 0, 0))
    width = KEY_VALUE_HEADS * HEAD_SIZE
    kv, own = jax.ShapeDtypeStruct((PROMPT_LENGTH, width), bf16), jax.ShapeDtypeStruct((total - rows, width), bf16)
    return pl.pallas_call(
        partial(attend_back_kernel, rows),
        grid=(KEY_VALUE_HEADS,),
        in_specs=[pl.BlockSpec((pair, total), lambda j: (j, 0)), col(PROMPT_LENGTH, HEAD_SIZE), col(PROMPT_LENGTH, HEAD_SIZE), col(total, HEAD_SIZE),
                  col(total, HEAD_SIZE), col(total, pair), col(total, pair), small, small, whole(gain), whole(cos), whole(sin), whole(past), whole(inside)],
        out_specs=[col(total, pair), col(PROMPT_LENGTH, HEAD_SIZE), col(PROMPT_LENGTH, HEAD_SIZE), col(total - rows, HEAD_SIZE), col(total - rows, HEAD_SIZE),
                   pl.BlockSpec((HEAD_SIZE, 128), lambda j: (0, 0))],
        out_shape=[jax.ShapeDtypeStruct((total, QUERY_HEADS * HEAD_SIZE), bf16), kv, kv, own, own, jax.ShapeDtypeStruct((HEAD_SIZE, 128), f32)],
        compiler_params=pltpu.CompilerParams(vmem_limit_bytes=60 << 20),
        name="attend_back",
    )(q_rot, ks, vs, k_own, v_own, d_out, out, lse, rs, gain, cos, sin, past, inside)


class Ring:
    def __init__(self, n, own, full, cols, sems, i):
        zs, zr, ss, sr, ls = sems
        A = n // 4
        rep, a, b, c = position(n)
        h = rep % 2
        rh = own.shape[1]
        k0 = rh * 3 // 4 if (rh * 3 // 4) % 8 == 0 else rh // 2
        lo, hi, every = pl.ds(0, k0), pl.ds(k0, rh - k0), slice(None)
        at = lambda *ix: full.at[(*ix, cols)]
        rank = lambda a, b, c: (a * 2 + b) * 2 + c
        ydev, xdev, cdev = (rep, rank(a, 1 - b, c)), (rep + 1 - 2 * h, rank(a, b, c)), (rep, rank(a, b, 1 - c))
        same = lambda ref, k, to: remote(ref, ref, ss.at[i, k], sr.at[i, k], to)
        mine = own.at[h, :, cols]
        self.local = lambda: [pltpu.make_async_copy(mine, at(a, b, c, h, every), ls.at[i])]
        self.along = lambda: [remote(mine, at(a, b, c, h, every), zs.at[i, d - 1], zr.at[i, d - 1], (rep, rank((a + d) % A, b, c))) for d in range(1, A)]
        self.second = lambda: [same(at(every, b, c, h, lo), 0, ydev), same(at(every, b, c, h, hi), 1, xdev)]
        self.third = lambda: [same(at(every, every, c, h, lo), 2, xdev), same(at(every, b, c, every, hi), 3, ydev)]
        self.last = lambda: [same(at(every, every, c, every, every), 4, cdev)]

    def begin(self):
        for q in self.local() + self.along():
            q.start()

    def turn(self, arrived, started):
        for q in arrived():
            q.wait_recv()
        for q in started():
            q.start()

    def step(self, k):
        if k == 0:
            for q in self.local():
                q.wait()
            self.turn(self.along, self.second)
        elif k == 1:
            self.turn(self.second, self.third)
        elif k == 2:
            self.turn(self.third, self.last)
        else:
            for q in self.last():
                q.wait_recv()

    def end(self):
        for q in self.along() + self.second() + self.third() + self.last():
            q.wait_send()


def forward_kernel(n, group, *refs):
    it = iter(refs)
    take = lambda count: [next(it) for _ in range(count)]
    index, x, hidden, wk, wv, wq, so, sg, su, sd, k_gain, q_gain, cos_r, sin_r, cos, sin, past, inside, valid, gain2, staged = take(21)
    wo, wg, wu, wd, moved, attended, q_out, lse_out, rs_out, k_pre, k_out, v, ks, vs, resid, h2, act, gate, up, mixed, stats = take(21)
    ordered, o_buf, g_buf, u_buf, d_buf, g_st, u_st = take(7)
    zs, zr, ss, sr, ls, lds, fs, fr, gs, gr, kls, ps, pr, pls, gos = take(15)
    rows = ks.shape[2]
    T = x.shape[0]
    half = group // 2
    rep, a, b, c = position(n)
    me = (a * 2 + b) * 2 + c
    first, slot = (me // group) * half, (me // 2) % half
    h = rep % 2
    meet([(rep, (me + d) % n) for d in range(1, n)] + [(rep + 1 - 2 * h, me)])

    OB, GB = o_buf.shape[-1], g_buf.shape[-1]
    n_out, n_mlp = wo.shape[-1] // OB, wg.shape[-1] // GB
    blocks = [(so, wo, pl.ds(q * OB, OB), o_buf.at[q]) for q in range(n_out)]
    for q in range(n_mlp):
        blocks += [(sg, wg, pl.ds(q * GB, GB), g_buf.at[q % 2]), (su, wu, pl.ds(q * GB, GB), u_buf.at[q % 2])]
    blocks += [(sd, wd, pl.ds(q * OB, OB), d_buf.at[q]) for q in range(n_out)]
    m = len(blocks)
    rings = [Ring(n, own, full, cols, (zs, zr, ss, sr, ls), i) for i, (own, full, cols, _) in enumerate(blocks)]

    def load(i):
        _, full, cols, buf = blocks[i]
        return pltpu.make_async_copy(full.at[:, :, :, :, :, cols], buf, lds.at[i])

    def tick(t):
        for k in range(4):
            if 0 <= t - k < m:
                rings[t - k].step(k)
                if k == 3:
                    load(t - k).start()

    S = ordered.shape[1]

    def put(j, _):
        ordered[j // S, j % S] = staged[index[j]]
        return 0

    lax.fori_loop(0, n * S, put, 0)
    pieces = [remote(ordered.at[(me + d) % n], moved.at[:, me], ps.at[d - 1], pr.at[d - 1], (rep, (me + d) % n)) for d in range(1, n)]
    own_piece = pltpu.make_async_copy(ordered.at[me], moved.at[:, me], pls.at[0])
    for r in rings[:2]:
        r.begin()
    own_piece.start()
    for q in pieces:
        q.start()
    for r in rings[2:]:
        r.begin()

    lane = lambda j, w: pl.ds(pl.multiple_of(j * w, w), w)
    heads = QUERY_HEADS // KEY_VALUE_HEADS
    pair = heads * HEAD_SIZE

    def kv_tile(j, _):
        kp = mm(hidden[...], wk[:, lane(j, 256)], 1, 0)
        k_pre[:, lane(j, 256)] = kp
        for g in range(2):
            y = kp[:, g * HEAD_SIZE:(g + 1) * HEAD_SIZE]
            y = y * lax.rsqrt(jnp.mean(y * y, axis=-1, keepdims=True) + norm_epsilon) * k_gain[...]
            k_out[:, lane(2 * j + g, HEAD_SIZE)] = (y * cos_r[...] + pltpu.roll(y, HEAD_SIZE // 2, 1) * sin_r[...]).astype(bf16)
        v[:, lane(j, 256)] = mm(hidden[...], wv[:, lane(j, 256)], 1, 0).astype(bf16)
        return 0

    lax.fori_loop(0, wk.shape[1] // 256, kv_tile, 0)
    parts = [(k_out, ks), (v, vs)]
    at = lambda s, c: (rep, (first + s) * 2 + c)
    mine = lambda i: parts[i][0].at[pl.ds(0, rows)]
    klocal = [pltpu.make_async_copy(mine(i), parts[i][1].at[slot, c], kls.at[i]) for i in range(2)]
    across = [remote(mine(i), parts[i][1].at[slot, c], fs.at[i, d - 1], fr.at[i, d - 1], at((slot + d) % half, c)) for i in range(2) for d in range(1, half)]
    sibling = [remote(mine(i), parts[i][1].at[slot, c], gs.at[i, 0], gr.at[i, 0], at(slot, 1 - c)) for i in range(2)]
    onward = []
    for i in range(2):
        for d in range(1, half):
            there = parts[i][1].at[(slot + half - d) % half, c]
            onward.append(remote(there, there, gs.at[i, d], gr.at[i, d], at(slot, 1 - c)))
    for q in across + sibling + klocal:
        q.start()
    tick(0)

    def q_tile(j, _):
        qp = mm(hidden[...], wq[:, lane(j, pair)], 1, 0)
        for g in range(heads):
            y = qp[:, g * HEAD_SIZE:(g + 1) * HEAD_SIZE].T
            rs = lax.rsqrt(jnp.mean(y * y, axis=0, keepdims=True) + norm_epsilon)
            rs_out[j, g:g + 1, :] = rs
            y = y * rs * q_gain[:, 0:1]
            lo, hi = y[:HEAD_SIZE // 2], y[HEAD_SIZE // 2:]
            y = jnp.concatenate([lo * cos[...] - hi * sin[...], hi * cos[...] + lo * sin[...]], axis=0)
            q_out[lane(j * heads + g, HEAD_SIZE), :] = y.astype(bf16)
        for when, t in ((3, 1), (7, 2)):
            pl.when(j == when)(partial(tick, t))
        return 0

    lax.fori_loop(0, KEY_VALUE_HEADS, q_tile, 0)
    for q in across:
        q.wait_recv()
    for q in onward:
        q.start()
    tick(3)
    for q in klocal:
        q.wait()
    for q in sibling + onward:
        q.wait_recv()

    scale = HEAD_SIZE ** -0.5 * LOG2E

    def attend_head(j, _):
        kl = lane(j, HEAD_SIZE)
        kb = ks[:, :, :, kl].reshape(PROMPT_LENGTH, HEAD_SIZE)
        vb = vs[:, :, :, kl].reshape(PROMPT_LENGTH, HEAD_SIZE)
        for g in range(heads):
            ql = lane(j * heads + g, HEAD_SIZE)
            q = q_out[ql, :]
            p = jnp.exp2(mm(kb, q[:, :rows], 1, 0) * scale + past[...])
            total = jnp.sum(p, axis=0, keepdims=True)
            o = mm(vb, p.astype(bf16), 0, 0) / total
            attended[:rows, ql] = o.T.astype(bf16)
            lse_out[j, g:g + 1, :rows] = jnp.log2(total)
            p = jnp.exp2(mm(kb, q[:, rows:], 1, 0) * scale)
            r = jnp.exp2(mm(k_out[rows:, kl], q[:, rows:], 1, 0) * scale + inside[...])
            total = jnp.sum(p, axis=0, keepdims=True) + jnp.sum(r, axis=0, keepdims=True)
            o = (mm(vb, p.astype(bf16), 0, 0) + mm(v[rows:, kl], r.astype(bf16), 0, 0)) / total
            attended[rows:, ql] = o.T.astype(bf16)
            lse_out[j, g:g + 1, rows:] = jnp.log2(total)
        for when, t in ((2, 4), (5, 5)):
            pl.when(j == when)(partial(tick, t))
        return 0

    lax.fori_loop(0, KEY_VALUE_HEADS, attend_head, 0)

    stats[...] = jnp.zeros_like(stats)
    for q in range(n_out):
        load(q).wait()

        def out_tile(j, _):
            cols = lane(q * (OB // 256) + j, 256)
            w = o_buf[q, :, :, :, :, :, lane(j, 256)].reshape(-1, 256)
            y = x[:, cols].astype(f32) + mm(attended[...], w, 1, 0)
            resid[:, cols] = y
            stats[1:2, :] += jnp.sum(valid[...] * y * y, axis=0, keepdims=True)
            return 0

        lax.fori_loop(0, OB // 256, out_tile, 0)
    RB = 32

    def norm_rows(j, _):
        y = resid[pl.ds(pl.multiple_of(j * RB, RB), RB), :]
        y = y * lax.rsqrt(jnp.mean(y * y, axis=-1, keepdims=True) + norm_epsilon) * gain2[...]
        h2[pl.ds(pl.multiple_of(j * RB, RB), RB), :] = y.astype(bf16)
        return 0

    lax.fori_loop(0, T // RB, norm_rows, 0)
    done = 6
    saved = lambda q: [pltpu.make_async_copy(g_st.at[q % 2], gate.at[:, pl.ds(q * GB, GB)], gos.at[q % 2, 0]),
                       pltpu.make_async_copy(u_st.at[q % 2], up.at[:, pl.ds(q * GB, GB)], gos.at[q % 2, 1])]
    for q in range(n_mlp):
        need = n_out + 2 * q + 1 + 3
        while done <= need:
            tick(done)
            done += 1
        load(n_out + 2 * q).wait()
        load(n_out + 2 * q + 1).wait()
        if q >= 2:
            for s in saved(q - 2):
                s.wait()

        def mlp_tile(j, _):
            g = mm(h2[...], g_buf[q % 2, :, :, :, :, :, lane(j, 256)].reshape(-1, 256), 1, 0)
            u = mm(h2[...], u_buf[q % 2, :, :, :, :, :, lane(j, 256)].reshape(-1, 256), 1, 0)
            g_st[q % 2, :, lane(j, 256)] = g.astype(bf16)
            u_st[q % 2, :, lane(j, 256)] = u.astype(bf16)
            act[:, lane(q * (GB // 256) + j, 256)] = (g / (1.0 + jnp.exp(-g)) * u).astype(bf16)
            return 0

        lax.fori_loop(0, GB // 256, mlp_tile, 0)
        for s in saved(q):
            s.start()
    for q in range(n_out):
        need = n_out + 2 * n_mlp + q + 3
        while done <= need:
            tick(done)
            done += 1
        load(n_out + 2 * n_mlp + q).wait()

        def down_tile(j, _):
            cols = lane(q * (OB // 256) + j, 256)
            w = d_buf[q, :, :, :, :, :, lane(j, 256)].reshape(-1, 256)
            y = resid[:, cols] + mm(act[...], w, 1, 0)
            mixed[:, cols] = y.astype(bf16)
            stats[0:1, :] += jnp.sum(valid[...] * y * y, axis=0, keepdims=True)
            return 0

        lax.fori_loop(0, OB // 256, down_tile, 0)
    for q in range(max(0, n_mlp - 2), n_mlp):
        for s in saved(q):
            s.wait()
    own_piece.wait()
    for q in pieces:
        q.wait()
    for q in across + sibling + onward:
        q.wait_send()
    for r in rings:
        r.end()


def forward(index, x, hidden, wk, wv, wq, shards, k_gain, q_gain, cos_r, sin_r, cos, sin, past, inside, valid, gain2, staged, rows, n, cid):
    group = PROMPT_LENGTH // rows
    half, A, T, W = group // 2, n // 4, x.shape[0], x.shape[1]
    S = staged.shape[1]
    halves = [s.reshape(2, s.shape[0] // 2, s.shape[1]) for s in shards]
    fulls = [jax.ShapeDtypeStruct((A, 2, 2) + s.shape, bf16) for s in halves]
    flat = staged.reshape((-1,) + staged.shape[2:])
    QW, KW, FW = wq.shape[1], wk.shape[1], shards[1].shape[1]
    sd_ = jax.ShapeDtypeStruct
    small = sd_((KEY_VALUE_HEADS, 2, T), f32)
    keys = sd_((half, 2, rows, KW), bf16)
    out_shape = fulls + [sd_((S, n) + staged.shape[2:], bf16), sd_((T, QW), bf16), sd_((QW, T), bf16), small, small, sd_((T, KW), f32),
        sd_((T, KW), bf16), sd_((T, KW), bf16), keys, keys, sd_((T, W), f32), sd_((T, W), bf16), sd_((T, FW), bf16),
        sd_((T, FW), bf16), sd_((T, FW), bf16), sd_((T, W), bf16), sd_((8, 256), f32)]
    vm, hbm, sm = pl.BlockSpec(memory_space=pltpu.VMEM), pl.BlockSpec(memory_space=pl.ANY), pl.BlockSpec(memory_space=pltpu.SMEM)
    D, V = pltpu.SemaphoreType.DMA, pltpu.VMEM
    OB, GB = 512, 768
    n_out, n_mlp = W // OB, FW // GB
    m = 2 * n_out + 2 * n_mlp
    buf = lambda i, k, w: V((k, A, 2, 2) + halves[i].shape[:2] + (w,), bf16)
    res = pl.pallas_call(
        partial(forward_kernel, n, group),
        out_shape=out_shape,
        in_specs=[sm] + [vm] * 20,
        out_specs=[hbm] * 5 + [vm] * 12 + [hbm] * 2 + [vm] * 2,
        scratch_shapes=[V(staged.shape, bf16), buf(0, n_out, OB), buf(1, 2, GB), buf(2, 2, GB), buf(3, n_out, OB), V((2, T, GB), bf16), V((2, T, GB), bf16)]
        + [D((m, A - 1))] * 2 + [D((m, 5))] * 2 + [D((m,))] * 2 + [D((2, max(half - 1, 1)))] * 2 + [D((2, half))] * 2 + [D((2,))]
        + [D((n - 1,))] * 2 + [D((1,))] + [D((2, 2))],
        compiler_params=pltpu.CompilerParams(collective_id=cid, has_side_effects=True, vmem_limit_bytes=63 << 20),
        name="forward",
    )(index, x, hidden, wk, wv, wq, *halves, k_gain, q_gain, cos_r, sin_r, cos, sin, past, inside, valid, gain2, flat)
    res = list(res)
    for i, s in enumerate(shards):
        res[i] = res[i].reshape(-1, s.shape[1])
    res[12], res[13] = res[12].reshape(PROMPT_LENGTH, KW), res[13].reshape(PROMPT_LENGTH, KW)
    return res


MLP_TICKS = (1, 2, 2, 2, 2, 2)
OUT_TICKS = 1
HEAD_TICKS = (1, 1, 1)
BACK_TICKS = (1, 1, 1, 1)


class Fold:
    def __init__(self, n, R, where, g, bufs, out, cols, sems, i):
        self.bufs, self.k, self.landing = bufs
        self.waited = set()
        self.g, self.out, self.cols, self.i, self.sems = g, out, cols, i, sems
        self.A, self.bits = n // 4, R.bit_length() - 1
        self.rep, self.a, self.b, self.c, self.h = where
        self.rh = self.bufs[0].shape[-2]
        self.k0 = fold_split(self.rh)

    b1 = property(lambda self: self.bufs[0].at[self.landing])
    b2y, b2x, b3, b4, s4, b5 = [property(lambda self, j=j: self.bufs[j].at[self.k]) for j in range(1, 7)]

    def device(self, da=0, db=0, dc=0, bit=None):
        rep, a, b, c = self.rep, self.a, self.b, self.c
        if bit is not None:
            rep = rep + (1 << bit) - 2 * (1 << bit) * ((rep // (1 << bit)) % 2)
        return (rep, (((a + da) % self.A) * 2 + (1 - b if db else b)) * 2 + (1 - c if dc else c))

    @property
    def ydev(self):
        return self.device(db=1)

    @property
    def xdev(self):
        return self.device(bit=0)

    @property
    def cdev(self):
        return self.device(dc=1)

    def zdev(self, d):
        return self.device(da=d)

    def flip(self, bit):
        return self.device(bit=bit)

    def hop(self, k):
        i, a, b, c, h, k0, rh = self.i, self.a, self.b, self.c, self.h, self.k0, self.rh
        s1s, s1r, s2s, s2r, s3s, s3r, s4s, s4r, s5s, s5r, _ = self.sems
        lo, hi = pl.ds(0, k0), pl.ds(k0, rh - k0)
        if k == 1:
            return [remote(self.g.at[:, :, 1 - c], self.b1, s1s.at[i], s1r.at[i], self.cdev)]
        if k == 2:
            q = [remote(self.b1.at[:, 1 - b, :, lo], self.b2y, s2s.at[i, 0], s2r.at[i, 0], self.ydev)]
            if k0 < rh:
                q.append(remote(self.b1.at[:, :, 1 - h, hi], self.b2x, s2s.at[i, 1], s2r.at[i, 1], self.xdev))
            return q
        if k == 3:
            q = [remote(self.b2y.at[:, 1 - h], self.b3.at[:, lo], s3s.at[i, 0], s3r.at[i, 0], self.xdev)]
            if k0 < rh:
                q.append(remote(self.b2x.at[:, 1 - b], self.b3.at[:, hi], s3s.at[i, 1], s3r.at[i, 1], self.ydev))
            return q
        if k == 4:
            return [remote(self.b3.at[(a + d) % self.A], self.b4.at[d - 1], s4s.at[i, d - 1], s4r.at[i, d - 1], self.zdev(d)) for d in range(1, self.A)]
        last = self.bits - 1
        return [remote(self.s4.at[last], self.b5.at[last], s5s.at[i, last], s5r.at[i, last], self.xdev)]

    def put(self, k):
        last = self.bits - 1
        half = self.h if k == 0 else 1 - self.h
        return pltpu.make_async_copy((self.s4 if k == 0 else self.b5).at[last], self.out.at[half, :, self.cols], self.sems[-1].at[self.i, k])

    def begin(self):
        for q in self.hop(1):
            q.start()

    def arrive(self, k):
        for q in self.hop(k):
            q.wait_recv()

    def go(self, k):
        for q in self.hop(k):
            q.start()

    def step(self, k):
        a, b, c, h, k0, rh = self.a, self.b, self.c, self.h, self.k0, self.rh
        self.arrive(k)
        lo, hi = pl.ds(0, k0), pl.ds(k0, rh - k0)
        if k == 1:
            for q in self.hop(1):
                q.wait_send()
            view = lambda ref: lambda j: ref.at[j // 4, (j // 2) % 2, j % 2]
            add_rows(self.A * 4, view(self.b1), view(self.b1), [lambda j: self.g.at[j // 4, (j // 2) % 2, c, j % 2]])
        elif k == 2:
            view = lambda ref: lambda j: ref.at[j // 2, j % 2]
            add_rows(self.A * 2, view(self.b2y), view(self.b2y), [lambda j: self.b1.at[j // 2, b, j % 2, lo]])
            if k0 < rh:
                add_rows(self.A * 2, view(self.b2x), view(self.b2x), [lambda j: self.b1.at[j // 2, j % 2, h, hi]])
        elif k == 3:
            view = lambda part: lambda j: self.b3.at[j, part]
            add_rows(self.A, view(lo), view(lo), [lambda j: self.b2y.at[j, h]])
            if k0 < rh:
                add_rows(self.A, view(hi), view(hi), [lambda j: self.b2x.at[j, b]])
        elif k == 4:
            add_rows(1, lambda j: self.s4.at[0], lambda j: self.b3.at[a], [lambda j, d=d: self.b4.at[d] for d in range(self.A - 1)])
            s5s, s5r = self.sems[8:10]
            for r in range(self.bits - 1):
                q = remote(self.s4.at[r], self.b5.at[r], s5s.at[self.i, r], s5r.at[self.i, r], self.flip(r + 1))
                q.start()
                q.wait()
                add_rows(1, lambda j, r=r: self.s4.at[r + 1], lambda j, r=r: self.s4.at[r], [lambda j, r=r: self.b5.at[r]])
            self.put(0).start()
        else:
            self.put(1).start()
            return
        self.go(k + 1)

    def sent(self, k):
        if k not in self.waited:
            self.waited.add(k)
            for q in self.hop(k):
                q.wait_send()

    def end(self):
        for k in range(2, 6):
            self.sent(k)
        self.put(0).wait()
        self.put(1).wait()


def fold_split(rh):
    if (rh // 2) % 16 == 0:
        return rh // 2
    return rh // 32 * 16 if rh >= 32 else rh


def backward_kernel(n, R, group, UD, UF, UO, *refs):
    it = iter(refs)
    take = lambda count: [next(it) for _ in range(count)]
    index, mixed, dm, h2, act, gate, up, resid, wd, wg, wu, wo, attended, q_rot, lse, rs_q, ks, vs, k_rot, v, k_pre, wq, wk, wv, hidden, x = take(26)
    k_gain, q_gain, cos_r, sin_r, cos, sin, past, inside, valid, gain1, gain2, sums = take(12)
    outs = take(7)
    vec, d_prompt, mixed_out, grad_out = take(4)
    classes = [take(7) for _ in range(3)]
    r1, r2, mixed_in, turned, grad_src, grad_in, vb, vz, dres = take(9)
    fold_sems = take(11)
    lds, hs, gs, gr, fs, fr, a2s, a2r, a2l, vs_, vr_, free = take(12)
    A, T, W = n // 4, dm.shape[0], dm.shape[1]
    half, rows, KW = group // 2, r1.shape[2], k_rot.shape[1]
    FW, QW = act.shape[1], attended.shape[1]
    bits = R.bit_length() - 1
    rep, a, b, c = position(n)
    h = rep % 2
    rank = lambda a, b, c: (a * 2 + b) * 2 + c
    me = rank(a, b, c)
    first, slot = (me // group) * half, (me // 2) % half
    flip = lambda bit: (rep + (1 << bit) - 2 * (1 << bit) * ((rep // (1 << bit)) % 2), me)
    meet([(rep, (me + d) % n) for d in range(1, n)] + [flip(k) for k in range(bits)])

    lane = lambda j, w: pl.ds(pl.multiple_of(j * w, w), w)
    heads = QUERY_HEADS // KEY_VALUE_HEADS
    loads = iter(range(lds.shape[0]))

    def fetch(src, dst):
        q = pltpu.make_async_copy(src, dst, lds.at[next(loads)])
        q.start()
        return q

    S = turned.shape[1]

    def spread_copies(src, dst, k):
        own = pltpu.make_async_copy(src.at[:, me], dst.at[me], a2l.at[k])
        return own, [remote(src.at[:, (me + d) % n], dst.at[me], a2s.at[k, d - 1], a2r.at[k, d - 1], (rep, (me + d) % n)) for d in range(1, n)]

    def collect_copies(src, dst, k):
        own = pltpu.make_async_copy(src.at[me], dst.at[:, me], a2l.at[k])
        return own, [remote(src.at[(me + d) % n], dst.at[:, me], a2s.at[k, d - 1], a2r.at[k, d - 1], (rep, (me + d) % n)) for d in range(1, n)]

    def begin_all(pair):
        pair[0].start()
        for q in pair[1]:
            q.start()

    def wait_all(pair):
        pair[0].wait()
        for q in pair[1]:
            q.wait()

    def reorder(src, dst):
        def put(j, _):
            s = index[j]
            dst[j // S, j % S] = src[s // S, s % S]
            return 0

        lax.fori_loop(0, n * S, put, 0)

    mixed_spread = spread_copies(mixed, mixed_in, 0)

    units = []

    def unit(cls, k, g, out, cols, landing=None):
        units.append(Fold(n, R, (rep, a, b, c, h), g, (classes[cls], k, k if landing is None else landing), outs[out], cols, fold_sems, len(units)))
        return units[-1]

    state = {"e1": 0, "tick": 0}

    def e1():
        units[state["e1"]].step(1)
        state["e1"] += 1

    def tick(count=1):
        for _ in range(count):
            t = state["tick"]
            for k in range(4):
                if 0 <= t - k < len(units) and (k or t < state["e1"]):
                    units[t - k].step(k + 2)
            state["tick"] += 1

    n_down, n_ff, n_out = W // UD, FW // UF, W // UO
    V = pltpu.VMEM
    rh = lambda k: classes[k][0].shape[-2]
    AT, QT = FW // A, QW // A

    def down(act_c, act_t, g_down, dm_v):
        got = fetch(dm, dm_v)
        pieces = [fetch(act.at[:, pl.ds(0, AT)], act_c.at[0])]
        begin_all(mixed_spread)
        got.wait()
        for i in range(A):
            if i + 1 < A:
                pieces.append(fetch(act.at[:, pl.ds((i + 1) * AT, AT)], act_c.at[(i + 1) % 2]))
            pieces[i].wait()
            act_t[...] = act_c[i % 2].T

            def down_tile(j, _):
                y = mm(act_t[...], dm_v[:, lane(j, UD)], 1, 0).astype(bf16)
                g_down[j, i] = y.reshape(g_down.shape[2:])
                return 0

            lax.fori_loop(0, n_down, down_tile, 0)
        for u in range(n_down):
            unit(0, u, g_down.at[u], 0, pl.ds(u * UD, UD)).begin()
        for u in range(n_down):
            e1()

    pl.run_scoped(down, V((2, T, AT), bf16), V((AT, T), bf16), V((n_down, A, 2, 2, 2, rh(0), UD), bf16), V((T, W), bf16))
    tick()
    RB = 32
    block = lambda j: pl.ds(pl.multiple_of(j * RB, RB), RB)

    def norm_back(value, gain, grad):
        r = lax.rsqrt(jnp.mean(value * value, axis=-1, keepdims=True) + norm_epsilon)
        u = value * r
        t = grad * gain
        return r * (t - u * jnp.mean(t * u, axis=-1, keepdims=True)), jnp.sum(grad * u, axis=0, keepdims=True)

    def persistent(dq, dkr, dvl):
        def after_mlp(drl):
            pl.run_scoped(partial(mlp, drl), V((4, A, 2, 2, 2, rh(1), UF), bf16), V((2, UF, W), bf16), V((2, W, UF), bf16), V((2, W, UF), bf16), V((2, T, UF), bf16),
                          V((2, T, UF), bf16), V((T, UF), bf16), V((T, UF), bf16), V((W, T), bf16), V((T, W), bf16), V((T, W), bf16), V((T, W), f32))
            pl.run_scoped(partial(out_grad, drl), V((2, T, QT), bf16), V((QT, T), bf16), V((n_out, A, 2, 2, 2, rh(2), UO), bf16))
            wait_all(mixed_spread)
            reorder(mixed_in, turned)
            mixed_collect = collect_copies(turned, mixed_out, 1)
            begin_all(mixed_collect)
            pl.run_scoped(partial(attention, drl, dq, dkr, dvl), V((half, 2, rows, KW), bf16), V((half, 2, rows, KW), bf16), V((2, PROMPT_LENGTH, HEAD_SIZE), bf16),
                          V((2, PROMPT_LENGTH, HEAD_SIZE), bf16), V((2, heads * HEAD_SIZE, T), bf16), V((2, T, heads * HEAD_SIZE), bf16), V((2, heads * HEAD_SIZE, W), bf16),
                          V((T, KW), bf16), V((T, KW), bf16))
            wait_all(mixed_collect)

        pl.run_scoped(after_mlp, V((T, W), bf16))
        pl.run_scoped(partial(weights_back, dq, dkr, dvl), V((2, 256, QW), bf16), V((2, 256, KW), bf16), V((2, 256, KW), bf16), V((T, W), bf16), V((W, T), bf16),
                      V((T, KW), f32), V((T, KW), bf16), V((4, A, 2, 2, 2, rh(1), UF), bf16), V((T, W), f32))

    def mlp(drl, g_ff, wd_c, wg_c, wu_c, gate_c, up_c, dg_c, du_c, h2_t, h2_v, dm_v, dhid):
        got = [fetch(h2, h2_v), fetch(dm, dm_v)]

        def fetch_ff(q):
            cols, s = pl.ds(q * UF, UF), q % 2
            return [fetch(wd.at[cols], wd_c.at[s]), fetch(gate.at[:, cols], gate_c.at[s]), fetch(up.at[:, cols], up_c.at[s]),
                    fetch(wg.at[:, cols], wg_c.at[s]), fetch(wu.at[:, cols], wu_c.at[s])]

        ff = [fetch_ff(0)]
        got_resid = fetch(resid, dres)
        for f in got:
            f.wait()
        h2_t[...] = h2_v[...].T
        for q in range(n_ff):
            s = q % 2
            if q + 1 < n_ff:
                ff.append(fetch_ff(q + 1))
            for f in ff[q]:
                f.wait()

            def act_tile(j, _):
                cols = lane(j, 256)
                g, u = gate_c[s, :, cols].astype(f32), up_c[s, :, cols].astype(f32)
                da = mm(dm_v[...], wd_c[s, lane(j, 256), :], 1, 1)
                sg = 1.0 / (1.0 + jnp.exp(-g))
                du_c[:, cols] = (da * (g * sg)).astype(bf16)
                dg_c[:, cols] = (da * u * (sg * (1.0 + g * (1.0 - sg)))).astype(bf16)
                return 0

            lax.fori_loop(0, UF // 256, act_tile, 0)
            for k, d in enumerate((dg_c, du_c)):
                while state["e1"] < len(units) - 1:
                    e1()

                def ff_tile(j, _):
                    y = mm(h2_t[...], d[:, lane(j, 256)], 1, 0).astype(bf16)
                    g_ff[(2 * q + k) % 4, :, :, :, :, :, lane(j, 256)] = y.reshape(g_ff.shape[1:6] + (256,))
                    return 0

                lax.fori_loop(0, UF // 256, ff_tile, 0)
                unit(1, 2 * q + k, g_ff.at[(2 * q + k) % 4], 1 + k, pl.ds(q * UF, UF)).begin()

            def hid_tile(j, _):
                cols = lane(j, 256)
                y = mm(dg_c[...], wg_c[s, cols, :], 1, 1) + mm(du_c[...], wu_c[s, cols, :], 1, 1)
                dhid[:, cols] = y if q == 0 else dhid[:, cols] + y
                return 0

            lax.fori_loop(0, W // 256, hid_tile, 0)
            for _ in range(MLP_TICKS[q % len(MLP_TICKS)]):
                tick()
        while state["e1"] < len(units):
            e1()
        got_resid.wait()

        def second_norm(j, total):
            d, gg = norm_back(dres[block(j), :], gain2[...], dhid[block(j), :])
            d = dm_v[block(j), :].astype(f32) + d
            dres[block(j), :] = d
            drl[block(j), :] = d.astype(bf16)
            return total + gg

        g2 = lax.fori_loop(0, T // RB, second_norm, jnp.zeros((1, W), f32))
        for k in range(W // 128):
            vec[W // 128 + k:W // 128 + k + 1, :] = g2[:, k * 128:(k + 1) * 128]

    def out_grad(drl, att_c, att_t, g_out):
        pieces = [fetch(attended.at[:, pl.ds(0, QT)], att_c.at[0])]
        for i in range(A):
            if i + 1 < A:
                pieces.append(fetch(attended.at[:, pl.ds((i + 1) * QT, QT)], att_c.at[(i + 1) % 2]))
            pieces[i].wait()
            att_t[...] = att_c[i % 2].T

            def out_tile(j, _):
                y = mm(att_t[...], drl[:, lane(j, UO)], 1, 0).astype(bf16)
                g_out[j, i] = y.reshape(g_out.shape[2:])
                return 0

            lax.fori_loop(0, n_out, out_tile, 0)
        for u in range(n_out):
            unit(2, u, g_out.at[u], 3, pl.ds(u * UO, UO)).begin()
        tick(OUT_TICKS)
        while state["e1"] < len(units):
            e1()

    def attention(drl, dq, dkr, dvl, dk, dv, ks_c, vs_c, q_c, att_c, wo_c, kr_v, v_v):
        others = [fetch(k_rot, kr_v), fetch(v, v_v)]
        pair = lambda j: lane(j, heads * HEAD_SIZE)

        def head_copies(j):
            s = j % 2
            moves = [(ks.at[:, lane(j, HEAD_SIZE)], ks_c), (vs.at[:, lane(j, HEAD_SIZE)], vs_c), (q_rot.at[pair(j), :], q_c),
                     (attended.at[:, pair(j)], att_c), (wo.at[pair(j), :], wo_c)]
            return [pltpu.make_async_copy(src, dst.at[s], hs.at[s, k]) for k, (src, dst) in enumerate(moves)]

        for q in head_copies(jnp.int32(0)):
            q.start()
        for q in others:
            q.wait()
        scale = HEAD_SIZE ** -0.5
        plus = lambda p, q: q if p is None else p + q

        def head(j, gain_grad):
            @pl.when(j + 1 < KEY_VALUE_HEADS)
            def _():
                for q in head_copies(j + 1):
                    q.start()

            for q in head_copies(j):
                q.wait()
            at = j % 2
            kl = lane(j, HEAD_SIZE)
            kb, vb_ = ks_c[at], vs_c[at]
            dkp = dvp = dks = dvs = None
            do_pair = mm(drl[...], wo_c[at], 1, 1)
            out_pair = att_c[at].astype(f32)
            for g in range(heads):
                sl = slice(g * HEAD_SIZE, (g + 1) * HEAD_SIZE)
                q = q_c[at, sl, :]
                do = do_pair[:, sl].astype(bf16)
                delta = jnp.sum((do.astype(f32) * out_pair[:, sl]).T, axis=0, keepdims=True)
                log_total = lse[j, g:g + 1, :]
                parts = []
                for suffix in range(2):
                    part = slice(rows, None) if suffix else slice(0, rows)
                    qp, dop, lp, dp = q[:, part], do[part], log_total[:, part], delta[:, part]
                    pieces = [(kb, vb_, None if suffix else past[...])]
                    if suffix:
                        pieces.append((kr_v[rows:, kl], v_v[rows:, kl], inside[...]))
                    total = None
                    for i, (kk, vv, bias) in enumerate(pieces):
                        s = mm(kk, qp, 1, 0) * (scale * LOG2E) - lp
                        p = jnp.exp2(s if bias is None else s + bias)
                        ds = (p * (mm(vv, dop, 1, 1) - dp)).astype(bf16)
                        gv, gk = mm(p.astype(bf16), dop, 1, 0), mm(ds, qp, 1, 1)
                        total = plus(total, mm(kk, ds, 0, 0))
                        if i:
                            dks, dvs = plus(dks, gk), plus(dvs, gv)
                        else:
                            dkp, dvp = plus(dkp, gk), plus(dvp, gv)
                    parts.append(total)
                d = jnp.concatenate(parts, axis=1) * scale
                m = HEAD_SIZE // 2
                cs, sn = cos[...], sin[...]
                dy = jnp.concatenate([d[:m] * cs + d[m:] * sn, d[m:] * cs - d[:m] * sn], axis=0)
                qf = q.astype(f32)
                u = jnp.concatenate([qf[:m] * cs + qf[m:] * sn, qf[m:] * cs - qf[:m] * sn], axis=0) / q_gain[:, 0:1]
                gg = dy * u
                for t in range(T // 128):
                    gain_grad = gain_grad + gg[:, t * 128:(t + 1) * 128]
                dy = dy * q_gain[:, 0:1]
                dx = rs_q[j, g:g + 1, :] * (dy - u * jnp.mean(dy * u, axis=0, keepdims=True))
                dq[:, lane(j * heads + g, HEAD_SIZE)] = dx.T.astype(bf16)
            dk[:, :, :, kl] = (dkp * scale).astype(bf16).reshape(half, 2, rows, HEAD_SIZE)
            dv[:, :, :, kl] = dvp.astype(bf16).reshape(half, 2, rows, HEAD_SIZE)
            dkr[rows:, kl] = dks * scale
            dvl[rows:, kl] = dvs.astype(bf16)
            return gain_grad

        gain_grad = jnp.zeros((HEAD_SIZE, 128), f32)
        for part in range(4):
            gain_grad = lax.fori_loop(2 * part, 2 * part + 2, head, gain_grad)
            if part < 3:
                tick(HEAD_TICKS[part])
        vec[2 * W // 128:2 * W // 128 + 1, :] = jnp.sum(gain_grad.T, axis=0, keepdims=True)
        grads = [dk, dv]
        home = lambda s, c: (rep, (first + s) * 2 + c)

        def to_sibling(i, d):
            return remote(grads[i].at[(slot + d) % half, 1 - c], r1.at[i, d], gs.at[i, d], gr.at[i, d], home(slot, 1 - c))

        order = list(range(1, half)) + [0]
        for d in order:
            for i in range(2):
                to_sibling(i, d).start()
        for d in order:
            for i in range(2):
                to_sibling(i, d).wait_recv()

                def one(j, _):
                    r1[i, d, block(j)] = (grads[i][(slot + d) % half, c, block(j)].astype(f32) + r1[i, d, block(j)].astype(f32)).astype(bf16)
                    return 0

                lax.fori_loop(0, rows // RB, one, 0)
                if d:
                    across(i, d).start()
        for d in order:
            for i in range(2):
                to_sibling(i, d).wait_send()

    def across(i, d):
        return remote(r1.at[i, d], r2.at[i, d - 1], fs.at[i, d - 1], fr.at[i, d - 1], (rep, (first + (slot + d) % half) * 2 + c))

    def weights_back(dq, dkr, dvl, wq_c, wk_c, wv_c, hid_v, hid_t, kp_v, dkl, g_qkv, dhid):
        got = [fetch(hidden, hid_v), fetch(k_pre, kp_v)]
        tiles = W // 256
        fetch_q = lambda j: fetch(wq.at[pl.ds(j * 256, 256)], wq_c.at[j % 2])
        fetch_kv = lambda j: [fetch(wk.at[pl.ds(j * 256, 256)], wk_c.at[j % 2]), fetch(wv.at[pl.ds(j * 256, 256)], wv_c.at[j % 2])]
        q_tiles, kv_tiles = [fetch_q(0), fetch_q(1)], [fetch_kv(0), fetch_kv(1)]
        got[0].wait()
        hid_t[...] = hid_v[...].T
        got_x = fetch(x, hid_v)
        count = [0]
        first_ff = n_down
        assert state["tick"] > first_ff + (QW + 2 * KW) // UF - 1
        for f in units[first_ff:first_ff + (QW + 2 * KW) // UF]:
            f.sent(2)
        pl.semaphore_signal(free, inc=1, device_id=(rep, rank(a, b, 1 - c)), device_id_type=MESH)
        pl.semaphore_wait(free, 1)

        def grad_unit(d, out, cols):
            k = count[0]
            count[0] += 1
            start = cols * UF

            def tile(j, _):
                y = mm(hid_t[...], d[:, pl.ds(pl.multiple_of(start + j * 256, 256), 256)], 1, 0).astype(bf16)
                g_qkv[k % 4, :, :, :, :, :, lane(j, 256)] = y.reshape(g_qkv.shape[1:6] + (256,))
                return 0

            lax.fori_loop(0, UF // 256, tile, 0)
            unit(1, 2 * n_ff + k, g_qkv.at[k % 4], out, pl.ds(start, UF), k).begin()

        for u in range(QW // UF):
            grad_unit(dq, 4, u)
        for u in range(QW // UF):
            e1()
        tick(BACK_TICKS[0])
        for j in range(tiles):
            q_tiles[j].wait()
            dhid[:, j * 256:(j + 1) * 256] = mm(dq[...], wq_c[j % 2], 1, 1)
            if j + 2 < tiles:
                q_tiles.append(fetch_q(j + 2))
        tick(BACK_TICKS[1])
        for i in range(2):
            for d in range(1, half):
                across(i, d).wait_recv()

        def own_keys(j, _):
            t, u = r1[0, 0, block(j)].astype(f32), r1[1, 0, block(j)].astype(f32)
            for d in range(1, half):
                t, u = t + r2[0, d - 1, block(j)].astype(f32), u + r2[1, d - 1, block(j)].astype(f32)
            dkr[block(j), :] = t
            dvl[block(j), :] = u.astype(bf16)
            return 0

        lax.fori_loop(0, rows // RB, own_keys, 0)
        for u in range(KW // UF):
            grad_unit(dvl, 6, u)
        got[1].wait()

        def key_head(j, total):
            lanes = lane(j, HEAD_SIZE)
            y = kp_v[:, lanes]
            r = lax.rsqrt(jnp.mean(y * y, axis=-1, keepdims=True) + norm_epsilon)
            u = y * r
            dy = dkr[:, lanes]
            dy = dy * cos_r[...] - pltpu.roll(dy, HEAD_SIZE // 2, 1) * sin_r[...]
            total = total + jnp.sum(dy * u, axis=0, keepdims=True)
            dy = dy * k_gain[...]
            dkl[:, lanes] = (r * (dy - u * jnp.mean(dy * u, axis=-1, keepdims=True))).astype(bf16)
            return total

        gk = lax.fori_loop(0, KEY_VALUE_HEADS, key_head, jnp.zeros((1, HEAD_SIZE), f32))
        vec[2 * W // 128 + 1:2 * W // 128 + 2, :] = gk
        for u in range(KW // UF):
            grad_unit(dkl, 5, u)
        while state["e1"] < len(units):
            e1()
        tick(BACK_TICKS[2])
        for j in range(tiles):
            for f in kv_tiles[j]:
                f.wait()
            dhid[:, j * 256:(j + 1) * 256] += mm(dkl[...], wk_c[j % 2], 1, 1) + mm(dvl[...], wv_c[j % 2], 1, 1)
            if j + 2 < tiles:
                kv_tiles.append(fetch_kv(j + 2))
        tick(BACK_TICKS[3])
        got_x.wait()

        def first_norm(j, carry):
            total, square = carry
            d, gg = norm_back(hid_v[block(j), :].astype(f32), gain1[...], dhid[block(j), :])
            d = dres[block(j), :] + d
            dres[block(j), :] = d
            return total + gg, square + jnp.sum(valid[block(j), :] * d * d, axis=0, keepdims=True)

        g1, square = lax.fori_loop(0, T // RB, first_norm, (jnp.zeros((1, W), f32), jnp.zeros((1, W), f32)))
        for k in range(W // 128):
            vec[k:k + 1, :] = g1[:, k * 128:(k + 1) * 128]
        place = lax.broadcasted_iota(jnp.int32, (1, 128), 1)
        row = jnp.zeros((1, 128), f32)
        whole = lambda y: jnp.sum(jnp.sum(y, axis=0, keepdims=True), axis=1, keepdims=True)
        for k, y in enumerate((sums[0:1, :], sums[1:2, :], square, valid[...])):
            row = jnp.where(place == k, whole(y), row)
        vec[2 * W // 128 + 2:2 * W // 128 + 3, :] = row
        vec[2 * W // 128 + 3:, :] = jnp.zeros((vec.shape[0] - 2 * W // 128 - 3, 128), f32)

    pl.run_scoped(persistent, V((T, QW), bf16), V((T, KW), f32), V((T, KW), bf16))
    for i in range(2):
        for d in range(1, half):
            across(i, d).wait_send()

    width = CONTINUATION_LEN // n

    step = max(width, 8)

    def pack(j, _):
        y = dres[pl.ds(pl.multiple_of(rows + j * step, step), step), :].astype(bf16)
        for k in range(step // width):
            i = j * (step // width) + k
            grad_src[i // n, i % n] = y[k * width:(k + 1) * width]
        return 0

    lax.fori_loop(0, S * CONTINUATION_LEN // step, pack, 0)
    grad_spread = spread_copies(grad_src, grad_in, 2)
    begin_all(grad_spread)
    prompt_out = fetch(dres.at[pl.ds(0, rows)], d_prompt)
    tick()
    rounds = [(rep, rank(a, b, 1 - c)), (rep, rank(a, 1 - b, c))] + [flip(k) for k in range(bits)]
    vb[0] = vec[...]
    for k, to in enumerate(rounds):
        q = remote(vb.at[2 * k], vb.at[2 * k + 1], vs_.at[k], vr_.at[k], to)
        q.start()
        q.wait()
        vb[2 * k + 2] = vb[2 * k] + vb[2 * k + 1]
        if k in (0, 1, 2):
            tick()
    last, nr = 2 * len(rounds), len(rounds)
    zs = [remote(vb.at[last], vz.at[a], vs_.at[nr + d - 1], vr_.at[nr + d - 1], (rep, rank((a + d) % A, b, c))) for d in range(1, A)]
    for q in zs:
        q.start()
    vz[a] = vb[last]
    wait_all(grad_spread)
    reorder(grad_in, turned)
    grad_collect = collect_copies(turned, grad_out, 3)
    begin_all(grad_collect)
    for q in zs:
        q.wait()
    total = vz[0]
    for k in range(1, A):
        total = total + vz[k]
    vec[...] = total
    while state["tick"] < len(units) + 3:
        tick()
    wait_all(grad_collect)
    prompt_out.wait()
    for f in units:
        f.end()


def backward(index, mixed, dm, h2, act, gate, up, resid, wd, wg, wu, wo, attended, q_rot, lse, rs_q, ks, vs, k_rot, v, k_pre, wq, wk, wv, hidden, x,
             k_gain, q_gain, cos_r, sin_r, cos, sin, past, inside, valid, gain1, gain2, sums, rows, n, R, cid):
    group = PROMPT_LENGTH // rows
    half, A, (T, W), bits = group // 2, n // 4, dm.shape, R.bit_length() - 1
    FW, QW, KW = act.shape[1], attended.shape[1], k_rot.shape[1]
    UD, UF, UO = 256, 512, 512
    S = mixed.shape[0]
    V, D = pltpu.VMEM, pltpu.SemaphoreType.DMA
    shape = jax.ShapeDtypeStruct
    vm, hbm, sm = pl.BlockSpec(memory_space=pltpu.VMEM), pl.BlockSpec(memory_space=pl.ANY), pl.BlockSpec(memory_space=pltpu.SMEM)
    rh = lambda w: w.shape[0] // (2 * n)
    out_shape = [shape((2, rh(w), w.shape[1]), bf16) for w in (wd, wg, wu, wo, wq, wk, wv)]
    vec_rows = 2 * W // 128 + 8
    out_shape += [shape((vec_rows, 128), f32), shape((rows, W), f32), shape(mixed.shape, bf16), shape(mixed.shape, bf16)]
    scratch = []
    for count, r, w in ((W // UD, rh(wd), UD), (2 * (FW // UF) + (QW + 2 * KW) // UF, rh(wg), UF), (W // UO, rh(wo), UO)):
        k0 = fold_split(r)
        k1 = max(r - k0, 8)
        landing = 2 * (FW // UF) if w == UF and r == rh(wg) else count
        scratch += [V((landing, A, 2, 2, r, w), bf16), V((count, A, 2, k0, w), bf16), V((count, A, 2, k1, w) if k0 < r else (1, 1, 1, 8, 128), bf16), V((count, A, r, w), bf16),
                    V((count, A - 1, r, w), bf16), V((count, bits, r, w), bf16), V((count, bits, r, w), bf16)]
    m = W // UD + 2 * (FW // UF) + (QW + 2 * KW) // UF + W // UO
    turned = (n, S) + mixed.shape[2:]
    kv = (2, half, rows, KW)
    scratch += [V(kv, bf16), V((2, max(half - 1, 1), rows, KW), bf16), V(turned, bf16), V(turned, bf16), V(mixed.shape, bf16), V(turned, bf16),
                V((2 * (2 + bits) + 1, vec_rows, 128), f32), V((A, vec_rows, 128), f32), V((T, W), f32)]
    scratch += [D((m,)), D((m,)), D((m, 2)), D((m, 2)), D((m, 2)), D((m, 2)), D((m, A - 1)), D((m, A - 1)), D((m, bits)), D((m, bits)), D((m, 2))]
    scratch += [D((2 * A + 5 * (FW // UF) + 32,)), D((2, 5)), D((2, half)), D((2, half)), D((2, max(half - 1, 1))), D((2, max(half - 1, 1))), D((4, n - 1)), D((4, n - 1)), D((4,)),
                D((2 + bits + A - 1,)), D((2 + bits + A - 1,)), pltpu.SemaphoreType.REGULAR]
    hbm_in = [mixed, dm, h2, act, gate, up, resid, wd, wg, wu, wo, attended, q_rot, lse, rs_q, ks, vs, k_rot, v, k_pre, wq, wk, wv, hidden, x]
    in_vmem = {13, 14}
    res = pl.pallas_call(
        partial(backward_kernel, n, R, group, UD, UF, UO),
        out_shape=out_shape,
        in_specs=[sm] + [vm if k in in_vmem else hbm for k in range(len(hbm_in))] + [vm] * 12,
        out_specs=[hbm] * 7 + [vm] + [hbm] * 3,
        scratch_shapes=scratch,
        compiler_params=pltpu.CompilerParams(collective_id=cid, has_side_effects=True, vmem_limit_bytes=63 << 20),
        name="backward",
    )(index, *hbm_in, k_gain, q_gain, cos_r, sin_r, cos, sin, past, inside, valid, gain1, gain2, sums)
    return [r.reshape(-1, r.shape[-1]) for r in res[:7]], res[7], res[8], res[9], res[10]


def root_mean_scale(values, gain_vector):
    return (
        values
        * lax.rsqrt(jnp.mean(values * values, axis=-1, keepdims=True) + norm_epsilon)
        * gain_vector
    )


def swiglu(gate_pre, up_pre):
    return jax.nn.silu(gate_pre) * up_pre


def dot(x, y):
    return jnp.dot(x, y, preferred_element_type=f32)


def dot_tn(x, y):
    return jnp.einsum("ra,rb->ab", x, y, preferred_element_type=f32)


def dot_nt(x, y):
    return jnp.einsum("ra,ba->rb", x, y, preferred_element_type=f32)


def per_device(
    prompt_rows,
    suffix_rows,
    assignment,
    lengths,
    attention_gain,
    query_weight,
    key_matrix,
    value_matrix,
    query_gain,
    key_norm_gain,
    out_weight,
    mlp_gain,
    gate_weight,
    up_weight,
    down_weight,
    prompt_cotangent,
    suffix_cotangent,
):
    n, R = lax.axis_size("fsdp"), lax.axis_size("rep")
    rank = lax.axis_index("fsdp")
    rows = prompt_rows.shape[0]
    suffix = suffix_rows.shape[0]
    S = suffix // CONTINUATION_LEN
    total = rows + suffix
    width = MODEL_WIDTH

    pad = lambda v: jnp.pad(v.astype(f32).reshape(-1), (0, 128 - v.size))
    tile = jnp.stack([pad(v) for v in (attention_gain, mlp_gain, query_gain, key_norm_gain, assignment, lengths)])
    tile = jnp.pad(tile, ((0, 2), (0, 0)))
    cut = lambda v: v.reshape(S, n, CONTINUATION_LEN // n, width)
    (w_key, w_value, w_query), tiles, (staged_rows, staged_cotangent) = gather(
        [key_matrix, value_matrix, query_weight], tile, [cut(suffix_rows), cut(suffix_cotangent)], n, 0
    )
    gain_first = tiles[:, 0, : attention_gain.size].reshape(-1)
    gain_second = tiles[:, 1, : mlp_gain.size].reshape(-1)
    query_scale = tiles[:, 2, : query_gain.size].reshape(-1)
    key_scale = tiles[:, 3, : key_norm_gain.size].reshape(-1)

    owner = tiles[:, 4, :S].reshape(-1).astype(jnp.int32) // CONT
    slot_count = n * S
    ids = jnp.arange(slot_count, dtype=jnp.int32)
    ahead = (owner[None, :] < owner[:, None]) | ((owner[None, :] == owner[:, None]) & (ids[None, :] < ids[:, None]))
    place = jnp.sum(ahead.astype(jnp.int32), axis=1)
    hits = place[None, :] == ids[:, None]
    order = jnp.sum(jnp.where(hits, ids[None, :], 0), axis=1)
    slot_lengths = jnp.sum(jnp.where(hits, tiles[:, 5, :S].reshape(-1).astype(jnp.int32)[None, :], 0), axis=1)
    own_lengths = lax.dynamic_slice_in_dim(slot_lengths, rank * S, S)

    moved_rows = collect(order, [staged_rows], n, 1)[0].reshape(suffix, width)

    prompt_place = (rank * rows) % PROMPT_LENGTH + jnp.arange(rows, dtype=jnp.int32)
    suffix_place = jnp.arange(suffix, dtype=jnp.int32) % CONTINUATION_LEN
    suffix_slot = jnp.arange(suffix, dtype=jnp.int32) // CONTINUATION_LEN
    length_rows = jnp.repeat(own_lengths, CONTINUATION_LEN)
    suffix_valid = suffix_place < length_rows
    valid_rows = jnp.concatenate([jnp.ones((rows,), f32), suffix_valid.astype(f32)])
    token_positions = jnp.concatenate([prompt_place, PROMPT_LENGTH + suffix_place]).astype(f32)
    half = HEAD_SIZE // 2
    inverse = rope_theta ** (jnp.arange(half, dtype=f32) * (-2.0 / HEAD_SIZE))
    angles_t = inverse[:, None] * token_positions[None, :]
    cos_t, sin_t = jnp.cos(angles_t), jnp.sin(angles_t)
    cos_r, sin_r = cos_t.T, sin_t.T
    cos_rows = jnp.concatenate([cos_r, cos_r], axis=1)
    sin_rows = jnp.concatenate([-sin_r, sin_r], axis=1)
    past = jnp.where(jnp.arange(PROMPT_LENGTH, dtype=jnp.int32)[:, None] <= prompt_place[None, :], 0.0, masked_score).astype(f32)
    inside = jnp.where(
        (suffix_slot[:, None] == suffix_slot[None, :]) & (suffix_place[:, None] <= suffix_place[None, :]) & suffix_valid[:, None], 0.0, masked_score
    ).astype(f32)

    rows_low = jnp.concatenate([prompt_rows, moved_rows], 0)
    hidden = root_mean_scale(rows_low.astype(f32), gain_first).astype(bf16)
    key_gain_row = key_scale.reshape(1, HEAD_SIZE)
    query_gain_col = jnp.broadcast_to(query_scale[:, None], (HEAD_SIZE, 128))
    (
        w_out, w_gate, w_up, w_down, moved_cotangent, attended, query_rot, lse, query_rs, key_pre, key_rot, values,
        prompt_keys, prompt_values, residual, hidden_two, act, gate_low, up_low, mixed_low, sums,
    ) = forward(
        order, rows_low, hidden, w_key, w_value, w_query, [out_weight, gate_weight, up_weight, down_weight], key_gain_row, query_gain_col,
        cos_rows, sin_rows, cos_t, sin_t, past, inside, valid_rows[:, None], gain_second[None, :], staged_cotangent, rows, n, 2,
    )
    moved_cotangent = moved_cotangent.reshape(suffix, width)
    d_mixed_low = jnp.concatenate([prompt_cotangent, moved_cotangent], 0) * valid_rows[:, None].astype(bf16)
    shards, vec_sum, prompt_grad, suffix_mixed, suffix_grad = backward(
        place, cut(mixed_low[rows:]), d_mixed_low, hidden_two, act, gate_low, up_low, residual, w_down, w_gate, w_up, w_out, attended, query_rot, lse, query_rs,
        prompt_keys, prompt_values, key_rot, values, key_pre, w_query, w_key, w_value, hidden, rows_low, key_gain_row, query_gain_col,
        cos_rows, sin_rows, cos_t, sin_t, past, inside, valid_rows[:, None], gain_first[None, :], gain_second[None, :], sums, rows, n, R, 3,
    )
    suffix_mixed, suffix_grad = suffix_mixed.reshape(suffix, width), suffix_grad.reshape(suffix, width)
    g_down, g_gate, g_up, g_out, g_query, g_key, g_value = [g.astype(f32) for g in shards]
    flat = vec_sum.reshape(-1)

    def mine(first, size, part):
        return lax.dynamic_slice_in_dim(flat[first : first + size], rank * part, part)

    g_first = mine(0, width, attention_gain.size)
    g_second = mine(width, width, mlp_gain.size)
    g_query_gain = mine(2 * width, HEAD_SIZE, query_gain.size)
    g_key_gain = mine(2 * width + HEAD_SIZE, HEAD_SIZE, key_norm_gain.size)
    stat_sums = flat[2 * width + 2 * HEAD_SIZE : 2 * width + 2 * HEAD_SIZE + 4]
    token_norms = jnp.sqrt(stat_sums[:3] / (stat_sums[3] * width))
    return (
        mixed_low[:rows],
        suffix_mixed,
        prompt_grad,
        suffix_grad.astype(f32),
        g_first,
        g_query,
        g_key,
        g_value,
        g_query_gain,
        g_key_gain,
        g_out,
        g_second,
        g_gate,
        g_up,
        g_down,
        token_norms,
    )


def solution(mesh):
    placed = (
        P(("rep", "fsdp"), None),
        P(("rep", "fsdp"), None),
        P("rep", "fsdp"),
        P("rep", "fsdp"),
        P("fsdp"),
        P("fsdp", None),
        P("fsdp", None),
        P("fsdp", None),
        P("fsdp"),
        P("fsdp"),
        P("fsdp", None),
        P("fsdp"),
        P("fsdp", None),
        P("fsdp", None),
        P("fsdp", None),
        P(("rep", "fsdp"), None),
        P(("rep", "fsdp"), None),
    )
    return jax.shard_map(
        per_device,
        mesh=mesh,
        in_specs=placed,
        out_specs=(
            P(("rep", "fsdp"), None),
            P(("rep", "fsdp"), None),
            P(("rep", "fsdp"), None),
            P(("rep", "fsdp"), None),
            P("fsdp"),
            P("fsdp", None),
            P("fsdp", None),
            P("fsdp", None),
            P("fsdp"),
            P("fsdp"),
            P("fsdp", None),
            P("fsdp"),
            P("fsdp", None),
            P("fsdp", None),
            P("fsdp", None),
            P(),
        ),
        check_vma=False,
    )
```

```python
from functools import partial

import jax
import jax.numpy as jnp
from jax import lax
from jax.experimental import pallas as pl
from jax.experimental.pallas import tpu as pltpu
from jax.sharding import PartitionSpec as P

MODEL_WIDTH = 1024
QUERY_HEADS = 16
KEY_VALUE_HEADS = 8
HEAD_SIZE = 128
PROMPT_LENGTH = 1024
CONT = 8
CONTINUATION_LEN = 128

norm_epsilon = 1e-06
rope_theta = 1000000.0
masked_score = -1e30
MESH = pl.DeviceIdType.MESH
bf16 = jnp.bfloat16
f32 = jnp.float32

def position(n):
    rep = lax.axis_index("rep")
    rank = lax.axis_index("fsdp")
    return rep, rank // 4, (rank // 2) % 2, rank % 2


def meet(peers):
    barrier = pltpu.get_barrier_semaphore()
    for p in peers:
        pl.semaphore_signal(barrier, inc=1, device_id=p, device_id_type=MESH)
    pl.semaphore_wait(barrier, len(peers))


def remote(src, dst, send, recv, to):
    return pltpu.make_async_remote_copy(src, dst, send, recv, device_id=to, device_id_type=MESH)


def add_rows(count, out, first, second, step=None):
    def one(j, _):
        o = out(j)
        total = first(j)[...].astype(jnp.float32)
        for s in second:
            total = total + s(j)[...].astype(jnp.float32)
        o[...] = total.astype(o.dtype)
        return 0
    lax.fori_loop(0, count, one, 0)


LOG2E = 1.4426950408889634


def mm(x, y, cx, cy):
    return lax.dot_general(x, y, (((cx,), (cy,)), ((), ())), preferred_element_type=f32)


class Ring:
    def __init__(self, n, own, full, cols, sems, i, x_first):
        zs, zr, ss, sr, ls = sems
        A = n // 4
        rep, a, b, c = position(n)
        h = rep % 2
        every = slice(None)
        at = lambda *ix: full.at[(*ix, every, cols)]
        rank = lambda a, b, c: (a * 2 + b) * 2 + c
        ydev, xdev, cdev = (rep, rank(a, 1 - b, c)), (rep + 1 - 2 * h, rank(a, b, c)), (rep, rank(a, b, 1 - c))
        same = lambda ref, k, to: remote(ref, ref, ss.at[i, k], sr.at[i, k], to)
        mine = own.at[h, :, cols]
        self.local = lambda: [pltpu.make_async_copy(mine, at(a, b, c, h), ls.at[i])]
        self.along = lambda: [remote(mine, at(a, b, c, h), zs.at[i, d - 1], zr.at[i, d - 1], (rep, rank((a + d) % A, b, c))) for d in range(1, A)]
        self.second = lambda: [same(at(every, b, c, h), 0, xdev if x_first else ydev)]
        self.third = lambda: [same(at(every, b, c, every), 1, ydev) if x_first else same(at(every, every, c, h), 1, xdev)]
        self.last = lambda: [same(at(every, every, c, every), 2, cdev)]

    def begin(self):
        for q in self.local() + self.along():
            q.start()

    def turn(self, arrived, started):
        for q in arrived():
            q.wait_recv()
        for q in started():
            q.start()

    def step(self, k):
        if k == 0:
            for q in self.local():
                q.wait()
            self.turn(self.along, self.second)
        elif k == 1:
            self.turn(self.second, self.third)
        elif k == 2:
            self.turn(self.third, self.last)
        else:
            for q in self.last():
                q.wait_recv()

    def end(self):
        for q in self.along() + self.second() + self.third() + self.last():
            q.wait_send()


class Ticker:
    def __init__(self, rings, arrived=lambda i: None):
        self.rings, self.arrived, self.done = rings, arrived, [0] * 5

    def begin(self, count):
        for r in self.rings[self.done[0]:self.done[0] + count]:
            r.begin()
            self.done[0] += 1

    def __call__(self, count=1, lag=1):
        for _ in range(count):
            before = list(self.done)
            for k in range(1, 5):
                i = self.done[k]
                if i < len(self.rings) and before[k - 1] - i >= lag:
                    self.rings[i].step(k - 1)
                    self.done[k] += 1
                    if k == 1:
                        self.begin(self.done[1] + ALONG - self.done[0])
                    if k == 4:
                        self.arrived(i)

    def until(self, count):
        while self.done[4] < count:
            self()


ALONG = 2


def slot_spread(n, src, dst, sems, k, where):
    s, r, l = sems
    rep, me = where
    own = pltpu.make_async_copy(src.at[:, me], dst.at[me], l.at[k])
    return own, [remote(src.at[:, (me + d) % n], dst.at[me], s.at[k, d - 1], r.at[k, d - 1], (rep, (me + d) % n)) for d in range(1, n)]


def slot_collect(n, src, dst, sems, k, where):
    s, r, l = sems
    rep, me = where
    own = pltpu.make_async_copy(src.at[me], dst.at[:, me], l.at[k])
    return own, [remote(src.at[(me + d) % n], dst.at[:, me], s.at[k, d - 1], r.at[k, d - 1], (rep, (me + d) % n)) for d in range(1, n)]


def begin_all(pair):
    pair[0].start()
    for q in pair[1]:
        q.start()


def wait_all(pair):
    pair[0].wait()
    for q in pair[1]:
        q.wait()


def gather_kernel(n, CB, *refs):
    so, sk, sv, tile, pieces, wq, wk, wv, tiles, staged, zs, zr, ss, sr, ls, ts, tr, ps, pr, pls = refs
    rep, a, b, c = position(n)
    me = (a * 2 + b) * 2 + c
    h = rep % 2
    meet([(rep, (me + d) % n) for d in range(1, n)] + [(rep + 1 - 2 * h, me)])
    blocks = []
    for own, full in ((sk, wk), (sv, wv), (so, wq)):
        blocks += [(own, full, pl.ds(q * CB, CB)) for q in range(full.shape[-1] // CB)]
    rings = [Ring(n, own, full, cols, (zs, zr, ss, sr, ls), i, i % 2 == 0) for i, (own, full, cols) in enumerate(blocks)]
    tick = Ticker(rings)
    share = [remote(tile, tiles.at[me], ts.at[d - 1], tr.at[d - 1], (rep, (me + d) % n)) for d in range(1, n)]
    rows = slot_spread(n, pieces, staged, (ps, pr, pls), 0, (rep, me))
    for q in share:
        q.start()
    tiles[me] = tile[...]
    tick.begin(ALONG)
    begin_all(rows)
    tick.until(len(rings))
    for q in share:
        q.wait()
    wait_all(rows)
    for r in rings:
        r.end()


def gather(wk, wv, wq, tile, slots, n, cid):
    A, CB = n // 4, 512
    halves = [w.reshape(2, w.shape[0] // 2, w.shape[1]) for w in (wq, wk, wv)]
    m = sum(w.shape[1] for w in (wk, wv, wq)) // CB
    D = pltpu.SemaphoreType.DMA
    vm, hbm = pl.BlockSpec(memory_space=pltpu.VMEM), pl.BlockSpec(memory_space=pl.ANY)
    shape = jax.ShapeDtypeStruct
    res = pl.pallas_call(
        partial(gather_kernel, n, CB),
        out_shape=[shape((A, 2, 2) + w.shape, bf16) for w in halves] + [shape((n,) + tile.shape, f32), shape((n, slots.shape[0]) + slots.shape[2:], bf16)],
        in_specs=[hbm] * 3 + [vm] + [hbm],
        out_specs=[hbm] * 3 + [vm, hbm],
        scratch_shapes=[D((m, A - 1))] * 2 + [D((m, 3))] * 2 + [D((m,))] + [D((n - 1,))] * 2 + [D((1, n - 1))] * 2 + [D((1,))],
        compiler_params=pltpu.CompilerParams(collective_id=cid, has_side_effects=True),
        name="gather",
    )(*halves, tile, slots)
    w_query, w_key, w_value = [f.reshape(-1, f.shape[-1]) for f in res[:3]]
    return w_key, w_value, w_query, res[3], res[4]


def forward_kernel(n, group, *refs):
    it = iter(refs)
    take = lambda count: [next(it) for _ in range(count)]
    index, prompt, staged, cot, wk_h, wv_h, wq_h, so, sg, su, sd, k_gain, q_gain, cos_r, sin_r, cos, sin, past, inside, valid, gain1, gain2 = take(22)
    wo, wg, wu, wd, moved, gate, up = take(7)
    outs = take(13)
    lse_out, rs_out, stats = take(3)
    x, hidden, attended, q_out, k_pre, k_out, v, ks, vs, resid, h2, act, mixed = bufs = take(13)
    wk, wv, wq, ordered, landed, cot_in, o_buf, g_buf, u_buf, d_buf, g_st, u_st = take(12)
    zs, zr, ss, sr, ls, lds, fs, fr, gs, gr, kls, ps, pr, pls, gos, outs_sem, ins_sem = take(17)
    rows = ks.shape[2]
    T, W = x.shape
    half = group // 2
    rep, a, b, c = position(n)
    me = (a * 2 + b) * 2 + c
    first, slot = (me // group) * half, (me // 2) % half
    h = rep % 2
    ins = [pltpu.make_async_copy(src, dst, ins_sem.at[k]) for k, (src, dst) in enumerate(((wk_h, wk), (wv_h, wv), (wq_h, wq)))]
    for q in ins:
        q.start()
    meet([(rep, (me + d) % n) for d in range(1, n)] + [(rep + 1 - 2 * h, me)])
    saves = {id(buf): pltpu.make_async_copy(buf, out, outs_sem.at[k]) for k, (buf, out) in enumerate(zip(bufs, outs))}

    def save(*which):
        for buf in which:
            saves[id(buf)].start()

    OB, GB = o_buf.shape[-1], g_buf.shape[-1]
    n_out, n_mlp = wo.shape[-1] // OB, wg.shape[-1] // GB
    blocks = [(so, wo, pl.ds(q * OB, OB), o_buf.at[q]) for q in range(n_out)]
    for q in range(n_mlp):
        blocks += [(sg, wg, pl.ds(q * GB, GB), g_buf.at[q % 2]), (su, wu, pl.ds(q * GB, GB), u_buf.at[q % 2])]
    blocks += [(sd, wd, pl.ds(q * OB, OB), d_buf.at[q]) for q in range(n_out)]
    m = len(blocks)
    rings = [Ring(n, own, full, cols, (zs, zr, ss, sr, ls), i, i < X_FIRST) for i, (own, full, cols, _) in enumerate(blocks)]

    def load(i):
        _, full, cols, buf = blocks[i]
        return pltpu.make_async_copy(full.at[:, :, :, :, :, cols], buf, lds.at[i])

    used, late = [0], []

    def arrived(i):
        q = (i - n_out) // 2 if n_out <= i < n_out + 2 * n_mlp else 0
        if q < used[0] + 2:
            load(i).start()
        else:
            late.append(i)

    def release():
        used[0] += 1
        now, late[:] = [i for i in late if (i - n_out) // 2 < used[0] + 2], [i for i in late if (i - n_out) // 2 >= used[0] + 2]
        for i in now:
            load(i).start()

    tick = Ticker(rings, arrived)
    S = ordered.shape[1]

    def reorder(src, flat):
        def put(j, _):
            s = index[j]
            ordered[j // S, j % S] = src[s] if flat else src[s // S, s % S]
            return 0

        lax.fori_loop(0, n * S, put, 0)

    sems = (ps, pr, pls)
    reorder(staged, True)
    rows_in = slot_collect(n, ordered, landed, sems, 0, (rep, me))
    cot_spread = slot_spread(n, cot, cot_in, sems, 1, (rep, me))
    cot_collect = slot_collect(n, ordered, moved, sems, 2, (rep, me))
    begin_all(rows_in)
    tick.begin(ALONG)

    lane = lambda j, w: pl.ds(pl.multiple_of(j * w, w), w)
    heads = QUERY_HEADS // KEY_VALUE_HEADS
    pair = heads * HEAD_SIZE
    RB = 32
    block = lambda j: pl.ds(pl.multiple_of(j * RB, RB), RB)

    def norm(y, gain):
        return (y * lax.rsqrt(jnp.mean(y * y, axis=-1, keepdims=True) + norm_epsilon) * gain[...]).astype(bf16)

    def prompt_rows(j, _):
        y = prompt[block(j), :]
        x[block(j), :] = y
        hidden[block(j), :] = norm(y.astype(f32), gain1)
        return 0

    def kv_tile(part, j, _):
        kp = mm(hidden[part, :], wk[:, lane(j, 256)], 1, 0)
        k_pre[part, lane(j, 256)] = kp
        for g in range(2):
            y = kp[:, g * HEAD_SIZE:(g + 1) * HEAD_SIZE]
            y = y * lax.rsqrt(jnp.mean(y * y, axis=-1, keepdims=True) + norm_epsilon) * k_gain[...]
            k_out[part, lane(2 * j + g, HEAD_SIZE)] = (y * cos_r[part, :] + pltpu.roll(y, HEAD_SIZE // 2, 1) * sin_r[part, :]).astype(bf16)
        v[part, lane(j, 256)] = mm(hidden[part, :], wv[:, lane(j, 256)], 1, 0).astype(bf16)
        return 0

    lax.fori_loop(0, rows // RB, prompt_rows, 0)
    ins[0].wait()
    ins[1].wait()
    lax.fori_loop(0, wk.shape[1] // 256, partial(kv_tile, pl.ds(0, rows)), 0)
    parts = [(k_out, ks), (v, vs)]
    at = lambda s, c: (rep, (first + s) * 2 + c)
    mine = lambda i: parts[i][0].at[pl.ds(0, rows)]
    klocal = [pltpu.make_async_copy(mine(i), parts[i][1].at[slot, c], kls.at[i]) for i in range(2)]
    across = [remote(mine(i), parts[i][1].at[slot, c], fs.at[i, d - 1], fr.at[i, d - 1], at((slot + d) % half, c)) for i in range(2) for d in range(1, half)]
    sibling = [remote(mine(i), parts[i][1].at[slot, c], gs.at[i, 0], gr.at[i, 0], at(slot, 1 - c)) for i in range(2)]
    onward = []
    for i in range(2):
        for d in range(1, half):
            there = parts[i][1].at[(slot + half - d) % half, c]
            onward.append(remote(there, there, gs.at[i, d], gr.at[i, d], at(slot, 1 - c)))
    for q in across + sibling + klocal:
        q.start()
    tick()
    wait_all(rows_in)
    width = landed.shape[2]

    def slot_rows(j, _):
        s, p = j // (n * width // RB), j % (n * width // RB)
        k = RB // width
        if width % 8 == 0:
            y = landed[s, pl.ds(p * k, k)].astype(f32).reshape(RB, W)
        else:
            y = jnp.concatenate([landed[s, p * k + i].astype(f32) for i in range(k)], axis=0)
        at = pl.ds(pl.multiple_of(rows + j * RB, RB), RB)
        x[at, :] = y.astype(bf16)
        hidden[at, :] = norm(y, gain1)
        return 0

    lax.fori_loop(0, (T - rows) // RB, slot_rows, 0)
    lax.fori_loop(0, wk.shape[1] // 256, partial(kv_tile, pl.ds(rows, T - rows)), 0)
    tick()
    save(x, hidden, k_pre, k_out, v)
    ins[2].wait()

    def q_tile(j, _):
        qp = mm(hidden[...], wq[:, lane(j, pair)], 1, 0)
        for g in range(heads):
            y = qp[:, g * HEAD_SIZE:(g + 1) * HEAD_SIZE].T
            rs = lax.rsqrt(jnp.mean(y * y, axis=0, keepdims=True) + norm_epsilon)
            rs_out[j, g:g + 1, :] = rs
            y = y * rs * q_gain[:, 0:1]
            lo, hi = y[:HEAD_SIZE // 2], y[HEAD_SIZE // 2:]
            y = jnp.concatenate([lo * cos[...] - hi * sin[...], hi * cos[...] + lo * sin[...]], axis=0)
            q_out[lane(j * heads + g, HEAD_SIZE), :] = y.astype(bf16)
        for k, plan in FORWARD_PLAN[0]:
            pl.when(j == k)(partial(tick, *plan))
        return 0

    lax.fori_loop(0, KEY_VALUE_HEADS, q_tile, 0)
    begin_all(cot_spread)
    save(q_out)
    for q in across:
        q.wait_recv()
    for q in onward:
        q.start()
    tick(*FORWARD_PLAN[1])
    for q in klocal:
        q.wait()
    for q in sibling + onward:
        q.wait_recv()
    save(ks, vs)
    scale = HEAD_SIZE ** -0.5 * LOG2E

    def attend_head(j, _):
        kl = lane(j, HEAD_SIZE)
        kb = ks[:, :, :, kl].reshape(PROMPT_LENGTH, HEAD_SIZE)
        vb = vs[:, :, :, kl].reshape(PROMPT_LENGTH, HEAD_SIZE)
        for g in range(heads):
            ql = lane(j * heads + g, HEAD_SIZE)
            q = q_out[ql, :]
            p = jnp.exp2(mm(kb, q[:, :rows], 1, 0) * scale + past[...])
            total = jnp.sum(p, axis=0, keepdims=True)
            o = mm(vb, p.astype(bf16), 0, 0) / total
            attended[:rows, ql] = o.T.astype(bf16)
            lse_out[j, g:g + 1, :rows] = jnp.log2(total)
            p = jnp.exp2(mm(kb, q[:, rows:], 1, 0) * scale)
            r = jnp.exp2(mm(k_out[rows:, kl], q[:, rows:], 1, 0) * scale + inside[...])
            total = jnp.sum(p, axis=0, keepdims=True) + jnp.sum(r, axis=0, keepdims=True)
            o = (mm(vb, p.astype(bf16), 0, 0) + mm(v[rows:, kl], r.astype(bf16), 0, 0)) / total
            attended[rows:, ql] = o.T.astype(bf16)
            lse_out[j, g:g + 1, rows:] = jnp.log2(total)
        for k, plan in FORWARD_PLAN[2]:
            pl.when(j == k)(partial(tick, *plan))
        return 0

    lax.fori_loop(0, KEY_VALUE_HEADS, attend_head, 0)
    save(attended)
    wait_all(cot_spread)
    reorder(cot_in, False)
    begin_all(cot_collect)

    stats[...] = jnp.zeros_like(stats)
    for q in range(n_out):
        tick.until(q + 1)
        load(q).wait()

        def out_tile(j, _):
            cols = lane(q * (OB // 256) + j, 256)
            w = o_buf[q, :, :, :, :, :, lane(j, 256)].reshape(-1, 256)
            y = x[:, cols].astype(f32) + mm(attended[...], w, 1, 0)
            resid[:, cols] = y
            stats[1:2, :] += jnp.sum(valid[...] * y * y, axis=0, keepdims=True)
            return 0

        lax.fori_loop(0, OB // 256, out_tile, 0)

    def norm_rows(j, _):
        h2[block(j), :] = norm(resid[block(j), :], gain2)
        return 0

    lax.fori_loop(0, T // RB, norm_rows, 0)
    save(resid, h2)
    saved = lambda q: [pltpu.make_async_copy(g_st.at[q % 2], gate.at[:, pl.ds(q * GB, GB)], gos.at[q % 2, 0]),
                       pltpu.make_async_copy(u_st.at[q % 2], up.at[:, pl.ds(q * GB, GB)], gos.at[q % 2, 1])]
    for q in range(n_mlp):
        tick.until(n_out + 2 * q + 2)
        load(n_out + 2 * q).wait()
        load(n_out + 2 * q + 1).wait()
        if q >= 2:
            for s in saved(q - 2):
                s.wait()

        def mlp_tile(j, _):
            g = mm(h2[...], g_buf[q % 2, :, :, :, :, :, lane(j, 256)].reshape(-1, 256), 1, 0)
            u = mm(h2[...], u_buf[q % 2, :, :, :, :, :, lane(j, 256)].reshape(-1, 256), 1, 0)
            g_st[q % 2, :, lane(j, 256)] = g.astype(bf16)
            u_st[q % 2, :, lane(j, 256)] = u.astype(bf16)
            act[:, lane(q * (GB // 256) + j, 256)] = (g / (1.0 + jnp.exp(-g)) * u).astype(bf16)
            return 0

        lax.fori_loop(0, GB // 256, mlp_tile, 0)
        release()
        for s in saved(q):
            s.start()
    save(act)
    for q in range(n_out):
        tick.until(n_out + 2 * n_mlp + q + 1)
        load(n_out + 2 * n_mlp + q).wait()

        def down_tile(j, _):
            cols = lane(q * (OB // 256) + j, 256)
            w = d_buf[q, :, :, :, :, :, lane(j, 256)].reshape(-1, 256)
            y = resid[:, cols] + mm(act[...], w, 1, 0)
            mixed[:, cols] = y.astype(bf16)
            stats[0:1, :] += jnp.sum(valid[...] * y * y, axis=0, keepdims=True)
            return 0

        lax.fori_loop(0, OB // 256, down_tile, 0)
    save(mixed)
    for q in range(max(0, n_mlp - 2), n_mlp):
        for s in saved(q):
            s.wait()
    wait_all(cot_collect)
    for q in across + sibling + onward:
        q.wait_send()
    for r in rings:
        r.end()
    for q in saves.values():
        q.wait()


X_FIRST = 4
FORWARD_PLAN = (((1, (1,)), (3, (1,)), (5, (1,)), (7, (1,))), (1,), ((1, (1,)), (3, (1,)), (5, (1,)), (7, (1,))))


def forward(index, prompt, staged, cot, wk, wv, wq, shards, k_gain, q_gain, cos_r, sin_r, cos, sin, past, inside, valid, gain1, gain2, n, cid):
    rows, W = prompt.shape
    S = staged.shape[1]
    T = rows + S * CONTINUATION_LEN
    group = PROMPT_LENGTH // rows
    half, A = group // 2, n // 4
    halves = [s.reshape(2, s.shape[0] // 2, s.shape[1]) for s in shards]
    flat = staged.reshape((-1,) + staged.shape[2:])
    QW, KW, FW = wq.shape[1], wk.shape[1], shards[1].shape[1]
    D, V = pltpu.SemaphoreType.DMA, pltpu.VMEM
    shape = jax.ShapeDtypeStruct
    small = shape((KEY_VALUE_HEADS, 2, T), f32)
    keys = ((half, 2, rows, KW), bf16)
    kept = [((T, W), bf16), ((T, W), bf16), ((T, QW), bf16), ((QW, T), bf16), ((T, KW), f32), ((T, KW), bf16), ((T, KW), bf16), keys, keys,
            ((T, W), f32), ((T, W), bf16), ((T, FW), bf16), ((T, W), bf16)]
    out_shape = [shape((A, 2, 2) + s.shape, bf16) for s in halves] + [shape((S, n) + staged.shape[2:], bf16), shape((T, FW), bf16), shape((T, FW), bf16)]
    out_shape += [shape(*k) for k in kept] + [small, small, shape((8, 256), f32)]
    vm, hbm, sm = pl.BlockSpec(memory_space=pltpu.VMEM), pl.BlockSpec(memory_space=pl.ANY), pl.BlockSpec(memory_space=pltpu.SMEM)
    OB, GB = 512, 768
    n_out, n_mlp = W // OB, FW // GB
    m = 2 * n_out + 2 * n_mlp
    buf = lambda i, k, w: V((k, A, 2, 2) + halves[i].shape[:2] + (w,), bf16)
    res = pl.pallas_call(
        partial(forward_kernel, n, group),
        out_shape=out_shape,
        in_specs=[sm, vm, vm, hbm] + [hbm] * 7 + [vm] * 11,
        out_specs=[hbm] * 20 + [vm] * 3,
        scratch_shapes=[V(*k) for k in kept] + [V(wk.shape, bf16), V(wv.shape, bf16), V(wq.shape, bf16), V(staged.shape, bf16), V((S, n) + staged.shape[2:], bf16),
            V(staged.shape, bf16), buf(0, n_out, OB), buf(1, 2, GB), buf(2, 2, GB), buf(3, n_out, OB), V((2, T, GB), bf16), V((2, T, GB), bf16)]
        + [D((m, A - 1))] * 2 + [D((m, 3))] * 2 + [D((m,))] * 2 + [D((2, max(half - 1, 1)))] * 2 + [D((2, half))] * 2 + [D((2,))]
        + [D((3, n - 1))] * 2 + [D((3,)), D((2, 2)), D((13,)), D((3,))],
        compiler_params=pltpu.CompilerParams(collective_id=cid, has_side_effects=True, vmem_limit_bytes=63 << 20),
        name="forward",
    )(index, prompt, flat, cot, wk, wv, wq, *halves, k_gain, q_gain, cos_r, sin_r, cos, sin, past, inside, valid, gain1, gain2)
    res = list(res)
    for i, s in enumerate(shards):
        res[i] = res[i].reshape(-1, s.shape[1])
    for i in (14, 15):
        res[i] = res[i].reshape(PROMPT_LENGTH, KW)
    return res


PLAN = ((3, 5), (1, 3), (2, 8), (4, 5), (5, 8), (0, 1), (6, 8), (2, 8), (3, 3), (1, 5), (2, 8), (1, 3), (3, 8), (3, 1), (0, 6), (6, 2), (2, 4), (5, 4), (1, 2), (5, 3))


class Fold:
    def __init__(self, n, R, where, g, bufs, out, cols, sems, i):
        self.bufs, self.k, self.landing = bufs
        self.waited = set()
        self.g, self.out, self.cols, self.i, self.sems = g, out, cols, i, sems
        self.A, self.bits = n // 4, R.bit_length() - 1
        self.rep, self.a, self.b, self.c, self.h = where
        self.rh = self.bufs[0].shape[-2]
        self.k0 = fold_split(self.rh)

    b1 = property(lambda self: self.bufs[0].at[self.landing])
    b2y, b2x, b3, b4, s4, b5 = [property(lambda self, j=j: self.bufs[j].at[self.k]) for j in range(1, 7)]

    def device(self, da=0, db=0, dc=0, bit=None):
        rep, a, b, c = self.rep, self.a, self.b, self.c
        if bit is not None:
            rep = rep + (1 << bit) - 2 * (1 << bit) * ((rep // (1 << bit)) % 2)
        return (rep, (((a + da) % self.A) * 2 + (1 - b if db else b)) * 2 + (1 - c if dc else c))

    @property
    def ydev(self):
        return self.device(db=1)

    @property
    def xdev(self):
        return self.device(bit=0)

    @property
    def cdev(self):
        return self.device(dc=1)

    def zdev(self, d):
        return self.device(da=d)

    def flip(self, bit):
        return self.device(bit=bit)

    def hop(self, k):
        i, a, b, c, h, k0, rh = self.i, self.a, self.b, self.c, self.h, self.k0, self.rh
        s1s, s1r, s2s, s2r, s3s, s3r, s4s, s4r, s5s, s5r, _ = self.sems
        lo, hi = pl.ds(0, k0), pl.ds(k0, rh - k0)
        if k == 1:
            return [remote(self.g.at[:, :, 1 - c], self.b1, s1s.at[i], s1r.at[i], self.cdev)]
        if k == 2:
            q = [remote(self.b1.at[:, 1 - b, :, lo], self.b2y, s2s.at[i, 0], s2r.at[i, 0], self.ydev)]
            if k0 < rh:
                q.append(remote(self.b1.at[:, :, 1 - h, hi], self.b2x, s2s.at[i, 1], s2r.at[i, 1], self.xdev))
            return q
        if k == 3:
            q = [remote(self.b2y.at[:, 1 - h], self.b3.at[:, lo], s3s.at[i, 0], s3r.at[i, 0], self.xdev)]
            if k0 < rh:
                q.append(remote(self.b2x.at[:, 1 - b], self.b3.at[:, hi], s3s.at[i, 1], s3r.at[i, 1], self.ydev))
            return q
        if k == 4:
            return [remote(self.b3.at[(a + d) % self.A], self.b4.at[d - 1], s4s.at[i, d - 1], s4r.at[i, d - 1], self.zdev(d)) for d in range(1, self.A)]
        last = self.bits - 1
        return [remote(self.s4.at[last], self.b5.at[last], s5s.at[i, last], s5r.at[i, last], self.xdev)]

    def put(self, k):
        last = self.bits - 1
        half = self.h if k == 0 else 1 - self.h
        return pltpu.make_async_copy((self.s4 if k == 0 else self.b5).at[last], self.out.at[half, :, self.cols], self.sems[-1].at[self.i, k])

    def begin(self):
        for q in self.hop(1):
            q.start()

    def arrive(self, k):
        for q in self.hop(k):
            q.wait_recv()

    def go(self, k):
        for q in self.hop(k):
            q.start()

    def step(self, k):
        a, b, c, h, k0, rh = self.a, self.b, self.c, self.h, self.k0, self.rh
        self.arrive(k)
        lo, hi = pl.ds(0, k0), pl.ds(k0, rh - k0)
        if k == 1:
            for q in self.hop(1):
                q.wait_send()
            view = lambda ref: lambda j: ref.at[j // 4, (j // 2) % 2, j % 2]
            add_rows(self.A * 4, view(self.b1), view(self.b1), [lambda j: self.g.at[j // 4, (j // 2) % 2, c, j % 2]])
            return
        elif k == 2:
            view = lambda ref: lambda j: ref.at[j // 2, j % 2]
            add_rows(self.A * 2, view(self.b2y), view(self.b2y), [lambda j: self.b1.at[j // 2, b, j % 2, lo]])
            if k0 < rh:
                add_rows(self.A * 2, view(self.b2x), view(self.b2x), [lambda j: self.b1.at[j // 2, j % 2, h, hi]])
        elif k == 3:
            view = lambda part: lambda j: self.b3.at[j, part]
            add_rows(self.A, view(lo), view(lo), [lambda j: self.b2y.at[j, h]])
            if k0 < rh:
                add_rows(self.A, view(hi), view(hi), [lambda j: self.b2x.at[j, b]])
        elif k == 4:
            add_rows(1, lambda j: self.s4.at[0], lambda j: self.b3.at[a], [lambda j, d=d: self.b4.at[d] for d in range(self.A - 1)])
            s5s, s5r = self.sems[8:10]
            for r in range(self.bits - 1):
                q = remote(self.s4.at[r], self.b5.at[r], s5s.at[self.i, r], s5r.at[self.i, r], self.flip(r + 1))
                q.start()
                q.wait()
                add_rows(1, lambda j, r=r: self.s4.at[r + 1], lambda j, r=r: self.s4.at[r], [lambda j, r=r: self.b5.at[r]])
            self.put(0).start()
        else:
            self.put(1).start()
            return
        self.go(k + 1)

    def sent(self, k):
        if k not in self.waited:
            self.waited.add(k)
            for q in self.hop(k):
                q.wait_send()

    def end(self):
        for k in range(2, 6):
            self.sent(k)
        self.put(0).wait()
        self.put(1).wait()


def fold_split(rh):
    if (rh // 2) % 16 == 0:
        return rh // 2
    return rh // 32 * 16 if rh >= 32 else rh


def backward_kernel(n, R, group, UD, UF, UO, *refs):
    it = iter(refs)
    take = lambda count: [next(it) for _ in range(count)]
    index, mixed, dm, h2, act, gate, up, resid, wd, wg, wu, wo, attended, q_rot, lse, rs_q, ks, vs, k_rot, v, k_pre, wq, wk, wv, hidden, x = take(26)
    k_gain, q_gain, cos_r, sin_r, cos, sin, past, inside, valid, gain1, gain2, sums = take(12)
    outs = take(7)
    vec, d_prompt, mixed_out, grad_out = take(4)
    classes = [take(7) for _ in range(3)]
    r1, r2, mixed_in, turned, grad_src, grad_in, vb, vz, dres = take(9)
    fold_sems = take(11)
    lds, hs, gs, gr, fs, fr, a2s, a2r, a2l, vs_, vr_, free = take(12)
    A, T, W = n // 4, dm.shape[0], dm.shape[1]
    half, rows, KW = group // 2, r1.shape[2], k_rot.shape[1]
    FW, QW = act.shape[1], attended.shape[1]
    bits = R.bit_length() - 1
    rep, a, b, c = position(n)
    h = rep % 2
    rank = lambda a, b, c: (a * 2 + b) * 2 + c
    me = rank(a, b, c)
    first, slot = (me // group) * half, (me // 2) % half
    flip = lambda bit: (rep + (1 << bit) - 2 * (1 << bit) * ((rep // (1 << bit)) % 2), me)
    meet([(rep, (me + d) % n) for d in range(1, n)] + [flip(k) for k in range(bits)])

    lane = lambda j, w: pl.ds(pl.multiple_of(j * w, w), w)
    heads = QUERY_HEADS // KEY_VALUE_HEADS
    loads = iter(range(lds.shape[0]))

    def fetch(src, dst):
        q = pltpu.make_async_copy(src, dst, lds.at[next(loads)])
        q.start()
        return q

    S = turned.shape[1]

    trips = (a2s, a2r, a2l)
    spread_copies = lambda src, dst, k: slot_spread(n, src, dst, trips, k, (rep, me))
    collect_copies = lambda src, dst, k: slot_collect(n, src, dst, trips, k, (rep, me))

    def reorder(src, dst):
        def put(j, _):
            s = index[j]
            dst[j // S, j % S] = src[s // S, s % S]
            return 0

        lax.fori_loop(0, n * S, put, 0)

    mixed_spread = spread_copies(mixed, mixed_in, 0)
    grad_spread, grad_collect = spread_copies(grad_src, grad_in, 2), collect_copies(turned, grad_out, 3)

    units = []

    def unit(cls, k, g, out, cols, landing=None):
        units.append(Fold(n, R, (rep, a, b, c, h), g, (classes[cls], k, k if landing is None else landing), outs[out], cols, fold_sems, len(units)))
        return units[-1]

    done = [0] * 6

    def e1():
        units[done[0]].step(1)
        done[0] += 1

    def tick(count=1, lag=2):
        for _ in range(count):
            before = list(done)
            if done[1] < before[0]:
                units[done[1]].go(2)
                done[1] += 1
            for k in range(2, 6):
                if before[k - 1] - done[k] >= lag:
                    units[done[k]].step(k)
                    done[k] += 1

    n_down, n_ff, n_out = W // UD, FW // UF, W // UO
    V = pltpu.VMEM
    rh = lambda k: classes[k][0].shape[-2]
    AT, QT = FW // A, QW // A

    def down(act_c, act_t, g_down, dm_v):
        got = fetch(dm, dm_v)
        pieces = [fetch(act.at[:, pl.ds(0, AT)], act_c.at[0])]
        begin_all(mixed_spread)
        got.wait()
        for i in range(A):
            if i + 1 < A:
                pieces.append(fetch(act.at[:, pl.ds((i + 1) * AT, AT)], act_c.at[(i + 1) % 2]))
            pieces[i].wait()
            act_t[...] = act_c[i % 2].T

            def down_tile(j, _):
                y = mm(act_t[...], dm_v[:, lane(j, UD)], 1, 0).astype(bf16)
                g_down[j, i] = y.reshape(g_down.shape[2:])
                return 0

            lax.fori_loop(0, n_down, down_tile, 0)
        for u in range(n_down):
            unit(0, u, g_down.at[u], 0, pl.ds(u * UD, UD)).begin()
        for u in range(n_down):
            e1()

    pl.run_scoped(down, V((2, T, AT), bf16), V((AT, T), bf16), V((n_down, A, 2, 2, 2, rh(0), UD), bf16), V((T, W), bf16))
    tick(*PLAN[0])
    RB = 32
    block = lambda j: pl.ds(pl.multiple_of(j * RB, RB), RB)

    def norm_back(value, gain, grad):
        r = lax.rsqrt(jnp.mean(value * value, axis=-1, keepdims=True) + norm_epsilon)
        u = value * r
        t = grad * gain
        return r * (t - u * jnp.mean(t * u, axis=-1, keepdims=True)), jnp.sum(grad * u, axis=0, keepdims=True)

    def persistent(dq, dkr, dvl):
        def after_mlp(drl):
            pl.run_scoped(partial(mlp, drl), V((4, A, 2, 2, 2, rh(1), UF), bf16), V((2, UF, W), bf16), V((2, W, UF), bf16), V((2, W, UF), bf16), V((2, T, UF), bf16),
                          V((2, T, UF), bf16), V((T, UF), bf16), V((T, UF), bf16), V((W, T), bf16), V((T, W), bf16), V((T, W), bf16), V((T, W), f32))
            pl.run_scoped(partial(out_grad, drl), V((2, T, QT), bf16), V((QT, T), bf16), V((n_out, A, 2, 2, 2, rh(2), UO), bf16))
            wait_all(mixed_spread)
            reorder(mixed_in, turned)
            mixed_collect = collect_copies(turned, mixed_out, 1)
            begin_all(mixed_collect)
            pl.run_scoped(partial(attention, drl, dq, dkr, dvl), V((half, 2, rows, KW), bf16), V((half, 2, rows, KW), bf16), V((2, PROMPT_LENGTH, HEAD_SIZE), bf16),
                          V((2, PROMPT_LENGTH, HEAD_SIZE), bf16), V((2, heads * HEAD_SIZE, T), bf16), V((2, T, heads * HEAD_SIZE), bf16), V((2, heads * HEAD_SIZE, W), bf16),
                          V((T, KW), bf16), V((T, KW), bf16))
            wait_all(mixed_collect)

        pl.run_scoped(after_mlp, V((T, W), bf16))
        pl.run_scoped(partial(weights_back, dq, dkr, dvl), V((2, 256, QW), bf16), V((2, 256, KW), bf16), V((2, 256, KW), bf16), V((T, W), bf16), V((W, T), bf16),
                      V((T, KW), f32), V((T, KW), bf16), V((4, A, 2, 2, 2, rh(1), UF), bf16), V((T, W), f32))

    def mlp(drl, g_ff, wd_c, wg_c, wu_c, gate_c, up_c, dg_c, du_c, h2_t, h2_v, dm_v, dhid):
        got = [fetch(h2, h2_v), fetch(dm, dm_v)]

        def fetch_ff(q):
            cols, s = pl.ds(q * UF, UF), q % 2
            return [fetch(wd.at[cols], wd_c.at[s]), fetch(gate.at[:, cols], gate_c.at[s]), fetch(up.at[:, cols], up_c.at[s]),
                    fetch(wg.at[:, cols], wg_c.at[s]), fetch(wu.at[:, cols], wu_c.at[s])]

        ff = [fetch_ff(0)]
        got_resid = fetch(resid, dres)
        for f in got:
            f.wait()
        h2_t[...] = h2_v[...].T
        for q in range(n_ff):
            s = q % 2
            if q + 1 < n_ff:
                ff.append(fetch_ff(q + 1))
            for f in ff[q]:
                f.wait()

            def act_tile(j, _):
                cols = lane(j, 256)
                g, u = gate_c[s, :, cols].astype(f32), up_c[s, :, cols].astype(f32)
                da = mm(dm_v[...], wd_c[s, lane(j, 256), :], 1, 1)
                sg = 1.0 / (1.0 + jnp.exp(-g))
                du_c[:, cols] = (da * (g * sg)).astype(bf16)
                dg_c[:, cols] = (da * u * (sg * (1.0 + g * (1.0 - sg)))).astype(bf16)
                return 0

            lax.fori_loop(0, UF // 256, act_tile, 0)
            for k, d in enumerate((dg_c, du_c)):
                while done[0] < len(units) - 1:
                    e1()

                def ff_tile(j, _):
                    y = mm(h2_t[...], d[:, lane(j, 256)], 1, 0).astype(bf16)
                    g_ff[(2 * q + k) % 4, :, :, :, :, :, lane(j, 256)] = y.reshape(g_ff.shape[1:6] + (256,))
                    return 0

                lax.fori_loop(0, UF // 256, ff_tile, 0)
                unit(1, 2 * q + k, g_ff.at[(2 * q + k) % 4], 1 + k, pl.ds(q * UF, UF)).begin()

            def hid_tile(j, _):
                cols = lane(j, 256)
                y = mm(dg_c[...], wg_c[s, cols, :], 1, 1) + mm(du_c[...], wu_c[s, cols, :], 1, 1)
                dhid[:, cols] = y if q == 0 else dhid[:, cols] + y
                return 0

            lax.fori_loop(0, W // 256, hid_tile, 0)
            tick(*PLAN[1 + q])
        while done[0] < len(units):
            e1()
        got_resid.wait()

        def second_norm(j, total):
            d, gg = norm_back(dres[block(j), :], gain2[...], dhid[block(j), :])
            d = dm_v[block(j), :].astype(f32) + d
            dres[block(j), :] = d
            drl[block(j), :] = d.astype(bf16)
            return total + gg

        g2 = lax.fori_loop(0, T // RB, second_norm, jnp.zeros((1, W), f32))
        for k in range(W // 128):
            vec[W // 128 + k:W // 128 + k + 1, :] = g2[:, k * 128:(k + 1) * 128]

    def out_grad(drl, att_c, att_t, g_out):
        pieces = [fetch(attended.at[:, pl.ds(0, QT)], att_c.at[0])]
        for i in range(A):
            if i + 1 < A:
                pieces.append(fetch(attended.at[:, pl.ds((i + 1) * QT, QT)], att_c.at[(i + 1) % 2]))
            pieces[i].wait()
            att_t[...] = att_c[i % 2].T

            def out_tile(j, _):
                y = mm(att_t[...], drl[:, lane(j, UO)], 1, 0).astype(bf16)
                g_out[j, i] = y.reshape(g_out.shape[2:])
                return 0

            lax.fori_loop(0, n_out, out_tile, 0)
        for u in range(n_out):
            unit(2, u, g_out.at[u], 3, pl.ds(u * UO, UO)).begin()
        while done[0] < len(units):
            e1()
        tick(*PLAN[7])

    def attention(drl, dq, dkr, dvl, dk, dv, ks_c, vs_c, q_c, att_c, wo_c, kr_v, v_v):
        others = [fetch(k_rot, kr_v), fetch(v, v_v)]
        pair = lambda j: lane(j, heads * HEAD_SIZE)

        def head_copies(j):
            s = j % 2
            moves = [(ks.at[:, lane(j, HEAD_SIZE)], ks_c), (vs.at[:, lane(j, HEAD_SIZE)], vs_c), (q_rot.at[pair(j), :], q_c),
                     (attended.at[:, pair(j)], att_c), (wo.at[pair(j), :], wo_c)]
            return [pltpu.make_async_copy(src, dst.at[s], hs.at[s, k]) for k, (src, dst) in enumerate(moves)]

        for q in head_copies(jnp.int32(0)):
            q.start()
        for q in others:
            q.wait()
        scale = HEAD_SIZE ** -0.5
        plus = lambda p, q: q if p is None else p + q

        def head(j, gain_grad):
            @pl.when(j + 1 < KEY_VALUE_HEADS)
            def _():
                for q in head_copies(j + 1):
                    q.start()

            for q in head_copies(j):
                q.wait()
            at = j % 2
            kl = lane(j, HEAD_SIZE)
            kb, vb_ = ks_c[at], vs_c[at]
            dkp = dvp = dks = dvs = None
            do_pair = mm(drl[...], wo_c[at], 1, 1)
            out_pair = att_c[at].astype(f32)
            for g in range(heads):
                sl = slice(g * HEAD_SIZE, (g + 1) * HEAD_SIZE)
                q = q_c[at, sl, :]
                do = do_pair[:, sl].astype(bf16)
                delta = jnp.sum((do.astype(f32) * out_pair[:, sl]).T, axis=0, keepdims=True)
                log_total = lse[j, g:g + 1, :]
                parts = []
                for suffix in range(2):
                    part = slice(rows, None) if suffix else slice(0, rows)
                    qp, dop, lp, dp = q[:, part], do[part], log_total[:, part], delta[:, part]
                    pieces = [(kb, vb_, None if suffix else past[...])]
                    if suffix:
                        pieces.append((kr_v[rows:, kl], v_v[rows:, kl], inside[...]))
                    total = None
                    for i, (kk, vv, bias) in enumerate(pieces):
                        s = mm(kk, qp, 1, 0) * (scale * LOG2E) - lp
                        p = jnp.exp2(s if bias is None else s + bias)
                        ds = (p * (mm(vv, dop, 1, 1) - dp)).astype(bf16)
                        gv, gk = mm(p.astype(bf16), dop, 1, 0), mm(ds, qp, 1, 1)
                        total = plus(total, mm(kk, ds, 0, 0))
                        if i:
                            dks, dvs = plus(dks, gk), plus(dvs, gv)
                        else:
                            dkp, dvp = plus(dkp, gk), plus(dvp, gv)
                    parts.append(total)
                d = jnp.concatenate(parts, axis=1) * scale
                m = HEAD_SIZE // 2
                cs, sn = cos[...], sin[...]
                dy = jnp.concatenate([d[:m] * cs + d[m:] * sn, d[m:] * cs - d[:m] * sn], axis=0)
                qf = q.astype(f32)
                u = jnp.concatenate([qf[:m] * cs + qf[m:] * sn, qf[m:] * cs - qf[:m] * sn], axis=0) / q_gain[:, 0:1]
                gg = dy * u
                for t in range(T // 128):
                    gain_grad = gain_grad + gg[:, t * 128:(t + 1) * 128]
                dy = dy * q_gain[:, 0:1]
                dx = rs_q[j, g:g + 1, :] * (dy - u * jnp.mean(dy * u, axis=0, keepdims=True))
                dq[:, lane(j * heads + g, HEAD_SIZE)] = dx.T.astype(bf16)
            dk[:, :, :, kl] = (dkp * scale).astype(bf16).reshape(half, 2, rows, HEAD_SIZE)
            dv[:, :, :, kl] = dvp.astype(bf16).reshape(half, 2, rows, HEAD_SIZE)
            dkr[rows:, kl] = dks * scale
            dvl[rows:, kl] = dvs.astype(bf16)
            for k in range(KEY_VALUE_HEADS - 1):
                if PLAN[8 + k][0]:
                    pl.when(j == k)(partial(tick, *PLAN[8 + k]))
            return gain_grad

        gain_grad = lax.fori_loop(0, KEY_VALUE_HEADS, head, jnp.zeros((HEAD_SIZE, 128), f32))
        vec[2 * W // 128:2 * W // 128 + 1, :] = jnp.sum(gain_grad.T, axis=0, keepdims=True)
        grads = [dk, dv]
        home = lambda s, c: (rep, (first + s) * 2 + c)

        def to_sibling(i, d):
            return remote(grads[i].at[(slot + d) % half, 1 - c], r1.at[i, d], gs.at[i, d], gr.at[i, d], home(slot, 1 - c))

        order = list(range(1, half)) + [0]
        for d in order:
            for i in range(2):
                to_sibling(i, d).start()
        for d in order:
            for i in range(2):
                to_sibling(i, d).wait_recv()

                def one(j, _):
                    r1[i, d, block(j)] = (grads[i][(slot + d) % half, c, block(j)].astype(f32) + r1[i, d, block(j)].astype(f32)).astype(bf16)
                    return 0

                lax.fori_loop(0, rows // RB, one, 0)
                if d:
                    across(i, d).start()
        for d in order:
            for i in range(2):
                to_sibling(i, d).wait_send()
        tick(*PLAN[15])

    def across(i, d):
        return remote(r1.at[i, d], r2.at[i, d - 1], fs.at[i, d - 1], fr.at[i, d - 1], (rep, (first + (slot + d) % half) * 2 + c))

    def weights_back(dq, dkr, dvl, wq_c, wk_c, wv_c, hid_v, hid_t, kp_v, dkl, g_qkv, dhid):
        got = [fetch(hidden, hid_v), fetch(k_pre, kp_v)]
        tiles = W // 256
        fetch_q = lambda j: fetch(wq.at[pl.ds(j * 256, 256)], wq_c.at[j % 2])
        fetch_kv = lambda j, s: [fetch(wk.at[pl.ds(j * 256, 256)], wk_c.at[s]), fetch(wv.at[pl.ds(j * 256, 256)], wv_c.at[s])]
        q_tiles, kv_tiles = [fetch_q(0), fetch_q(1)], [fetch_kv(0, 0), fetch_kv(1, 1)]
        got[0].wait()
        hid_t[...] = hid_v[...].T
        got_x = fetch(x, hid_v)
        count = [0]
        first_ff = n_down
        while done[2] < first_ff + (QW + 2 * KW) // UF:
            tick()
        for f in units[first_ff:first_ff + (QW + 2 * KW) // UF]:
            f.sent(2)
        pl.semaphore_signal(free, inc=1, device_id=(rep, rank(a, b, 1 - c)), device_id_type=MESH)
        pl.semaphore_wait(free, 1)

        def grad_unit(d, out, cols):
            k = count[0]
            count[0] += 1
            start = cols * UF

            def tile(j, _):
                y = mm(hid_t[...], d[:, pl.ds(pl.multiple_of(start + j * 256, 256), 256)], 1, 0).astype(bf16)
                g_qkv[k % 4, :, :, :, :, :, lane(j, 256)] = y.reshape(g_qkv.shape[1:6] + (256,))
                return 0

            lax.fori_loop(0, UF // 256, tile, 0)
            unit(1, 2 * n_ff + k, g_qkv.at[k % 4], out, pl.ds(start, UF), k).begin()

        for u in range(QW // UF):
            grad_unit(dq, 4, u)
        for u in range(QW // UF):
            e1()
        tick(*PLAN[16])
        got[1].wait()

        def key_head(part, j, total):
            lanes = lane(j, HEAD_SIZE)
            y = kp_v[part, lanes]
            r = lax.rsqrt(jnp.mean(y * y, axis=-1, keepdims=True) + norm_epsilon)
            u = y * r
            dy = dkr[part, lanes]
            dy = dy * cos_r[part, :] - pltpu.roll(dy, HEAD_SIZE // 2, 1) * sin_r[part, :]
            total = total + jnp.sum(dy * u, axis=0, keepdims=True)
            dy = dy * k_gain[...]
            dkl[part, lanes] = (r * (dy - u * jnp.mean(dy * u, axis=-1, keepdims=True))).astype(bf16)
            return total

        def first_norm(j, carry):
            total, square = carry
            d, gg = norm_back(hid_v[block(j), :].astype(f32), gain1[...], dhid[block(j), :])
            d = dres[block(j), :] + d
            dres[block(j), :] = d
            return total + gg, square + jnp.sum(valid[block(j), :] * d * d, axis=0, keepdims=True)

        ours, theirs = pl.ds(rows, T - rows), pl.ds(0, rows)
        gk = lax.fori_loop(0, KEY_VALUE_HEADS, partial(key_head, ours), jnp.zeros((1, HEAD_SIZE), f32))
        for j in range(tiles):
            cols = pl.ds(j * 256, 256)
            q_tiles[j].wait()
            for f in kv_tiles[j]:
                f.wait()
            dhid[:, cols] = mm(dq[...], wq_c[j % 2], 1, 1)
            dhid[ours, cols] += mm(dkl[ours, :], wk_c[j % 2], 1, 1) + mm(dvl[ours, :], wv_c[j % 2], 1, 1)
            if j + 2 < tiles:
                q_tiles.append(fetch_q(j + 2))
            kv_tiles.append(fetch_kv((j + 2) % tiles, j % 2))
        got_x.wait()
        zero = jnp.zeros((1, W), f32)
        g1, square = lax.fori_loop(rows // RB, T // RB, first_norm, (zero, zero))
        width = CONTINUATION_LEN // n
        step = max(width, 8)

        def pack(j, _):
            y = dres[pl.ds(pl.multiple_of(rows + j * step, step), step), :].astype(bf16)
            for k in range(step // width):
                i = j * (step // width) + k
                grad_src[i // n, i % n] = y[k * width:(k + 1) * width]
            return 0

        lax.fori_loop(0, S * CONTINUATION_LEN // step, pack, 0)
        begin_all(grad_spread)
        tick(*PLAN[17])
        for i in range(2):
            for d in range(1, half):
                across(i, d).wait_recv()

        def own_keys(j, _):
            t, u = r1[0, 0, block(j)].astype(f32), r1[1, 0, block(j)].astype(f32)
            for d in range(1, half):
                t, u = t + r2[0, d - 1, block(j)].astype(f32), u + r2[1, d - 1, block(j)].astype(f32)
            dkr[block(j), :] = t
            dvl[block(j), :] = u.astype(bf16)
            return 0

        lax.fori_loop(0, rows // RB, own_keys, 0)
        for u in range(KW // UF):
            grad_unit(dvl, 6, u)
        gk = lax.fori_loop(0, KEY_VALUE_HEADS, partial(key_head, theirs), gk)
        vec[2 * W // 128 + 1:2 * W // 128 + 2, :] = gk
        for u in range(KW // UF):
            grad_unit(dkl, 5, u)
        while done[0] < len(units):
            e1()
        tick(*PLAN[18])
        wait_all(grad_spread)
        reorder(grad_in, turned)
        begin_all(grad_collect)
        for j in range(tiles):
            cols, s = pl.ds(j * 256, 256), (tiles + j) % 2
            for f in kv_tiles[tiles + j]:
                f.wait()
            dhid[theirs, cols] += mm(dkl[theirs, :], wk_c[s], 1, 1) + mm(dvl[theirs, :], wv_c[s], 1, 1)
            if j + 2 < tiles:
                kv_tiles.append(fetch_kv(j + 2, s))
        tick(*PLAN[19])
        g1, square = lax.fori_loop(0, rows // RB, first_norm, (g1, square))
        for k in range(W // 128):
            vec[k:k + 1, :] = g1[:, k * 128:(k + 1) * 128]
        place = lax.broadcasted_iota(jnp.int32, (1, 128), 1)
        row = jnp.zeros((1, 128), f32)
        whole = lambda y: jnp.sum(jnp.sum(y, axis=0, keepdims=True), axis=1, keepdims=True)
        for k, y in enumerate((sums[0:1, :], sums[1:2, :], square, valid[...])):
            row = jnp.where(place == k, whole(y), row)
        vec[2 * W // 128 + 2:2 * W // 128 + 3, :] = row
        vec[2 * W // 128 + 3:, :] = jnp.zeros((vec.shape[0] - 2 * W // 128 - 3, 128), f32)

    pl.run_scoped(persistent, V((T, QW), bf16), V((T, KW), f32), V((T, KW), bf16))
    for i in range(2):
        for d in range(1, half):
            across(i, d).wait_send()

    prompt_out = fetch(dres.at[pl.ds(0, rows)], d_prompt)
    tick(2, 1)
    rounds = [(rep, rank(a, b, 1 - c)), (rep, rank(a, 1 - b, c))] + [flip(k) for k in range(bits)]
    vb[0] = vec[...]
    for k, to in enumerate(rounds):
        q = remote(vb.at[2 * k], vb.at[2 * k + 1], vs_.at[k], vr_.at[k], to)
        q.start()
        q.wait()
        vb[2 * k + 2] = vb[2 * k] + vb[2 * k + 1]
        tick(2, 1)
    last, nr = 2 * len(rounds), len(rounds)
    zs = [remote(vb.at[last], vz.at[a], vs_.at[nr + d - 1], vr_.at[nr + d - 1], (rep, rank((a + d) % A, b, c))) for d in range(1, A)]
    for q in zs:
        q.start()
    vz[a] = vb[last]
    for q in zs:
        q.wait()
    total = vz[0]
    for k in range(1, A):
        total = total + vz[k]
    vec[...] = total
    while done[5] < len(units):
        tick(lag=1)
    wait_all(grad_collect)
    prompt_out.wait()
    for f in units:
        f.end()


def backward(index, mixed, dm, h2, act, gate, up, resid, wd, wg, wu, wo, attended, q_rot, lse, rs_q, ks, vs, k_rot, v, k_pre, wq, wk, wv, hidden, x,
             k_gain, q_gain, cos_r, sin_r, cos, sin, past, inside, valid, gain1, gain2, sums, rows, n, R, cid):
    group = PROMPT_LENGTH // rows
    half, A, (T, W), bits = group // 2, n // 4, dm.shape, R.bit_length() - 1
    FW, QW, KW = act.shape[1], attended.shape[1], k_rot.shape[1]
    UD, UF, UO = 256, 512, 512
    S = mixed.shape[0]
    V, D = pltpu.VMEM, pltpu.SemaphoreType.DMA
    shape = jax.ShapeDtypeStruct
    vm, hbm, sm = pl.BlockSpec(memory_space=pltpu.VMEM), pl.BlockSpec(memory_space=pl.ANY), pl.BlockSpec(memory_space=pltpu.SMEM)
    rh = lambda w: w.shape[0] // (2 * n)
    out_shape = [shape((2, rh(w), w.shape[1]), bf16) for w in (wd, wg, wu, wo, wq, wk, wv)]
    vec_rows = 2 * W // 128 + 8
    out_shape += [shape((vec_rows, 128), f32), shape((rows, W), f32), shape(mixed.shape, bf16), shape(mixed.shape, bf16)]
    scratch = []
    for count, r, w in ((W // UD, rh(wd), UD), (2 * (FW // UF) + (QW + 2 * KW) // UF, rh(wg), UF), (W // UO, rh(wo), UO)):
        k0 = fold_split(r)
        k1 = max(r - k0, 8)
        landing = 2 * (FW // UF) if w == UF and r == rh(wg) else count
        scratch += [V((landing, A, 2, 2, r, w), bf16), V((count, A, 2, k0, w), bf16), V((count, A, 2, k1, w) if k0 < r else (1, 1, 1, 8, 128), bf16), V((count, A, r, w), bf16),
                    V((count, A - 1, r, w), bf16), V((count, bits, r, w), bf16), V((count, bits, r, w), bf16)]
    m = W // UD + 2 * (FW // UF) + (QW + 2 * KW) // UF + W // UO
    turned = (n, S) + mixed.shape[2:]
    kv = (2, half, rows, KW)
    scratch += [V(kv, bf16), V((2, max(half - 1, 1), rows, KW), bf16), V(turned, bf16), V(turned, bf16), V(mixed.shape, bf16), V(turned, bf16),
                V((2 * (2 + bits) + 1, vec_rows, 128), f32), V((A, vec_rows, 128), f32), V((T, W), f32)]
    scratch += [D((m,)), D((m,)), D((m, 2)), D((m, 2)), D((m, 2)), D((m, 2)), D((m, A - 1)), D((m, A - 1)), D((m, bits)), D((m, bits)), D((m, 2))]
    scratch += [D((2 * A + 5 * (FW // UF) + 32,)), D((2, 5)), D((2, half)), D((2, half)), D((2, max(half - 1, 1))), D((2, max(half - 1, 1))), D((4, n - 1)), D((4, n - 1)), D((4,)),
                D((2 + bits + A - 1,)), D((2 + bits + A - 1,)), pltpu.SemaphoreType.REGULAR]
    hbm_in = [mixed, dm, h2, act, gate, up, resid, wd, wg, wu, wo, attended, q_rot, lse, rs_q, ks, vs, k_rot, v, k_pre, wq, wk, wv, hidden, x]
    in_vmem = {13, 14}
    res = pl.pallas_call(
        partial(backward_kernel, n, R, group, UD, UF, UO),
        out_shape=out_shape,
        in_specs=[sm] + [vm if k in in_vmem else hbm for k in range(len(hbm_in))] + [vm] * 12,
        out_specs=[hbm] * 7 + [vm] + [hbm] * 3,
        scratch_shapes=scratch,
        compiler_params=pltpu.CompilerParams(collective_id=cid, has_side_effects=True, vmem_limit_bytes=63 << 20),
        name="backward",
    )(index, *hbm_in, k_gain, q_gain, cos_r, sin_r, cos, sin, past, inside, valid, gain1, gain2, sums)
    return [r.reshape(-1, r.shape[-1]) for r in res[:7]], res[7], res[8], res[9], res[10]


def per_device(
    prompt_rows,
    suffix_rows,
    assignment,
    lengths,
    attention_gain,
    query_weight,
    key_matrix,
    value_matrix,
    query_gain,
    key_norm_gain,
    out_weight,
    mlp_gain,
    gate_weight,
    up_weight,
    down_weight,
    prompt_cotangent,
    suffix_cotangent,
):
    n, R = lax.axis_size("fsdp"), lax.axis_size("rep")
    rank = lax.axis_index("fsdp")
    rows = prompt_rows.shape[0]
    suffix = suffix_rows.shape[0]
    S = suffix // CONTINUATION_LEN
    total = rows + suffix
    width = MODEL_WIDTH

    pad = lambda v: jnp.pad(v.astype(f32).reshape(-1), (0, 128 - v.size))
    tile = jnp.stack([pad(v) for v in (attention_gain, mlp_gain, query_gain, key_norm_gain, assignment, lengths)])
    tile = jnp.pad(tile, ((0, 2), (0, 0)))
    cut = lambda v: v.reshape(S, n, CONTINUATION_LEN // n, width)
    w_key, w_value, w_query, tiles, staged = gather(key_matrix, value_matrix, query_weight, tile, cut(suffix_rows), n, 0)
    gain_first = tiles[:, 0, : attention_gain.size].reshape(-1)
    gain_second = tiles[:, 1, : mlp_gain.size].reshape(-1)
    query_scale = tiles[:, 2, : query_gain.size].reshape(-1)
    key_scale = tiles[:, 3, : key_norm_gain.size].reshape(-1)

    owner = tiles[:, 4, :S].reshape(-1).astype(jnp.int32) // CONT
    slot_count = n * S
    ids = jnp.arange(slot_count, dtype=jnp.int32)
    ahead = (owner[None, :] < owner[:, None]) | ((owner[None, :] == owner[:, None]) & (ids[None, :] < ids[:, None]))
    place = jnp.sum(ahead.astype(jnp.int32), axis=1)
    hits = place[None, :] == ids[:, None]
    order = jnp.sum(jnp.where(hits, ids[None, :], 0), axis=1)
    slot_lengths = jnp.sum(jnp.where(hits, tiles[:, 5, :S].reshape(-1).astype(jnp.int32)[None, :], 0), axis=1)
    own_lengths = lax.dynamic_slice_in_dim(slot_lengths, rank * S, S)

    prompt_place = (rank * rows) % PROMPT_LENGTH + jnp.arange(rows, dtype=jnp.int32)
    suffix_place = jnp.arange(suffix, dtype=jnp.int32) % CONTINUATION_LEN
    suffix_slot = jnp.arange(suffix, dtype=jnp.int32) // CONTINUATION_LEN
    length_rows = jnp.repeat(own_lengths, CONTINUATION_LEN)
    suffix_valid = suffix_place < length_rows
    valid_rows = jnp.concatenate([jnp.ones((rows,), f32), suffix_valid.astype(f32)])
    token_positions = jnp.concatenate([prompt_place, PROMPT_LENGTH + suffix_place]).astype(f32)
    half = HEAD_SIZE // 2
    inverse = rope_theta ** (jnp.arange(half, dtype=f32) * (-2.0 / HEAD_SIZE))
    angles_t = inverse[:, None] * token_positions[None, :]
    cos_t, sin_t = jnp.cos(angles_t), jnp.sin(angles_t)
    cos_r, sin_r = cos_t.T, sin_t.T
    cos_rows = jnp.concatenate([cos_r, cos_r], axis=1)
    sin_rows = jnp.concatenate([-sin_r, sin_r], axis=1)
    past = jnp.where(jnp.arange(PROMPT_LENGTH, dtype=jnp.int32)[:, None] <= prompt_place[None, :], 0.0, masked_score).astype(f32)
    inside = jnp.where(
        (suffix_slot[:, None] == suffix_slot[None, :]) & (suffix_place[:, None] <= suffix_place[None, :]) & suffix_valid[:, None], 0.0, masked_score
    ).astype(f32)

    key_gain_row = key_scale.reshape(1, HEAD_SIZE)
    query_gain_col = jnp.broadcast_to(query_scale[:, None], (HEAD_SIZE, 128))
    (
        w_out, w_gate, w_up, w_down, moved_cotangent, gate_low, up_low, rows_low, hidden, attended, query_rot, key_pre, key_rot, values,
        prompt_keys, prompt_values, residual, hidden_two, act, mixed_low, lse, query_rs, sums,
    ) = forward(
        order, prompt_rows, staged, cut(suffix_cotangent), w_key, w_value, w_query, [out_weight, gate_weight, up_weight, down_weight], key_gain_row,
        query_gain_col, cos_rows, sin_rows, cos_t, sin_t, past, inside, valid_rows[:, None], gain_first[None, :], gain_second[None, :], n, 2,
    )
    moved_cotangent = moved_cotangent.reshape(suffix, width)
    d_mixed_low = jnp.concatenate([prompt_cotangent, moved_cotangent], 0) * valid_rows[:, None].astype(bf16)
    shards, vec_sum, prompt_grad, suffix_mixed, suffix_grad = backward(
        place, cut(mixed_low[rows:]), d_mixed_low, hidden_two, act, gate_low, up_low, residual, w_down, w_gate, w_up, w_out, attended, query_rot, lse, query_rs,
        prompt_keys, prompt_values, key_rot, values, key_pre, w_query, w_key, w_value, hidden, rows_low, key_gain_row, query_gain_col,
        cos_rows, sin_rows, cos_t, sin_t, past, inside, valid_rows[:, None], gain_first[None, :], gain_second[None, :], sums, rows, n, R, 3,
    )
    suffix_mixed, suffix_grad = suffix_mixed.reshape(suffix, width), suffix_grad.reshape(suffix, width)
    g_down, g_gate, g_up, g_out, g_query, g_key, g_value = [g.astype(f32) for g in shards]
    flat = vec_sum.reshape(-1)

    def mine(first, size, part):
        return lax.dynamic_slice_in_dim(flat[first : first + size], rank * part, part)

    g_first = mine(0, width, attention_gain.size)
    g_second = mine(width, width, mlp_gain.size)
    g_query_gain = mine(2 * width, HEAD_SIZE, query_gain.size)
    g_key_gain = mine(2 * width + HEAD_SIZE, HEAD_SIZE, key_norm_gain.size)
    stat_sums = flat[2 * width + 2 * HEAD_SIZE : 2 * width + 2 * HEAD_SIZE + 4]
    token_norms = jnp.sqrt(stat_sums[:3] / (stat_sums[3] * width))
    return (
        mixed_low[:rows],
        suffix_mixed,
        prompt_grad,
        suffix_grad.astype(f32),
        g_first,
        g_query,
        g_key,
        g_value,
        g_query_gain,
        g_key_gain,
        g_out,
        g_second,
        g_gate,
        g_up,
        g_down,
        token_norms,
    )


def solution(mesh):
    placed = (
        P(("rep", "fsdp"), None),
        P(("rep", "fsdp"), None),
        P("rep", "fsdp"),
        P("rep", "fsdp"),
        P("fsdp"),
        P("fsdp", None),
        P("fsdp", None),
        P("fsdp", None),
        P("fsdp"),
        P("fsdp"),
        P("fsdp", None),
        P("fsdp"),
        P("fsdp", None),
        P("fsdp", None),
        P("fsdp", None),
        P(("rep", "fsdp"), None),
        P(("rep", "fsdp"), None),
    )
    return jax.shard_map(
        per_device,
        mesh=mesh,
        in_specs=placed,
        out_specs=(
            P(("rep", "fsdp"), None),
            P(("rep", "fsdp"), None),
            P(("rep", "fsdp"), None),
            P(("rep", "fsdp"), None),
            P("fsdp"),
            P("fsdp", None),
            P("fsdp", None),
            P("fsdp", None),
            P("fsdp"),
            P("fsdp"),
            P("fsdp", None),
            P("fsdp"),
            P("fsdp", None),
            P("fsdp", None),
            P("fsdp", None),
            P(),
        ),
        check_vma=False,
    )
```

```python
from functools import partial

import jax
import jax.numpy as jnp
from jax import lax
from jax.experimental import pallas as pl
from jax.experimental.pallas import tpu as pltpu
from jax.sharding import PartitionSpec as P

MODEL_WIDTH = 1024
QUERY_HEADS = 16
KEY_VALUE_HEADS = 8
HEAD_SIZE = 128
PROMPT_LENGTH = 1024
CONT = 8
CONTINUATION_LEN = 128

norm_epsilon = 1e-06
rope_theta = 1000000.0
masked_score = -1e30
MESH = pl.DeviceIdType.MESH
bf16 = jnp.bfloat16
f32 = jnp.float32

def position(n):
    rep = lax.axis_index("rep")
    rank = lax.axis_index("fsdp")
    return rep, rank // 4, (rank // 2) % 2, rank % 2


def meet(peers):
    barrier = pltpu.get_barrier_semaphore()
    for p in peers:
        pl.semaphore_signal(barrier, inc=1, device_id=p, device_id_type=MESH)
    pl.semaphore_wait(barrier, len(peers))


def remote(src, dst, send, recv, to):
    return pltpu.make_async_remote_copy(src, dst, send, recv, device_id=to, device_id_type=MESH)


def add_rows(count, out, first, second, step=None):
    def one(j, _):
        o = out(j)
        total = first(j)[...].astype(jnp.float32)
        for s in second:
            total = total + s(j)[...].astype(jnp.float32)
        o[...] = total.astype(o.dtype)
        return 0
    lax.fori_loop(0, count, one, 0)


LOG2E = 1.4426950408889634


def mm(x, y, cx, cy):
    return lax.dot_general(x, y, (((cx,), (cy,)), ((), ())), preferred_element_type=f32)


class Ring:
    def __init__(self, n, own, full, cols, sems, i, x_first):
        zs, zr, ss, sr, ls = sems
        A = n // 4
        rep, a, b, c = position(n)
        h = rep % 2
        every = slice(None)
        at = lambda *ix: full.at[(*ix, every, cols)]
        rank = lambda a, b, c: (a * 2 + b) * 2 + c
        ydev, xdev, cdev = (rep, rank(a, 1 - b, c)), (rep + 1 - 2 * h, rank(a, b, c)), (rep, rank(a, b, 1 - c))
        same = lambda ref, k, to: remote(ref, ref, ss.at[i, k], sr.at[i, k], to)
        mine = own.at[h, :, cols]
        self.local = lambda: [pltpu.make_async_copy(mine, at(a, b, c, h), ls.at[i])]
        self.along = lambda: [remote(mine, at(a, b, c, h), zs.at[i, d - 1], zr.at[i, d - 1], (rep, rank((a + d) % A, b, c))) for d in range(1, A)]
        self.second = lambda: [same(at(every, b, c, h), 0, xdev if x_first else ydev)]
        self.third = lambda: [same(at(every, b, c, every), 1, ydev) if x_first else same(at(every, every, c, h), 1, xdev)]
        self.last = lambda: [same(at(every, every, c, every), 2, cdev)]

    def begin(self):
        for q in self.local() + self.along():
            q.start()

    def turn(self, arrived, started):
        for q in arrived():
            q.wait_recv()
        for q in started():
            q.start()

    def step(self, k):
        if k == 0:
            for q in self.local():
                q.wait()
            self.turn(self.along, self.second)
        elif k == 1:
            self.turn(self.second, self.third)
        elif k == 2:
            self.turn(self.third, self.last)
        else:
            for q in self.last():
                q.wait_recv()

    def end(self):
        for q in self.along() + self.second() + self.third() + self.last():
            q.wait_send()


class Ticker:
    def __init__(self, rings, arrived=lambda i: None):
        self.rings, self.arrived, self.done, self.noted = rings, arrived, [0] * 5, None

    def run(self, f):
        f() if self.noted is None else self.noted.append(f)

    def note(self, f):
        self.noted = []
        f()
        noted, self.noted = self.noted, None
        return noted

    def begin(self, count):
        for r in self.rings[self.done[0]:self.done[0] + max(count, 0)]:
            self.run(r.begin)
            self.done[0] += 1

    def __call__(self, count=1, lag=1):
        for _ in range(count):
            before = list(self.done)
            for k in range(1, 5):
                i = self.done[k]
                if i < len(self.rings) and before[k - 1] - i >= lag:
                    self.run(partial(self.rings[i].step, k - 1))
                    self.done[k] += 1
                    if k == 1:
                        self.begin(self.done[1] + ALONG - self.done[0])
                    if k == 4:
                        self.arrived(i)

    def until(self, count):
        while self.done[4] < count:
            before = list(self.done)
            self(1, 2)
            if before == self.done:
                self()


ALONG = 2


def slot_spread(n, src, dst, sems, k, where):
    s, r, l = sems
    rep, me = where
    own = pltpu.make_async_copy(src.at[:, me], dst.at[me], l.at[k])
    return own, [remote(src.at[:, (me + d) % n], dst.at[me], s.at[k, d - 1], r.at[k, d - 1], (rep, (me + d) % n)) for d in range(1, n)]


def slot_collect(n, src, dst, sems, k, where):
    s, r, l = sems
    rep, me = where
    own = pltpu.make_async_copy(src.at[me], dst.at[:, me], l.at[k])
    return own, [remote(src.at[(me + d) % n], dst.at[:, me], s.at[k, d - 1], r.at[k, d - 1], (rep, (me + d) % n)) for d in range(1, n)]


def begin_all(pair):
    pair[0].start()
    for q in pair[1]:
        q.start()


def wait_all(pair):
    pair[0].wait()
    for q in pair[1]:
        q.wait()


def gather_kernel(n, CB, *refs):
    so, sk, sv, tile, pieces, wq, wk, wv, tiles, staged, zs, zr, ss, sr, ls, ts, tr, ps, pr, pls = refs
    rep, a, b, c = position(n)
    me = (a * 2 + b) * 2 + c
    h = rep % 2
    meet([(rep, (me + d) % n) for d in range(1, n)] + [(rep + 1 - 2 * h, me)])
    blocks = []
    for own, full in ((sk, wk), (sv, wv), (so, wq)):
        blocks += [(own, full, pl.ds(q * CB, CB)) for q in range(full.shape[-1] // CB)]
    rings = [Ring(n, own, full, cols, (zs, zr, ss, sr, ls), i, i % 2 == 0) for i, (own, full, cols) in enumerate(blocks)]
    tick = Ticker(rings)
    share = [remote(tile, tiles.at[me], ts.at[d - 1], tr.at[d - 1], (rep, (me + d) % n)) for d in range(1, n)]
    rows = slot_spread(n, pieces, staged, (ps, pr, pls), 0, (rep, me))
    for q in share:
        q.start()
    tiles[me] = tile[...]
    tick.begin(ALONG)
    begin_all(rows)
    tick.until(len(rings))
    for q in share:
        q.wait()
    wait_all(rows)
    for r in rings:
        r.end()


def gather(wk, wv, wq, tile, slots, n, cid):
    A, CB = n // 4, 512
    halves = [w.reshape(2, w.shape[0] // 2, w.shape[1]) for w in (wq, wk, wv)]
    m = sum(w.shape[1] for w in (wk, wv, wq)) // CB
    D = pltpu.SemaphoreType.DMA
    vm, hbm = pl.BlockSpec(memory_space=pltpu.VMEM), pl.BlockSpec(memory_space=pl.ANY)
    shape = jax.ShapeDtypeStruct
    res = pl.pallas_call(
        partial(gather_kernel, n, CB),
        out_shape=[shape((A, 2, 2) + w.shape, bf16) for w in halves] + [shape((n,) + tile.shape, f32), shape((n, slots.shape[0]) + slots.shape[2:], bf16)],
        in_specs=[hbm] * 3 + [vm] + [hbm],
        out_specs=[hbm] * 3 + [vm, hbm],
        scratch_shapes=[D((m, A - 1))] * 2 + [D((m, 3))] * 2 + [D((m,))] + [D((n - 1,))] * 2 + [D((1, n - 1))] * 2 + [D((1,))],
        compiler_params=pltpu.CompilerParams(collective_id=cid, has_side_effects=True),
        name="gather",
    )(*halves, tile, slots)
    w_query, w_key, w_value = [f.reshape(-1, f.shape[-1]) for f in res[:3]]
    return w_key, w_value, w_query, res[3], res[4]


def forward_kernel(n, group, *refs):
    it = iter(refs)
    take = lambda count: [next(it) for _ in range(count)]
    index, prompt, staged, cot, wk_h, wv_h, wq_h, so, sg, su, sd, k_gain, q_gain, cos_r, sin_r, cos, sin, past, inside, valid, gain1, gain2 = take(22)
    wo, wg, wu, wd, moved, gate, up = take(7)
    outs = take(13)
    lse_out, rs_out, stats = take(3)
    x, hidden, attended, q_out, k_pre, k_out, v, ks, vs, resid, h2, act, mixed = bufs = take(13)
    wk, wv, wq, ordered, landed, cot_in, o_buf, g_buf, u_buf, d_buf, g_st, u_st = take(12)
    zs, zr, ss, sr, ls, lds, fs, fr, gs, gr, kls, ps, pr, pls, gos, outs_sem, ins_sem = take(17)
    rows = ks.shape[2]
    T, W = x.shape
    half = group // 2
    rep, a, b, c = position(n)
    me = (a * 2 + b) * 2 + c
    first, slot = (me // group) * half, (me // 2) % half
    h = rep % 2
    ins = [pltpu.make_async_copy(src, dst, ins_sem.at[k]) for k, (src, dst) in enumerate(((wk_h, wk), (wv_h, wv), (wq_h, wq)))]
    for q in ins:
        q.start()
    meet([(rep, (me + d) % n) for d in range(1, n)] + [(rep + 1 - 2 * h, me)])
    saves = {id(buf): pltpu.make_async_copy(buf, out, outs_sem.at[k]) for k, (buf, out) in enumerate(zip(bufs, outs))}

    def save(*which):
        for buf in which:
            saves[id(buf)].start()

    OB, GB = o_buf.shape[-1], g_buf.shape[-1]
    n_out, n_mlp = wo.shape[-1] // OB, wg.shape[-1] // GB
    blocks = [(so, wo, pl.ds(q * OB, OB), o_buf.at[q]) for q in range(n_out)]
    for q in range(n_mlp):
        blocks += [(sg, wg, pl.ds(q * GB, GB), g_buf.at[q % 2]), (su, wu, pl.ds(q * GB, GB), u_buf.at[q % 2])]
    blocks += [(sd, wd, pl.ds(q * OB, OB), d_buf.at[q]) for q in range(n_out)]
    m = len(blocks)
    rings = [Ring(n, own, full, cols, (zs, zr, ss, sr, ls), i, i % 2 == 0) for i, (own, full, cols, _) in enumerate(blocks)]

    def load(i):
        _, full, cols, buf = blocks[i]
        return pltpu.make_async_copy(full.at[:, :, :, :, :, cols], buf, lds.at[i])

    used, late = [0], []

    def arrived(i):
        q = (i - n_out) // 2 if n_out <= i < n_out + 2 * n_mlp else 0
        if q < used[0] + 2:
            tick.run(lambda: load(i).start())
        else:
            late.append(i)

    def release():
        used[0] += 1
        now, late[:] = [i for i in late if (i - n_out) // 2 < used[0] + 2], [i for i in late if (i - n_out) // 2 >= used[0] + 2]
        for i in now:
            tick.run(lambda i=i: load(i).start())

    tick = Ticker(rings, arrived)
    S = ordered.shape[1]

    def reorder(src, flat):
        def put(j, _):
            s = index[j]
            ordered[j // S, j % S] = src[s] if flat else src[s // S, s % S]
            return 0

        lax.fori_loop(0, n * S, put, 0)

    sems = (ps, pr, pls)
    reorder(staged, True)
    rows_in = slot_collect(n, ordered, landed, sems, 0, (rep, me))
    cot_spread = slot_spread(n, cot, cot_in, sems, 1, (rep, me))
    cot_collect = slot_collect(n, ordered, moved, sems, 2, (rep, me))
    begin_all(rows_in)
    tick.begin(ALONG)

    lane = lambda j, w: pl.ds(pl.multiple_of(j * w, w), w)
    heads = QUERY_HEADS // KEY_VALUE_HEADS
    pair = heads * HEAD_SIZE
    RB = 32
    block = lambda j: pl.ds(pl.multiple_of(j * RB, RB), RB)

    def norm(y, gain):
        return (y * lax.rsqrt(jnp.mean(y * y, axis=-1, keepdims=True) + norm_epsilon) * gain[...]).astype(bf16)

    def prompt_rows(j, _):
        y = prompt[block(j), :]
        x[block(j), :] = y
        hidden[block(j), :] = norm(y.astype(f32), gain1)
        return 0

    def kv_tile(part, j, _):
        kp = mm(hidden[part, :], wk[:, lane(j, 256)], 1, 0)
        k_pre[part, lane(j, 256)] = kp
        for g in range(2):
            y = kp[:, g * HEAD_SIZE:(g + 1) * HEAD_SIZE]
            y = y * lax.rsqrt(jnp.mean(y * y, axis=-1, keepdims=True) + norm_epsilon) * k_gain[...]
            k_out[part, lane(2 * j + g, HEAD_SIZE)] = (y * cos_r[part, :] + pltpu.roll(y, HEAD_SIZE // 2, 1) * sin_r[part, :]).astype(bf16)
        v[part, lane(j, 256)] = mm(hidden[part, :], wv[:, lane(j, 256)], 1, 0).astype(bf16)
        return 0

    lax.fori_loop(0, rows // RB, prompt_rows, 0)
    ins[0].wait()
    ins[1].wait()
    lax.fori_loop(0, wk.shape[1] // 256, partial(kv_tile, pl.ds(0, rows)), 0)
    parts = [(k_out, ks), (v, vs)]
    at = lambda s, c: (rep, (first + s) * 2 + c)
    mine = lambda i: parts[i][0].at[pl.ds(0, rows)]
    klocal = [pltpu.make_async_copy(mine(i), parts[i][1].at[slot, c], kls.at[i]) for i in range(2)]
    across = [remote(mine(i), parts[i][1].at[slot, c], fs.at[i, d - 1], fr.at[i, d - 1], at((slot + d) % half, c)) for i in range(2) for d in range(1, half)]
    sibling = [remote(mine(i), parts[i][1].at[slot, c], gs.at[i, 0], gr.at[i, 0], at(slot, 1 - c)) for i in range(2)]
    onward = []
    for i in range(2):
        for d in range(1, half):
            there = parts[i][1].at[(slot + half - d) % half, c]
            onward.append(remote(there, there, gs.at[i, d], gr.at[i, d], at(slot, 1 - c)))
    for q in across + sibling + klocal:
        q.start()
    tick()
    wait_all(rows_in)
    width = landed.shape[2]

    def slot_rows(j, _):
        s, p = j // (n * width // RB), j % (n * width // RB)
        k = RB // width
        if width % 8 == 0:
            y = landed[s, pl.ds(p * k, k)].astype(f32).reshape(RB, W)
        else:
            y = jnp.concatenate([landed[s, p * k + i].astype(f32) for i in range(k)], axis=0)
        at = pl.ds(pl.multiple_of(rows + j * RB, RB), RB)
        x[at, :] = y.astype(bf16)
        hidden[at, :] = norm(y, gain1)
        return 0

    lax.fori_loop(0, (T - rows) // RB, slot_rows, 0)
    lax.fori_loop(0, wk.shape[1] // 256, partial(kv_tile, pl.ds(rows, T - rows)), 0)
    tick()
    save(x, hidden, k_pre, k_out, v)
    ins[2].wait()

    def q_tile(j, _):
        qp = mm(hidden[...], wq[:, lane(j, pair)], 1, 0)
        for g in range(heads):
            y = qp[:, g * HEAD_SIZE:(g + 1) * HEAD_SIZE].T
            rs = lax.rsqrt(jnp.mean(y * y, axis=0, keepdims=True) + norm_epsilon)
            rs_out[j, g:g + 1, :] = rs
            y = y * rs * q_gain[:, 0:1]
            lo, hi = y[:HEAD_SIZE // 2], y[HEAD_SIZE // 2:]
            y = jnp.concatenate([lo * cos[...] - hi * sin[...], hi * cos[...] + lo * sin[...]], axis=0)
            q_out[lane(j * heads + g, HEAD_SIZE), :] = y.astype(bf16)
        for k, plan in FORWARD_PLAN[0]:
            pl.when(j == k)(partial(tick, *plan))
        return 0

    lax.fori_loop(0, KEY_VALUE_HEADS, q_tile, 0)
    begin_all(cot_spread)
    save(q_out)
    for q in across:
        q.wait_recv()
    for q in onward:
        q.start()
    tick(*FORWARD_PLAN[1])
    for q in klocal:
        q.wait()
    for q in sibling + onward:
        q.wait_recv()
    save(ks, vs)
    scale = HEAD_SIZE ** -0.5 * LOG2E

    def attend_head(j, _):
        kl = lane(j, HEAD_SIZE)
        kb = ks[:, :, :, kl].reshape(PROMPT_LENGTH, HEAD_SIZE)
        vb = vs[:, :, :, kl].reshape(PROMPT_LENGTH, HEAD_SIZE)
        for g in range(heads):
            ql = lane(j * heads + g, HEAD_SIZE)
            q = q_out[ql, :]
            p = jnp.exp2(mm(kb, q[:, :rows], 1, 0) * scale + past[...])
            total = jnp.sum(p, axis=0, keepdims=True)
            o = mm(vb, p.astype(bf16), 0, 0) / total
            attended[:rows, ql] = o.T.astype(bf16)
            lse_out[j, g:g + 1, :rows] = jnp.log2(total)
            p = jnp.exp2(mm(kb, q[:, rows:], 1, 0) * scale)
            r = jnp.exp2(mm(k_out[rows:, kl], q[:, rows:], 1, 0) * scale + inside[...])
            total = jnp.sum(p, axis=0, keepdims=True) + jnp.sum(r, axis=0, keepdims=True)
            o = (mm(vb, p.astype(bf16), 0, 0) + mm(v[rows:, kl], r.astype(bf16), 0, 0)) / total
            attended[rows:, ql] = o.T.astype(bf16)
            lse_out[j, g:g + 1, rows:] = jnp.log2(total)
        for k, plan in FORWARD_PLAN[2]:
            pl.when(j == k)(partial(tick, *plan))
        return 0

    lax.fori_loop(0, KEY_VALUE_HEADS, attend_head, 0)
    save(attended)
    wait_all(cot_spread)
    reorder(cot_in, False)
    begin_all(cot_collect)

    stats[...] = jnp.zeros_like(stats)

    def at_block(q, noted):
        for k, fs_ in enumerate(noted):
            if fs_:
                pl.when(q == k)(lambda fs_=fs_: [f() for f in fs_] and None)

    def arrived_block(q, first, full, width, buf):
        pltpu.make_async_copy(full.at[:, :, :, :, :, lane(q, width)], buf, lds.at[first]).wait()

    before_out = [tick.note(partial(tick.until, k + 1)) for k in range(n_out)]

    def out_block(q, _):
        at_block(q, before_out)
        arrived_block(q, q, wo, OB, o_buf.at[q])
        cols = lane(q, OB)
        y = x[:, cols].astype(f32) + mm(attended[...], o_buf[q].reshape(-1, OB), 1, 0)
        resid[:, cols] = y
        stats[1:2, :] += jnp.sum(valid[...] * y * y, axis=0, keepdims=True)
        return 0

    lax.fori_loop(0, n_out, out_block, 0)

    def norm_rows(j, _):
        h2[block(j), :] = norm(resid[block(j), :], gain2)
        return 0

    lax.fori_loop(0, T // RB, norm_rows, 0)
    save(resid, h2)
    saved = lambda q: [pltpu.make_async_copy(g_st.at[q % 2], gate.at[:, lane(q, GB)], gos.at[q % 2, 0]),
                       pltpu.make_async_copy(u_st.at[q % 2], up.at[:, lane(q, GB)], gos.at[q % 2, 1])]
    before_mlp, after_mlp = [], []
    for k in range(n_mlp):
        before_mlp.append(tick.note(partial(tick.until, n_out + 2 * k + 2)))
        after_mlp.append(tick.note(release))

    def mlp_block(q, _):
        at_block(q, before_mlp)
        arrived_block(q, n_out + 2 * q, wg, GB, g_buf.at[q % 2])
        arrived_block(q, n_out + 2 * q + 1, wu, GB, u_buf.at[q % 2])

        @pl.when(q >= 2)
        def _():
            for s in saved(q - 2):
                s.wait()

        def mlp_tile(j, _):
            g = mm(h2[...], g_buf[q % 2, :, :, :, :, :, lane(j, 256)].reshape(-1, 256), 1, 0)
            u = mm(h2[...], u_buf[q % 2, :, :, :, :, :, lane(j, 256)].reshape(-1, 256), 1, 0)
            g_st[q % 2, :, lane(j, 256)] = g.astype(bf16)
            u_st[q % 2, :, lane(j, 256)] = u.astype(bf16)
            act[:, lane(q * (GB // 256) + j, 256)] = (g / (1.0 + jnp.exp(-g)) * u).astype(bf16)
            return 0

        lax.fori_loop(0, GB // 256, mlp_tile, 0)
        at_block(q, after_mlp)
        for s in saved(q):
            s.start()
        return 0

    lax.fori_loop(0, n_mlp, mlp_block, 0)
    save(act)
    before_down = [tick.note(partial(tick.until, n_out + 2 * n_mlp + k + 1)) for k in range(n_out)]

    def down_block(q, _):
        at_block(q, before_down)
        arrived_block(q, n_out + 2 * n_mlp + q, wd, OB, d_buf.at[q])
        cols = lane(q, OB)
        y = resid[:, cols] + mm(act[...], d_buf[q].reshape(-1, OB), 1, 0)
        mixed[:, cols] = y.astype(bf16)
        stats[0:1, :] += jnp.sum(valid[...] * y * y, axis=0, keepdims=True)
        return 0

    lax.fori_loop(0, n_out, down_block, 0)
    save(mixed)
    for q in range(max(0, n_mlp - 2), n_mlp):
        for s in saved(jnp.int32(q)):
            s.wait()
    wait_all(cot_collect)
    for q in across + sibling + onward:
        q.wait_send()
    for r in rings:
        r.end()
    for q in saves.values():
        q.wait()


FORWARD_PLAN = (tuple((j, (1, 2)) for j in (1, 3, 5, 7)), (2, 2), tuple((j, (1, 2)) for j in range(8)))


def forward(index, prompt, staged, cot, wk, wv, wq, shards, k_gain, q_gain, cos_r, sin_r, cos, sin, past, inside, valid, gain1, gain2, n, cid):
    rows, W = prompt.shape
    S = staged.shape[1]
    T = rows + S * CONTINUATION_LEN
    group = PROMPT_LENGTH // rows
    half, A = group // 2, n // 4
    halves = [s.reshape(2, s.shape[0] // 2, s.shape[1]) for s in shards]
    flat = staged.reshape((-1,) + staged.shape[2:])
    QW, KW, FW = wq.shape[1], wk.shape[1], shards[1].shape[1]
    D, V = pltpu.SemaphoreType.DMA, pltpu.VMEM
    shape = jax.ShapeDtypeStruct
    small = shape((KEY_VALUE_HEADS, 2, T), f32)
    keys = ((half, 2, rows, KW), bf16)
    kept = [((T, W), bf16), ((T, W), bf16), ((T, QW), bf16), ((QW, T), bf16), ((T, KW), f32), ((T, KW), bf16), ((T, KW), bf16), keys, keys,
            ((T, W), f32), ((T, W), bf16), ((T, FW), bf16), ((T, W), bf16)]
    out_shape = [shape((A, 2, 2) + s.shape, bf16) for s in halves] + [shape((S, n) + staged.shape[2:], bf16), shape((T, FW), bf16), shape((T, FW), bf16)]
    out_shape += [shape(*k) for k in kept] + [small, small, shape((8, 256), f32)]
    vm, hbm, sm = pl.BlockSpec(memory_space=pltpu.VMEM), pl.BlockSpec(memory_space=pl.ANY), pl.BlockSpec(memory_space=pltpu.SMEM)
    OB, GB = 256, 512
    n_out, n_mlp = W // OB, FW // GB
    m = 2 * n_out + 2 * n_mlp
    buf = lambda i, k, w: V((k, A, 2, 2) + halves[i].shape[:2] + (w,), bf16)
    res = pl.pallas_call(
        partial(forward_kernel, n, group),
        out_shape=out_shape,
        in_specs=[sm, vm, vm, hbm] + [hbm] * 7 + [vm] * 11,
        out_specs=[hbm] * 20 + [vm] * 3,
        scratch_shapes=[V(*k) for k in kept] + [V(wk.shape, bf16), V(wv.shape, bf16), V(wq.shape, bf16), V(staged.shape, bf16), V((S, n) + staged.shape[2:], bf16),
            V(staged.shape, bf16), buf(0, n_out, OB), buf(1, 2, GB), buf(2, 2, GB), buf(3, n_out, OB), V((2, T, GB), bf16), V((2, T, GB), bf16)]
        + [D((m, A - 1))] * 2 + [D((m, 3))] * 2 + [D((m,))] * 2 + [D((2, max(half - 1, 1)))] * 2 + [D((2, half))] * 2 + [D((2,))]
        + [D((3, n - 1))] * 2 + [D((3,)), D((2, 2)), D((13,)), D((3,))],
        compiler_params=pltpu.CompilerParams(collective_id=cid, has_side_effects=True, vmem_limit_bytes=63 << 20),
        name="forward",
    )(index, prompt, flat, cot, wk, wv, wq, *halves, k_gain, q_gain, cos_r, sin_r, cos, sin, past, inside, valid, gain1, gain2)
    res = list(res)
    for i, s in enumerate(shards):
        res[i] = res[i].reshape(-1, s.shape[1])
    for i in (14, 15):
        res[i] = res[i].reshape(PROMPT_LENGTH, KW)
    return res


PLAN = ((3, 5), (1, 3), (2, 8), (4, 5), (5, 8), (0, 1), (6, 8), (2, 8), (3, 3), (1, 5), (2, 8), (1, 3), (3, 8), (3, 1), (0, 6), (6, 2), (2, 4), (5, 4), (1, 2), (5, 3))


class Fold:
    def __init__(self, n, R, where, g, bufs, out, cols, sems, i):
        self.bufs, self.k, self.landing = bufs
        self.waited = set()
        self.g, self.out, self.cols, self.i, self.sems = g, out, cols, i, sems
        self.A, self.bits = n // 4, R.bit_length() - 1
        self.rep, self.a, self.b, self.c, self.h = where
        self.rh = self.bufs[0].shape[-2]
        self.k0 = fold_split(self.rh)

    b1 = property(lambda self: self.bufs[0].at[self.landing])
    b2y, b2x, b3, b4, s4, b5 = [property(lambda self, j=j: self.bufs[j].at[self.k]) for j in range(1, 7)]

    def device(self, da=0, db=0, dc=0, bit=None):
        rep, a, b, c = self.rep, self.a, self.b, self.c
        if bit is not None:
            rep = rep + (1 << bit) - 2 * (1 << bit) * ((rep // (1 << bit)) % 2)
        return (rep, (((a + da) % self.A) * 2 + (1 - b if db else b)) * 2 + (1 - c if dc else c))

    @property
    def ydev(self):
        return self.device(db=1)

    @property
    def xdev(self):
        return self.device(bit=0)

    @property
    def cdev(self):
        return self.device(dc=1)

    def zdev(self, d):
        return self.device(da=d)

    def flip(self, bit):
        return self.device(bit=bit)

    def hop(self, k):
        i, a, b, c, h, k0, rh = self.i, self.a, self.b, self.c, self.h, self.k0, self.rh
        s1s, s1r, s2s, s2r, s3s, s3r, s4s, s4r, s5s, s5r, _ = self.sems
        lo, hi = pl.ds(0, k0), pl.ds(k0, rh - k0)
        if k == 1:
            return [remote(self.g.at[:, :, 1 - c], self.b1, s1s.at[i], s1r.at[i], self.cdev)]
        if k == 2:
            q = [remote(self.b1.at[:, 1 - b, :, lo], self.b2y, s2s.at[i, 0], s2r.at[i, 0], self.ydev)]
            if k0 < rh:
                q.append(remote(self.b1.at[:, :, 1 - h, hi], self.b2x, s2s.at[i, 1], s2r.at[i, 1], self.xdev))
            return q
        if k == 3:
            q = [remote(self.b2y.at[:, 1 - h], self.b3.at[:, lo], s3s.at[i, 0], s3r.at[i, 0], self.xdev)]
            if k0 < rh:
                q.append(remote(self.b2x.at[:, 1 - b], self.b3.at[:, hi], s3s.at[i, 1], s3r.at[i, 1], self.ydev))
            return q
        if k == 4:
            return [remote(self.b3.at[(a + d) % self.A], self.b4.at[d - 1], s4s.at[i, d - 1], s4r.at[i, d - 1], self.zdev(d)) for d in range(1, self.A)]
        last = self.bits - 1
        return [remote(self.s4.at[last], self.b5.at[last], s5s.at[i, last], s5r.at[i, last], self.xdev)]

    def put(self, k):
        last = self.bits - 1
        half = self.h if k == 0 else 1 - self.h
        return pltpu.make_async_copy((self.s4 if k == 0 else self.b5).at[last], self.out.at[half, :, self.cols], self.sems[-1].at[self.i, k])

    def begin(self):
        for q in self.hop(1):
            q.start()

    def arrive(self, k):
        for q in self.hop(k):
            q.wait_recv()

    def go(self, k):
        for q in self.hop(k):
            q.start()

    def step(self, k):
        a, b, c, h, k0, rh = self.a, self.b, self.c, self.h, self.k0, self.rh
        self.arrive(k)
        lo, hi = pl.ds(0, k0), pl.ds(k0, rh - k0)
        if k == 1:
            for q in self.hop(1):
                q.wait_send()
            view = lambda ref: lambda j: ref.at[j // 4, (j // 2) % 2, j % 2]
            add_rows(self.A * 4, view(self.b1), view(self.b1), [lambda j: self.g.at[j // 4, (j // 2) % 2, c, j % 2]])
            return
        elif k == 2:
            view = lambda ref: lambda j: ref.at[j // 2, j % 2]
            add_rows(self.A * 2, view(self.b2y), view(self.b2y), [lambda j: self.b1.at[j // 2, b, j % 2, lo]])
            if k0 < rh:
                add_rows(self.A * 2, view(self.b2x), view(self.b2x), [lambda j: self.b1.at[j // 2, j % 2, h, hi]])
        elif k == 3:
            view = lambda part: lambda j: self.b3.at[j, part]
            add_rows(self.A, view(lo), view(lo), [lambda j: self.b2y.at[j, h]])
            if k0 < rh:
                add_rows(self.A, view(hi), view(hi), [lambda j: self.b2x.at[j, b]])
        elif k == 4:
            add_rows(1, lambda j: self.s4.at[0], lambda j: self.b3.at[a], [lambda j, d=d: self.b4.at[d] for d in range(self.A - 1)])
            s5s, s5r = self.sems[8:10]
            for r in range(self.bits - 1):
                q = remote(self.s4.at[r], self.b5.at[r], s5s.at[self.i, r], s5r.at[self.i, r], self.flip(r + 1))
                q.start()
                q.wait()
                add_rows(1, lambda j, r=r: self.s4.at[r + 1], lambda j, r=r: self.s4.at[r], [lambda j, r=r: self.b5.at[r]])
            self.put(0).start()
        else:
            self.put(1).start()
            return
        self.go(k + 1)

    def sent(self, k):
        if k not in self.waited:
            self.waited.add(k)
            for q in self.hop(k):
                q.wait_send()

    def end(self):
        for k in range(2, 6):
            self.sent(k)
        self.put(0).wait()
        self.put(1).wait()


def fold_split(rh):
    if (rh // 2) % 16 == 0:
        return rh // 2
    return rh // 32 * 16 if rh >= 32 else rh


def backward_kernel(n, R, group, UD, UF, UO, *refs):
    it = iter(refs)
    take = lambda count: [next(it) for _ in range(count)]
    index, mixed, dm, h2, act, gate, up, resid, wd, wg, wu, wo, attended, q_rot, lse, rs_q, ks, vs, k_rot, v, k_pre, wq, wk, wv, hidden, x = take(26)
    k_gain, q_gain, cos_r, sin_r, cos, sin, past, inside, valid, gain1, gain2, sums = take(12)
    outs = take(7)
    vec, d_prompt, mixed_out, grad_out = take(4)
    classes = [take(7) for _ in range(3)]
    r1, r2, mixed_in, turned, grad_src, grad_in, vb, vz, dres = take(9)
    fold_sems = take(11)
    lds, hs, gs, gr, fs, fr, a2s, a2r, a2l, vs_, vr_, free = take(12)
    A, T, W = n // 4, dm.shape[0], dm.shape[1]
    half, rows, KW = group // 2, r1.shape[2], k_rot.shape[1]
    FW, QW = act.shape[1], attended.shape[1]
    bits = R.bit_length() - 1
    rep, a, b, c = position(n)
    h = rep % 2
    rank = lambda a, b, c: (a * 2 + b) * 2 + c
    me = rank(a, b, c)
    first, slot = (me // group) * half, (me // 2) % half
    flip = lambda bit: (rep + (1 << bit) - 2 * (1 << bit) * ((rep // (1 << bit)) % 2), me)
    meet([(rep, (me + d) % n) for d in range(1, n)] + [flip(k) for k in range(bits)])

    lane = lambda j, w: pl.ds(pl.multiple_of(j * w, w), w)
    heads = QUERY_HEADS // KEY_VALUE_HEADS
    loads = iter(range(lds.shape[0]))

    def fetch(src, dst):
        q = pltpu.make_async_copy(src, dst, lds.at[next(loads)])
        q.start()
        return q

    S = turned.shape[1]

    trips = (a2s, a2r, a2l)
    spread_copies = lambda src, dst, k: slot_spread(n, src, dst, trips, k, (rep, me))
    collect_copies = lambda src, dst, k: slot_collect(n, src, dst, trips, k, (rep, me))

    def reorder(src, dst):
        def put(j, _):
            s = index[j]
            dst[j // S, j % S] = src[s // S, s % S]
            return 0

        lax.fori_loop(0, n * S, put, 0)

    mixed_spread = spread_copies(mixed, mixed_in, 0)
    grad_spread, grad_collect = spread_copies(grad_src, grad_in, 2), collect_copies(turned, grad_out, 3)

    units = []

    def unit(cls, k, g, out, cols, landing=None):
        units.append(Fold(n, R, (rep, a, b, c, h), g, (classes[cls], k, k if landing is None else landing), outs[out], cols, fold_sems, len(units)))
        return units[-1]

    done = [0] * 6

    noted = [None]

    def run(f):
        f() if noted[0] is None else noted[0].append(f)

    def note(f):
        noted[0] = []
        f()
        fs_, noted[0] = noted[0], None
        return fs_

    def at_block(q, lists):
        for k, fs_ in enumerate(lists):
            if fs_:
                pl.when(q == k)(lambda fs_=fs_: [f() for f in fs_] and None)

    def e1(upto=None):
        while done[0] < (done[0] + 1 if upto is None else upto):
            run(partial(units[done[0]].step, 1))
            done[0] += 1
            if upto is None:
                break

    def tick(count=1, lag=2):
        for _ in range(count):
            before = list(done)
            if done[1] < before[0]:
                run(partial(units[done[1]].go, 2))
                done[1] += 1
            for k in range(2, 6):
                if before[k - 1] - done[k] >= lag:
                    run(partial(units[done[k]].step, k))
                    done[k] += 1

    n_down, n_ff, n_out = W // UD, FW // UF, W // UO
    V = pltpu.VMEM
    rh = lambda k: classes[k][0].shape[-2]
    AT, QT = FW // A, QW // A

    def down(act_c, act_t, g_down, dm_v):
        got = fetch(dm, dm_v)
        pieces = [fetch(act.at[:, pl.ds(0, AT)], act_c.at[0])]
        begin_all(mixed_spread)
        got.wait()
        for i in range(A):
            if i + 1 < A:
                pieces.append(fetch(act.at[:, pl.ds((i + 1) * AT, AT)], act_c.at[(i + 1) % 2]))
            pieces[i].wait()
            act_t[...] = act_c[i % 2].T

            def down_tile(j, _):
                y = mm(act_t[...], dm_v[:, lane(j, UD)], 1, 0).astype(bf16)
                g_down[j, i] = y.reshape(g_down.shape[2:])
                return 0

            lax.fori_loop(0, n_down, down_tile, 0)
        for u in range(n_down):
            unit(0, u, g_down.at[u], 0, pl.ds(u * UD, UD)).begin()
        for u in range(n_down):
            e1()

    pl.run_scoped(down, V((2, T, AT), bf16), V((AT, T), bf16), V((n_down, A, 2, 2, 2, rh(0), UD), bf16), V((T, W), bf16))
    tick(*PLAN[0])
    RB = 32
    block = lambda j: pl.ds(pl.multiple_of(j * RB, RB), RB)

    def norm_back(value, gain, grad):
        r = lax.rsqrt(jnp.mean(value * value, axis=-1, keepdims=True) + norm_epsilon)
        u = value * r
        t = grad * gain
        return r * (t - u * jnp.mean(t * u, axis=-1, keepdims=True)), jnp.sum(grad * u, axis=0, keepdims=True)

    def persistent(dq, dkr, dvl):
        def after_mlp(drl):
            pl.run_scoped(partial(mlp, drl), V((4, A, 2, 2, 2, rh(1), UF), bf16), V((2, UF, W), bf16), V((2, W, UF), bf16), V((2, W, UF), bf16), V((2, T, UF), bf16),
                          V((2, T, UF), bf16), V((T, UF), bf16), V((T, UF), bf16), V((W, T), bf16), V((T, W), bf16), V((T, W), bf16), V((T, W), f32))
            pl.run_scoped(partial(out_grad, drl), V((2, T, QT), bf16), V((QT, T), bf16), V((n_out, A, 2, 2, 2, rh(2), UO), bf16))
            wait_all(mixed_spread)
            reorder(mixed_in, turned)
            mixed_collect = collect_copies(turned, mixed_out, 1)
            begin_all(mixed_collect)
            pl.run_scoped(partial(attention, drl, dq, dkr, dvl), V((half, 2, rows, KW), bf16), V((half, 2, rows, KW), bf16), V((2, PROMPT_LENGTH, HEAD_SIZE), bf16),
                          V((2, PROMPT_LENGTH, HEAD_SIZE), bf16), V((2, heads * HEAD_SIZE, T), bf16), V((2, T, heads * HEAD_SIZE), bf16), V((2, heads * HEAD_SIZE, W), bf16),
                          V((T, KW), bf16), V((T, KW), bf16))
            wait_all(mixed_collect)

        pl.run_scoped(after_mlp, V((T, W), bf16))
        pl.run_scoped(partial(weights_back, dq, dkr, dvl), V((2, 256, QW), bf16), V((2, 256, KW), bf16), V((2, 256, KW), bf16), V((T, W), bf16), V((W, T), bf16),
                      V((T, KW), f32), V((T, KW), bf16), V((4, A, 2, 2, 2, rh(1), UF), bf16), V((T, W), f32))

    def mlp(drl, g_ff, wd_c, wg_c, wu_c, gate_c, up_c, dg_c, du_c, h2_t, h2_v, dm_v, dhid):
        got = [fetch(h2, h2_v), fetch(dm, dm_v)]

        def fetch_ff(q):
            cols, s = lane(q, UF), q % 2
            moves = ((wd.at[cols], wd_c), (gate.at[:, cols], gate_c), (up.at[:, cols], up_c), (wg.at[:, cols], wg_c), (wu.at[:, cols], wu_c))
            return [pltpu.make_async_copy(src, dst.at[s], hs.at[s, k]) for k, (src, dst) in enumerate(moves)]

        for f in fetch_ff(jnp.int32(0)):
            f.start()
        got_resid = fetch(resid, dres)
        for f in got:
            f.wait()
        h2_t[...] = h2_v[...].T
        dhid[...] = jnp.zeros_like(dhid)
        free_slot, begun, after = ([], []), ([], []), []
        for q in range(n_ff):
            for k in range(2):
                free_slot[k].append(note(lambda: e1(len(units) - 1)))
                unit(1, 2 * q + k, g_ff.at[(2 * q + k) % 4], 1 + k, pl.ds(q * UF, UF))
                begun[k].append([units[-1].begin])
            after.append(note(partial(tick, *PLAN[1 + q])))

        def ff_block(q, _):
            s = q % 2

            @pl.when(q + 1 < n_ff)
            def _():
                for f in fetch_ff(q + 1):
                    f.start()

            for f in fetch_ff(q):
                f.wait()

            def act_tile(j, _):
                cols = lane(j, 256)
                g, u = gate_c[s, :, cols].astype(f32), up_c[s, :, cols].astype(f32)
                da = mm(dm_v[...], wd_c[s, lane(j, 256), :], 1, 1)
                sg = 1.0 / (1.0 + jnp.exp(-g))
                du_c[:, cols] = (da * (g * sg)).astype(bf16)
                dg_c[:, cols] = (da * u * (sg * (1.0 + g * (1.0 - sg)))).astype(bf16)
                return 0

            lax.fori_loop(0, UF // 256, act_tile, 0)
            for k, d in enumerate((dg_c, du_c)):
                at_block(q, free_slot[k])

                def ff_tile(j, _):
                    y = mm(h2_t[...], d[:, lane(j, 256)], 1, 0).astype(bf16)
                    g_ff[(2 * q + k) % 4, :, :, :, :, :, lane(j, 256)] = y.reshape(g_ff.shape[1:6] + (256,))
                    return 0

                lax.fori_loop(0, UF // 256, ff_tile, 0)
                at_block(q, begun[k])

            def hid_tile(j, _):
                cols = lane(j, 256)
                dhid[:, cols] += mm(dg_c[...], wg_c[s, cols, :], 1, 1) + mm(du_c[...], wu_c[s, cols, :], 1, 1)
                return 0

            lax.fori_loop(0, W // 256, hid_tile, 0)
            at_block(q, after)
            return 0

        lax.fori_loop(0, n_ff, ff_block, 0)
        while done[0] < len(units):
            e1()
        got_resid.wait()

        def second_norm(j, total):
            d, gg = norm_back(dres[block(j), :], gain2[...], dhid[block(j), :])
            d = dm_v[block(j), :].astype(f32) + d
            dres[block(j), :] = d
            drl[block(j), :] = d.astype(bf16)
            return total + gg

        g2 = lax.fori_loop(0, T // RB, second_norm, jnp.zeros((1, W), f32))
        for k in range(W // 128):
            vec[W // 128 + k:W // 128 + k + 1, :] = g2[:, k * 128:(k + 1) * 128]

    def out_grad(drl, att_c, att_t, g_out):
        pieces = [fetch(attended.at[:, pl.ds(0, QT)], att_c.at[0])]
        for i in range(A):
            if i + 1 < A:
                pieces.append(fetch(attended.at[:, pl.ds((i + 1) * QT, QT)], att_c.at[(i + 1) % 2]))
            pieces[i].wait()
            att_t[...] = att_c[i % 2].T

            def out_tile(j, _):
                y = mm(att_t[...], drl[:, lane(j, UO)], 1, 0).astype(bf16)
                g_out[j, i] = y.reshape(g_out.shape[2:])
                return 0

            lax.fori_loop(0, n_out, out_tile, 0)
        for u in range(n_out):
            unit(2, u, g_out.at[u], 3, pl.ds(u * UO, UO)).begin()
        while done[0] < len(units):
            e1()
        tick(*PLAN[7])

    def attention(drl, dq, dkr, dvl, dk, dv, ks_c, vs_c, q_c, att_c, wo_c, kr_v, v_v):
        others = [fetch(k_rot, kr_v), fetch(v, v_v)]
        pair = lambda j: lane(j, heads * HEAD_SIZE)

        def head_copies(j):
            s = j % 2
            moves = [(ks.at[:, lane(j, HEAD_SIZE)], ks_c), (vs.at[:, lane(j, HEAD_SIZE)], vs_c), (q_rot.at[pair(j), :], q_c),
                     (attended.at[:, pair(j)], att_c), (wo.at[pair(j), :], wo_c)]
            return [pltpu.make_async_copy(src, dst.at[s], hs.at[s, k]) for k, (src, dst) in enumerate(moves)]

        for q in head_copies(jnp.int32(0)):
            q.start()
        for q in others:
            q.wait()
        scale = HEAD_SIZE ** -0.5
        plus = lambda p, q: q if p is None else p + q

        def head(j, gain_grad):
            @pl.when(j + 1 < KEY_VALUE_HEADS)
            def _():
                for q in head_copies(j + 1):
                    q.start()

            for q in head_copies(j):
                q.wait()
            at = j % 2
            kl = lane(j, HEAD_SIZE)
            kb, vb_ = ks_c[at], vs_c[at]
            dkp = dvp = dks = dvs = None
            do_pair = mm(drl[...], wo_c[at], 1, 1)
            out_pair = att_c[at].astype(f32)
            for g in range(heads):
                sl = slice(g * HEAD_SIZE, (g + 1) * HEAD_SIZE)
                q = q_c[at, sl, :]
                do = do_pair[:, sl].astype(bf16)
                delta = jnp.sum((do.astype(f32) * out_pair[:, sl]).T, axis=0, keepdims=True)
                log_total = lse[j, g:g + 1, :]
                parts = []
                for suffix in range(2):
                    part = slice(rows, None) if suffix else slice(0, rows)
                    qp, dop, lp, dp = q[:, part], do[part], log_total[:, part], delta[:, part]
                    pieces = [(kb, vb_, None if suffix else past[...])]
                    if suffix:
                        pieces.append((kr_v[rows:, kl], v_v[rows:, kl], inside[...]))
                    total = None
                    for i, (kk, vv, bias) in enumerate(pieces):
                        s = mm(kk, qp, 1, 0) * (scale * LOG2E) - lp
                        p = jnp.exp2(s if bias is None else s + bias)
                        ds = (p * (mm(vv, dop, 1, 1) - dp)).astype(bf16)
                        gv, gk = mm(p.astype(bf16), dop, 1, 0), mm(ds, qp, 1, 1)
                        total = plus(total, mm(kk, ds, 0, 0))
                        if i:
                            dks, dvs = plus(dks, gk), plus(dvs, gv)
                        else:
                            dkp, dvp = plus(dkp, gk), plus(dvp, gv)
                    parts.append(total)
                d = jnp.concatenate(parts, axis=1) * scale
                m = HEAD_SIZE // 2
                cs, sn = cos[...], sin[...]
                dy = jnp.concatenate([d[:m] * cs + d[m:] * sn, d[m:] * cs - d[:m] * sn], axis=0)
                qf = q.astype(f32)
                u = jnp.concatenate([qf[:m] * cs + qf[m:] * sn, qf[m:] * cs - qf[:m] * sn], axis=0) / q_gain[:, 0:1]
                gg = dy * u
                for t in range(T // 128):
                    gain_grad = gain_grad + gg[:, t * 128:(t + 1) * 128]
                dy = dy * q_gain[:, 0:1]
                dx = rs_q[j, g:g + 1, :] * (dy - u * jnp.mean(dy * u, axis=0, keepdims=True))
                dq[:, lane(j * heads + g, HEAD_SIZE)] = dx.T.astype(bf16)
            dk[:, :, :, kl] = (dkp * scale).astype(bf16).reshape(half, 2, rows, HEAD_SIZE)
            dv[:, :, :, kl] = dvp.astype(bf16).reshape(half, 2, rows, HEAD_SIZE)
            dkr[rows:, kl] = dks * scale
            dvl[rows:, kl] = dvs.astype(bf16)
            for k in range(KEY_VALUE_HEADS - 1):
                if PLAN[8 + k][0]:
                    pl.when(j == k)(partial(tick, *PLAN[8 + k]))
            return gain_grad

        gain_grad = lax.fori_loop(0, KEY_VALUE_HEADS, head, jnp.zeros((HEAD_SIZE, 128), f32))
        vec[2 * W // 128:2 * W // 128 + 1, :] = jnp.sum(gain_grad.T, axis=0, keepdims=True)
        grads = [dk, dv]
        home = lambda s, c: (rep, (first + s) * 2 + c)

        def to_sibling(i, d):
            return remote(grads[i].at[(slot + d) % half, 1 - c], r1.at[i, d], gs.at[i, d], gr.at[i, d], home(slot, 1 - c))

        order = list(range(1, half)) + [0]
        for d in order:
            for i in range(2):
                to_sibling(i, d).start()
        for d in order:
            for i in range(2):
                to_sibling(i, d).wait_recv()

                def one(j, _):
                    r1[i, d, block(j)] = (grads[i][(slot + d) % half, c, block(j)].astype(f32) + r1[i, d, block(j)].astype(f32)).astype(bf16)
                    return 0

                lax.fori_loop(0, rows // RB, one, 0)
                if d:
                    across(i, d).start()
        for d in order:
            for i in range(2):
                to_sibling(i, d).wait_send()
        tick(*PLAN[15])

    def across(i, d):
        return remote(r1.at[i, d], r2.at[i, d - 1], fs.at[i, d - 1], fr.at[i, d - 1], (rep, (first + (slot + d) % half) * 2 + c))

    def weights_back(dq, dkr, dvl, wq_c, wk_c, wv_c, hid_v, hid_t, kp_v, dkl, g_qkv, dhid):
        got = [fetch(hidden, hid_v), fetch(k_pre, kp_v)]
        tiles = W // 256
        fetch_q = lambda j: fetch(wq.at[pl.ds(j * 256, 256)], wq_c.at[j % 2])
        fetch_kv = lambda j, s: [fetch(wk.at[pl.ds(j * 256, 256)], wk_c.at[s]), fetch(wv.at[pl.ds(j * 256, 256)], wv_c.at[s])]
        q_tiles, kv_tiles = [fetch_q(0), fetch_q(1)], [fetch_kv(0, 0), fetch_kv(1, 1)]
        got[0].wait()
        hid_t[...] = hid_v[...].T
        got_x = fetch(x, hid_v)
        count = [0]
        first_ff = n_down
        while done[2] < first_ff + (QW + 2 * KW) // UF:
            tick()
        for f in units[first_ff:first_ff + (QW + 2 * KW) // UF]:
            f.sent(2)
        pl.semaphore_signal(free, inc=1, device_id=(rep, rank(a, b, 1 - c)), device_id_type=MESH)
        pl.semaphore_wait(free, 1)

        def grad_units(d, out, width):
            base, begun = count[0], []
            for u in range(width // UF):
                unit(1, 2 * n_ff + base + u, g_qkv.at[(base + u) % 4], out, pl.ds(u * UF, UF), base + u)
                begun.append([units[-1].begin])
            count[0] += width // UF

            def tile(t, _):
                u, j = t // (UF // 256), t % (UF // 256)
                y = mm(hid_t[...], d[:, lane(t, 256)], 1, 0).astype(bf16)
                g_qkv[(base + u) % 4, :, :, :, :, :, lane(j, 256)] = y.reshape(g_qkv.shape[1:6] + (256,))

                @pl.when(j == UF // 256 - 1)
                def _():
                    at_block(u, begun)

                return 0

            lax.fori_loop(0, width // 256, tile, 0)

        grad_units(dq, 4, QW)
        for u in range(QW // UF):
            e1()
        tick(*PLAN[16])
        got[1].wait()

        def key_head(part, j, total):
            lanes = lane(j, HEAD_SIZE)
            y = kp_v[part, lanes]
            r = lax.rsqrt(jnp.mean(y * y, axis=-1, keepdims=True) + norm_epsilon)
            u = y * r
            dy = dkr[part, lanes]
            dy = dy * cos_r[part, :] - pltpu.roll(dy, HEAD_SIZE // 2, 1) * sin_r[part, :]
            total = total + jnp.sum(dy * u, axis=0, keepdims=True)
            dy = dy * k_gain[...]
            dkl[part, lanes] = (r * (dy - u * jnp.mean(dy * u, axis=-1, keepdims=True))).astype(bf16)
            return total

        def first_norm(j, carry):
            total, square = carry
            d, gg = norm_back(hid_v[block(j), :].astype(f32), gain1[...], dhid[block(j), :])
            d = dres[block(j), :] + d
            dres[block(j), :] = d
            return total + gg, square + jnp.sum(valid[block(j), :] * d * d, axis=0, keepdims=True)

        ours, theirs = pl.ds(rows, T - rows), pl.ds(0, rows)
        gk = lax.fori_loop(0, KEY_VALUE_HEADS, partial(key_head, ours), jnp.zeros((1, HEAD_SIZE), f32))
        for j in range(tiles):
            cols = pl.ds(j * 256, 256)
            q_tiles[j].wait()
            for f in kv_tiles[j]:
                f.wait()
            dhid[:, cols] = mm(dq[...], wq_c[j % 2], 1, 1)
            dhid[ours, cols] += mm(dkl[ours, :], wk_c[j % 2], 1, 1) + mm(dvl[ours, :], wv_c[j % 2], 1, 1)
            if j + 2 < tiles:
                q_tiles.append(fetch_q(j + 2))
            kv_tiles.append(fetch_kv((j + 2) % tiles, j % 2))
        got_x.wait()
        zero = jnp.zeros((1, W), f32)
        g1, square = lax.fori_loop(rows // RB, T // RB, first_norm, (zero, zero))
        width = CONTINUATION_LEN // n
        step = max(width, 8)

        def pack(j, _):
            y = dres[pl.ds(pl.multiple_of(rows + j * step, step), step), :].astype(bf16)
            for k in range(step // width):
                i = j * (step // width) + k
                grad_src[i // n, i % n] = y[k * width:(k + 1) * width]
            return 0

        lax.fori_loop(0, S * CONTINUATION_LEN // step, pack, 0)
        begin_all(grad_spread)
        tick(*PLAN[17])
        for i in range(2):
            for d in range(1, half):
                across(i, d).wait_recv()

        def own_keys(j, _):
            t, u = r1[0, 0, block(j)].astype(f32), r1[1, 0, block(j)].astype(f32)
            for d in range(1, half):
                t, u = t + r2[0, d - 1, block(j)].astype(f32), u + r2[1, d - 1, block(j)].astype(f32)
            dkr[block(j), :] = t
            dvl[block(j), :] = u.astype(bf16)
            return 0

        lax.fori_loop(0, rows // RB, own_keys, 0)
        grad_units(dvl, 6, KW)
        gk = lax.fori_loop(0, KEY_VALUE_HEADS, partial(key_head, theirs), gk)
        vec[2 * W // 128 + 1:2 * W // 128 + 2, :] = gk
        grad_units(dkl, 5, KW)
        while done[0] < len(units):
            e1()
        tick(*PLAN[18])
        wait_all(grad_spread)
        reorder(grad_in, turned)
        begin_all(grad_collect)
        for j in range(tiles):
            cols, s = pl.ds(j * 256, 256), (tiles + j) % 2
            for f in kv_tiles[tiles + j]:
                f.wait()
            dhid[theirs, cols] += mm(dkl[theirs, :], wk_c[s], 1, 1) + mm(dvl[theirs, :], wv_c[s], 1, 1)
            if j + 2 < tiles:
                kv_tiles.append(fetch_kv(j + 2, s))
        tick(*PLAN[19])
        g1, square = lax.fori_loop(0, rows // RB, first_norm, (g1, square))
        for k in range(W // 128):
            vec[k:k + 1, :] = g1[:, k * 128:(k + 1) * 128]
        place = lax.broadcasted_iota(jnp.int32, (1, 128), 1)
        row = jnp.zeros((1, 128), f32)
        whole = lambda y: jnp.sum(jnp.sum(y, axis=0, keepdims=True), axis=1, keepdims=True)
        for k, y in enumerate((sums[0:1, :], sums[1:2, :], square, valid[...])):
            row = jnp.where(place == k, whole(y), row)
        vec[2 * W // 128 + 2:2 * W // 128 + 3, :] = row
        vec[2 * W // 128 + 3:, :] = jnp.zeros((vec.shape[0] - 2 * W // 128 - 3, 128), f32)

    pl.run_scoped(persistent, V((T, QW), bf16), V((T, KW), f32), V((T, KW), bf16))
    for i in range(2):
        for d in range(1, half):
            across(i, d).wait_send()

    prompt_out = fetch(dres.at[pl.ds(0, rows)], d_prompt)
    tick(2, 1)
    rounds = [(rep, rank(a, b, 1 - c)), (rep, rank(a, 1 - b, c))] + [flip(k) for k in range(bits)]
    vb[0] = vec[...]
    for k, to in enumerate(rounds):
        q = remote(vb.at[2 * k], vb.at[2 * k + 1], vs_.at[k], vr_.at[k], to)
        q.start()
        q.wait()
        vb[2 * k + 2] = vb[2 * k] + vb[2 * k + 1]
        tick(2, 1)
    last, nr = 2 * len(rounds), len(rounds)
    zs = [remote(vb.at[last], vz.at[a], vs_.at[nr + d - 1], vr_.at[nr + d - 1], (rep, rank((a + d) % A, b, c))) for d in range(1, A)]
    for q in zs:
        q.start()
    vz[a] = vb[last]
    for q in zs:
        q.wait()
    total = vz[0]
    for k in range(1, A):
        total = total + vz[k]
    vec[...] = total
    while done[5] < len(units):
        tick(lag=1)
    wait_all(grad_collect)
    prompt_out.wait()
    for f in units:
        f.end()


def backward(index, mixed, dm, h2, act, gate, up, resid, wd, wg, wu, wo, attended, q_rot, lse, rs_q, ks, vs, k_rot, v, k_pre, wq, wk, wv, hidden, x,
             k_gain, q_gain, cos_r, sin_r, cos, sin, past, inside, valid, gain1, gain2, sums, rows, n, R, cid):
    group = PROMPT_LENGTH // rows
    half, A, (T, W), bits = group // 2, n // 4, dm.shape, R.bit_length() - 1
    FW, QW, KW = act.shape[1], attended.shape[1], k_rot.shape[1]
    UD, UF, UO = 256, 512, 512
    S = mixed.shape[0]
    V, D = pltpu.VMEM, pltpu.SemaphoreType.DMA
    shape = jax.ShapeDtypeStruct
    vm, hbm, sm = pl.BlockSpec(memory_space=pltpu.VMEM), pl.BlockSpec(memory_space=pl.ANY), pl.BlockSpec(memory_space=pltpu.SMEM)
    rh = lambda w: w.shape[0] // (2 * n)
    out_shape = [shape((2, rh(w), w.shape[1]), bf16) for w in (wd, wg, wu, wo, wq, wk, wv)]
    vec_rows = 2 * W // 128 + 8
    out_shape += [shape((vec_rows, 128), f32), shape((rows, W), f32), shape(mixed.shape, bf16), shape(mixed.shape, bf16)]
    scratch = []
    for count, r, w in ((W // UD, rh(wd), UD), (2 * (FW // UF) + (QW + 2 * KW) // UF, rh(wg), UF), (W // UO, rh(wo), UO)):
        k0 = fold_split(r)
        k1 = max(r - k0, 8)
        landing = 2 * (FW // UF) if w == UF and r == rh(wg) else count
        scratch += [V((landing, A, 2, 2, r, w), bf16), V((count, A, 2, k0, w), bf16), V((count, A, 2, k1, w) if k0 < r else (1, 1, 1, 8, 128), bf16), V((count, A, r, w), bf16),
                    V((count, A - 1, r, w), bf16), V((count, bits, r, w), bf16), V((count, bits, r, w), bf16)]
    m = W // UD + 2 * (FW // UF) + (QW + 2 * KW) // UF + W // UO
    turned = (n, S) + mixed.shape[2:]
    kv = (2, half, rows, KW)
    scratch += [V(kv, bf16), V((2, max(half - 1, 1), rows, KW), bf16), V(turned, bf16), V(turned, bf16), V(mixed.shape, bf16), V(turned, bf16),
                V((2 * (2 + bits) + 1, vec_rows, 128), f32), V((A, vec_rows, 128), f32), V((T, W), f32)]
    scratch += [D((m,)), D((m,)), D((m, 2)), D((m, 2)), D((m, 2)), D((m, 2)), D((m, A - 1)), D((m, A - 1)), D((m, bits)), D((m, bits)), D((m, 2))]
    scratch += [D((2 * A + 5 * (FW // UF) + 32,)), D((2, 5)), D((2, half)), D((2, half)), D((2, max(half - 1, 1))), D((2, max(half - 1, 1))), D((4, n - 1)), D((4, n - 1)), D((4,)),
                D((2 + bits + A - 1,)), D((2 + bits + A - 1,)), pltpu.SemaphoreType.REGULAR]
    hbm_in = [mixed, dm, h2, act, gate, up, resid, wd, wg, wu, wo, attended, q_rot, lse, rs_q, ks, vs, k_rot, v, k_pre, wq, wk, wv, hidden, x]
    in_vmem = {13, 14}
    res = pl.pallas_call(
        partial(backward_kernel, n, R, group, UD, UF, UO),
        out_shape=out_shape,
        in_specs=[sm] + [vm if k in in_vmem else hbm for k in range(len(hbm_in))] + [vm] * 12,
        out_specs=[hbm] * 7 + [vm] + [hbm] * 3,
        scratch_shapes=scratch,
        compiler_params=pltpu.CompilerParams(collective_id=cid, has_side_effects=True, vmem_limit_bytes=63 << 20),
        name="backward",
    )(index, *hbm_in, k_gain, q_gain, cos_r, sin_r, cos, sin, past, inside, valid, gain1, gain2, sums)
    return [r.reshape(-1, r.shape[-1]) for r in res[:7]], res[7], res[8], res[9], res[10]


def per_device(
    prompt_rows,
    suffix_rows,
    assignment,
    lengths,
    attention_gain,
    query_weight,
    key_matrix,
    value_matrix,
    query_gain,
    key_norm_gain,
    out_weight,
    mlp_gain,
    gate_weight,
    up_weight,
    down_weight,
    prompt_cotangent,
    suffix_cotangent,
):
    n, R = lax.axis_size("fsdp"), lax.axis_size("rep")
    rank = lax.axis_index("fsdp")
    rows = prompt_rows.shape[0]
    suffix = suffix_rows.shape[0]
    S = suffix // CONTINUATION_LEN
    total = rows + suffix
    width = MODEL_WIDTH

    pad = lambda v: jnp.pad(v.astype(f32).reshape(-1), (0, 128 - v.size))
    tile = jnp.stack([pad(v) for v in (attention_gain, mlp_gain, query_gain, key_norm_gain, assignment, lengths)])
    tile = jnp.pad(tile, ((0, 2), (0, 0)))
    cut = lambda v: v.reshape(S, n, CONTINUATION_LEN // n, width)
    w_key, w_value, w_query, tiles, staged = gather(key_matrix, value_matrix, query_weight, tile, cut(suffix_rows), n, 0)
    gain_first = tiles[:, 0, : attention_gain.size].reshape(-1)
    gain_second = tiles[:, 1, : mlp_gain.size].reshape(-1)
    query_scale = tiles[:, 2, : query_gain.size].reshape(-1)
    key_scale = tiles[:, 3, : key_norm_gain.size].reshape(-1)

    owner = tiles[:, 4, :S].reshape(-1).astype(jnp.int32) // CONT
    slot_count = n * S
    ids = jnp.arange(slot_count, dtype=jnp.int32)
    ahead = (owner[None, :] < owner[:, None]) | ((owner[None, :] == owner[:, None]) & (ids[None, :] < ids[:, None]))
    place = jnp.sum(ahead.astype(jnp.int32), axis=1)
    hits = place[None, :] == ids[:, None]
    order = jnp.sum(jnp.where(hits, ids[None, :], 0), axis=1)
    slot_lengths = jnp.sum(jnp.where(hits, tiles[:, 5, :S].reshape(-1).astype(jnp.int32)[None, :], 0), axis=1)
    own_lengths = lax.dynamic_slice_in_dim(slot_lengths, rank * S, S)

    prompt_place = (rank * rows) % PROMPT_LENGTH + jnp.arange(rows, dtype=jnp.int32)
    suffix_place = jnp.arange(suffix, dtype=jnp.int32) % CONTINUATION_LEN
    suffix_slot = jnp.arange(suffix, dtype=jnp.int32) // CONTINUATION_LEN
    length_rows = jnp.repeat(own_lengths, CONTINUATION_LEN)
    suffix_valid = suffix_place < length_rows
    valid_rows = jnp.concatenate([jnp.ones((rows,), f32), suffix_valid.astype(f32)])
    token_positions = jnp.concatenate([prompt_place, PROMPT_LENGTH + suffix_place]).astype(f32)
    half = HEAD_SIZE // 2
    inverse = rope_theta ** (jnp.arange(half, dtype=f32) * (-2.0 / HEAD_SIZE))
    angles_t = inverse[:, None] * token_positions[None, :]
    cos_t, sin_t = jnp.cos(angles_t), jnp.sin(angles_t)
    cos_r, sin_r = cos_t.T, sin_t.T
    cos_rows = jnp.concatenate([cos_r, cos_r], axis=1)
    sin_rows = jnp.concatenate([-sin_r, sin_r], axis=1)
    past = jnp.where(jnp.arange(PROMPT_LENGTH, dtype=jnp.int32)[:, None] <= prompt_place[None, :], 0.0, masked_score).astype(f32)
    inside = jnp.where(
        (suffix_slot[:, None] == suffix_slot[None, :]) & (suffix_place[:, None] <= suffix_place[None, :]) & suffix_valid[:, None], 0.0, masked_score
    ).astype(f32)

    key_gain_row = key_scale.reshape(1, HEAD_SIZE)
    query_gain_col = jnp.broadcast_to(query_scale[:, None], (HEAD_SIZE, 128))
    (
        w_out, w_gate, w_up, w_down, moved_cotangent, gate_low, up_low, rows_low, hidden, attended, query_rot, key_pre, key_rot, values,
        prompt_keys, prompt_values, residual, hidden_two, act, mixed_low, lse, query_rs, sums,
    ) = forward(
        order, prompt_rows, staged, cut(suffix_cotangent), w_key, w_value, w_query, [out_weight, gate_weight, up_weight, down_weight], key_gain_row,
        query_gain_col, cos_rows, sin_rows, cos_t, sin_t, past, inside, valid_rows[:, None], gain_first[None, :], gain_second[None, :], n, 2,
    )
    moved_cotangent = moved_cotangent.reshape(suffix, width)
    d_mixed_low = jnp.concatenate([prompt_cotangent, moved_cotangent], 0) * valid_rows[:, None].astype(bf16)
    shards, vec_sum, prompt_grad, suffix_mixed, suffix_grad = backward(
        place, cut(mixed_low[rows:]), d_mixed_low, hidden_two, act, gate_low, up_low, residual, w_down, w_gate, w_up, w_out, attended, query_rot, lse, query_rs,
        prompt_keys, prompt_values, key_rot, values, key_pre, w_query, w_key, w_value, hidden, rows_low, key_gain_row, query_gain_col,
        cos_rows, sin_rows, cos_t, sin_t, past, inside, valid_rows[:, None], gain_first[None, :], gain_second[None, :], sums, rows, n, R, 3,
    )
    suffix_mixed, suffix_grad = suffix_mixed.reshape(suffix, width), suffix_grad.reshape(suffix, width)
    g_down, g_gate, g_up, g_out, g_query, g_key, g_value = [g.astype(f32) for g in shards]
    flat = vec_sum.reshape(-1)

    def mine(first, size, part):
        return lax.dynamic_slice_in_dim(flat[first : first + size], rank * part, part)

    g_first = mine(0, width, attention_gain.size)
    g_second = mine(width, width, mlp_gain.size)
    g_query_gain = mine(2 * width, HEAD_SIZE, query_gain.size)
    g_key_gain = mine(2 * width + HEAD_SIZE, HEAD_SIZE, key_norm_gain.size)
    stat_sums = flat[2 * width + 2 * HEAD_SIZE : 2 * width + 2 * HEAD_SIZE + 4]
    token_norms = jnp.sqrt(stat_sums[:3] / (stat_sums[3] * width))
    return (
        mixed_low[:rows],
        suffix_mixed,
        prompt_grad,
        suffix_grad.astype(f32),
        g_first,
        g_query,
        g_key,
        g_value,
        g_query_gain,
        g_key_gain,
        g_out,
        g_second,
        g_gate,
        g_up,
        g_down,
        token_norms,
    )


def solution(mesh):
    placed = (
        P(("rep", "fsdp"), None),
        P(("rep", "fsdp"), None),
        P("rep", "fsdp"),
        P("rep", "fsdp"),
        P("fsdp"),
        P("fsdp", None),
        P("fsdp", None),
        P("fsdp", None),
        P("fsdp"),
        P("fsdp"),
        P("fsdp", None),
        P("fsdp"),
        P("fsdp", None),
        P("fsdp", None),
        P("fsdp", None),
        P(("rep", "fsdp"), None),
        P(("rep", "fsdp"), None),
    )
    return jax.shard_map(
        per_device,
        mesh=mesh,
        in_specs=placed,
        out_specs=(
            P(("rep", "fsdp"), None),
            P(("rep", "fsdp"), None),
            P(("rep", "fsdp"), None),
            P(("rep", "fsdp"), None),
            P("fsdp"),
            P("fsdp", None),
            P("fsdp", None),
            P("fsdp", None),
            P("fsdp"),
            P("fsdp"),
            P("fsdp", None),
            P("fsdp"),
            P("fsdp", None),
            P("fsdp", None),
            P("fsdp", None),
            P(),
        ),
        check_vma=False,
    )
```

```python
from functools import partial

import jax
import jax.numpy as jnp
from jax import lax
from jax.experimental import pallas as pl
from jax.experimental.pallas import tpu as pltpu
from jax.sharding import PartitionSpec as P

MODEL_WIDTH = 1024
QUERY_HEADS = 16
KEY_VALUE_HEADS = 8
HEAD_SIZE = 128
PROMPT_LENGTH = 1024
CONT = 8
CONTINUATION_LEN = 128

norm_epsilon = 1e-06
rope_theta = 1000000.0
masked_score = -1e30
MESH = pl.DeviceIdType.MESH
bf16 = jnp.bfloat16
f32 = jnp.float32

def position(n):
    rep = lax.axis_index("rep")
    rank = lax.axis_index("fsdp")
    return rep, rank // 4, (rank // 2) % 2, rank % 2


def meet(peers):
    barrier = pltpu.get_barrier_semaphore()
    for p in peers:
        pl.semaphore_signal(barrier, inc=1, device_id=p, device_id_type=MESH)
    pl.semaphore_wait(barrier, len(peers))


def remote(src, dst, send, recv, to):
    return pltpu.make_async_remote_copy(src, dst, send, recv, device_id=to, device_id_type=MESH)


def add_rows(count, out, first, second, step=None):
    def one(j, _):
        o = out(j)
        total = first(j)[...].astype(jnp.float32)
        for s in second:
            total = total + s(j)[...].astype(jnp.float32)
        o[...] = total.astype(o.dtype)
        return 0
    lax.fori_loop(0, count, one, 0)


LOG2E = 1.4426950408889634


def mm(x, y, cx, cy):
    return lax.dot_general(x, y, (((cx,), (cy,)), ((), ())), preferred_element_type=f32)


class Ring:
    def __init__(self, n, own, full, cols, sems, i, x_first):
        zs, zr, ss, sr, ls = sems
        A = n // 4
        rep, a, b, c = position(n)
        h = rep % 2
        every = slice(None)
        at = lambda *ix: full.at[(*ix, every, cols)]
        rank = lambda a, b, c: (a * 2 + b) * 2 + c
        ydev, xdev, cdev = (rep, rank(a, 1 - b, c)), (rep + 1 - 2 * h, rank(a, b, c)), (rep, rank(a, b, 1 - c))
        same = lambda ref, k, to: remote(ref, ref, ss.at[i, k], sr.at[i, k], to)
        mine = own.at[h, :, cols]
        self.local = lambda: [pltpu.make_async_copy(mine, at(a, b, c, h), ls.at[i])]
        self.along = lambda: [remote(mine, at(a, b, c, h), zs.at[i, d - 1], zr.at[i, d - 1], (rep, rank((a + d) % A, b, c))) for d in range(1, A)]
        self.second = lambda: [same(at(every, b, c, h), 0, xdev if x_first else ydev)]
        self.third = lambda: [same(at(every, b, c, every), 1, ydev) if x_first else same(at(every, every, c, h), 1, xdev)]
        self.last = lambda: [same(at(every, every, c, every), 2, cdev)]

    def begin(self):
        for q in self.local() + self.along():
            q.start()

    def turn(self, arrived, started):
        for q in arrived():
            q.wait_recv()
        for q in started():
            q.start()

    def step(self, k):
        if k == 0:
            for q in self.local():
                q.wait()
            self.turn(self.along, self.second)
        elif k == 1:
            self.turn(self.second, self.third)
        elif k == 2:
            self.turn(self.third, self.last)
        else:
            for q in self.last():
                q.wait_recv()

    def end(self):
        for q in self.along() + self.second() + self.third() + self.last():
            q.wait_send()


class Ticker:
    def __init__(self, rings, arrived=lambda i: None):
        self.rings, self.arrived, self.done, self.noted = rings, arrived, [0] * 5, None

    def run(self, f):
        f() if self.noted is None else self.noted.append(f)

    def note(self, f):
        self.noted = []
        f()
        noted, self.noted = self.noted, None
        return noted

    def begin(self, count):
        for r in self.rings[self.done[0]:self.done[0] + max(count, 0)]:
            self.run(r.begin)
            self.done[0] += 1

    def __call__(self, count=1, lag=1):
        for _ in range(count):
            before = list(self.done)
            for k in range(1, 5):
                i = self.done[k]
                if i < len(self.rings) and before[k - 1] - i >= lag:
                    self.run(partial(self.rings[i].step, k - 1))
                    self.done[k] += 1
                    if k == 1:
                        self.begin(self.done[1] + ALONG - self.done[0])
                    if k == 4:
                        self.arrived(i)

    def until(self, count):
        while self.done[4] < count:
            before = list(self.done)
            self(1, 2)
            if before == self.done:
                self()


ALONG = 2


def slot_spread(n, src, dst, sems, k, where):
    s, r, l = sems
    rep, me = where
    own = pltpu.make_async_copy(src.at[:, me], dst.at[me], l.at[k])
    return own, [remote(src.at[:, (me + d) % n], dst.at[me], s.at[k, d - 1], r.at[k, d - 1], (rep, (me + d) % n)) for d in range(1, n)]


def slot_collect(n, src, dst, sems, k, where):
    s, r, l = sems
    rep, me = where
    own = pltpu.make_async_copy(src.at[me], dst.at[:, me], l.at[k])
    return own, [remote(src.at[(me + d) % n], dst.at[:, me], s.at[k, d - 1], r.at[k, d - 1], (rep, (me + d) % n)) for d in range(1, n)]


def begin_all(pair):
    pair[0].start()
    for q in pair[1]:
        q.start()


def wait_all(pair):
    pair[0].wait()
    for q in pair[1]:
        q.wait()


def gather_kernel(n, CB, *refs):
    so, sk, sv, tile, pieces, wq, wk, wv, tiles, staged, zs, zr, ss, sr, ls, ts, tr, ps, pr, pls = refs
    rep, a, b, c = position(n)
    me = (a * 2 + b) * 2 + c
    h = rep % 2
    meet([(rep, (me + d) % n) for d in range(1, n)] + [(rep + 1 - 2 * h, me)])
    blocks = []
    for own, full in ((sk, wk), (sv, wv), (so, wq)):
        blocks += [(own, full, pl.ds(q * CB, CB)) for q in range(full.shape[-1] // CB)]
    rings = [Ring(n, own, full, cols, (zs, zr, ss, sr, ls), i, i % 2 == 0) for i, (own, full, cols) in enumerate(blocks)]
    tick = Ticker(rings)
    share = [remote(tile, tiles.at[me], ts.at[d - 1], tr.at[d - 1], (rep, (me + d) % n)) for d in range(1, n)]
    rows = slot_spread(n, pieces, staged, (ps, pr, pls), 0, (rep, me))
    for q in share:
        q.start()
    tiles[me] = tile[...]
    tick.begin(ALONG)
    begin_all(rows)
    tick.until(len(rings))
    for q in share:
        q.wait()
    wait_all(rows)
    for r in rings:
        r.end()


def gather(wk, wv, wq, tile, slots, n, cid):
    A, CB = n // 4, 512
    halves = [w.reshape(2, w.shape[0] // 2, w.shape[1]) for w in (wq, wk, wv)]
    m = sum(w.shape[1] for w in (wk, wv, wq)) // CB
    D = pltpu.SemaphoreType.DMA
    vm, hbm = pl.BlockSpec(memory_space=pltpu.VMEM), pl.BlockSpec(memory_space=pl.ANY)
    shape = jax.ShapeDtypeStruct
    res = pl.pallas_call(
        partial(gather_kernel, n, CB),
        out_shape=[shape((A, 2, 2) + w.shape, bf16) for w in halves] + [shape((n,) + tile.shape, f32), shape((n, slots.shape[0]) + slots.shape[2:], bf16)],
        in_specs=[hbm] * 3 + [vm] + [hbm],
        out_specs=[hbm] * 3 + [vm, hbm],
        scratch_shapes=[D((m, A - 1))] * 2 + [D((m, 3))] * 2 + [D((m,))] + [D((n - 1,))] * 2 + [D((1, n - 1))] * 2 + [D((1,))],
        compiler_params=pltpu.CompilerParams(collective_id=cid, has_side_effects=True),
        name="gather",
    )(*halves, tile, slots)
    w_query, w_key, w_value = [f.reshape(-1, f.shape[-1]) for f in res[:3]]
    return w_key, w_value, w_query, res[3], res[4]


def forward_kernel(n, group, *refs):
    it = iter(refs)
    take = lambda count: [next(it) for _ in range(count)]
    index, prompt, staged, cot, wk_h, wv_h, wq_h, so, sg, su, sd, k_gain, q_gain, cos_r, sin_r, cos, sin, past, inside, valid, gain1, gain2 = take(22)
    wo, wg, wu, wd, moved, gate, up = take(7)
    outs = take(13)
    lse_out, rs_out, stats = take(3)
    x, hidden, attended, q_out, k_pre, k_out, v, ks, vs, resid, h2, act, mixed = bufs = take(13)
    wk, wv, wq, ordered, landed, cot_in, o_buf, g_buf, u_buf, d_buf, g_st, u_st = take(12)
    zs, zr, ss, sr, ls, lds, fs, fr, gs, gr, kls, ps, pr, pls, gos, outs_sem, ins_sem = take(17)
    rows = ks.shape[2]
    T, W = x.shape
    half = group // 2
    rep, a, b, c = position(n)
    me = (a * 2 + b) * 2 + c
    first, slot = (me // group) * half, (me // 2) % half
    h = rep % 2
    ins = [pltpu.make_async_copy(src, dst, ins_sem.at[k]) for k, (src, dst) in enumerate(((wk_h, wk), (wv_h, wv), (wq_h, wq)))]
    for q in ins:
        q.start()
    meet([(rep, (me + d) % n) for d in range(1, n)] + [(rep + 1 - 2 * h, me)])
    saves = {id(buf): pltpu.make_async_copy(buf, out, outs_sem.at[k]) for k, (buf, out) in enumerate(zip(bufs, outs))}

    def save(*which):
        for buf in which:
            saves[id(buf)].start()

    OB, GB = o_buf.shape[-1], g_buf.shape[-1]
    n_out, n_mlp = wo.shape[-1] // OB, wg.shape[-1] // GB
    blocks = [(so, wo, pl.ds(q * OB, OB), o_buf.at[q]) for q in range(n_out)]
    for q in range(n_mlp):
        blocks += [(sg, wg, pl.ds(q * GB, GB), g_buf.at[q % 2]), (su, wu, pl.ds(q * GB, GB), u_buf.at[q % 2])]
    blocks += [(sd, wd, pl.ds(q * OB, OB), d_buf.at[q]) for q in range(n_out)]
    m = len(blocks)
    rings = [Ring(n, own, full, cols, (zs, zr, ss, sr, ls), i, i % 2 == 0) for i, (own, full, cols, _) in enumerate(blocks)]

    def load(i):
        _, full, cols, buf = blocks[i]
        return pltpu.make_async_copy(full.at[:, :, :, :, :, cols], buf, lds.at[i])

    used, late = [0], []

    def arrived(i):
        q = (i - n_out) // 2 if n_out <= i < n_out + 2 * n_mlp else 0
        if q < used[0] + 2:
            tick.run(lambda: load(i).start())
        else:
            late.append(i)

    def release():
        used[0] += 1
        now, late[:] = [i for i in late if (i - n_out) // 2 < used[0] + 2], [i for i in late if (i - n_out) // 2 >= used[0] + 2]
        for i in now:
            tick.run(lambda i=i: load(i).start())

    tick = Ticker(rings, arrived)
    S = ordered.shape[1]

    def reorder(src, flat):
        def put(j, _):
            s = index[j]
            ordered[j // S, j % S] = src[s] if flat else src[s // S, s % S]
            return 0

        lax.fori_loop(0, n * S, put, 0)

    sems = (ps, pr, pls)
    reorder(staged, True)
    rows_in = slot_collect(n, ordered, landed, sems, 0, (rep, me))
    cot_spread = slot_spread(n, cot, cot_in, sems, 1, (rep, me))
    cot_collect = slot_collect(n, ordered, moved, sems, 2, (rep, me))
    begin_all(rows_in)
    tick.begin(ALONG)

    lane = lambda j, w: pl.ds(pl.multiple_of(j * w, w), w)
    heads = QUERY_HEADS // KEY_VALUE_HEADS
    pair = heads * HEAD_SIZE
    RB = 32
    block = lambda j: pl.ds(pl.multiple_of(j * RB, RB), RB)

    def norm(y, gain):
        return (y * lax.rsqrt(jnp.mean(y * y, axis=-1, keepdims=True) + norm_epsilon) * gain[...]).astype(bf16)

    def prompt_rows(j, _):
        y = prompt[block(j), :]
        x[block(j), :] = y
        hidden[block(j), :] = norm(y.astype(f32), gain1)
        return 0

    def kv_tile(part, j, _):
        kp = mm(hidden[part, :], wk[:, lane(j, 256)], 1, 0)
        k_pre[part, lane(j, 256)] = kp
        for g in range(2):
            y = kp[:, g * HEAD_SIZE:(g + 1) * HEAD_SIZE]
            y = y * lax.rsqrt(jnp.mean(y * y, axis=-1, keepdims=True) + norm_epsilon) * k_gain[...]
            k_out[part, lane(2 * j + g, HEAD_SIZE)] = (y * cos_r[part, :] + pltpu.roll(y, HEAD_SIZE // 2, 1) * sin_r[part, :]).astype(bf16)
        v[part, lane(j, 256)] = mm(hidden[part, :], wv[:, lane(j, 256)], 1, 0).astype(bf16)
        return 0

    lax.fori_loop(0, rows // RB, prompt_rows, 0)
    ins[0].wait()
    ins[1].wait()
    lax.fori_loop(0, wk.shape[1] // 256, partial(kv_tile, pl.ds(0, rows)), 0)
    parts = [(k_out, ks), (v, vs)]
    at = lambda s, c: (rep, (first + s) * 2 + c)
    mine = lambda i: parts[i][0].at[pl.ds(0, rows)]
    klocal = [pltpu.make_async_copy(mine(i), parts[i][1].at[slot, c], kls.at[i]) for i in range(2)]
    across = [remote(mine(i), parts[i][1].at[slot, c], fs.at[i, d - 1], fr.at[i, d - 1], at((slot + d) % half, c)) for i in range(2) for d in range(1, half)]
    sibling = [remote(mine(i), parts[i][1].at[slot, c], gs.at[i, 0], gr.at[i, 0], at(slot, 1 - c)) for i in range(2)]
    onward = []
    for i in range(2):
        for d in range(1, half):
            there = parts[i][1].at[(slot + half - d) % half, c]
            onward.append(remote(there, there, gs.at[i, d], gr.at[i, d], at(slot, 1 - c)))
    for q in across + sibling + klocal:
        q.start()
    tick()
    wait_all(rows_in)
    width = landed.shape[2]

    def slot_rows(j, _):
        s, p = j // (n * width // RB), j % (n * width // RB)
        k = RB // width
        if width % 8 == 0:
            y = landed[s, pl.ds(p * k, k)].astype(f32).reshape(RB, W)
        else:
            y = jnp.concatenate([landed[s, p * k + i].astype(f32) for i in range(k)], axis=0)
        at = pl.ds(pl.multiple_of(rows + j * RB, RB), RB)
        x[at, :] = y.astype(bf16)
        hidden[at, :] = norm(y, gain1)
        return 0

    lax.fori_loop(0, (T - rows) // RB, slot_rows, 0)
    lax.fori_loop(0, wk.shape[1] // 256, partial(kv_tile, pl.ds(rows, T - rows)), 0)
    tick()
    save(x, hidden, k_pre, k_out, v)
    ins[2].wait()

    def q_tile(j, _):
        qp = mm(hidden[...], wq[:, lane(j, pair)], 1, 0)
        for g in range(heads):
            y = qp[:, g * HEAD_SIZE:(g + 1) * HEAD_SIZE].T
            rs = lax.rsqrt(jnp.mean(y * y, axis=0, keepdims=True) + norm_epsilon)
            rs_out[j, g:g + 1, :] = rs
            y = y * rs * q_gain[:, 0:1]
            lo, hi = y[:HEAD_SIZE // 2], y[HEAD_SIZE // 2:]
            y = jnp.concatenate([lo * cos[...] - hi * sin[...], hi * cos[...] + lo * sin[...]], axis=0)
            q_out[lane(j * heads + g, HEAD_SIZE), :] = y.astype(bf16)
        for k, plan in FORWARD_PLAN[0]:
            pl.when(j == k)(partial(tick, *plan))
        return 0

    lax.fori_loop(0, KEY_VALUE_HEADS, q_tile, 0)
    begin_all(cot_spread)
    save(q_out)
    for q in across:
        q.wait_recv()
    for q in onward:
        q.start()
    tick(*FORWARD_PLAN[1])
    for q in klocal:
        q.wait()
    for q in sibling + onward:
        q.wait_recv()
    save(ks, vs)
    scale = HEAD_SIZE ** -0.5 * LOG2E

    def attend_head(j, _):
        kl = lane(j, HEAD_SIZE)
        kb = ks[:, :, :, kl].reshape(PROMPT_LENGTH, HEAD_SIZE)
        vb = vs[:, :, :, kl].reshape(PROMPT_LENGTH, HEAD_SIZE)
        for g in range(heads):
            ql = lane(j * heads + g, HEAD_SIZE)
            q = q_out[ql, :]
            p = jnp.exp2(mm(kb, q[:, :rows], 1, 0) * scale + past[...])
            total = jnp.sum(p, axis=0, keepdims=True)
            o = mm(vb, p.astype(bf16), 0, 0) / total
            attended[:rows, ql] = o.T.astype(bf16)
            lse_out[j, g:g + 1, :rows] = jnp.log2(total)
            p = jnp.exp2(mm(kb, q[:, rows:], 1, 0) * scale)
            r = jnp.exp2(mm(k_out[rows:, kl], q[:, rows:], 1, 0) * scale + inside[...])
            total = jnp.sum(p, axis=0, keepdims=True) + jnp.sum(r, axis=0, keepdims=True)
            o = (mm(vb, p.astype(bf16), 0, 0) + mm(v[rows:, kl], r.astype(bf16), 0, 0)) / total
            attended[rows:, ql] = o.T.astype(bf16)
            lse_out[j, g:g + 1, rows:] = jnp.log2(total)
        for k, plan in FORWARD_PLAN[2]:
            pl.when(j == k)(partial(tick, *plan))
        return 0

    lax.fori_loop(0, KEY_VALUE_HEADS, attend_head, 0)
    save(attended)
    wait_all(cot_spread)
    reorder(cot_in, False)
    begin_all(cot_collect)

    stats[...] = jnp.zeros_like(stats)

    def at_block(q, noted):
        for k, fs_ in enumerate(noted):
            if fs_:
                pl.when(q == k)(lambda fs_=fs_: [f() for f in fs_] and None)

    def arrived_block(q, first, full, width, buf):
        pltpu.make_async_copy(full.at[:, :, :, :, :, lane(q, width)], buf, lds.at[first]).wait()

    before_out = [tick.note(partial(tick.until, k + 1)) for k in range(n_out)]

    def out_block(q, _):
        at_block(q, before_out)
        arrived_block(q, q, wo, OB, o_buf.at[q])
        cols = lane(q, OB)
        y = x[:, cols].astype(f32) + mm(attended[...], o_buf[q].reshape(-1, OB), 1, 0)
        resid[:, cols] = y
        stats[1:2, :] += jnp.sum(valid[...] * y * y, axis=0, keepdims=True)
        return 0

    lax.fori_loop(0, n_out, out_block, 0)

    def norm_rows(j, _):
        h2[block(j), :] = norm(resid[block(j), :], gain2)
        return 0

    lax.fori_loop(0, T // RB, norm_rows, 0)
    save(resid, h2)
    saved = lambda q: [pltpu.make_async_copy(g_st.at[q % 2], gate.at[:, lane(q, GB)], gos.at[q % 2, 0]),
                       pltpu.make_async_copy(u_st.at[q % 2], up.at[:, lane(q, GB)], gos.at[q % 2, 1])]
    before_mlp, after_mlp = [], []
    for k in range(n_mlp):
        before_mlp.append(tick.note(partial(tick.until, n_out + 2 * k + 2)))
        after_mlp.append(tick.note(release))

    def mlp_block(q, _):
        at_block(q, before_mlp)
        arrived_block(q, n_out + 2 * q, wg, GB, g_buf.at[q % 2])
        arrived_block(q, n_out + 2 * q + 1, wu, GB, u_buf.at[q % 2])

        @pl.when(q >= 2)
        def _():
            for s in saved(q - 2):
                s.wait()

        def mlp_tile(j, _):
            g = mm(h2[...], g_buf[q % 2, :, :, :, :, :, lane(j, 256)].reshape(-1, 256), 1, 0)
            u = mm(h2[...], u_buf[q % 2, :, :, :, :, :, lane(j, 256)].reshape(-1, 256), 1, 0)
            g_st[q % 2, :, lane(j, 256)] = g.astype(bf16)
            u_st[q % 2, :, lane(j, 256)] = u.astype(bf16)
            act[:, lane(q * (GB // 256) + j, 256)] = (g / (1.0 + jnp.exp(-g)) * u).astype(bf16)
            return 0

        lax.fori_loop(0, GB // 256, mlp_tile, 0)
        at_block(q, after_mlp)
        for s in saved(q):
            s.start()
        return 0

    lax.fori_loop(0, n_mlp, mlp_block, 0)
    save(act)
    before_down = [tick.note(partial(tick.until, n_out + 2 * n_mlp + k + 1)) for k in range(n_out)]

    def down_block(q, _):
        at_block(q, before_down)
        arrived_block(q, n_out + 2 * n_mlp + q, wd, OB, d_buf.at[q])
        cols = lane(q, OB)
        y = resid[:, cols] + mm(act[...], d_buf[q].reshape(-1, OB), 1, 0)
        mixed[:, cols] = y.astype(bf16)
        stats[0:1, :] += jnp.sum(valid[...] * y * y, axis=0, keepdims=True)
        return 0

    lax.fori_loop(0, n_out, down_block, 0)
    save(mixed)
    for q in range(max(0, n_mlp - 2), n_mlp):
        for s in saved(jnp.int32(q)):
            s.wait()
    wait_all(cot_collect)
    for q in across + sibling + onward:
        q.wait_send()
    for r in rings:
        r.end()
    for q in saves.values():
        q.wait()


FORWARD_PLAN = (tuple((j, (1, 2)) for j in (1, 3, 5, 7)), (2, 2), tuple((j, (1, 2)) for j in range(8)))


def forward(index, prompt, staged, cot, wk, wv, wq, shards, k_gain, q_gain, cos_r, sin_r, cos, sin, past, inside, valid, gain1, gain2, n, cid):
    rows, W = prompt.shape
    S = staged.shape[1]
    T = rows + S * CONTINUATION_LEN
    group = PROMPT_LENGTH // rows
    half, A = group // 2, n // 4
    halves = [s.reshape(2, s.shape[0] // 2, s.shape[1]) for s in shards]
    flat = staged.reshape((-1,) + staged.shape[2:])
    QW, KW, FW = wq.shape[1], wk.shape[1], shards[1].shape[1]
    D, V = pltpu.SemaphoreType.DMA, pltpu.VMEM
    shape = jax.ShapeDtypeStruct
    small = shape((KEY_VALUE_HEADS, 2, T), f32)
    keys = ((half, 2, rows, KW), bf16)
    kept = [((T, W), bf16), ((T, W), bf16), ((T, QW), bf16), ((QW, T), bf16), ((T, KW), f32), ((T, KW), bf16), ((T, KW), bf16), keys, keys,
            ((T, W), f32), ((T, W), bf16), ((T, FW), bf16), ((T, W), bf16)]
    out_shape = [shape((A, 2, 2) + s.shape, bf16) for s in halves] + [shape((S, n) + staged.shape[2:], bf16), shape((T, FW), bf16), shape((T, FW), bf16)]
    out_shape += [shape(*k) for k in kept] + [small, small, shape((8, 256), f32)]
    vm, hbm, sm = pl.BlockSpec(memory_space=pltpu.VMEM), pl.BlockSpec(memory_space=pl.ANY), pl.BlockSpec(memory_space=pltpu.SMEM)
    OB, GB = 256, 512
    n_out, n_mlp = W // OB, FW // GB
    m = 2 * n_out + 2 * n_mlp
    buf = lambda i, k, w: V((k, A, 2, 2) + halves[i].shape[:2] + (w,), bf16)
    res = pl.pallas_call(
        partial(forward_kernel, n, group),
        out_shape=out_shape,
        in_specs=[sm, vm, vm, hbm] + [hbm] * 7 + [vm] * 11,
        out_specs=[hbm] * 20 + [vm] * 3,
        scratch_shapes=[V(*k) for k in kept] + [V(wk.shape, bf16), V(wv.shape, bf16), V(wq.shape, bf16), V(staged.shape, bf16), V((S, n) + staged.shape[2:], bf16),
            V(staged.shape, bf16), buf(0, n_out, OB), buf(1, 2, GB), buf(2, 2, GB), buf(3, n_out, OB), V((2, T, GB), bf16), V((2, T, GB), bf16)]
        + [D((m, A - 1))] * 2 + [D((m, 3))] * 2 + [D((m,))] * 2 + [D((2, max(half - 1, 1)))] * 2 + [D((2, half))] * 2 + [D((2,))]
        + [D((3, n - 1))] * 2 + [D((3,)), D((2, 2)), D((13,)), D((3,))],
        compiler_params=pltpu.CompilerParams(collective_id=cid, has_side_effects=True, vmem_limit_bytes=63 << 20),
        name="forward",
    )(index, prompt, flat, cot, wk, wv, wq, *halves, k_gain, q_gain, cos_r, sin_r, cos, sin, past, inside, valid, gain1, gain2)
    res = list(res)
    for i, s in enumerate(shards):
        res[i] = res[i].reshape(-1, s.shape[1])
    for i in (14, 15):
        res[i] = res[i].reshape(PROMPT_LENGTH, KW)
    return res


PLAN = ((3, 8), (1, 8), (2, 3), (2, 3), (5, 5), (2, 4), (4, 5), (1, 3), (6, 8), (1, 1), (2, 8), (2, 3), (6, 8), (3, 1), (0, 2), (3, 1), (2, 6), (1, 1), (3, 2), (6, 6))


class Fold:
    def __init__(self, n, R, where, g, bufs, out, cols, sems, i):
        self.bufs, self.k, self.landing = bufs
        self.waited = set()
        self.g, self.out, self.cols, self.i, self.sems = g, out, cols, i, sems
        self.A, self.bits = n // 4, R.bit_length() - 1
        self.rep, self.a, self.b, self.c, self.h = where
        self.rh = self.bufs[0].shape[-2]
        self.k0 = fold_split(self.rh)

    b1 = property(lambda self: self.bufs[0].at[self.landing])
    b2y, b2x, b3, b4, s4, b5 = [property(lambda self, j=j: self.bufs[j].at[self.k]) for j in range(1, 7)]

    def device(self, da=0, db=0, dc=0, bit=None):
        rep, a, b, c = self.rep, self.a, self.b, self.c
        if bit is not None:
            rep = rep + (1 << bit) - 2 * (1 << bit) * ((rep // (1 << bit)) % 2)
        return (rep, (((a + da) % self.A) * 2 + (1 - b if db else b)) * 2 + (1 - c if dc else c))

    @property
    def ydev(self):
        return self.device(db=1)

    @property
    def xdev(self):
        return self.device(bit=0)

    @property
    def cdev(self):
        return self.device(dc=1)

    def zdev(self, d):
        return self.device(da=d)

    def flip(self, bit):
        return self.device(bit=bit)

    def hop(self, k):
        i, a, b, c, h, k0, rh = self.i, self.a, self.b, self.c, self.h, self.k0, self.rh
        s1s, s1r, s2s, s2r, s3s, s3r, s4s, s4r, s5s, s5r, _ = self.sems
        lo, hi = pl.ds(0, k0), pl.ds(k0, rh - k0)
        if k == 1:
            return [remote(self.g.at[:, :, 1 - c], self.b1, s1s.at[i], s1r.at[i], self.cdev)]
        if k == 2:
            q = [remote(self.b1.at[:, 1 - b, :, lo], self.b2y, s2s.at[i, 0], s2r.at[i, 0], self.ydev)]
            if k0 < rh:
                q.append(remote(self.b1.at[:, :, 1 - h, hi], self.b2x, s2s.at[i, 1], s2r.at[i, 1], self.xdev))
            return q
        if k == 3:
            q = [remote(self.b2y.at[:, 1 - h], self.b3.at[:, lo], s3s.at[i, 0], s3r.at[i, 0], self.xdev)]
            if k0 < rh:
                q.append(remote(self.b2x.at[:, 1 - b], self.b3.at[:, hi], s3s.at[i, 1], s3r.at[i, 1], self.ydev))
            return q
        if k == 4:
            return [remote(self.b3.at[(a + d) % self.A], self.b4.at[d - 1], s4s.at[i, d - 1], s4r.at[i, d - 1], self.zdev(d)) for d in range(1, self.A)]
        last = self.bits - 1
        return [remote(self.s4.at[last], self.b5.at[last], s5s.at[i, last], s5r.at[i, last], self.xdev)]

    def put(self, k):
        last = self.bits - 1
        half = self.h if k == 0 else 1 - self.h
        return pltpu.make_async_copy((self.s4 if k == 0 else self.b5).at[last], self.out.at[half, :, self.cols], self.sems[-1].at[self.i, k])

    def begin(self):
        for q in self.hop(1):
            q.start()

    def arrive(self, k):
        for q in self.hop(k):
            q.wait_recv()

    def go(self, k):
        for q in self.hop(k):
            q.start()

    def step(self, k):
        a, b, c, h, k0, rh = self.a, self.b, self.c, self.h, self.k0, self.rh
        self.arrive(k)
        lo, hi = pl.ds(0, k0), pl.ds(k0, rh - k0)
        if k == 1:
            for q in self.hop(1):
                q.wait_send()
            view = lambda ref: lambda j: ref.at[j // 4, (j // 2) % 2, j % 2]
            add_rows(self.A * 4, view(self.b1), view(self.b1), [lambda j: self.g.at[j // 4, (j // 2) % 2, c, j % 2]])
            return
        elif k == 2:
            view = lambda ref: lambda j: ref.at[j // 2, j % 2]
            add_rows(self.A * 2, view(self.b2y), view(self.b2y), [lambda j: self.b1.at[j // 2, b, j % 2, lo]])
            if k0 < rh:
                add_rows(self.A * 2, view(self.b2x), view(self.b2x), [lambda j: self.b1.at[j // 2, j % 2, h, hi]])
        elif k == 3:
            view = lambda part: lambda j: self.b3.at[j, part]
            add_rows(self.A, view(lo), view(lo), [lambda j: self.b2y.at[j, h]])
            if k0 < rh:
                add_rows(self.A, view(hi), view(hi), [lambda j: self.b2x.at[j, b]])
        elif k == 4:
            add_rows(1, lambda j: self.s4.at[0], lambda j: self.b3.at[a], [lambda j, d=d: self.b4.at[d] for d in range(self.A - 1)])
            s5s, s5r = self.sems[8:10]
            for r in range(self.bits - 1):
                q = remote(self.s4.at[r], self.b5.at[r], s5s.at[self.i, r], s5r.at[self.i, r], self.flip(r + 1))
                q.start()
                q.wait()
                add_rows(1, lambda j, r=r: self.s4.at[r + 1], lambda j, r=r: self.s4.at[r], [lambda j, r=r: self.b5.at[r]])
            self.put(0).start()
        else:
            self.put(1).start()
            return
        self.go(k + 1)

    def sent(self, k):
        if k not in self.waited:
            self.waited.add(k)
            for q in self.hop(k):
                q.wait_send()

    def end(self):
        for k in range(2, 6):
            self.sent(k)
        self.put(0).wait()
        self.put(1).wait()


def fold_split(rh):
    if (rh // 2) % 16 == 0:
        return rh // 2
    return rh // 32 * 16 if rh >= 32 else rh


def backward_kernel(n, R, group, UD, UF, UO, *refs):
    it = iter(refs)
    take = lambda count: [next(it) for _ in range(count)]
    index, mixed, dm, h2, act, gate, up, resid, wd, wg, wu, wo, attended, q_rot, lse, rs_q, ks, vs, k_rot, v, k_pre, wq, wk, wv, hidden, x = take(26)
    k_gain, q_gain, cos_r, sin_r, cos, sin, past, inside, valid, gain1, gain2, sums = take(12)
    outs = take(7)
    vec, d_prompt, mixed_out, grad_out = take(4)
    classes = [take(7) for _ in range(3)]
    r1, r2, mixed_in, turned, grad_src, grad_in, vb, vz, dres = take(9)
    fold_sems = take(11)
    lds, hs, gs, gr, fs, fr, a2s, a2r, a2l, vs_, vr_, free = take(12)
    A, T, W = n // 4, dm.shape[0], dm.shape[1]
    half, rows, KW = group // 2, r1.shape[2], k_rot.shape[1]
    FW, QW = act.shape[1], attended.shape[1]
    bits = R.bit_length() - 1
    rep, a, b, c = position(n)
    h = rep % 2
    rank = lambda a, b, c: (a * 2 + b) * 2 + c
    me = rank(a, b, c)
    first, slot = (me // group) * half, (me // 2) % half
    flip = lambda bit: (rep + (1 << bit) - 2 * (1 << bit) * ((rep // (1 << bit)) % 2), me)
    meet([(rep, (me + d) % n) for d in range(1, n)] + [flip(k) for k in range(bits)])

    lane = lambda j, w: pl.ds(pl.multiple_of(j * w, w), w)
    heads = QUERY_HEADS // KEY_VALUE_HEADS
    loads = iter(range(lds.shape[0]))

    def fetch(src, dst):
        q = pltpu.make_async_copy(src, dst, lds.at[next(loads)])
        q.start()
        return q

    S = turned.shape[1]

    trips = (a2s, a2r, a2l)
    spread_copies = lambda src, dst, k: slot_spread(n, src, dst, trips, k, (rep, me))
    collect_copies = lambda src, dst, k: slot_collect(n, src, dst, trips, k, (rep, me))

    def reorder(src, dst):
        def put(j, _):
            s = index[j]
            dst[j // S, j % S] = src[s // S, s % S]
            return 0

        lax.fori_loop(0, n * S, put, 0)

    mixed_spread = spread_copies(mixed, mixed_in, 0)
    grad_spread, grad_collect = spread_copies(grad_src, grad_in, 2), collect_copies(turned, grad_out, 3)

    units = []

    def unit(cls, k, g, out, cols, landing=None):
        units.append(Fold(n, R, (rep, a, b, c, h), g, (classes[cls], k, k if landing is None else landing), outs[out], cols, fold_sems, len(units)))
        return units[-1]

    done = [0] * 6

    noted = [None]

    def run(f):
        f() if noted[0] is None else noted[0].append(f)

    def note(f):
        noted[0] = []
        f()
        fs_, noted[0] = noted[0], None
        return fs_

    def at_block(q, lists):
        for k, fs_ in enumerate(lists):
            if fs_:
                pl.when(q == k)(lambda fs_=fs_: [f() for f in fs_] and None)

    def e1(upto=None):
        while done[0] < (done[0] + 1 if upto is None else upto):
            run(partial(units[done[0]].step, 1))
            done[0] += 1
            if upto is None:
                break

    def tick(count=1, lag=2):
        for _ in range(count):
            before = list(done)
            if done[1] < before[0]:
                run(partial(units[done[1]].go, 2))
                done[1] += 1
            for k in range(2, 6):
                if before[k - 1] - done[k] >= lag:
                    run(partial(units[done[k]].step, k))
                    done[k] += 1

    n_down, n_ff, n_out = W // UD, FW // UF, W // UO
    V = pltpu.VMEM
    rh = lambda k: classes[k][0].shape[-2]
    AT, QT = FW // A, QW // A

    def down(act_c, act_t, g_down, dm_v):
        got = fetch(dm, dm_v)
        pieces = [fetch(act.at[:, pl.ds(0, AT)], act_c.at[0])]
        begin_all(mixed_spread)
        got.wait()
        for i in range(A):
            if i + 1 < A:
                pieces.append(fetch(act.at[:, pl.ds((i + 1) * AT, AT)], act_c.at[(i + 1) % 2]))
            pieces[i].wait()
            act_t[...] = act_c[i % 2].T

            def down_tile(j, _):
                y = mm(act_t[...], dm_v[:, lane(j, UD)], 1, 0).astype(bf16)
                g_down[j, i] = y.reshape(g_down.shape[2:])
                return 0

            lax.fori_loop(0, n_down, down_tile, 0)
        for u in range(n_down):
            unit(0, u, g_down.at[u], 0, pl.ds(u * UD, UD)).begin()
        for u in range(n_down):
            e1()

    pl.run_scoped(down, V((2, T, AT), bf16), V((AT, T), bf16), V((n_down, A, 2, 2, 2, rh(0), UD), bf16), V((T, W), bf16))
    tick(*PLAN[0])
    RB = 32
    block = lambda j: pl.ds(pl.multiple_of(j * RB, RB), RB)

    def norm_back(value, gain, grad):
        r = lax.rsqrt(jnp.mean(value * value, axis=-1, keepdims=True) + norm_epsilon)
        u = value * r
        t = grad * gain
        return r * (t - u * jnp.mean(t * u, axis=-1, keepdims=True)), jnp.sum(grad * u, axis=0, keepdims=True)

    def persistent(dq, dkr, dvl):
        def after_mlp(drl):
            pl.run_scoped(partial(mlp, drl), V((4, A, 2, 2, 2, rh(1), UF), bf16), V((2, UF, W), bf16), V((2, W, UF), bf16), V((2, W, UF), bf16), V((2, T, UF), bf16),
                          V((2, T, UF), bf16), V((T, UF), bf16), V((T, UF), bf16), V((W, T), bf16), V((T, W), bf16), V((T, W), bf16), V((T, W), f32))
            pl.run_scoped(partial(out_grad, drl), V((2, T, QT), bf16), V((QT, T), bf16), V((n_out, A, 2, 2, 2, rh(2), UO), bf16))
            wait_all(mixed_spread)
            reorder(mixed_in, turned)
            mixed_collect = collect_copies(turned, mixed_out, 1)
            begin_all(mixed_collect)
            pl.run_scoped(partial(attention, drl, dq, dkr, dvl), V((half, 2, rows, KW), bf16), V((half, 2, rows, KW), bf16), V((2, PROMPT_LENGTH, HEAD_SIZE), bf16),
                          V((2, PROMPT_LENGTH, HEAD_SIZE), bf16), V((2, heads * HEAD_SIZE, T), bf16), V((2, T, heads * HEAD_SIZE), bf16), V((2, heads * HEAD_SIZE, W), bf16),
                          V((T, KW), bf16), V((T, KW), bf16))
            wait_all(mixed_collect)

        pl.run_scoped(after_mlp, V((T, W), bf16))
        pl.run_scoped(partial(weights_back, dq, dkr, dvl), V((2, 256, QW), bf16), V((2, 256, KW), bf16), V((2, 256, KW), bf16), V((T, W), bf16), V((W, T), bf16),
                      V((T, KW), f32), V((T, KW), bf16), V((4, A, 2, 2, 2, rh(1), UF), bf16), V((T, W), f32))

    def mlp(drl, g_ff, wd_c, wg_c, wu_c, gate_c, up_c, dg_c, du_c, h2_t, h2_v, dm_v, dhid):
        got = [fetch(h2, h2_v), fetch(dm, dm_v)]

        def fetch_ff(q):
            cols, s = lane(q, UF), q % 2
            moves = ((wd.at[cols], wd_c), (gate.at[:, cols], gate_c), (up.at[:, cols], up_c), (wg.at[:, cols], wg_c), (wu.at[:, cols], wu_c))
            return [pltpu.make_async_copy(src, dst.at[s], hs.at[s, k]) for k, (src, dst) in enumerate(moves)]

        for f in fetch_ff(jnp.int32(0)):
            f.start()
        got_resid = fetch(resid, dres)
        for f in got:
            f.wait()
        h2_t[...] = h2_v[...].T
        dhid[...] = jnp.zeros_like(dhid)
        free_slot, begun, after = ([], []), ([], []), []
        for q in range(n_ff):
            for k in range(2):
                free_slot[k].append(note(lambda: e1(len(units) - 1)))
                unit(1, 2 * q + k, g_ff.at[(2 * q + k) % 4], 1 + k, pl.ds(q * UF, UF))
                begun[k].append([units[-1].begin])
            after.append(note(partial(tick, *PLAN[1 + q])))

        def ff_block(q, _):
            s = q % 2

            @pl.when(q + 1 < n_ff)
            def _():
                for f in fetch_ff(q + 1):
                    f.start()

            for f in fetch_ff(q):
                f.wait()

            def act_tile(j, _):
                cols = lane(j, 256)
                g, u = gate_c[s, :, cols].astype(f32), up_c[s, :, cols].astype(f32)
                da = mm(dm_v[...], wd_c[s, lane(j, 256), :], 1, 1)
                sg = 1.0 / (1.0 + jnp.exp(-g))
                du_c[:, cols] = (da * (g * sg)).astype(bf16)
                dg_c[:, cols] = (da * u * (sg * (1.0 + g * (1.0 - sg)))).astype(bf16)
                return 0

            lax.fori_loop(0, UF // 256, act_tile, 0)
            for k, d in enumerate((dg_c, du_c)):
                at_block(q, free_slot[k])

                def ff_tile(j, _):
                    y = mm(h2_t[...], d[:, lane(j, 256)], 1, 0).astype(bf16)
                    g_ff[(2 * q + k) % 4, :, :, :, :, :, lane(j, 256)] = y.reshape(g_ff.shape[1:6] + (256,))
                    return 0

                lax.fori_loop(0, UF // 256, ff_tile, 0)
                at_block(q, begun[k])

            def hid_tile(j, _):
                cols = lane(j, 256)
                dhid[:, cols] += mm(dg_c[...], wg_c[s, cols, :], 1, 1) + mm(du_c[...], wu_c[s, cols, :], 1, 1)
                return 0

            lax.fori_loop(0, W // 256, hid_tile, 0)
            at_block(q, after)
            return 0

        lax.fori_loop(0, n_ff, ff_block, 0)
        while done[0] < len(units):
            e1()
        got_resid.wait()

        def second_norm(j, total):
            d, gg = norm_back(dres[block(j), :], gain2[...], dhid[block(j), :])
            d = dm_v[block(j), :].astype(f32) + d
            dres[block(j), :] = d
            drl[block(j), :] = d.astype(bf16)
            return total + gg

        g2 = lax.fori_loop(0, T // RB, second_norm, jnp.zeros((1, W), f32))
        for k in range(W // 128):
            vec[W // 128 + k:W // 128 + k + 1, :] = g2[:, k * 128:(k + 1) * 128]

    def out_grad(drl, att_c, att_t, g_out):
        pieces = [fetch(attended.at[:, pl.ds(0, QT)], att_c.at[0])]
        for i in range(A):
            if i + 1 < A:
                pieces.append(fetch(attended.at[:, pl.ds((i + 1) * QT, QT)], att_c.at[(i + 1) % 2]))
            pieces[i].wait()
            att_t[...] = att_c[i % 2].T

            def out_tile(j, _):
                y = mm(att_t[...], drl[:, lane(j, UO)], 1, 0).astype(bf16)
                g_out[j, i] = y.reshape(g_out.shape[2:])
                return 0

            lax.fori_loop(0, n_out, out_tile, 0)
        for u in range(n_out):
            unit(2, u, g_out.at[u], 3, pl.ds(u * UO, UO)).begin()
        while done[0] < len(units):
            e1()
        tick(*PLAN[7])

    def attention(drl, dq, dkr, dvl, dk, dv, ks_c, vs_c, q_c, att_c, wo_c, kr_v, v_v):
        others = [fetch(k_rot, kr_v), fetch(v, v_v)]
        pair = lambda j: lane(j, heads * HEAD_SIZE)

        def head_copies(j):
            s = j % 2
            moves = [(ks.at[:, lane(j, HEAD_SIZE)], ks_c), (vs.at[:, lane(j, HEAD_SIZE)], vs_c), (q_rot.at[pair(j), :], q_c),
                     (attended.at[:, pair(j)], att_c), (wo.at[pair(j), :], wo_c)]
            return [pltpu.make_async_copy(src, dst.at[s], hs.at[s, k]) for k, (src, dst) in enumerate(moves)]

        for q in head_copies(jnp.int32(0)):
            q.start()
        for q in others:
            q.wait()
        scale = HEAD_SIZE ** -0.5
        plus = lambda p, q: q if p is None else p + q

        def head(j, gain_grad):
            @pl.when(j + 1 < KEY_VALUE_HEADS)
            def _():
                for q in head_copies(j + 1):
                    q.start()

            for q in head_copies(j):
                q.wait()
            at = j % 2
            kl = lane(j, HEAD_SIZE)
            kb, vb_ = ks_c[at], vs_c[at]
            dkp = dvp = dks = dvs = None
            do_pair = mm(drl[...], wo_c[at], 1, 1)
            out_pair = att_c[at].astype(f32)
            for g in range(heads):
                sl = slice(g * HEAD_SIZE, (g + 1) * HEAD_SIZE)
                q = q_c[at, sl, :]
                do = do_pair[:, sl].astype(bf16)
                delta = jnp.sum((do.astype(f32) * out_pair[:, sl]).T, axis=0, keepdims=True)
                log_total = lse[j, g:g + 1, :]
                parts = []
                for suffix in range(2):
                    part = slice(rows, None) if suffix else slice(0, rows)
                    qp, dop, lp, dp = q[:, part], do[part], log_total[:, part], delta[:, part]
                    pieces = [(kb, vb_, None if suffix else past[...])]
                    if suffix:
                        pieces.append((kr_v[rows:, kl], v_v[rows:, kl], inside[...]))
                    total = None
                    for i, (kk, vv, bias) in enumerate(pieces):
                        s = mm(kk, qp, 1, 0) * (scale * LOG2E) - lp
                        p = jnp.exp2(s if bias is None else s + bias)
                        ds = (p * (mm(vv, dop, 1, 1) - dp)).astype(bf16)
                        gv, gk = mm(p.astype(bf16), dop, 1, 0), mm(ds, qp, 1, 1)
                        total = plus(total, mm(kk, ds, 0, 0))
                        if i:
                            dks, dvs = plus(dks, gk), plus(dvs, gv)
                        else:
                            dkp, dvp = plus(dkp, gk), plus(dvp, gv)
                    parts.append(total)
                d = jnp.concatenate(parts, axis=1) * scale
                m = HEAD_SIZE // 2
                cs, sn = cos[...], sin[...]
                dy = jnp.concatenate([d[:m] * cs + d[m:] * sn, d[m:] * cs - d[:m] * sn], axis=0)
                qf = q.astype(f32)
                u = jnp.concatenate([qf[:m] * cs + qf[m:] * sn, qf[m:] * cs - qf[:m] * sn], axis=0) / q_gain[:, 0:1]
                gg = dy * u
                for t in range(T // 128):
                    gain_grad = gain_grad + gg[:, t * 128:(t + 1) * 128]
                dy = dy * q_gain[:, 0:1]
                dx = rs_q[j, g:g + 1, :] * (dy - u * jnp.mean(dy * u, axis=0, keepdims=True))
                dq[:, lane(j * heads + g, HEAD_SIZE)] = dx.T.astype(bf16)
            dk[:, :, :, kl] = (dkp * scale).astype(bf16).reshape(half, 2, rows, HEAD_SIZE)
            dv[:, :, :, kl] = dvp.astype(bf16).reshape(half, 2, rows, HEAD_SIZE)
            dkr[rows:, kl] = dks * scale
            dvl[rows:, kl] = dvs.astype(bf16)
            for k in range(KEY_VALUE_HEADS - 1):
                if PLAN[8 + k][0]:
                    pl.when(j == k)(partial(tick, *PLAN[8 + k]))
            return gain_grad

        gain_grad = lax.fori_loop(0, KEY_VALUE_HEADS, head, jnp.zeros((HEAD_SIZE, 128), f32))
        vec[2 * W // 128:2 * W // 128 + 1, :] = jnp.sum(gain_grad.T, axis=0, keepdims=True)
        grads = [dk, dv]
        home = lambda s, c: (rep, (first + s) * 2 + c)

        def to_sibling(i, d):
            return remote(grads[i].at[(slot + d) % half, 1 - c], r1.at[i, d], gs.at[i, d], gr.at[i, d], home(slot, 1 - c))

        order = list(range(1, half)) + [0]
        for d in order:
            for i in range(2):
                to_sibling(i, d).start()
        for d in order:
            for i in range(2):
                to_sibling(i, d).wait_recv()

                def one(j, _):
                    r1[i, d, block(j)] = (grads[i][(slot + d) % half, c, block(j)].astype(f32) + r1[i, d, block(j)].astype(f32)).astype(bf16)
                    return 0

                lax.fori_loop(0, rows // RB, one, 0)
                if d:
                    across(i, d).start()
        for d in order:
            for i in range(2):
                to_sibling(i, d).wait_send()
        tick(*PLAN[15])

    def across(i, d):
        return remote(r1.at[i, d], r2.at[i, d - 1], fs.at[i, d - 1], fr.at[i, d - 1], (rep, (first + (slot + d) % half) * 2 + c))

    def weights_back(dq, dkr, dvl, wq_c, wk_c, wv_c, hid_v, hid_t, kp_v, dkl, g_qkv, dhid):
        got = [fetch(hidden, hid_v), fetch(k_pre, kp_v)]
        tiles = W // 256
        fetch_q = lambda j: fetch(wq.at[pl.ds(j * 256, 256)], wq_c.at[j % 2])
        fetch_kv = lambda j, s: [fetch(wk.at[pl.ds(j * 256, 256)], wk_c.at[s]), fetch(wv.at[pl.ds(j * 256, 256)], wv_c.at[s])]
        q_tiles, kv_tiles = [fetch_q(0), fetch_q(1)], [fetch_kv(0, 0), fetch_kv(1, 1)]
        got[0].wait()
        hid_t[...] = hid_v[...].T
        got_x = fetch(x, hid_v)
        count = [0]
        first_ff = n_down
        while done[2] < first_ff + (QW + 2 * KW) // UF:
            tick()
        for f in units[first_ff:first_ff + (QW + 2 * KW) // UF]:
            f.sent(2)
        pl.semaphore_signal(free, inc=1, device_id=(rep, rank(a, b, 1 - c)), device_id_type=MESH)
        pl.semaphore_wait(free, 1)

        def grad_units(d, out, width):
            base, begun = count[0], []
            for u in range(width // UF):
                unit(1, 2 * n_ff + base + u, g_qkv.at[(base + u) % 4], out, pl.ds(u * UF, UF), base + u)
                begun.append([units[-1].begin])
            count[0] += width // UF

            def tile(t, _):
                u, j = t // (UF // 256), t % (UF // 256)
                y = mm(hid_t[...], d[:, lane(t, 256)], 1, 0).astype(bf16)
                g_qkv[(base + u) % 4, :, :, :, :, :, lane(j, 256)] = y.reshape(g_qkv.shape[1:6] + (256,))

                @pl.when(j == UF // 256 - 1)
                def _():
                    at_block(u, begun)

                return 0

            lax.fori_loop(0, width // 256, tile, 0)

        grad_units(dq, 4, QW)
        for u in range(QW // UF):
            e1()
        tick(*PLAN[16])
        got[1].wait()

        def key_head(part, j, total):
            lanes = lane(j, HEAD_SIZE)
            y = kp_v[part, lanes]
            r = lax.rsqrt(jnp.mean(y * y, axis=-1, keepdims=True) + norm_epsilon)
            u = y * r
            dy = dkr[part, lanes]
            dy = dy * cos_r[part, :] - pltpu.roll(dy, HEAD_SIZE // 2, 1) * sin_r[part, :]
            total = total + jnp.sum(dy * u, axis=0, keepdims=True)
            dy = dy * k_gain[...]
            dkl[part, lanes] = (r * (dy - u * jnp.mean(dy * u, axis=-1, keepdims=True))).astype(bf16)
            return total

        def first_norm(j, carry):
            total, square = carry
            d, gg = norm_back(hid_v[block(j), :].astype(f32), gain1[...], dhid[block(j), :])
            d = dres[block(j), :] + d
            dres[block(j), :] = d
            return total + gg, square + jnp.sum(valid[block(j), :] * d * d, axis=0, keepdims=True)

        ours, theirs = pl.ds(rows, T - rows), pl.ds(0, rows)
        gk = lax.fori_loop(0, KEY_VALUE_HEADS, partial(key_head, ours), jnp.zeros((1, HEAD_SIZE), f32))
        for j in range(tiles):
            cols = pl.ds(j * 256, 256)
            q_tiles[j].wait()
            for f in kv_tiles[j]:
                f.wait()
            dhid[:, cols] = mm(dq[...], wq_c[j % 2], 1, 1)
            dhid[ours, cols] += mm(dkl[ours, :], wk_c[j % 2], 1, 1) + mm(dvl[ours, :], wv_c[j % 2], 1, 1)
            if j + 2 < tiles:
                q_tiles.append(fetch_q(j + 2))
            kv_tiles.append(fetch_kv((j + 2) % tiles, j % 2))
        got_x.wait()
        zero = jnp.zeros((1, W), f32)
        g1, square = lax.fori_loop(rows // RB, T // RB, first_norm, (zero, zero))
        width = CONTINUATION_LEN // n
        step = max(width, 8)

        def pack(j, _):
            y = dres[pl.ds(pl.multiple_of(rows + j * step, step), step), :].astype(bf16)
            for k in range(step // width):
                i = j * (step // width) + k
                grad_src[i // n, i % n] = y[k * width:(k + 1) * width]
            return 0

        lax.fori_loop(0, S * CONTINUATION_LEN // step, pack, 0)
        begin_all(grad_spread)
        tick(*PLAN[17])
        for i in range(2):
            for d in range(1, half):
                across(i, d).wait_recv()

        def own_keys(j, _):
            t, u = r1[0, 0, block(j)].astype(f32), r1[1, 0, block(j)].astype(f32)
            for d in range(1, half):
                t, u = t + r2[0, d - 1, block(j)].astype(f32), u + r2[1, d - 1, block(j)].astype(f32)
            dkr[block(j), :] = t
            dvl[block(j), :] = u.astype(bf16)
            return 0

        lax.fori_loop(0, rows // RB, own_keys, 0)
        grad_units(dvl, 6, KW)
        gk = lax.fori_loop(0, KEY_VALUE_HEADS, partial(key_head, theirs), gk)
        vec[2 * W // 128 + 1:2 * W // 128 + 2, :] = gk
        grad_units(dkl, 5, KW)
        while done[0] < len(units):
            e1()
        tick(*PLAN[18])
        wait_all(grad_spread)
        reorder(grad_in, turned)
        begin_all(grad_collect)
        for j in range(tiles):
            cols, s = pl.ds(j * 256, 256), (tiles + j) % 2
            for f in kv_tiles[tiles + j]:
                f.wait()
            dhid[theirs, cols] += mm(dkl[theirs, :], wk_c[s], 1, 1) + mm(dvl[theirs, :], wv_c[s], 1, 1)
            if j + 2 < tiles:
                kv_tiles.append(fetch_kv(j + 2, s))
        tick(*PLAN[19])
        g1, square = lax.fori_loop(0, rows // RB, first_norm, (g1, square))
        for k in range(W // 128):
            vec[k:k + 1, :] = g1[:, k * 128:(k + 1) * 128]
        place = lax.broadcasted_iota(jnp.int32, (1, 128), 1)
        row = jnp.zeros((1, 128), f32)
        whole = lambda y: jnp.sum(jnp.sum(y, axis=0, keepdims=True), axis=1, keepdims=True)
        for k, y in enumerate((sums[0:1, :], sums[1:2, :], square, valid[...])):
            row = jnp.where(place == k, whole(y), row)
        vec[2 * W // 128 + 2:2 * W // 128 + 3, :] = row
        vec[2 * W // 128 + 3:, :] = jnp.zeros((vec.shape[0] - 2 * W // 128 - 3, 128), f32)

    pl.run_scoped(persistent, V((T, QW), bf16), V((T, KW), f32), V((T, KW), bf16))
    for i in range(2):
        for d in range(1, half):
            across(i, d).wait_send()

    prompt_out = fetch(dres.at[pl.ds(0, rows)], d_prompt)
    tick(2, 1)
    rounds = [(rep, rank(a, b, 1 - c)), (rep, rank(a, 1 - b, c))] + [flip(k) for k in range(bits)]
    vb[0] = vec[...]
    for k, to in enumerate(rounds):
        q = remote(vb.at[2 * k], vb.at[2 * k + 1], vs_.at[k], vr_.at[k], to)
        q.start()
        q.wait()
        vb[2 * k + 2] = vb[2 * k] + vb[2 * k + 1]
        tick(2, 1)
    last, nr = 2 * len(rounds), len(rounds)
    zs = [remote(vb.at[last], vz.at[a], vs_.at[nr + d - 1], vr_.at[nr + d - 1], (rep, rank((a + d) % A, b, c))) for d in range(1, A)]
    for q in zs:
        q.start()
    vz[a] = vb[last]
    for q in zs:
        q.wait()
    total = vz[0]
    for k in range(1, A):
        total = total + vz[k]
    vec[...] = total
    while done[5] < len(units):
        tick(lag=1)
    wait_all(grad_collect)
    prompt_out.wait()
    for f in units:
        f.end()


def backward(index, mixed, dm, h2, act, gate, up, resid, wd, wg, wu, wo, attended, q_rot, lse, rs_q, ks, vs, k_rot, v, k_pre, wq, wk, wv, hidden, x,
             k_gain, q_gain, cos_r, sin_r, cos, sin, past, inside, valid, gain1, gain2, sums, rows, n, R, cid):
    group = PROMPT_LENGTH // rows
    half, A, (T, W), bits = group // 2, n // 4, dm.shape, R.bit_length() - 1
    FW, QW, KW = act.shape[1], attended.shape[1], k_rot.shape[1]
    UD, UF, UO = 256, 512, 512
    S = mixed.shape[0]
    V, D = pltpu.VMEM, pltpu.SemaphoreType.DMA
    shape = jax.ShapeDtypeStruct
    vm, hbm, sm = pl.BlockSpec(memory_space=pltpu.VMEM), pl.BlockSpec(memory_space=pl.ANY), pl.BlockSpec(memory_space=pltpu.SMEM)
    rh = lambda w: w.shape[0] // (2 * n)
    out_shape = [shape((2, rh(w), w.shape[1]), bf16) for w in (wd, wg, wu, wo, wq, wk, wv)]
    vec_rows = 2 * W // 128 + 8
    out_shape += [shape((vec_rows, 128), f32), shape((rows, W), f32), shape(mixed.shape, bf16), shape(mixed.shape, bf16)]
    scratch = []
    for count, r, w in ((W // UD, rh(wd), UD), (2 * (FW // UF) + (QW + 2 * KW) // UF, rh(wg), UF), (W // UO, rh(wo), UO)):
        k0 = fold_split(r)
        k1 = max(r - k0, 8)
        landing = 2 * (FW // UF) if w == UF and r == rh(wg) else count
        scratch += [V((landing, A, 2, 2, r, w), bf16), V((count, A, 2, k0, w), bf16), V((count, A, 2, k1, w) if k0 < r else (1, 1, 1, 8, 128), bf16), V((count, A, r, w), bf16),
                    V((count, A - 1, r, w), bf16), V((count, bits, r, w), bf16), V((count, bits, r, w), bf16)]
    m = W // UD + 2 * (FW // UF) + (QW + 2 * KW) // UF + W // UO
    turned = (n, S) + mixed.shape[2:]
    kv = (2, half, rows, KW)
    scratch += [V(kv, bf16), V((2, max(half - 1, 1), rows, KW), bf16), V(turned, bf16), V(turned, bf16), V(mixed.shape, bf16), V(turned, bf16),
                V((2 * (2 + bits) + 1, vec_rows, 128), f32), V((A, vec_rows, 128), f32), V((T, W), f32)]
    scratch += [D((m,)), D((m,)), D((m, 2)), D((m, 2)), D((m, 2)), D((m, 2)), D((m, A - 1)), D((m, A - 1)), D((m, bits)), D((m, bits)), D((m, 2))]
    scratch += [D((2 * A + 5 * (FW // UF) + 32,)), D((2, 5)), D((2, half)), D((2, half)), D((2, max(half - 1, 1))), D((2, max(half - 1, 1))), D((4, n - 1)), D((4, n - 1)), D((4,)),
                D((2 + bits + A - 1,)), D((2 + bits + A - 1,)), pltpu.SemaphoreType.REGULAR]
    hbm_in = [mixed, dm, h2, act, gate, up, resid, wd, wg, wu, wo, attended, q_rot, lse, rs_q, ks, vs, k_rot, v, k_pre, wq, wk, wv, hidden, x]
    in_vmem = {13, 14}
    res = pl.pallas_call(
        partial(backward_kernel, n, R, group, UD, UF, UO),
        out_shape=out_shape,
        in_specs=[sm] + [vm if k in in_vmem else hbm for k in range(len(hbm_in))] + [vm] * 12,
        out_specs=[hbm] * 7 + [vm] + [hbm] * 3,
        scratch_shapes=scratch,
        compiler_params=pltpu.CompilerParams(collective_id=cid, has_side_effects=True, vmem_limit_bytes=63 << 20),
        name="backward",
    )(index, *hbm_in, k_gain, q_gain, cos_r, sin_r, cos, sin, past, inside, valid, gain1, gain2, sums)
    return [r.reshape(-1, r.shape[-1]) for r in res[:7]], res[7], res[8], res[9], res[10]


def per_device(
    prompt_rows,
    suffix_rows,
    assignment,
    lengths,
    attention_gain,
    query_weight,
    key_matrix,
    value_matrix,
    query_gain,
    key_norm_gain,
    out_weight,
    mlp_gain,
    gate_weight,
    up_weight,
    down_weight,
    prompt_cotangent,
    suffix_cotangent,
):
    n, R = lax.axis_size("fsdp"), lax.axis_size("rep")
    rank = lax.axis_index("fsdp")
    rows = prompt_rows.shape[0]
    suffix = suffix_rows.shape[0]
    S = suffix // CONTINUATION_LEN
    total = rows + suffix
    width = MODEL_WIDTH

    pad = lambda v: jnp.pad(v.astype(f32).reshape(-1), (0, 128 - v.size))
    tile = jnp.stack([pad(v) for v in (attention_gain, mlp_gain, query_gain, key_norm_gain, assignment, lengths)])
    tile = jnp.pad(tile, ((0, 2), (0, 0)))
    cut = lambda v: v.reshape(S, n, CONTINUATION_LEN // n, width)
    w_key, w_value, w_query, tiles, staged = gather(key_matrix, value_matrix, query_weight, tile, cut(suffix_rows), n, 0)
    gain_first = tiles[:, 0, : attention_gain.size].reshape(-1)
    gain_second = tiles[:, 1, : mlp_gain.size].reshape(-1)
    query_scale = tiles[:, 2, : query_gain.size].reshape(-1)
    key_scale = tiles[:, 3, : key_norm_gain.size].reshape(-1)

    owner = tiles[:, 4, :S].reshape(-1).astype(jnp.int32) // CONT
    slot_count = n * S
    ids = jnp.arange(slot_count, dtype=jnp.int32)
    ahead = (owner[None, :] < owner[:, None]) | ((owner[None, :] == owner[:, None]) & (ids[None, :] < ids[:, None]))
    place = jnp.sum(ahead.astype(jnp.int32), axis=1)
    hits = place[None, :] == ids[:, None]
    order = jnp.sum(jnp.where(hits, ids[None, :], 0), axis=1)
    slot_lengths = jnp.sum(jnp.where(hits, tiles[:, 5, :S].reshape(-1).astype(jnp.int32)[None, :], 0), axis=1)
    own_lengths = lax.dynamic_slice_in_dim(slot_lengths, rank * S, S)

    prompt_place = (rank * rows) % PROMPT_LENGTH + jnp.arange(rows, dtype=jnp.int32)
    suffix_place = jnp.arange(suffix, dtype=jnp.int32) % CONTINUATION_LEN
    suffix_slot = jnp.arange(suffix, dtype=jnp.int32) // CONTINUATION_LEN
    length_rows = jnp.repeat(own_lengths, CONTINUATION_LEN)
    suffix_valid = suffix_place < length_rows
    valid_rows = jnp.concatenate([jnp.ones((rows,), f32), suffix_valid.astype(f32)])
    token_positions = jnp.concatenate([prompt_place, PROMPT_LENGTH + suffix_place]).astype(f32)
    half = HEAD_SIZE // 2
    inverse = rope_theta ** (jnp.arange(half, dtype=f32) * (-2.0 / HEAD_SIZE))
    angles_t = inverse[:, None] * token_positions[None, :]
    cos_t, sin_t = jnp.cos(angles_t), jnp.sin(angles_t)
    cos_r, sin_r = cos_t.T, sin_t.T
    cos_rows = jnp.concatenate([cos_r, cos_r], axis=1)
    sin_rows = jnp.concatenate([-sin_r, sin_r], axis=1)
    past = jnp.where(jnp.arange(PROMPT_LENGTH, dtype=jnp.int32)[:, None] <= prompt_place[None, :], 0.0, masked_score).astype(f32)
    inside = jnp.where(
        (suffix_slot[:, None] == suffix_slot[None, :]) & (suffix_place[:, None] <= suffix_place[None, :]) & suffix_valid[:, None], 0.0, masked_score
    ).astype(f32)

    key_gain_row = key_scale.reshape(1, HEAD_SIZE)
    query_gain_col = jnp.broadcast_to(query_scale[:, None], (HEAD_SIZE, 128))
    (
        w_out, w_gate, w_up, w_down, moved_cotangent, gate_low, up_low, rows_low, hidden, attended, query_rot, key_pre, key_rot, values,
        prompt_keys, prompt_values, residual, hidden_two, act, mixed_low, lse, query_rs, sums,
    ) = forward(
        order, prompt_rows, staged, cut(suffix_cotangent), w_key, w_value, w_query, [out_weight, gate_weight, up_weight, down_weight], key_gain_row,
        query_gain_col, cos_rows, sin_rows, cos_t, sin_t, past, inside, valid_rows[:, None], gain_first[None, :], gain_second[None, :], n, 2,
    )
    moved_cotangent = moved_cotangent.reshape(suffix, width)
    d_mixed_low = jnp.concatenate([prompt_cotangent, moved_cotangent], 0) * valid_rows[:, None].astype(bf16)
    shards, vec_sum, prompt_grad, suffix_mixed, suffix_grad = backward(
        place, cut(mixed_low[rows:]), d_mixed_low, hidden_two, act, gate_low, up_low, residual, w_down, w_gate, w_up, w_out, attended, query_rot, lse, query_rs,
        prompt_keys, prompt_values, key_rot, values, key_pre, w_query, w_key, w_value, hidden, rows_low, key_gain_row, query_gain_col,
        cos_rows, sin_rows, cos_t, sin_t, past, inside, valid_rows[:, None], gain_first[None, :], gain_second[None, :], sums, rows, n, R, 3,
    )
    suffix_mixed, suffix_grad = suffix_mixed.reshape(suffix, width), suffix_grad.reshape(suffix, width)
    g_down, g_gate, g_up, g_out, g_query, g_key, g_value = [g.astype(f32) for g in shards]
    flat = vec_sum.reshape(-1)

    def mine(first, size, part):
        return lax.dynamic_slice_in_dim(flat[first : first + size], rank * part, part)

    g_first = mine(0, width, attention_gain.size)
    g_second = mine(width, width, mlp_gain.size)
    g_query_gain = mine(2 * width, HEAD_SIZE, query_gain.size)
    g_key_gain = mine(2 * width + HEAD_SIZE, HEAD_SIZE, key_norm_gain.size)
    stat_sums = flat[2 * width + 2 * HEAD_SIZE : 2 * width + 2 * HEAD_SIZE + 4]
    token_norms = jnp.sqrt(stat_sums[:3] / (stat_sums[3] * width))
    return (
        mixed_low[:rows],
        suffix_mixed,
        prompt_grad,
        suffix_grad.astype(f32),
        g_first,
        g_query,
        g_key,
        g_value,
        g_query_gain,
        g_key_gain,
        g_out,
        g_second,
        g_gate,
        g_up,
        g_down,
        token_norms,
    )


def solution(mesh):
    placed = (
        P(("rep", "fsdp"), None),
        P(("rep", "fsdp"), None),
        P("rep", "fsdp"),
        P("rep", "fsdp"),
        P("fsdp"),
        P("fsdp", None),
        P("fsdp", None),
        P("fsdp", None),
        P("fsdp"),
        P("fsdp"),
        P("fsdp", None),
        P("fsdp"),
        P("fsdp", None),
        P("fsdp", None),
        P("fsdp", None),
        P(("rep", "fsdp"), None),
        P(("rep", "fsdp"), None),
    )
    return jax.shard_map(
        per_device,
        mesh=mesh,
        in_specs=placed,
        out_specs=(
            P(("rep", "fsdp"), None),
            P(("rep", "fsdp"), None),
            P(("rep", "fsdp"), None),
            P(("rep", "fsdp"), None),
            P("fsdp"),
            P("fsdp", None),
            P("fsdp", None),
            P("fsdp", None),
            P("fsdp"),
            P("fsdp"),
            P("fsdp", None),
            P("fsdp"),
            P("fsdp", None),
            P("fsdp", None),
            P("fsdp", None),
            P(),
        ),
        check_vma=False,
    )
```

```python
from functools import partial

import jax
import jax.numpy as jnp
from jax import lax
from jax.experimental import pallas as pl
from jax.experimental.pallas import tpu as pltpu
from jax.sharding import PartitionSpec as P

MODEL_WIDTH = 1024
QUERY_HEADS = 16
KEY_VALUE_HEADS = 8
HEAD_SIZE = 128
PROMPT_LENGTH = 1024
CONT = 8
CONTINUATION_LEN = 128

norm_epsilon = 1e-06
rope_theta = 1000000.0
masked_score = -1e30
MESH = pl.DeviceIdType.MESH
bf16 = jnp.bfloat16
f32 = jnp.float32

def position(n):
    rep = lax.axis_index("rep")
    rank = lax.axis_index("fsdp")
    return rep, rank // 4, (rank // 2) % 2, rank % 2


def meet(peers):
    barrier = pltpu.get_barrier_semaphore()
    for p in peers:
        pl.semaphore_signal(barrier, inc=1, device_id=p, device_id_type=MESH)
    pl.semaphore_wait(barrier, len(peers))


def remote(src, dst, send, recv, to):
    return pltpu.make_async_remote_copy(src, dst, send, recv, device_id=to, device_id_type=MESH)


def add_rows(count, out, first, second, step=None):
    def one(j, _):
        o = out(j)
        total = first(j)[...].astype(jnp.float32)
        for s in second:
            total = total + s(j)[...].astype(jnp.float32)
        o[...] = total.astype(o.dtype)
        return 0
    lax.fori_loop(0, count, one, 0)


LOG2E = 1.4426950408889634


def mm(x, y, cx, cy):
    return lax.dot_general(x, y, (((cx,), (cy,)), ((), ())), preferred_element_type=f32)


class Ring:
    def __init__(self, n, own, full, cols, sems, i, x_first):
        zs, zr, ss, sr, ls = sems
        A = n // 4
        rep, a, b, c = position(n)
        h = rep % 2
        every = slice(None)
        at = lambda *ix: full.at[(*ix, every, cols)]
        rank = lambda a, b, c: (a * 2 + b) * 2 + c
        ydev, xdev, cdev = (rep, rank(a, 1 - b, c)), (rep + 1 - 2 * h, rank(a, b, c)), (rep, rank(a, b, 1 - c))
        same = lambda ref, k, to: remote(ref, ref, ss.at[i, k], sr.at[i, k], to)
        mine = own.at[h, :, cols]
        self.local = lambda: [pltpu.make_async_copy(mine, at(a, b, c, h), ls.at[i])]
        self.along = lambda: [remote(mine, at(a, b, c, h), zs.at[i, d - 1], zr.at[i, d - 1], (rep, rank((a + d) % A, b, c))) for d in range(1, A)]
        self.second = lambda: [same(at(every, b, c, h), 0, xdev if x_first else ydev)]
        self.third = lambda: [same(at(every, b, c, every), 1, ydev) if x_first else same(at(every, every, c, h), 1, xdev)]
        self.last = lambda: [same(at(every, every, c, every), 2, cdev)]

    def begin(self):
        for q in self.local() + self.along():
            q.start()

    def turn(self, arrived, started):
        for q in arrived():
            q.wait_recv()
        for q in started():
            q.start()

    def step(self, k):
        if k == 0:
            for q in self.local():
                q.wait()
            self.turn(self.along, self.second)
        elif k == 1:
            self.turn(self.second, self.third)
        elif k == 2:
            self.turn(self.third, self.last)
        else:
            for q in self.last():
                q.wait_recv()

    def end(self):
        for q in self.along() + self.second() + self.third() + self.last():
            q.wait_send()


class Ticker:
    def __init__(self, rings, arrived=lambda i: None):
        self.rings, self.arrived, self.done, self.noted = rings, arrived, [0] * 5, None

    def run(self, f):
        f() if self.noted is None else self.noted.append(f)

    def note(self, f):
        self.noted = []
        f()
        noted, self.noted = self.noted, None
        return noted

    def begin(self, count):
        for r in self.rings[self.done[0]:self.done[0] + max(count, 0)]:
            self.run(r.begin)
            self.done[0] += 1

    def __call__(self, count=1, lag=1):
        for _ in range(count):
            before = list(self.done)
            for k in range(1, 5):
                i = self.done[k]
                if i < len(self.rings) and before[k - 1] - i >= lag:
                    self.run(partial(self.rings[i].step, k - 1))
                    self.done[k] += 1
                    if k == 1:
                        self.begin(self.done[1] + ALONG - self.done[0])
                    if k == 4:
                        self.arrived(i)

    def until(self, count):
        while self.done[4] < count:
            before = list(self.done)
            self(1, 2)
            if before == self.done:
                self()


ALONG = 2


def slot_spread(n, src, dst, sems, k, where):
    s, r, l = sems
    rep, me = where
    own = pltpu.make_async_copy(src.at[:, me], dst.at[me], l.at[k])
    return own, [remote(src.at[:, (me + d) % n], dst.at[me], s.at[k, d - 1], r.at[k, d - 1], (rep, (me + d) % n)) for d in range(1, n)]


def slot_collect(n, src, dst, sems, k, where):
    s, r, l = sems
    rep, me = where
    own = pltpu.make_async_copy(src.at[me], dst.at[:, me], l.at[k])
    return own, [remote(src.at[(me + d) % n], dst.at[:, me], s.at[k, d - 1], r.at[k, d - 1], (rep, (me + d) % n)) for d in range(1, n)]


def begin_all(pair):
    pair[0].start()
    for q in pair[1]:
        q.start()


def wait_all(pair):
    pair[0].wait()
    for q in pair[1]:
        q.wait()


def gather_kernel(n, CB, *refs):
    so, sk, sv, tile, pieces, wq, wk, wv, tiles, staged, zs, zr, ss, sr, ls, ts, tr, ps, pr, pls = refs
    rep, a, b, c = position(n)
    me = (a * 2 + b) * 2 + c
    h = rep % 2
    meet([(rep, (me + d) % n) for d in range(1, n)] + [(rep + 1 - 2 * h, me)])
    blocks = []
    for own, full in ((sk, wk), (sv, wv), (so, wq)):
        blocks += [(own, full, pl.ds(q * CB, CB)) for q in range(full.shape[-1] // CB)]
    rings = [Ring(n, own, full, cols, (zs, zr, ss, sr, ls), i, i % 2 == 0) for i, (own, full, cols) in enumerate(blocks)]
    tick = Ticker(rings)
    share = [remote(tile, tiles.at[me], ts.at[d - 1], tr.at[d - 1], (rep, (me + d) % n)) for d in range(1, n)]
    rows = slot_spread(n, pieces, staged, (ps, pr, pls), 0, (rep, me))
    for q in share:
        q.start()
    tiles[me] = tile[...]
    tick.begin(ALONG)
    begin_all(rows)
    tick.until(len(rings))
    for q in share:
        q.wait()
    wait_all(rows)
    for r in rings:
        r.end()


def gather(wk, wv, wq, tile, slots, n, cid):
    A, CB = n // 4, 512
    halves = [w.reshape(2, w.shape[0] // 2, w.shape[1]) for w in (wq, wk, wv)]
    m = sum(w.shape[1] for w in (wk, wv, wq)) // CB
    D = pltpu.SemaphoreType.DMA
    vm, hbm = pl.BlockSpec(memory_space=pltpu.VMEM), pl.BlockSpec(memory_space=pl.ANY)
    shape = jax.ShapeDtypeStruct
    res = pl.pallas_call(
        partial(gather_kernel, n, CB),
        out_shape=[shape((A, 2, 2) + w.shape, bf16) for w in halves] + [shape((n,) + tile.shape, f32), shape((n, slots.shape[0]) + slots.shape[2:], bf16)],
        in_specs=[hbm] * 3 + [vm] + [hbm],
        out_specs=[hbm] * 3 + [vm, hbm],
        scratch_shapes=[D((m, A - 1))] * 2 + [D((m, 3))] * 2 + [D((m,))] + [D((n - 1,))] * 2 + [D((1, n - 1))] * 2 + [D((1,))],
        compiler_params=pltpu.CompilerParams(collective_id=cid, has_side_effects=True),
        name="gather",
    )(*halves, tile, slots)
    w_query, w_key, w_value = [f.reshape(-1, f.shape[-1]) for f in res[:3]]
    return w_key, w_value, w_query, res[3], res[4]


def forward_kernel(n, group, *refs):
    it = iter(refs)
    take = lambda count: [next(it) for _ in range(count)]
    index, prompt, staged, cot, wk_h, wv_h, wq_h, so, sg, su, sd, k_gain, q_gain, cos_r, sin_r, cos, sin, past, inside, valid, gain1, gain2 = take(22)
    wo, wg, wu, wd, moved, gate, up = take(7)
    outs = take(13)
    lse_out, rs_out, stats = take(3)
    x, hidden, attended, q_out, k_pre, k_out, v, ks, vs, resid, h2, act, mixed = bufs = take(13)
    wk, wv, wq, ordered, landed, cot_in, o_buf, g_buf, u_buf, d_buf, g_st, u_st = take(12)
    zs, zr, ss, sr, ls, lds, fs, fr, gs, gr, kls, ps, pr, pls, gos, outs_sem, ins_sem = take(17)
    rows = ks.shape[2]
    T, W = x.shape
    half = group // 2
    rep, a, b, c = position(n)
    me = (a * 2 + b) * 2 + c
    first, slot = (me // group) * half, (me // 2) % half
    h = rep % 2
    ins = [pltpu.make_async_copy(src, dst, ins_sem.at[k]) for k, (src, dst) in enumerate(((wk_h, wk), (wv_h, wv), (wq_h, wq)))]
    for q in ins:
        q.start()
    meet([(rep, (me + d) % n) for d in range(1, n)] + [(rep + 1 - 2 * h, me)])
    saves = {id(buf): pltpu.make_async_copy(buf, out, outs_sem.at[k]) for k, (buf, out) in enumerate(zip(bufs, outs))}

    def save(*which):
        for buf in which:
            saves[id(buf)].start()

    OB, GB = o_buf.shape[-1], g_buf.shape[-1]
    n_out, n_mlp = wo.shape[-1] // OB, wg.shape[-1] // GB
    blocks = [(so, wo, pl.ds(q * OB, OB), o_buf.at[q]) for q in range(n_out)]
    for q in range(n_mlp):
        blocks += [(sg, wg, pl.ds(q * GB, GB), g_buf.at[q % 2]), (su, wu, pl.ds(q * GB, GB), u_buf.at[q % 2])]
    blocks += [(sd, wd, pl.ds(q * OB, OB), d_buf.at[q]) for q in range(n_out)]
    m = len(blocks)
    rings = [Ring(n, own, full, cols, (zs, zr, ss, sr, ls), i, i % 2 == 0) for i, (own, full, cols, _) in enumerate(blocks)]

    def load(i):
        _, full, cols, buf = blocks[i]
        return pltpu.make_async_copy(full.at[:, :, :, :, :, cols], buf, lds.at[i])

    used, late = [0], []

    def arrived(i):
        q = (i - n_out) // 2 if n_out <= i < n_out + 2 * n_mlp else 0
        if q < used[0] + 2:
            tick.run(lambda: load(i).start())
        else:
            late.append(i)

    def release():
        used[0] += 1
        now, late[:] = [i for i in late if (i - n_out) // 2 < used[0] + 2], [i for i in late if (i - n_out) // 2 >= used[0] + 2]
        for i in now:
            tick.run(lambda i=i: load(i).start())

    tick = Ticker(rings, arrived)
    S = ordered.shape[1]

    def reorder(src, flat):
        def put(j, _):
            s = index[j]
            ordered[j // S, j % S] = src[s] if flat else src[s // S, s % S]
            return 0

        lax.fori_loop(0, n * S, put, 0)

    sems = (ps, pr, pls)
    reorder(staged, True)
    rows_in = slot_collect(n, ordered, landed, sems, 0, (rep, me))
    cot_spread = slot_spread(n, cot, cot_in, sems, 1, (rep, me))
    cot_collect = slot_collect(n, ordered, moved, sems, 2, (rep, me))
    begin_all(rows_in)
    tick.begin(ALONG)

    lane = lambda j, w: pl.ds(pl.multiple_of(j * w, w), w)
    heads = QUERY_HEADS // KEY_VALUE_HEADS
    pair = heads * HEAD_SIZE
    RB = 32
    block = lambda j: pl.ds(pl.multiple_of(j * RB, RB), RB)

    def norm(y, gain):
        return (y * lax.rsqrt(jnp.mean(y * y, axis=-1, keepdims=True) + norm_epsilon) * gain[...]).astype(bf16)

    def prompt_rows(j, _):
        y = prompt[block(j), :]
        x[block(j), :] = y
        hidden[block(j), :] = norm(y.astype(f32), gain1)
        return 0

    def kv_tile(part, j, _):
        kp = mm(hidden[part, :], wk[:, lane(j, 256)], 1, 0)
        k_pre[part, lane(j, 256)] = kp
        for g in range(2):
            y = kp[:, g * HEAD_SIZE:(g + 1) * HEAD_SIZE]
            y = y * lax.rsqrt(jnp.mean(y * y, axis=-1, keepdims=True) + norm_epsilon) * k_gain[...]
            k_out[part, lane(2 * j + g, HEAD_SIZE)] = (y * cos_r[part, :] + pltpu.roll(y, HEAD_SIZE // 2, 1) * sin_r[part, :]).astype(bf16)
        v[part, lane(j, 256)] = mm(hidden[part, :], wv[:, lane(j, 256)], 1, 0).astype(bf16)
        return 0

    lax.fori_loop(0, rows // RB, prompt_rows, 0)
    ins[0].wait()
    ins[1].wait()
    lax.fori_loop(0, wk.shape[1] // 256, partial(kv_tile, pl.ds(0, rows)), 0)
    parts = [(k_out, ks), (v, vs)]
    at = lambda s, c: (rep, (first + s) * 2 + c)
    mine = lambda i: parts[i][0].at[pl.ds(0, rows)]
    klocal = [pltpu.make_async_copy(mine(i), parts[i][1].at[slot, c], kls.at[i]) for i in range(2)]
    across = [remote(mine(i), parts[i][1].at[slot, c], fs.at[i, d - 1], fr.at[i, d - 1], at((slot + d) % half, c)) for i in range(2) for d in range(1, half)]
    sibling = [remote(mine(i), parts[i][1].at[slot, c], gs.at[i, 0], gr.at[i, 0], at(slot, 1 - c)) for i in range(2)]
    onward = []
    for i in range(2):
        for d in range(1, half):
            there = parts[i][1].at[(slot + half - d) % half, c]
            onward.append(remote(there, there, gs.at[i, d], gr.at[i, d], at(slot, 1 - c)))
    for q in across + sibling + klocal:
        q.start()
    tick()
    wait_all(rows_in)
    width = landed.shape[2]

    def slot_rows(j, _):
        s, p = j // (n * width // RB), j % (n * width // RB)
        k = RB // width
        if width % 8 == 0:
            y = landed[s, pl.ds(p * k, k)].astype(f32).reshape(RB, W)
        else:
            y = jnp.concatenate([landed[s, p * k + i].astype(f32) for i in range(k)], axis=0)
        at = pl.ds(pl.multiple_of(rows + j * RB, RB), RB)
        x[at, :] = y.astype(bf16)
        hidden[at, :] = norm(y, gain1)
        return 0

    lax.fori_loop(0, (T - rows) // RB, slot_rows, 0)
    lax.fori_loop(0, wk.shape[1] // 256, partial(kv_tile, pl.ds(rows, T - rows)), 0)
    tick()
    save(x, hidden, k_pre, k_out, v)
    ins[2].wait()

    def q_tile(j, _):
        qp = mm(hidden[...], wq[:, lane(j, pair)], 1, 0)
        for g in range(heads):
            y = qp[:, g * HEAD_SIZE:(g + 1) * HEAD_SIZE].T
            rs = lax.rsqrt(jnp.mean(y * y, axis=0, keepdims=True) + norm_epsilon)
            rs_out[j, g:g + 1, :] = rs
            y = y * rs * q_gain[:, 0:1]
            lo, hi = y[:HEAD_SIZE // 2], y[HEAD_SIZE // 2:]
            y = jnp.concatenate([lo * cos[...] - hi * sin[...], hi * cos[...] + lo * sin[...]], axis=0)
            q_out[lane(j * heads + g, HEAD_SIZE), :] = y.astype(bf16)
        for k, plan in FORWARD_PLAN[0]:
            pl.when(j == k)(partial(tick, *plan))
        return 0

    lax.fori_loop(0, KEY_VALUE_HEADS, q_tile, 0)
    begin_all(cot_spread)
    save(q_out)
    for q in across:
        q.wait_recv()
    for q in onward:
        q.start()
    tick(*FORWARD_PLAN[1])
    for q in klocal:
        q.wait()
    for q in sibling + onward:
        q.wait_recv()
    save(ks, vs)
    scale = HEAD_SIZE ** -0.5 * LOG2E

    def attend_head(j, _):
        kl = lane(j, HEAD_SIZE)
        kb = ks[:, :, :, kl].reshape(PROMPT_LENGTH, HEAD_SIZE)
        vb = vs[:, :, :, kl].reshape(PROMPT_LENGTH, HEAD_SIZE)
        for g in range(heads):
            ql = lane(j * heads + g, HEAD_SIZE)
            q = q_out[ql, :]
            p = jnp.exp2(mm(kb, q[:, :rows], 1, 0) * scale + past[...])
            total = jnp.sum(p, axis=0, keepdims=True)
            o = mm(vb, p.astype(bf16), 0, 0) / total
            attended[:rows, ql] = o.T.astype(bf16)
            lse_out[j, g:g + 1, :rows] = jnp.log2(total)
            p = jnp.exp2(mm(kb, q[:, rows:], 1, 0) * scale)
            r = jnp.exp2(mm(k_out[rows:, kl], q[:, rows:], 1, 0) * scale + inside[...])
            total = jnp.sum(p, axis=0, keepdims=True) + jnp.sum(r, axis=0, keepdims=True)
            o = (mm(vb, p.astype(bf16), 0, 0) + mm(v[rows:, kl], r.astype(bf16), 0, 0)) / total
            attended[rows:, ql] = o.T.astype(bf16)
            lse_out[j, g:g + 1, rows:] = jnp.log2(total)
        for k, plan in FORWARD_PLAN[2]:
            pl.when(j == k)(partial(tick, *plan))
        return 0

    lax.fori_loop(0, KEY_VALUE_HEADS, attend_head, 0)
    save(attended)
    wait_all(cot_spread)
    reorder(cot_in, False)
    begin_all(cot_collect)

    stats[...] = jnp.zeros_like(stats)

    def at_block(q, noted):
        for k, fs_ in enumerate(noted):
            if fs_:
                pl.when(q == k)(lambda fs_=fs_: [f() for f in fs_] and None)

    def arrived_block(q, first, full, width, buf):
        pltpu.make_async_copy(full.at[:, :, :, :, :, lane(q, width)], buf, lds.at[first]).wait()

    before_out = [tick.note(partial(tick.until, k + 1)) for k in range(n_out)]

    def out_block(q, _):
        at_block(q, before_out)
        arrived_block(q, q, wo, OB, o_buf.at[q])
        cols = lane(q, OB)
        y = x[:, cols].astype(f32) + mm(attended[...], o_buf[q].reshape(-1, OB), 1, 0)
        resid[:, cols] = y
        stats[1:2, :] += jnp.sum(valid[...] * y * y, axis=0, keepdims=True)
        return 0

    lax.fori_loop(0, n_out, out_block, 0)

    def norm_rows(j, _):
        h2[block(j), :] = norm(resid[block(j), :], gain2)
        return 0

    lax.fori_loop(0, T // RB, norm_rows, 0)
    save(resid, h2)
    saved = lambda q: [pltpu.make_async_copy(g_st.at[q % 2], gate.at[:, lane(q, GB)], gos.at[q % 2, 0]),
                       pltpu.make_async_copy(u_st.at[q % 2], up.at[:, lane(q, GB)], gos.at[q % 2, 1])]
    before_mlp, after_mlp = [], []
    for k in range(n_mlp):
        before_mlp.append(tick.note(partial(tick.until, n_out + 2 * k + 2)))
        after_mlp.append(tick.note(release))

    def mlp_block(q, _):
        at_block(q, before_mlp)
        arrived_block(q, n_out + 2 * q, wg, GB, g_buf.at[q % 2])
        arrived_block(q, n_out + 2 * q + 1, wu, GB, u_buf.at[q % 2])

        @pl.when(q >= 2)
        def _():
            for s in saved(q - 2):
                s.wait()

        def mlp_tile(j, _):
            g = mm(h2[...], g_buf[q % 2, :, :, :, :, :, lane(j, 256)].reshape(-1, 256), 1, 0)
            u = mm(h2[...], u_buf[q % 2, :, :, :, :, :, lane(j, 256)].reshape(-1, 256), 1, 0)
            g_st[q % 2, :, lane(j, 256)] = g.astype(bf16)
            u_st[q % 2, :, lane(j, 256)] = u.astype(bf16)
            act[:, lane(q * (GB // 256) + j, 256)] = (g / (1.0 + jnp.exp(-g)) * u).astype(bf16)
            return 0

        lax.fori_loop(0, GB // 256, mlp_tile, 0)
        at_block(q, after_mlp)
        for s in saved(q):
            s.start()
        return 0

    lax.fori_loop(0, n_mlp, mlp_block, 0)
    save(act)
    before_down = [tick.note(partial(tick.until, n_out + 2 * n_mlp + k + 1)) for k in range(n_out)]

    def down_block(q, _):
        at_block(q, before_down)
        arrived_block(q, n_out + 2 * n_mlp + q, wd, OB, d_buf.at[q])
        cols = lane(q, OB)
        y = resid[:, cols] + mm(act[...], d_buf[q].reshape(-1, OB), 1, 0)
        mixed[:, cols] = y.astype(bf16)
        stats[0:1, :] += jnp.sum(valid[...] * y * y, axis=0, keepdims=True)
        return 0

    lax.fori_loop(0, n_out, down_block, 0)
    save(mixed)
    for q in range(max(0, n_mlp - 2), n_mlp):
        for s in saved(jnp.int32(q)):
            s.wait()
    wait_all(cot_collect)
    for q in across + sibling + onward:
        q.wait_send()
    for r in rings:
        r.end()
    for q in saves.values():
        q.wait()


FORWARD_PLAN = (tuple((j, (1, 2)) for j in (1, 3, 5, 7)), (2, 2), tuple((j, (1, 2)) for j in range(8)))


def forward(index, prompt, staged, cot, wk, wv, wq, shards, k_gain, q_gain, cos_r, sin_r, cos, sin, past, inside, valid, gain1, gain2, n, cid):
    rows, W = prompt.shape
    S = staged.shape[1]
    T = rows + S * CONTINUATION_LEN
    group = PROMPT_LENGTH // rows
    half, A = group // 2, n // 4
    halves = [s.reshape(2, s.shape[0] // 2, s.shape[1]) for s in shards]
    flat = staged.reshape((-1,) + staged.shape[2:])
    QW, KW, FW = wq.shape[1], wk.shape[1], shards[1].shape[1]
    D, V = pltpu.SemaphoreType.DMA, pltpu.VMEM
    shape = jax.ShapeDtypeStruct
    small = shape((KEY_VALUE_HEADS, 2, T), f32)
    keys = ((half, 2, rows, KW), bf16)
    kept = [((T, W), bf16), ((T, W), bf16), ((T, QW), bf16), ((QW, T), bf16), ((T, KW), f32), ((T, KW), bf16), ((T, KW), bf16), keys, keys,
            ((T, W), f32), ((T, W), bf16), ((T, FW), bf16), ((T, W), bf16)]
    out_shape = [shape((A, 2, 2) + s.shape, bf16) for s in halves] + [shape((S, n) + staged.shape[2:], bf16), shape((T, FW), bf16), shape((T, FW), bf16)]
    out_shape += [shape(*k) for k in kept] + [small, small, shape((8, 256), f32)]
    vm, hbm, sm = pl.BlockSpec(memory_space=pltpu.VMEM), pl.BlockSpec(memory_space=pl.ANY), pl.BlockSpec(memory_space=pltpu.SMEM)
    OB, GB = 256, 512
    n_out, n_mlp = W // OB, FW // GB
    m = 2 * n_out + 2 * n_mlp
    buf = lambda i, k, w: V((k, A, 2, 2) + halves[i].shape[:2] + (w,), bf16)
    res = pl.pallas_call(
        partial(forward_kernel, n, group),
        out_shape=out_shape,
        in_specs=[sm, vm, vm, hbm] + [hbm] * 7 + [vm] * 11,
        out_specs=[hbm] * 20 + [vm] * 3,
        scratch_shapes=[V(*k) for k in kept] + [V(wk.shape, bf16), V(wv.shape, bf16), V(wq.shape, bf16), V(staged.shape, bf16), V((S, n) + staged.shape[2:], bf16),
            V(staged.shape, bf16), buf(0, n_out, OB), buf(1, 2, GB), buf(2, 2, GB), buf(3, n_out, OB), V((2, T, GB), bf16), V((2, T, GB), bf16)]
        + [D((m, A - 1))] * 2 + [D((m, 3))] * 2 + [D((m,))] * 2 + [D((2, max(half - 1, 1)))] * 2 + [D((2, half))] * 2 + [D((2,))]
        + [D((3, n - 1))] * 2 + [D((3,)), D((2, 2)), D((13,)), D((3,))],
        compiler_params=pltpu.CompilerParams(collective_id=cid, has_side_effects=True, vmem_limit_bytes=63 << 20),
        name="forward",
    )(index, prompt, flat, cot, wk, wv, wq, *halves, k_gain, q_gain, cos_r, sin_r, cos, sin, past, inside, valid, gain1, gain2)
    res = list(res)
    for i, s in enumerate(shards):
        res[i] = res[i].reshape(-1, s.shape[1])
    for i in (14, 15):
        res[i] = res[i].reshape(PROMPT_LENGTH, KW)
    return res


PLAN = ((3, 8), (1, 8), (2, 3), (2, 3), (5, 5), (2, 4), (4, 5), (1, 3), (6, 8), (1, 1), (2, 8), (2, 3), (6, 8), (3, 1), (0, 2), (3, 1), (2, 6), (1, 1), (3, 2), (6, 6))


class Fold:
    def __init__(self, n, R, where, g, bufs, out, cols, sems, i):
        self.bufs, self.k, self.landing = bufs
        self.waited = set()
        self.g, self.out, self.cols, self.i, self.sems = g, out, cols, i, sems
        self.A, self.bits = n // 4, R.bit_length() - 1
        self.rep, self.a, self.b, self.c, self.h = where
        self.rh = self.bufs[0].shape[-2]
        self.k0 = fold_split(self.rh)

    b1 = property(lambda self: self.bufs[0].at[self.landing])
    b2y, b2x, b3, b4, s4, b5 = [property(lambda self, j=j: self.bufs[j].at[self.k]) for j in range(1, 7)]

    def device(self, da=0, db=0, dc=0, bit=None):
        rep, a, b, c = self.rep, self.a, self.b, self.c
        if bit is not None:
            rep = rep + (1 << bit) - 2 * (1 << bit) * ((rep // (1 << bit)) % 2)
        return (rep, (((a + da) % self.A) * 2 + (1 - b if db else b)) * 2 + (1 - c if dc else c))

    @property
    def ydev(self):
        return self.device(db=1)

    @property
    def xdev(self):
        return self.device(bit=0)

    @property
    def cdev(self):
        return self.device(dc=1)

    def zdev(self, d):
        return self.device(da=d)

    def flip(self, bit):
        return self.device(bit=bit)

    def hop(self, k):
        i, a, b, c, h, k0, rh = self.i, self.a, self.b, self.c, self.h, self.k0, self.rh
        s1s, s1r, s2s, s2r, s3s, s3r, s4s, s4r, s5s, s5r, _ = self.sems
        lo, hi = pl.ds(0, k0), pl.ds(k0, rh - k0)
        if k == 1:
            return [remote(self.g.at[:, :, 1 - c], self.b1, s1s.at[i], s1r.at[i], self.cdev)]
        if k == 2:
            q = [remote(self.b1.at[:, 1 - b, :, lo], self.b2y, s2s.at[i, 0], s2r.at[i, 0], self.ydev)]
            if k0 < rh:
                q.append(remote(self.b1.at[:, :, 1 - h, hi], self.b2x, s2s.at[i, 1], s2r.at[i, 1], self.xdev))
            return q
        if k == 3:
            q = [remote(self.b2y.at[:, 1 - h], self.b3.at[:, lo], s3s.at[i, 0], s3r.at[i, 0], self.xdev)]
            if k0 < rh:
                q.append(remote(self.b2x.at[:, 1 - b], self.b3.at[:, hi], s3s.at[i, 1], s3r.at[i, 1], self.ydev))
            return q
        if k == 4:
            return [remote(self.b3.at[(a + d) % self.A], self.b4.at[d - 1], s4s.at[i, d - 1], s4r.at[i, d - 1], self.zdev(d)) for d in range(1, self.A)]
        last = self.bits - 1
        return [remote(self.s4.at[last], self.b5.at[last], s5s.at[i, last], s5r.at[i, last], self.xdev)]

    def put(self, k):
        last = self.bits - 1
        half = self.h if k == 0 else 1 - self.h
        return pltpu.make_async_copy((self.s4 if k == 0 else self.b5).at[last], self.out.at[half, :, self.cols], self.sems[-1].at[self.i, k])

    def begin(self):
        for q in self.hop(1):
            q.start()

    def arrive(self, k):
        for q in self.hop(k):
            q.wait_recv()

    def go(self, k):
        for q in self.hop(k):
            q.start()

    def step(self, k):
        a, b, c, h, k0, rh = self.a, self.b, self.c, self.h, self.k0, self.rh
        self.arrive(k)
        lo, hi = pl.ds(0, k0), pl.ds(k0, rh - k0)
        if k == 1:
            for q in self.hop(1):
                q.wait_send()
            view = lambda ref: lambda j: ref.at[j // 4, (j // 2) % 2, j % 2]
            add_rows(self.A * 4, view(self.b1), view(self.b1), [lambda j: self.g.at[j // 4, (j // 2) % 2, c, j % 2]])
            return
        elif k == 2:
            view = lambda ref: lambda j: ref.at[j // 2, j % 2]
            add_rows(self.A * 2, view(self.b2y), view(self.b2y), [lambda j: self.b1.at[j // 2, b, j % 2, lo]])
            if k0 < rh:
                add_rows(self.A * 2, view(self.b2x), view(self.b2x), [lambda j: self.b1.at[j // 2, j % 2, h, hi]])
        elif k == 3:
            view = lambda part: lambda j: self.b3.at[j, part]
            add_rows(self.A, view(lo), view(lo), [lambda j: self.b2y.at[j, h]])
            if k0 < rh:
                add_rows(self.A, view(hi), view(hi), [lambda j: self.b2x.at[j, b]])
        elif k == 4:
            add_rows(1, lambda j: self.s4.at[0], lambda j: self.b3.at[a], [lambda j, d=d: self.b4.at[d] for d in range(self.A - 1)])
            s5s, s5r = self.sems[8:10]
            for r in range(self.bits - 1):
                q = remote(self.s4.at[r], self.b5.at[r], s5s.at[self.i, r], s5r.at[self.i, r], self.flip(r + 1))
                q.start()
                q.wait()
                add_rows(1, lambda j, r=r: self.s4.at[r + 1], lambda j, r=r: self.s4.at[r], [lambda j, r=r: self.b5.at[r]])
            self.put(0).start()
        else:
            self.put(1).start()
            return
        self.go(k + 1)

    def sent(self, k):
        if k not in self.waited:
            self.waited.add(k)
            for q in self.hop(k):
                q.wait_send()

    def end(self):
        for k in range(2, 6):
            self.sent(k)
        self.put(0).wait()
        self.put(1).wait()


def fold_split(rh):
    if (rh // 2) % 16 == 0:
        return rh // 2
    return rh // 32 * 16 if rh >= 32 else rh


def backward_kernel(n, R, group, UD, UF, UO, *refs):
    it = iter(refs)
    take = lambda count: [next(it) for _ in range(count)]
    index, mixed, dm, h2, act, gate, up, resid, wd, wg, wu, wo, attended, q_rot, lse, rs_q, ks, vs, k_rot, v, k_pre, wq, wk, wv, hidden, x = take(26)
    k_gain, q_gain, cos_r, sin_r, cos, sin, past, inside, valid, gain1, gain2, sums = take(12)
    outs = take(7)
    vec, d_prompt, mixed_out, grad_out = take(4)
    classes = [take(7) for _ in range(3)]
    r1, r2, mixed_in, turned, grad_src, grad_in, vb, vz, dres = take(9)
    fold_sems = take(11)
    lds, hs, gs, gr, fs, fr, a2s, a2r, a2l, vs_, vr_, free = take(12)
    A, T, W = n // 4, dm.shape[0], dm.shape[1]
    half, rows, KW = group // 2, r1.shape[2], k_rot.shape[1]
    FW, QW = act.shape[1], attended.shape[1]
    bits = R.bit_length() - 1
    rep, a, b, c = position(n)
    h = rep % 2
    rank = lambda a, b, c: (a * 2 + b) * 2 + c
    me = rank(a, b, c)
    first, slot = (me // group) * half, (me // 2) % half
    flip = lambda bit: (rep + (1 << bit) - 2 * (1 << bit) * ((rep // (1 << bit)) % 2), me)
    meet([(rep, (me + d) % n) for d in range(1, n)] + [flip(k) for k in range(bits)])

    lane = lambda j, w: pl.ds(pl.multiple_of(j * w, w), w)
    heads = QUERY_HEADS // KEY_VALUE_HEADS
    loads = iter(range(lds.shape[0]))

    def fetch(src, dst):
        q = pltpu.make_async_copy(src, dst, lds.at[next(loads)])
        q.start()
        return q

    S = turned.shape[1]

    trips = (a2s, a2r, a2l)
    spread_copies = lambda src, dst, k: slot_spread(n, src, dst, trips, k, (rep, me))
    collect_copies = lambda src, dst, k: slot_collect(n, src, dst, trips, k, (rep, me))

    def reorder(src, dst):
        def put(j, _):
            s = index[j]
            dst[j // S, j % S] = src[s // S, s % S]
            return 0

        lax.fori_loop(0, n * S, put, 0)

    mixed_spread = spread_copies(mixed, mixed_in, 0)
    grad_spread, grad_collect = spread_copies(grad_src, grad_in, 2), collect_copies(turned, grad_out, 3)

    units = []

    def unit(cls, k, g, out, cols, landing=None):
        units.append(Fold(n, R, (rep, a, b, c, h), g, (classes[cls], k, k if landing is None else landing), outs[out], cols, fold_sems, len(units)))
        return units[-1]

    done = [0] * 6

    noted = [None]

    def run(f):
        f() if noted[0] is None else noted[0].append(f)

    def note(f):
        noted[0] = []
        f()
        fs_, noted[0] = noted[0], None
        return fs_

    def at_block(q, lists):
        for k, fs_ in enumerate(lists):
            if fs_:
                pl.when(q == k)(lambda fs_=fs_: [f() for f in fs_] and None)

    def e1(upto=None):
        while done[0] < (done[0] + 1 if upto is None else upto):
            run(partial(units[done[0]].step, 1))
            done[0] += 1
            if upto is None:
                break

    def tick(count=1, lag=2):
        for _ in range(count):
            before = list(done)
            if done[1] < before[0]:
                run(partial(units[done[1]].go, 2))
                done[1] += 1
            for k in range(2, 6):
                if before[k - 1] - done[k] >= lag:
                    run(partial(units[done[k]].step, k))
                    done[k] += 1

    n_down, n_ff, n_out = W // UD, FW // UF, W // UO
    V = pltpu.VMEM
    rh = lambda k: classes[k][0].shape[-2]
    AT, QT = FW // A, QW // A

    def down(act_c, act_t, g_down, dm_v):
        got = fetch(dm, dm_v)
        piece = lambda i: pltpu.make_async_copy(act.at[:, lane(i, AT)], act_c.at[i % 2], hs.at[i % 2, 0])
        piece(jnp.int32(0)).start()
        begin_all(mixed_spread)
        got.wait()

        def down_part(i, _):
            pl.when(i + 1 < A)(lambda: piece(i + 1).start())
            piece(i).wait()
            act_t[...] = act_c[i % 2].T

            def down_tile(j, _):
                y = mm(act_t[...], dm_v[:, lane(j, UD)], 1, 0).astype(bf16)
                g_down[j, i] = y.reshape(g_down.shape[2:])
                return 0

            return lax.fori_loop(0, n_down, down_tile, 0)

        lax.fori_loop(0, A, down_part, 0)
        for u in range(n_down):
            unit(0, u, g_down.at[u], 0, pl.ds(u * UD, UD)).begin()
        for u in range(n_down):
            e1()

    pl.run_scoped(down, V((2, T, AT), bf16), V((AT, T), bf16), V((n_down, A, 2, 2, 2, rh(0), UD), bf16), V((T, W), bf16))
    tick(*PLAN[0])
    RB = 32
    block = lambda j: pl.ds(pl.multiple_of(j * RB, RB), RB)

    def norm_back(value, gain, grad):
        r = lax.rsqrt(jnp.mean(value * value, axis=-1, keepdims=True) + norm_epsilon)
        u = value * r
        t = grad * gain
        return r * (t - u * jnp.mean(t * u, axis=-1, keepdims=True)), jnp.sum(grad * u, axis=0, keepdims=True)

    def persistent(dq, dkr, dvl):
        def after_mlp(drl):
            pl.run_scoped(partial(mlp, drl), V((4, A, 2, 2, 2, rh(1), UF), bf16), V((2, UF, W), bf16), V((2, W, UF), bf16), V((2, W, UF), bf16), V((2, T, UF), bf16),
                          V((2, T, UF), bf16), V((T, UF), bf16), V((T, UF), bf16), V((W, T), bf16), V((T, W), bf16), V((T, W), bf16), V((T, W), f32))
            pl.run_scoped(partial(out_grad, drl), V((2, T, QT), bf16), V((QT, T), bf16), V((n_out, A, 2, 2, 2, rh(2), UO), bf16))
            wait_all(mixed_spread)
            reorder(mixed_in, turned)
            mixed_collect = collect_copies(turned, mixed_out, 1)
            begin_all(mixed_collect)
            pl.run_scoped(partial(attention, drl, dq, dkr, dvl), V((half, 2, rows, KW), bf16), V((half, 2, rows, KW), bf16), V((2, PROMPT_LENGTH, HEAD_SIZE), bf16),
                          V((2, PROMPT_LENGTH, HEAD_SIZE), bf16), V((2, heads * HEAD_SIZE, T), bf16), V((2, T, heads * HEAD_SIZE), bf16), V((2, heads * HEAD_SIZE, W), bf16),
                          V((T, KW), bf16), V((T, KW), bf16))
            wait_all(mixed_collect)

        pl.run_scoped(after_mlp, V((T, W), bf16))
        pl.run_scoped(partial(weights_back, dq, dkr, dvl), V((2, 256, QW), bf16), V((2, 256, KW), bf16), V((2, 256, KW), bf16), V((T, W), bf16), V((W, T), bf16),
                      V((T, KW), f32), V((T, KW), bf16), V((4, A, 2, 2, 2, rh(1), UF), bf16), V((T, W), f32))

    def mlp(drl, g_ff, wd_c, wg_c, wu_c, gate_c, up_c, dg_c, du_c, h2_t, h2_v, dm_v, dhid):
        got = [fetch(h2, h2_v), fetch(dm, dm_v)]

        def fetch_ff(q):
            cols, s = lane(q, UF), q % 2
            moves = ((wd.at[cols], wd_c), (gate.at[:, cols], gate_c), (up.at[:, cols], up_c), (wg.at[:, cols], wg_c), (wu.at[:, cols], wu_c))
            return [pltpu.make_async_copy(src, dst.at[s], hs.at[s, k]) for k, (src, dst) in enumerate(moves)]

        for f in fetch_ff(jnp.int32(0)):
            f.start()
        got_resid = fetch(resid, dres)
        for f in got:
            f.wait()
        h2_t[...] = h2_v[...].T
        dhid[...] = jnp.zeros_like(dhid)
        free_slot, begun, after = ([], []), ([], []), []
        for q in range(n_ff):
            for k in range(2):
                free_slot[k].append(note(lambda: e1(len(units) - 1)))
                unit(1, 2 * q + k, g_ff.at[(2 * q + k) % 4], 1 + k, pl.ds(q * UF, UF))
                begun[k].append([units[-1].begin])
            after.append(note(partial(tick, *PLAN[1 + q])))

        def ff_block(q, _):
            s = q % 2

            @pl.when(q + 1 < n_ff)
            def _():
                for f in fetch_ff(q + 1):
                    f.start()

            for f in fetch_ff(q):
                f.wait()

            def act_tile(j, _):
                cols = lane(j, 256)
                g, u = gate_c[s, :, cols].astype(f32), up_c[s, :, cols].astype(f32)
                da = mm(dm_v[...], wd_c[s, lane(j, 256), :], 1, 1)
                sg = 1.0 / (1.0 + jnp.exp(-g))
                du_c[:, cols] = (da * (g * sg)).astype(bf16)
                dg_c[:, cols] = (da * u * (sg * (1.0 + g * (1.0 - sg)))).astype(bf16)
                return 0

            lax.fori_loop(0, UF // 256, act_tile, 0)
            for k, d in enumerate((dg_c, du_c)):
                at_block(q, free_slot[k])

                def ff_tile(j, _):
                    y = mm(h2_t[...], d[:, lane(j, 256)], 1, 0).astype(bf16)
                    g_ff[(2 * q + k) % 4, :, :, :, :, :, lane(j, 256)] = y.reshape(g_ff.shape[1:6] + (256,))
                    return 0

                lax.fori_loop(0, UF // 256, ff_tile, 0)
                at_block(q, begun[k])

            def hid_tile(j, _):
                cols = lane(j, 256)
                dhid[:, cols] += mm(dg_c[...], wg_c[s, cols, :], 1, 1) + mm(du_c[...], wu_c[s, cols, :], 1, 1)
                return 0

            lax.fori_loop(0, W // 256, hid_tile, 0)
            at_block(q, after)
            return 0

        lax.fori_loop(0, n_ff, ff_block, 0)
        while done[0] < len(units):
            e1()
        got_resid.wait()

        def second_norm(j, total):
            d, gg = norm_back(dres[block(j), :], gain2[...], dhid[block(j), :])
            d = dm_v[block(j), :].astype(f32) + d
            dres[block(j), :] = d
            drl[block(j), :] = d.astype(bf16)
            return total + gg

        g2 = lax.fori_loop(0, T // RB, second_norm, jnp.zeros((1, W), f32))
        for k in range(W // 128):
            vec[W // 128 + k:W // 128 + k + 1, :] = g2[:, k * 128:(k + 1) * 128]

    def out_grad(drl, att_c, att_t, g_out):
        piece = lambda i: pltpu.make_async_copy(attended.at[:, lane(i, QT)], att_c.at[i % 2], hs.at[i % 2, 0])
        piece(jnp.int32(0)).start()

        def out_part(i, _):
            pl.when(i + 1 < A)(lambda: piece(i + 1).start())
            piece(i).wait()
            att_t[...] = att_c[i % 2].T

            def out_tile(j, _):
                y = mm(att_t[...], drl[:, lane(j, UO)], 1, 0).astype(bf16)
                g_out[j, i] = y.reshape(g_out.shape[2:])
                return 0

            return lax.fori_loop(0, n_out, out_tile, 0)

        lax.fori_loop(0, A, out_part, 0)
        for u in range(n_out):
            unit(2, u, g_out.at[u], 3, pl.ds(u * UO, UO)).begin()
        while done[0] < len(units):
            e1()
        tick(*PLAN[7])

    def attention(drl, dq, dkr, dvl, dk, dv, ks_c, vs_c, q_c, att_c, wo_c, kr_v, v_v):
        others = [fetch(k_rot, kr_v), fetch(v, v_v)]
        pair = lambda j: lane(j, heads * HEAD_SIZE)

        def head_copies(j):
            s = j % 2
            moves = [(ks.at[:, lane(j, HEAD_SIZE)], ks_c), (vs.at[:, lane(j, HEAD_SIZE)], vs_c), (q_rot.at[pair(j), :], q_c),
                     (attended.at[:, pair(j)], att_c), (wo.at[pair(j), :], wo_c)]
            return [pltpu.make_async_copy(src, dst.at[s], hs.at[s, k]) for k, (src, dst) in enumerate(moves)]

        for q in head_copies(jnp.int32(0)):
            q.start()
        for q in others:
            q.wait()
        scale = HEAD_SIZE ** -0.5
        plus = lambda p, q: q if p is None else p + q

        def head(j, gain_grad):
            @pl.when(j + 1 < KEY_VALUE_HEADS)
            def _():
                for q in head_copies(j + 1):
                    q.start()

            for q in head_copies(j):
                q.wait()
            at = j % 2
            kl = lane(j, HEAD_SIZE)
            kb, vb_ = ks_c[at], vs_c[at]
            dkp = dvp = dks = dvs = None
            do_pair = mm(drl[...], wo_c[at], 1, 1)
            out_pair = att_c[at].astype(f32)
            for g in range(heads):
                sl = slice(g * HEAD_SIZE, (g + 1) * HEAD_SIZE)
                q = q_c[at, sl, :]
                do = do_pair[:, sl].astype(bf16)
                delta = jnp.sum((do.astype(f32) * out_pair[:, sl]).T, axis=0, keepdims=True)
                log_total = lse[j, g:g + 1, :]
                parts = []
                for suffix in range(2):
                    part = slice(rows, None) if suffix else slice(0, rows)
                    qp, dop, lp, dp = q[:, part], do[part], log_total[:, part], delta[:, part]
                    pieces = [(kb, vb_, None if suffix else past[...])]
                    if suffix:
                        pieces.append((kr_v[rows:, kl], v_v[rows:, kl], inside[...]))
                    total = None
                    for i, (kk, vv, bias) in enumerate(pieces):
                        s = mm(kk, qp, 1, 0) * (scale * LOG2E) - lp
                        p = jnp.exp2(s if bias is None else s + bias)
                        ds = (p * (mm(vv, dop, 1, 1) - dp)).astype(bf16)
                        gv, gk = mm(p.astype(bf16), dop, 1, 0), mm(ds, qp, 1, 1)
                        total = plus(total, mm(kk, ds, 0, 0))
                        if i:
                            dks, dvs = plus(dks, gk), plus(dvs, gv)
                        else:
                            dkp, dvp = plus(dkp, gk), plus(dvp, gv)
                    parts.append(total)
                d = jnp.concatenate(parts, axis=1) * scale
                m = HEAD_SIZE // 2
                cs, sn = cos[...], sin[...]
                dy = jnp.concatenate([d[:m] * cs + d[m:] * sn, d[m:] * cs - d[:m] * sn], axis=0)
                qf = q.astype(f32)
                u = jnp.concatenate([qf[:m] * cs + qf[m:] * sn, qf[m:] * cs - qf[:m] * sn], axis=0) / q_gain[:, 0:1]
                gg = dy * u
                for t in range(T // 128):
                    gain_grad = gain_grad + gg[:, t * 128:(t + 1) * 128]
                dy = dy * q_gain[:, 0:1]
                dx = rs_q[j, g:g + 1, :] * (dy - u * jnp.mean(dy * u, axis=0, keepdims=True))
                dq[:, lane(j * heads + g, HEAD_SIZE)] = dx.T.astype(bf16)
            dk[:, :, :, kl] = (dkp * scale).astype(bf16).reshape(half, 2, rows, HEAD_SIZE)
            dv[:, :, :, kl] = dvp.astype(bf16).reshape(half, 2, rows, HEAD_SIZE)
            dkr[rows:, kl] = dks * scale
            dvl[rows:, kl] = dvs.astype(bf16)
            for k in range(KEY_VALUE_HEADS - 1):
                if PLAN[8 + k][0]:
                    pl.when(j == k)(partial(tick, *PLAN[8 + k]))
            return gain_grad

        gain_grad = lax.fori_loop(0, KEY_VALUE_HEADS, head, jnp.zeros((HEAD_SIZE, 128), f32))
        vec[2 * W // 128:2 * W // 128 + 1, :] = jnp.sum(gain_grad.T, axis=0, keepdims=True)
        grads = [dk, dv]
        home = lambda s, c: (rep, (first + s) * 2 + c)

        def to_sibling(i, d):
            return remote(grads[i].at[(slot + d) % half, 1 - c], r1.at[i, d], gs.at[i, d], gr.at[i, d], home(slot, 1 - c))

        order = list(range(1, half)) + [0]
        for d in order:
            for i in range(2):
                to_sibling(i, d).start()
        for d in order:
            for i in range(2):
                to_sibling(i, d).wait_recv()

                def one(j, _):
                    r1[i, d, block(j)] = (grads[i][(slot + d) % half, c, block(j)].astype(f32) + r1[i, d, block(j)].astype(f32)).astype(bf16)
                    return 0

                lax.fori_loop(0, rows // RB, one, 0)
                if d:
                    across(i, d).start()
        for d in order:
            for i in range(2):
                to_sibling(i, d).wait_send()
        tick(*PLAN[15])

    def across(i, d):
        return remote(r1.at[i, d], r2.at[i, d - 1], fs.at[i, d - 1], fr.at[i, d - 1], (rep, (first + (slot + d) % half) * 2 + c))

    def weights_back(dq, dkr, dvl, wq_c, wk_c, wv_c, hid_v, hid_t, kp_v, dkl, g_qkv, dhid):
        got = [fetch(hidden, hid_v), fetch(k_pre, kp_v)]
        tiles = W // 256
        fetch_q = lambda j: fetch(wq.at[pl.ds(j * 256, 256)], wq_c.at[j % 2])
        fetch_kv = lambda j, s: [fetch(wk.at[pl.ds(j * 256, 256)], wk_c.at[s]), fetch(wv.at[pl.ds(j * 256, 256)], wv_c.at[s])]
        q_tiles, kv_tiles = [fetch_q(0), fetch_q(1)], [fetch_kv(0, 0), fetch_kv(1, 1)]
        got[0].wait()
        hid_t[...] = hid_v[...].T
        got_x = fetch(x, hid_v)
        count = [0]
        first_ff = n_down
        while done[2] < first_ff + (QW + 2 * KW) // UF:
            tick()
        for f in units[first_ff:first_ff + (QW + 2 * KW) // UF]:
            f.sent(2)
        pl.semaphore_signal(free, inc=1, device_id=(rep, rank(a, b, 1 - c)), device_id_type=MESH)
        pl.semaphore_wait(free, 1)

        def grad_units(d, out, width):
            base, begun = count[0], []
            for u in range(width // UF):
                unit(1, 2 * n_ff + base + u, g_qkv.at[(base + u) % 4], out, pl.ds(u * UF, UF), base + u)
                begun.append([units[-1].begin])
            count[0] += width // UF

            def tile(t, _):
                u, j = t // (UF // 256), t % (UF // 256)
                y = mm(hid_t[...], d[:, lane(t, 256)], 1, 0).astype(bf16)
                g_qkv[(base + u) % 4, :, :, :, :, :, lane(j, 256)] = y.reshape(g_qkv.shape[1:6] + (256,))

                @pl.when(j == UF // 256 - 1)
                def _():
                    at_block(u, begun)

                return 0

            lax.fori_loop(0, width // 256, tile, 0)

        grad_units(dq, 4, QW)
        for u in range(QW // UF):
            e1()
        tick(*PLAN[16])
        got[1].wait()

        def key_head(part, j, total):
            lanes = lane(j, HEAD_SIZE)
            y = kp_v[part, lanes]
            r = lax.rsqrt(jnp.mean(y * y, axis=-1, keepdims=True) + norm_epsilon)
            u = y * r
            dy = dkr[part, lanes]
            dy = dy * cos_r[part, :] - pltpu.roll(dy, HEAD_SIZE // 2, 1) * sin_r[part, :]
            total = total + jnp.sum(dy * u, axis=0, keepdims=True)
            dy = dy * k_gain[...]
            dkl[part, lanes] = (r * (dy - u * jnp.mean(dy * u, axis=-1, keepdims=True))).astype(bf16)
            return total

        def first_norm(j, carry):
            total, square = carry
            d, gg = norm_back(hid_v[block(j), :].astype(f32), gain1[...], dhid[block(j), :])
            d = dres[block(j), :] + d
            dres[block(j), :] = d
            return total + gg, square + jnp.sum(valid[block(j), :] * d * d, axis=0, keepdims=True)

        ours, theirs = pl.ds(rows, T - rows), pl.ds(0, rows)
        gk = lax.fori_loop(0, KEY_VALUE_HEADS, partial(key_head, ours), jnp.zeros((1, HEAD_SIZE), f32))
        for j in range(tiles):
            cols = pl.ds(j * 256, 256)
            q_tiles[j].wait()
            for f in kv_tiles[j]:
                f.wait()
            dhid[:, cols] = mm(dq[...], wq_c[j % 2], 1, 1)
            dhid[ours, cols] += mm(dkl[ours, :], wk_c[j % 2], 1, 1) + mm(dvl[ours, :], wv_c[j % 2], 1, 1)
            if j + 2 < tiles:
                q_tiles.append(fetch_q(j + 2))
            kv_tiles.append(fetch_kv((j + 2) % tiles, j % 2))
        got_x.wait()
        zero = jnp.zeros((1, W), f32)
        g1, square = lax.fori_loop(rows // RB, T // RB, first_norm, (zero, zero))
        width = CONTINUATION_LEN // n
        step = max(width, 8)

        def pack(j, _):
            y = dres[pl.ds(pl.multiple_of(rows + j * step, step), step), :].astype(bf16)
            for k in range(step // width):
                i = j * (step // width) + k
                grad_src[i // n, i % n] = y[k * width:(k + 1) * width]
            return 0

        lax.fori_loop(0, S * CONTINUATION_LEN // step, pack, 0)
        begin_all(grad_spread)
        tick(*PLAN[17])
        for i in range(2):
            for d in range(1, half):
                across(i, d).wait_recv()

        def own_keys(j, _):
            t, u = r1[0, 0, block(j)].astype(f32), r1[1, 0, block(j)].astype(f32)
            for d in range(1, half):
                t, u = t + r2[0, d - 1, block(j)].astype(f32), u + r2[1, d - 1, block(j)].astype(f32)
            dkr[block(j), :] = t
            dvl[block(j), :] = u.astype(bf16)
            return 0

        lax.fori_loop(0, rows // RB, own_keys, 0)
        grad_units(dvl, 6, KW)
        gk = lax.fori_loop(0, KEY_VALUE_HEADS, partial(key_head, theirs), gk)
        vec[2 * W // 128 + 1:2 * W // 128 + 2, :] = gk
        grad_units(dkl, 5, KW)
        while done[0] < len(units):
            e1()
        tick(*PLAN[18])
        wait_all(grad_spread)
        reorder(grad_in, turned)
        begin_all(grad_collect)
        for j in range(tiles):
            cols, s = pl.ds(j * 256, 256), (tiles + j) % 2
            for f in kv_tiles[tiles + j]:
                f.wait()
            dhid[theirs, cols] += mm(dkl[theirs, :], wk_c[s], 1, 1) + mm(dvl[theirs, :], wv_c[s], 1, 1)
            if j + 2 < tiles:
                kv_tiles.append(fetch_kv(j + 2, s))
        tick(*PLAN[19])
        g1, square = lax.fori_loop(0, rows // RB, first_norm, (g1, square))
        for k in range(W // 128):
            vec[k:k + 1, :] = g1[:, k * 128:(k + 1) * 128]
        place = lax.broadcasted_iota(jnp.int32, (1, 128), 1)
        row = jnp.zeros((1, 128), f32)
        whole = lambda y: jnp.sum(jnp.sum(y, axis=0, keepdims=True), axis=1, keepdims=True)
        for k, y in enumerate((sums[0:1, :], sums[1:2, :], square, valid[...])):
            row = jnp.where(place == k, whole(y), row)
        vec[2 * W // 128 + 2:2 * W // 128 + 3, :] = row
        vec[2 * W // 128 + 3:, :] = jnp.zeros((vec.shape[0] - 2 * W // 128 - 3, 128), f32)

    pl.run_scoped(persistent, V((T, QW), bf16), V((T, KW), f32), V((T, KW), bf16))
    for i in range(2):
        for d in range(1, half):
            across(i, d).wait_send()

    prompt_out = fetch(dres.at[pl.ds(0, rows)], d_prompt)
    tick(2, 1)
    rounds = [(rep, rank(a, b, 1 - c)), (rep, rank(a, 1 - b, c))] + [flip(k) for k in range(bits)]
    vb[0] = vec[...]
    for k, to in enumerate(rounds):
        q = remote(vb.at[2 * k], vb.at[2 * k + 1], vs_.at[k], vr_.at[k], to)
        q.start()
        q.wait()
        vb[2 * k + 2] = vb[2 * k] + vb[2 * k + 1]
        tick(2, 1)
    last, nr = 2 * len(rounds), len(rounds)
    zs = [remote(vb.at[last], vz.at[a], vs_.at[nr + d - 1], vr_.at[nr + d - 1], (rep, rank((a + d) % A, b, c))) for d in range(1, A)]
    for q in zs:
        q.start()
    vz[a] = vb[last]
    for q in zs:
        q.wait()
    total = vz[0]
    for k in range(1, A):
        total = total + vz[k]
    vec[...] = total
    while done[5] < len(units):
        tick(lag=1)
    wait_all(grad_collect)
    prompt_out.wait()
    for f in units:
        f.end()


def backward(index, mixed, dm, h2, act, gate, up, resid, wd, wg, wu, wo, attended, q_rot, lse, rs_q, ks, vs, k_rot, v, k_pre, wq, wk, wv, hidden, x,
             k_gain, q_gain, cos_r, sin_r, cos, sin, past, inside, valid, gain1, gain2, sums, rows, n, R, cid):
    group = PROMPT_LENGTH // rows
    half, A, (T, W), bits = group // 2, n // 4, dm.shape, R.bit_length() - 1
    FW, QW, KW = act.shape[1], attended.shape[1], k_rot.shape[1]
    UD, UF, UO = 256, 512, 512
    S = mixed.shape[0]
    V, D = pltpu.VMEM, pltpu.SemaphoreType.DMA
    shape = jax.ShapeDtypeStruct
    vm, hbm, sm = pl.BlockSpec(memory_space=pltpu.VMEM), pl.BlockSpec(memory_space=pl.ANY), pl.BlockSpec(memory_space=pltpu.SMEM)
    rh = lambda w: w.shape[0] // (2 * n)
    out_shape = [shape((2, rh(w), w.shape[1]), bf16) for w in (wd, wg, wu, wo, wq, wk, wv)]
    vec_rows = 2 * W // 128 + 8
    out_shape += [shape((vec_rows, 128), f32), shape((rows, W), f32), shape(mixed.shape, bf16), shape(mixed.shape, bf16)]
    scratch = []
    for count, r, w in ((W // UD, rh(wd), UD), (2 * (FW // UF) + (QW + 2 * KW) // UF, rh(wg), UF), (W // UO, rh(wo), UO)):
        k0 = fold_split(r)
        k1 = max(r - k0, 8)
        landing = 2 * (FW // UF) if w == UF and r == rh(wg) else count
        scratch += [V((landing, A, 2, 2, r, w), bf16), V((count, A, 2, k0, w), bf16), V((count, A, 2, k1, w) if k0 < r else (1, 1, 1, 8, 128), bf16), V((count, A, r, w), bf16),
                    V((count, A - 1, r, w), bf16), V((count, bits, r, w), bf16), V((count, bits, r, w), bf16)]
    m = W // UD + 2 * (FW // UF) + (QW + 2 * KW) // UF + W // UO
    turned = (n, S) + mixed.shape[2:]
    kv = (2, half, rows, KW)
    scratch += [V(kv, bf16), V((2, max(half - 1, 1), rows, KW), bf16), V(turned, bf16), V(turned, bf16), V(mixed.shape, bf16), V(turned, bf16),
                V((2 * (2 + bits) + 1, vec_rows, 128), f32), V((A, vec_rows, 128), f32), V((T, W), f32)]
    scratch += [D((m,)), D((m,)), D((m, 2)), D((m, 2)), D((m, 2)), D((m, 2)), D((m, A - 1)), D((m, A - 1)), D((m, bits)), D((m, bits)), D((m, 2))]
    scratch += [D((2 * A + 5 * (FW // UF) + 32,)), D((2, 5)), D((2, half)), D((2, half)), D((2, max(half - 1, 1))), D((2, max(half - 1, 1))), D((4, n - 1)), D((4, n - 1)), D((4,)),
                D((2 + bits + A - 1,)), D((2 + bits + A - 1,)), pltpu.SemaphoreType.REGULAR]
    hbm_in = [mixed, dm, h2, act, gate, up, resid, wd, wg, wu, wo, attended, q_rot, lse, rs_q, ks, vs, k_rot, v, k_pre, wq, wk, wv, hidden, x]
    in_vmem = {13, 14}
    res = pl.pallas_call(
        partial(backward_kernel, n, R, group, UD, UF, UO),
        out_shape=out_shape,
        in_specs=[sm] + [vm if k in in_vmem else hbm for k in range(len(hbm_in))] + [vm] * 12,
        out_specs=[hbm] * 7 + [vm] + [hbm] * 3,
        scratch_shapes=scratch,
        compiler_params=pltpu.CompilerParams(collective_id=cid, has_side_effects=True, vmem_limit_bytes=63 << 20),
        name="backward",
    )(index, *hbm_in, k_gain, q_gain, cos_r, sin_r, cos, sin, past, inside, valid, gain1, gain2, sums)
    return [r.reshape(-1, r.shape[-1]) for r in res[:7]], res[7], res[8], res[9], res[10]


def per_device(
    prompt_rows,
    suffix_rows,
    assignment,
    lengths,
    attention_gain,
    query_weight,
    key_matrix,
    value_matrix,
    query_gain,
    key_norm_gain,
    out_weight,
    mlp_gain,
    gate_weight,
    up_weight,
    down_weight,
    prompt_cotangent,
    suffix_cotangent,
):
    n, R = lax.axis_size("fsdp"), lax.axis_size("rep")
    rank = lax.axis_index("fsdp")
    rows = prompt_rows.shape[0]
    suffix = suffix_rows.shape[0]
    S = suffix // CONTINUATION_LEN
    total = rows + suffix
    width = MODEL_WIDTH

    pad = lambda v: jnp.pad(v.astype(f32).reshape(-1), (0, 128 - v.size))
    tile = jnp.stack([pad(v) for v in (attention_gain, mlp_gain, query_gain, key_norm_gain, assignment, lengths)])
    tile = jnp.pad(tile, ((0, 2), (0, 0)))
    cut = lambda v: v.reshape(S, n, CONTINUATION_LEN // n, width)
    w_key, w_value, w_query, tiles, staged = gather(key_matrix, value_matrix, query_weight, tile, cut(suffix_rows), n, 0)
    gain_first = tiles[:, 0, : attention_gain.size].reshape(-1)
    gain_second = tiles[:, 1, : mlp_gain.size].reshape(-1)
    query_scale = tiles[:, 2, : query_gain.size].reshape(-1)
    key_scale = tiles[:, 3, : key_norm_gain.size].reshape(-1)

    owner = tiles[:, 4, :S].reshape(-1).astype(jnp.int32) // CONT
    slot_count = n * S
    ids = jnp.arange(slot_count, dtype=jnp.int32)
    ahead = (owner[None, :] < owner[:, None]) | ((owner[None, :] == owner[:, None]) & (ids[None, :] < ids[:, None]))
    place = jnp.sum(ahead.astype(jnp.int32), axis=1)
    hits = place[None, :] == ids[:, None]
    order = jnp.sum(jnp.where(hits, ids[None, :], 0), axis=1)
    slot_lengths = jnp.sum(jnp.where(hits, tiles[:, 5, :S].reshape(-1).astype(jnp.int32)[None, :], 0), axis=1)
    own_lengths = lax.dynamic_slice_in_dim(slot_lengths, rank * S, S)

    prompt_place = (rank * rows) % PROMPT_LENGTH + jnp.arange(rows, dtype=jnp.int32)
    suffix_place = jnp.arange(suffix, dtype=jnp.int32) % CONTINUATION_LEN
    suffix_slot = jnp.arange(suffix, dtype=jnp.int32) // CONTINUATION_LEN
    length_rows = jnp.repeat(own_lengths, CONTINUATION_LEN)
    suffix_valid = suffix_place < length_rows
    valid_rows = jnp.concatenate([jnp.ones((rows,), f32), suffix_valid.astype(f32)])
    token_positions = jnp.concatenate([prompt_place, PROMPT_LENGTH + suffix_place]).astype(f32)
    half = HEAD_SIZE // 2
    inverse = rope_theta ** (jnp.arange(half, dtype=f32) * (-2.0 / HEAD_SIZE))
    angles_t = inverse[:, None] * token_positions[None, :]
    cos_t, sin_t = jnp.cos(angles_t), jnp.sin(angles_t)
    cos_r, sin_r = cos_t.T, sin_t.T
    cos_rows = jnp.concatenate([cos_r, cos_r], axis=1)
    sin_rows = jnp.concatenate([-sin_r, sin_r], axis=1)
    past = jnp.where(jnp.arange(PROMPT_LENGTH, dtype=jnp.int32)[:, None] <= prompt_place[None, :], 0.0, masked_score).astype(f32)
    inside = jnp.where(
        (suffix_slot[:, None] == suffix_slot[None, :]) & (suffix_place[:, None] <= suffix_place[None, :]) & suffix_valid[:, None], 0.0, masked_score
    ).astype(f32)

    key_gain_row = key_scale.reshape(1, HEAD_SIZE)
    query_gain_col = jnp.broadcast_to(query_scale[:, None], (HEAD_SIZE, 128))
    (
        w_out, w_gate, w_up, w_down, moved_cotangent, gate_low, up_low, rows_low, hidden, attended, query_rot, key_pre, key_rot, values,
        prompt_keys, prompt_values, residual, hidden_two, act, mixed_low, lse, query_rs, sums,
    ) = forward(
        order, prompt_rows, staged, cut(suffix_cotangent), w_key, w_value, w_query, [out_weight, gate_weight, up_weight, down_weight], key_gain_row,
        query_gain_col, cos_rows, sin_rows, cos_t, sin_t, past, inside, valid_rows[:, None], gain_first[None, :], gain_second[None, :], n, 2,
    )
    moved_cotangent = moved_cotangent.reshape(suffix, width)
    d_mixed_low = jnp.concatenate([prompt_cotangent, moved_cotangent], 0) * valid_rows[:, None].astype(bf16)
    shards, vec_sum, prompt_grad, suffix_mixed, suffix_grad = backward(
        place, cut(mixed_low[rows:]), d_mixed_low, hidden_two, act, gate_low, up_low, residual, w_down, w_gate, w_up, w_out, attended, query_rot, lse, query_rs,
        prompt_keys, prompt_values, key_rot, values, key_pre, w_query, w_key, w_value, hidden, rows_low, key_gain_row, query_gain_col,
        cos_rows, sin_rows, cos_t, sin_t, past, inside, valid_rows[:, None], gain_first[None, :], gain_second[None, :], sums, rows, n, R, 3,
    )
    suffix_mixed, suffix_grad = suffix_mixed.reshape(suffix, width), suffix_grad.reshape(suffix, width)
    g_down, g_gate, g_up, g_out, g_query, g_key, g_value = [g.astype(f32) for g in shards]
    flat = vec_sum.reshape(-1)

    def mine(first, size, part):
        return lax.dynamic_slice_in_dim(flat[first : first + size], rank * part, part)

    g_first = mine(0, width, attention_gain.size)
    g_second = mine(width, width, mlp_gain.size)
    g_query_gain = mine(2 * width, HEAD_SIZE, query_gain.size)
    g_key_gain = mine(2 * width + HEAD_SIZE, HEAD_SIZE, key_norm_gain.size)
    stat_sums = flat[2 * width + 2 * HEAD_SIZE : 2 * width + 2 * HEAD_SIZE + 4]
    token_norms = jnp.sqrt(stat_sums[:3] / (stat_sums[3] * width))
    return (
        mixed_low[:rows],
        suffix_mixed,
        prompt_grad,
        suffix_grad.astype(f32),
        g_first,
        g_query,
        g_key,
        g_value,
        g_query_gain,
        g_key_gain,
        g_out,
        g_second,
        g_gate,
        g_up,
        g_down,
        token_norms,
    )


def solution(mesh):
    placed = (
        P(("rep", "fsdp"), None),
        P(("rep", "fsdp"), None),
        P("rep", "fsdp"),
        P("rep", "fsdp"),
        P("fsdp"),
        P("fsdp", None),
        P("fsdp", None),
        P("fsdp", None),
        P("fsdp"),
        P("fsdp"),
        P("fsdp", None),
        P("fsdp"),
        P("fsdp", None),
        P("fsdp", None),
        P("fsdp", None),
        P(("rep", "fsdp"), None),
        P(("rep", "fsdp"), None),
    )
    return jax.shard_map(
        per_device,
        mesh=mesh,
        in_specs=placed,
        out_specs=(
            P(("rep", "fsdp"), None),
            P(("rep", "fsdp"), None),
            P(("rep", "fsdp"), None),
            P(("rep", "fsdp"), None),
            P("fsdp"),
            P("fsdp", None),
            P("fsdp", None),
            P("fsdp", None),
            P("fsdp"),
            P("fsdp"),
            P("fsdp", None),
            P("fsdp"),
            P("fsdp", None),
            P("fsdp", None),
            P("fsdp", None),
            P(),
        ),
        check_vma=False,
    )
```
